32 devices in a mesh: seq: 8 (over z, y), feat: 4 (over x, core).
Axes of the slice: x: 2, y: 2, z: 4, core: 2. Of those that a mesh axis runs over, the one named last changes fastest.
Arguments:
- activations_in: bfloat16 [6144, 512], P('seq', 'feat'), may hold values from -6 to 6
- cotangent: bfloat16 [6144, 512], P('seq', 'feat'), may hold values from -6 to 6
- seq_start: int32 [16], P('seq'), may hold values from 0 to 768, as said below
- seq_length: int32 [16], P('seq'), may hold values from 0 to 768, as said below
- input_matrix: float32 [2, 512, 768], P(None, 'feat'), may hold values from -0.25 to 0.25
- output_matrix: float32 [2, 1536, 512], P(None, None, 'feat'), may hold values from -1.25 to 1.25
- gate_matrix: float32 [2, 512, 512], P(None, None, 'feat'), may hold values from -0.25 to 0.25
- feature_vectors: float32 [2, 4, 512], P(None, None, 'feat'), may hold values from 0.1 to 1.9
- state_vectors: float32 [2, 3, 384], replicated, may hold values from -20 to 20, as said below
- velocity_input: float32 [2, 512, 768], P(None, 'feat'), may hold values from -6 to 6
- velocity_output: float32 [2, 1536, 512], P(None, None, 'feat'), may hold values from -6 to 6
- velocity_gate: float32 [2, 512, 512], P(None, None, 'feat'), may hold values from -6 to 6
- velocity_feature: float32 [2, 4, 512], P(None, None, 'feat'), may hold values from -6 to 6
- velocity_state: float32 [2, 3, 384], replicated, may hold values from -6 to 6
- average_input: float32 [2, 512, 768], P(None, 'feat'), may hold values from -0.25 to 0.25
- average_output: float32 [2, 1536, 512], P(None, None, 'feat'), may hold values from -1.25 to 1.25
- average_gate: float32 [2, 512, 512], P(None, None, 'feat'), may hold values from -0.25 to 0.25
- average_feature: float32 [2, 4, 512], P(None, None, 'feat'), may hold values from 0.1 to 1.9
- average_state: float32 [2, 3, 384], replicated, may hold values from -3 to 1
Outputs:
- activations_out: float32 [6144, 512], P('seq', 'feat')
- input_gradient: float32 [6144, 512], P('seq', 'feat')
- gradient_input: float32 [2, 512, 768], P(None, 'feat')
- gradient_output: float32 [2, 1536, 512], P(None, None, 'feat')
- gradient_gate: float32 [2, 512, 512], P(None, None, 'feat')
- gradient_feature: float32 [2, 4, 512], P(None, None, 'feat')
- gradient_state: float32 [2, 3, 384], replicated
- updated_input: float32 [2, 512, 768], P(None, 'feat')
- updated_output: float32 [2, 1536, 512], P(None, None, 'feat')
- updated_gate: float32 [2, 512, 512], P(None, None, 'feat')
- updated_feature: float32 [2, 4, 512], P(None, None, 'feat')
- state_change: float32 [2, 3, 384], replicated
- momentum_input: float32 [2, 512, 768], P(None, 'feat')
- momentum_output: float32 [2, 1536, 512], P(None, None, 'feat')
- momentum_gate: float32 [2, 512, 512], P(None, None, 'feat')
- momentum_feature: float32 [2, 4, 512], P(None, None, 'feat')
- momentum_state: float32 [2, 3, 384], replicated
- smoothed_input: float32 [2, 512, 768], P(None, 'feat')
- smoothed_output: float32 [2, 1536, 512], P(None, None, 'feat')
- smoothed_gate: float32 [2, 512, 512], P(None, None, 'feat')
- smoothed_feature: float32 [2, 4, 512], P(None, None, 'feat')
- smoothed_state: float32 [2, 3, 384], replicated
The draws below stay inside these ranges and needn't reach their ends.
Inputs may be any that keep to these rules, and one draw needn't show every extreme that they name: `seq_length`: sequences of a device lie in its own buffer, ordered and without intersection; one device holds a single sequence of 768 tokens and an empty slot, every other device two sequences of 192 to 384 tokens. `seq_start`: positions within a device's buffer; a slot of length zero starts at 768. `state_vectors`: rows hold log(-Re Lambda), Im Lambda and the log timestep.
All inputs are finite; a program needn't handle non-finite values.
Results may differ from the reference program's by a relative error of at most 0.012.
The reference program's roundings to bfloat16 on the way count: a program that leaves them out, or rounds other values in their place, can miss the bound.
Values may be sent and summed in bfloat16 or wider, within the bound.
A program may use at most 448 MiB of HBM per device.

```python
import math
import jax
import jax.numpy as jnp
from jax import lax

H = 512
P_SIZE = 384
LAYERS = 2
SLOTS = 2
TOK_DEV = 768
TOKENS = 6144
SEQS = 16


def layout(key):
    base = jax.random.fold_in(key, 11)
    keys = jax.random.split(base, 4)
    count = SEQS // SLOTS
    first = jax.random.randint(keys[0], (count,), TOK_DEV // 4, TOK_DEV // 2 + 1)
    second = jax.random.randint(keys[1], (count,), TOK_DEV // 4, TOK_DEV // 2 + 1)
    spare = TOK_DEV - first - second
    front = jax.random.randint(keys[2], (count,), 0, spare + 1)
    chosen = jax.random.randint(keys[3], (), 0, count)
    single = jnp.arange(count) == chosen
    margin = (spare - front) // 2
    first = jnp.where(single, TOK_DEV, first)
    second = jnp.where(single, 0, second)
    front = jnp.where(single, 0, front)
    margin = jnp.where(single, 0, margin)
    later = front + first + margin
    starts = jnp.stack([front, later], 1).reshape(-1).astype(jnp.int32)
    lengths = jnp.stack([first, second], 1).reshape(-1).astype(jnp.int32)
    return (starts, lengths)


def draw_seq_start(key, part):
    return layout(key)[0]


def draw_seq_length(key, part):
    return layout(key)[1]


def draw_state_vectors(key, part):
    keys = jax.random.split(jax.random.fold_in(key, 5), 3)
    shape = (LAYERS, P_SIZE)
    rate_log = jax.random.uniform(keys[0], shape, jnp.float32, math.log(0.2), 0.0)
    frequency = jax.random.uniform(keys[1], shape, jnp.float32, -20.0, 20.0)
    step_log = jax.random.uniform(keys[2], shape, jnp.float32, math.log(0.001), math.log(0.1))
    return jnp.stack([rate_log, frequency, step_log], 1)


def levels(rng, dims, cuts, low, top_value):
    def one(dim, blocks):
        heights = jax.random.uniform(jax.random.fold_in(jax.random.fold_in(rng, 6), dim), (blocks,), jnp.float32, low / len(cuts), top_value / len(cuts))
        return jnp.repeat(jnp.exp(heights), dims[dim] // blocks).reshape((-1,) + (1,) * (len(dims) - dim - 1))

    level = one(*cuts[0])
    for cut in cuts[1:]:
        level = level * one(*cut)
    return level


def scatter_about(stream_key, shape, scale, bound, cuts=(), kind=jnp.bfloat16):
    factor_of = levels(stream_key, shape, cuts, -0.22, 0.18) if cuts else 1.0
    entries = jax.random.normal(stream_key, shape, jnp.float32) * scale * factor_of
    return jnp.minimum(jnp.maximum(entries, -bound), bound).astype(kind)


def setup_inputs(seed: int = 0) -> dict:
    key_list = jax.random.split(jax.random.key(seed), 20)
    activations_in = scatter_about(key_list[0], (TOKENS, H), 1.0, 6.0, ((0, 8), (1, 4)))
    cotangent = scatter_about(key_list[1], (TOKENS, H), 1.0, 6.0, ((0, 8), (1, 4)))
    seq_start = draw_seq_start(jax.random.fold_in(key_list[19], 71), 0)
    seq_length = draw_seq_length(jax.random.fold_in(key_list[19], 71), 0)
    input_matrix = scatter_about(key_list[4], (LAYERS, H, 2 * P_SIZE), H ** -0.5, 0.25, ((1, 4),), jnp.float32)
    output_matrix = scatter_about(key_list[5], (LAYERS, 4 * P_SIZE, H), (max(4 * P_SIZE // 64, 1)) ** -0.5, 1.25, ((2, 4),), jnp.float32)
    gate_matrix = scatter_about(key_list[6], (LAYERS, H, H), H ** -0.5, 0.25, ((2, 4),), jnp.float32)
    feature_vectors = jnp.clip(1.0 + 0.18 * jax.random.normal(key_list[7], (LAYERS, 4, H), jnp.float32), 0.1, 1.9)
    state_vectors = draw_state_vectors(jax.random.fold_in(key_list[19], 71), 0)
    velocity_input = scatter_about(key_list[9], (LAYERS, H, 2 * P_SIZE), 1.0, 6.0, ((1, 4),), jnp.float32)
    velocity_output = scatter_about(key_list[10], (LAYERS, 4 * P_SIZE, H), 1.0, 6.0, ((2, 4),), jnp.float32)
    velocity_gate = scatter_about(key_list[11], (LAYERS, H, H), 1.0, 6.0, ((2, 4),), jnp.float32)
    velocity_feature = scatter_about(key_list[12], (LAYERS, 4, H), 1.0, 6.0, ((2, 4),), jnp.float32)
    velocity_state = scatter_about(key_list[13], (LAYERS, 3, P_SIZE), 1.0, 6.0, (), jnp.float32)
    average_input = scatter_about(key_list[14], (LAYERS, H, 2 * P_SIZE), H ** -0.5, 0.25, ((1, 4),), jnp.float32)
    average_output = scatter_about(key_list[15], (LAYERS, 4 * P_SIZE, H), (max(4 * P_SIZE // 64, 1)) ** -0.5, 1.25, ((2, 4),), jnp.float32)
    average_gate = scatter_about(key_list[16], (LAYERS, H, H), H ** -0.5, 0.25, ((2, 4),), jnp.float32)
    average_feature = jnp.clip(1.0 + 0.18 * jax.random.normal(key_list[17], (LAYERS, 4, H), jnp.float32), 0.1, 1.9)
    average_state = jnp.clip(jax.random.uniform(key_list[18], (LAYERS, 3, P_SIZE), jnp.float32, -3.0, 1.0), -3.0, 1.0)
    return {"activations_in": activations_in, "cotangent": cotangent, "seq_start": seq_start, "seq_length": seq_length, "input_matrix": input_matrix, "output_matrix": output_matrix, "gate_matrix": gate_matrix, "feature_vectors": feature_vectors, "state_vectors": state_vectors, "velocity_input": velocity_input, "velocity_output": velocity_output, "velocity_gate": velocity_gate, "velocity_feature": velocity_feature, "velocity_state": velocity_state, "average_input": average_input, "average_output": average_output, "average_gate": average_gate, "average_feature": average_feature, "average_state": average_state}


@jax.custom_vjp
def low(v):
    return lax.optimization_barrier(v.astype(jnp.bfloat16)).astype(jnp.float32)

@jax.custom_vjp
def low_back(v):
    return v

def low_keep(v):
    return (low(v), None)

def low_pass(kept, grad):
    return (grad,)

def back_keep(v):
    return (v, None)

def back_low(kept, grad):
    return (low(grad),)
low.defvjp(low_keep, low_pass)
low_back.defvjp(back_keep, back_low)
epsilon = 1e-05
momentum = 0.9
smoothing = 0.5
slow_rate = 0.02
main_rate = 0.05
weight_decay = 0.1
highest = lax.Precision.HIGHEST

def smooth(value):
    return jax.nn.gelu(value, approximate=False)

def combine(earlier, later):
    mult_real = later[0] * earlier[0] - later[1] * earlier[1]
    mult_imag = later[0] * earlier[1] + later[1] * earlier[0]
    add_real = later[0] * earlier[2] - later[1] * earlier[3] + later[2]
    add_imag = later[0] * earlier[3] + later[1] * earlier[2] + later[3]
    return (mult_real, mult_imag, add_real, add_imag)

def masks_of(starts, lengths, count):
    position = jnp.arange(count, dtype=jnp.int32)[:, None]
    begin = starts.astype(jnp.int32)[None, :]
    finish = begin + lengths.astype(jnp.int32)[None, :]
    inside = (position >= begin) & (position < finish)
    alive = jnp.any(inside, 1)
    opening = jnp.any(inside & (position == begin), 1)
    closing = jnp.any(inside & (position == finish - 1), 1)
    return (alive.astype(jnp.float32), (alive & ~opening).astype(jnp.float32), (alive & ~closing).astype(jnp.float32))

def scan_states(drive, state_row, alive, carry_prev, carry_next):
    width = state_row.shape[1]
    rate = -jnp.exp(state_row[0])
    frequency = state_row[1]
    timestep = jnp.exp(state_row[2])
    decay = jnp.exp(rate * timestep)
    angle = frequency * timestep
    pole_real = decay * jnp.cos(angle)
    pole_imag = decay * jnp.sin(angle)
    denom = rate * rate + frequency * frequency
    factor_real = ((pole_real - 1.0) * rate + pole_imag * frequency) / denom
    factor_imag = (pole_imag * rate - (pole_real - 1.0) * frequency) / denom
    drive_real = drive[:, :width]
    drive_imag = drive[:, width:]
    input_real = (drive_real * factor_real - drive_imag * factor_imag) * alive[:, None]
    input_imag = (drive_real * factor_imag + drive_imag * factor_real) * alive[:, None]
    ahead = lax.associative_scan(combine, (carry_prev[:, None] * pole_real, carry_prev[:, None] * pole_imag, input_real, input_imag), axis=0)
    behind = lax.associative_scan(combine, (carry_next[:, None] * pole_real, carry_next[:, None] * pole_imag, input_real, input_imag), reverse=True, axis=0)
    return jnp.concatenate([ahead[2], ahead[3], behind[2], behind[3]], 1)

def update(weight, gradient, velocity, average, rate, decay):
    adjusted = gradient + decay * weight
    velocity_new = momentum * velocity + adjusted
    change = -rate * (adjusted + momentum * velocity_new)
    weight_new = weight + change
    average_new = smoothing * average + (1.0 - smoothing) * weight_new
    return (weight_new, velocity_new, average_new, change)

def product(left, right):
    return jnp.dot(low(left), low(right), precision=highest, preferred_element_type=jnp.float32)

def one_layer(stream, masks, in_weight, out_weight, gate_weight, feature_row, state_row):
    center = lax.optimization_barrier(jnp.mean(stream, 1, keepdims=True))
    spread = stream - center
    unit = spread * lax.rsqrt(lax.optimization_barrier(jnp.mean(spread * spread, 1, keepdims=True)) + epsilon)
    normed = unit * feature_row[0] + feature_row[1]
    drive = low_back(product(normed, in_weight))
    states = scan_states(drive, state_row, masks[0], masks[1], masks[2])
    mixed = low_back(product(states, out_weight)) + feature_row[2] * normed
    act = smooth(mixed)
    pre = low_back(product(act, gate_weight) + feature_row[3])
    return stream + act * jax.nn.sigmoid(pre)

def forward(stream, in_all, out_all, gate_all, feature_all, state_all, starts, lengths):
    count = SEQS // SLOTS

    def per_block(item):
        block, first, sizes = item
        masks = masks_of(first, sizes, TOK_DEV)
        for layer in range(LAYERS):
            block = one_layer(block, masks, in_all[layer], out_all[layer], gate_all[layer], feature_all[layer], state_all[layer])
        return block
    out = lax.map(jax.checkpoint(per_block), (stream.reshape(count, TOK_DEV, H), starts.reshape(count, SLOTS), lengths.reshape(count, SLOTS)))
    return out.reshape(count * TOK_DEV, H)

def reference(activations_in, cotangent, seq_start, seq_length, input_matrix, output_matrix, gate_matrix, feature_vectors, state_vectors, velocity_input, velocity_output, velocity_gate, velocity_feature, velocity_state, average_input, average_output, average_gate, average_feature, average_state):
    count = SEQS // SLOTS
    inputs = activations_in.astype(jnp.float32)
    alive = jax.vmap(lambda first, sizes: masks_of(first, sizes, TOK_DEV)[0])(seq_start.reshape(count, SLOTS), seq_length.reshape(count, SLOTS)).reshape(-1)
    seed_grad = cotangent.astype(jnp.float32) * alive[:, None]

    def wrapped(stream, in_all, out_all, gate_all, feature_all, state_all):
        return forward(stream, in_all, out_all, gate_all, feature_all, state_all, seq_start, seq_length)
    result, pull = jax.vjp(wrapped, inputs, input_matrix, output_matrix, gate_matrix, feature_vectors, state_vectors)
    grads = pull(seed_grad)
    factor = 1.0 / math.sqrt(TOKENS)
    grad_in = grads[1] * factor
    grad_out = grads[2] * factor
    grad_gate = grads[3] * factor
    grad_feature = grads[4] * factor
    grad_state = grads[5] * factor
    new_in = update(input_matrix, grad_in, velocity_input, average_input, slow_rate, 0.0)
    new_out = update(output_matrix, grad_out, velocity_output, average_output, slow_rate, 0.0)
    new_gate = update(gate_matrix, grad_gate, velocity_gate, average_gate, main_rate, weight_decay)
    new_feature = update(feature_vectors, grad_feature, velocity_feature, average_feature, main_rate, weight_decay)
    new_state = update(state_vectors, grad_state, velocity_state, average_state, slow_rate, 0.0)
    return (result, grads[0], grad_in, grad_out, grad_gate, grad_feature, grad_state, new_in[0], new_out[0], new_gate[0], new_feature[0], new_state[3], new_in[1], new_out[1], new_gate[1], new_feature[1], new_state[1], new_in[2], new_out[2], new_gate[2], new_feature[2], new_state[2])
```

```python
import math

import jax
import jax.numpy as jnp
from jax import lax
from jax.experimental import pallas as pl
from jax.experimental.pallas import tpu as pltpu
from jax.sharding import PartitionSpec as P

epsilon = 1e-05
momentum = 0.9
smoothing = 0.5
slow_rate = 0.02
main_rate = 0.05
weight_decay = 0.1


def smooth(value):
    return jax.nn.gelu(value, approximate=False)


def masks_of(starts, lengths, count):
    position = jnp.arange(count, dtype=jnp.int32)[:, None]
    begin = starts[None, :]
    finish = begin + lengths[None, :]
    inside = (position >= begin) & (position < finish)
    alive = jnp.any(inside, 1)
    opening = jnp.any(inside & (position == begin), 1)
    closing = jnp.any(inside & (position == finish - 1), 1)
    return (
        alive.astype(jnp.float32),
        (alive & ~opening).astype(jnp.float32),
        (alive & ~closing).astype(jnp.float32),
    )


def coefficients(state_row):
    rate = -jnp.exp(state_row[0])
    frequency = state_row[1]
    timestep = jnp.exp(state_row[2])
    decay = jnp.exp(rate * timestep)
    angle = frequency * timestep
    pole_real = decay * jnp.cos(angle)
    pole_imag = decay * jnp.sin(angle)
    denom = rate * rate + frequency * frequency
    factor_real = ((pole_real - 1.0) * rate + pole_imag * frequency) / denom
    factor_imag = (pole_imag * rate - (pole_real - 1.0) * frequency) / denom
    return (pole_real, pole_imag, factor_real, factor_imag)


def recurrence_kernel(ma_ref, mb_ref, w_ref, xa_ref, xb_ref, out_ref):
    count = xa_ref.shape[0]
    width = w_ref.shape[1]
    w_re = w_ref[0:1, :]
    w_im = w_ref[1:2, :]

    def advance(h_re, h_im, keep, x_ref, row):
        h_re = h_re * keep
        h_im = h_im * keep
        new_re = w_re * h_re - w_im * h_im + x_ref[pl.ds(row, 1), pl.ds(0, width)]
        new_im = w_re * h_im + w_im * h_re + x_ref[pl.ds(row, 1), pl.ds(width, width)]
        return new_re, new_im

    def step(i, carry):
        a_re, a_im, b_re, b_im = carry
        up = i
        down = count - 1 - i
        a_re, a_im = advance(a_re, a_im, ma_ref[up], xa_ref, up)
        b_re, b_im = advance(b_re, b_im, mb_ref[down], xb_ref, down)
        out_ref[pl.ds(up, 1), pl.ds(0, width)] = a_re
        out_ref[pl.ds(up, 1), pl.ds(width, width)] = a_im
        out_ref[pl.ds(down, 1), pl.ds(2 * width, width)] = b_re
        out_ref[pl.ds(down, 1), pl.ds(3 * width, width)] = b_im
        return (a_re, a_im, b_re, b_im)

    zeros = jnp.zeros((1, width), jnp.float32)
    lax.fori_loop(0, count, step, (zeros, zeros, zeros, zeros), unroll=8)


def recurrence(ma, mb, w, xa, xb):
    count, double = xa.shape
    return pl.pallas_call(
        recurrence_kernel,
        out_shape=jax.ShapeDtypeStruct((count, 2 * double), jnp.float32),
        in_specs=[
            pl.BlockSpec(memory_space=pltpu.SMEM),
            pl.BlockSpec(memory_space=pltpu.SMEM),
            pl.BlockSpec(memory_space=pltpu.VMEM),
            pl.BlockSpec(memory_space=pltpu.VMEM),
            pl.BlockSpec(memory_space=pltpu.VMEM),
        ],
        out_specs=pl.BlockSpec(memory_space=pltpu.VMEM),
        cost_estimate=pl.CostEstimate(
            flops=20 * count * double, transcendentals=0, bytes_accessed=16 * count * double
        ),
    )(ma, mb, w, xa, xb)


def update(weight, gradient, velocity, average, rate, decay):
    adjusted = gradient + decay * weight
    velocity_new = momentum * velocity + adjusted
    change = -rate * (adjusted + momentum * velocity_new)
    weight_new = weight + change
    average_new = smoothing * average + (1.0 - smoothing) * weight_new
    return (weight_new, velocity_new, average_new, change)


def contract_rows(left, right):
    return lax.dot_general(
        left, right, (((0,), (0,)), ((), ())), preferred_element_type=jnp.float32
    )


def contract_cols(left, right):
    return lax.dot_general(
        left, right, (((1,), (1,)), ((), ())), preferred_element_type=jnp.float32
    )


def gather_feat(value, axis):
    return lax.all_gather(value, "feat", axis=axis, tiled=True)


def body(
    activations_in,
    cotangent,
    seq_start,
    seq_length,
    input_matrix,
    output_matrix,
    gate_matrix,
    feature_vectors,
    state_vectors,
    velocity_input,
    velocity_output,
    velocity_gate,
    velocity_feature,
    velocity_state,
    average_input,
    average_output,
    average_gate,
    average_feature,
    average_state,
):
    count = activations_in.shape[0]
    shard = activations_in.shape[1]
    layers = input_matrix.shape[0]
    width = state_vectors.shape[2]
    me = lax.axis_index("feat")
    offset = me * shard

    def mine(value):
        return lax.dynamic_slice_in_dim(value, offset, shard, axis=value.ndim - 1)

    alive, carry_prev, carry_next = masks_of(seq_start, seq_length, count)
    zero = jnp.zeros((1,), jnp.float32)
    after_next = jnp.concatenate([zero, carry_next[:-1]])
    before_prev = jnp.concatenate([carry_prev[1:], zero])

    in_all = gather_feat(input_matrix.astype(jnp.bfloat16), 1)
    out_all = gather_feat(output_matrix.astype(jnp.bfloat16), 2)
    gate_all = gather_feat(gate_matrix.astype(jnp.bfloat16), 2)
    feature_all = gather_feat(feature_vectors, 2)
    stream = gather_feat(activations_in, 1).astype(jnp.float32)

    saved = []
    for layer in range(layers):
        in_low = in_all[layer]
        out_low = out_all[layer]
        gate_low = gate_all[layer]
        feature_row = feature_all[layer]
        pole_re, pole_im, factor_re, factor_im = coefficients(state_vectors[layer])
        center = jnp.mean(stream, 1, keepdims=True)
        spread = stream - center
        scale = lax.rsqrt(jnp.mean(spread * spread, 1, keepdims=True) + epsilon)
        unit = spread * scale
        normed = unit * feature_row[0] + feature_row[1]
        normed_low = normed.astype(jnp.bfloat16)
        drive = jnp.dot(normed_low, in_low, preferred_element_type=jnp.float32)
        drive_re = drive[:, :width]
        drive_im = drive[:, width:]
        source = jnp.concatenate(
            [
                (drive_re * factor_re - drive_im * factor_im) * alive[:, None],
                (drive_re * factor_im + drive_im * factor_re) * alive[:, None],
            ],
            1,
        )
        poles = jnp.stack([pole_re, pole_im])
        states = recurrence(carry_prev, carry_next, poles, source, source)
        states_low = states.astype(jnp.bfloat16)
        mixed = (
            jnp.dot(states_low, out_low, preferred_element_type=jnp.float32)
            + feature_row[2] * normed
        )
        act = smooth(mixed)
        act_low = act.astype(jnp.bfloat16)
        pre = jnp.dot(act_low, gate_low, preferred_element_type=jnp.float32) + feature_row[3]
        saved.append((scale, unit, normed_low, drive, states, states_low, mixed, act, act_low, pre))
        stream = stream + act * jax.nn.sigmoid(pre)

    grad = gather_feat(cotangent, 1).astype(jnp.float32) * alive[:, None]
    layer_grads = [None] * layers
    for layer in reversed(range(layers)):
        scale, unit, normed_low, drive, states, states_low, mixed, act, act_low, pre = saved[layer]
        in_low = in_all[layer]
        out_low = out_all[layer]
        gate_low = gate_all[layer]
        feature_row = feature_all[layer]
        state_row = state_vectors[layer]
        pole_re, pole_im, factor_re, factor_im = coefficients(state_row)
        gate = jax.nn.sigmoid(pre)
        pre_grad = (grad * act * gate * (1.0 - gate)).astype(jnp.bfloat16)
        gate_grad = contract_rows(act_low, mine(pre_grad))
        gate_bias_grad = jnp.sum(pre_grad.astype(jnp.float32), 0)
        act_grad = grad * gate + contract_cols(pre_grad, gate_low)
        mixed_grad = jax.vjp(smooth, mixed)[1](act_grad)[0]
        normed = unit * feature_row[0] + feature_row[1]
        skip_grad = jnp.sum(mixed_grad * normed, 0)
        mixed_low = mixed_grad.astype(jnp.bfloat16)
        out_grad = contract_rows(states_low, mine(mixed_low))
        states_grad = contract_cols(mixed_low, out_low)
        conj = jnp.stack([pole_re, -pole_im])
        lambdas = recurrence(
            after_next, before_prev, conj, states_grad[:, 2 * width :], states_grad[:, : 2 * width]
        )
        lb_re = lambdas[:, :width]
        lb_im = lambdas[:, width : 2 * width]
        la_re = lambdas[:, 2 * width : 3 * width]
        la_im = lambdas[:, 3 * width :]
        gu_re = la_re + lb_re
        gu_im = la_im + lb_im
        live = alive[:, None]
        dg_re = (factor_re * gu_re + factor_im * gu_im) * live
        dg_im = (factor_re * gu_im - factor_im * gu_re) * live
        drive_low = jnp.concatenate([dg_re, dg_im], 1).astype(jnp.bfloat16)
        d_re = drive[:, :width] * live
        d_im = drive[:, width:] * live
        gf_re = jnp.sum(d_re * gu_re + d_im * gu_im, 0)
        gf_im = jnp.sum(d_re * gu_im - d_im * gu_re, 0)
        zero_row = jnp.zeros((1, width), jnp.float32)
        a_re = jnp.concatenate([zero_row, states[:-1, :width]], 0) * carry_prev[:, None]
        a_im = jnp.concatenate([zero_row, states[:-1, width : 2 * width]], 0) * carry_prev[:, None]
        b_re = jnp.concatenate([states[1:, 2 * width : 3 * width], zero_row], 0) * carry_next[:, None]
        b_im = jnp.concatenate([states[1:, 3 * width :], zero_row], 0) * carry_next[:, None]
        gp_re = jnp.sum(a_re * la_re + a_im * la_im + b_re * lb_re + b_im * lb_im, 0)
        gp_im = jnp.sum(a_re * la_im - a_im * la_re + b_re * lb_im - b_im * lb_re, 0)
        row_grad = jax.vjp(coefficients, state_row)[1]((gp_re, gp_im, gf_re, gf_im))[0]
        in_grad = contract_rows(mine(normed_low), drive_low)
        normed_grad = mixed_grad * feature_row[2] + jnp.dot(
            drive_low, in_low.T, preferred_element_type=jnp.float32
        )
        gain_grad = jnp.sum(normed_grad * unit, 0)
        bias_grad = jnp.sum(normed_grad, 0)
        unit_grad = normed_grad * feature_row[0]
        first_mean = jnp.mean(unit_grad, 1, keepdims=True)
        second_mean = jnp.mean(unit_grad * unit, 1, keepdims=True)
        grad = grad + scale * (unit_grad - first_mean - unit * second_mean)
        feature_grad = mine(jnp.stack([gain_grad, bias_grad, skip_grad, gate_bias_grad]))
        layer_grads[layer] = (in_grad, out_grad, gate_grad, feature_grad, row_grad)
    stacked_in = jnp.stack([entry[0] for entry in layer_grads])
    stacked_out = jnp.stack([entry[1] for entry in layer_grads])
    stacked_gate = jnp.stack([entry[2] for entry in layer_grads])
    stacked_feature = jnp.stack([entry[3] for entry in layer_grads])
    stacked_state = jnp.stack([entry[4] for entry in layer_grads])
    summed = lax.psum(
        (stacked_in, stacked_out, stacked_gate, stacked_feature, stacked_state), "seq"
    )
    factor = 1.0 / math.sqrt(count * lax.axis_size("seq"))
    grad_in = summed[0] * factor
    grad_out = summed[1] * factor
    grad_gate = summed[2] * factor
    grad_feature = summed[3] * factor
    grad_state = summed[4] * factor
    new_in = update(input_matrix, grad_in, velocity_input, average_input, slow_rate, 0.0)
    new_out = update(output_matrix, grad_out, velocity_output, average_output, slow_rate, 0.0)
    new_gate = update(gate_matrix, grad_gate, velocity_gate, average_gate, main_rate, weight_decay)
    new_feature = update(
        feature_vectors, grad_feature, velocity_feature, average_feature, main_rate, weight_decay
    )
    new_state = update(state_vectors, grad_state, velocity_state, average_state, slow_rate, 0.0)
    return (
        mine(stream),
        mine(grad),
        grad_in,
        grad_out,
        grad_gate,
        grad_feature,
        grad_state,
        new_in[0],
        new_out[0],
        new_gate[0],
        new_feature[0],
        new_state[3],
        new_in[1],
        new_out[1],
        new_gate[1],
        new_feature[1],
        new_state[1],
        new_in[2],
        new_out[2],
        new_gate[2],
        new_feature[2],
        new_state[2],
    )


def solution(mesh):
    feat = P(None, None, "feat")
    rows = P(None, "feat", None)
    tokens = P("seq", "feat")
    return jax.shard_map(
        body,
        mesh=mesh,
        in_specs=(
            tokens,
            tokens,
            P("seq"),
            P("seq"),
            rows,
            feat,
            feat,
            feat,
            P(),
            rows,
            feat,
            feat,
            feat,
            P(),
            rows,
            feat,
            feat,
            feat,
            P(),
        ),
        out_specs=(
            tokens,
            tokens,
            rows,
            feat,
            feat,
            feat,
            P(),
            rows,
            feat,
            feat,
            feat,
            P(),
            rows,
            feat,
            feat,
            feat,
            P(),
            rows,
            feat,
            feat,
            feat,
            P(),
        ),
        check_vma=False,
    )
```

```python
import math

import jax
import jax.numpy as jnp
from jax import lax
from jax.experimental import pallas as pl
from jax.experimental.pallas import tpu as pltpu
from jax.sharding import PartitionSpec as P

epsilon = 1e-05
momentum = 0.9
smoothing = 0.5
slow_rate = 0.02
main_rate = 0.05
weight_decay = 0.1


def smooth(value):
    return jax.nn.gelu(value, approximate=False)


def masks_of(starts, lengths, count):
    position = jnp.arange(count, dtype=jnp.int32)[:, None]
    begin = starts[None, :]
    finish = begin + lengths[None, :]
    inside = (position >= begin) & (position < finish)
    alive = jnp.any(inside, 1)
    opening = jnp.any(inside & (position == begin), 1)
    closing = jnp.any(inside & (position == finish - 1), 1)
    return (
        alive.astype(jnp.float32),
        (alive & ~opening).astype(jnp.float32),
        (alive & ~closing).astype(jnp.float32),
    )


def coefficients(state_row):
    rate = -jnp.exp(state_row[0])
    frequency = state_row[1]
    timestep = jnp.exp(state_row[2])
    decay = jnp.exp(rate * timestep)
    angle = frequency * timestep
    pole_real = decay * jnp.cos(angle)
    pole_imag = decay * jnp.sin(angle)
    denom = rate * rate + frequency * frequency
    factor_real = ((pole_real - 1.0) * rate + pole_imag * frequency) / denom
    factor_imag = (pole_imag * rate - (pole_real - 1.0) * frequency) / denom
    return (pole_real, pole_imag, factor_real, factor_imag)


def recurrence_kernel(ma_ref, mb_ref, w_ref, xa_ref, xb_ref, out_ref):
    count = xa_ref.shape[0]
    width = w_ref.shape[1]
    w_re = w_ref[0:1, :]
    w_im = w_ref[1:2, :]

    def advance(h_re, h_im, keep, x_ref, row):
        h_re = h_re * keep
        h_im = h_im * keep
        new_re = w_re * h_re - w_im * h_im + x_ref[pl.ds(row, 1), pl.ds(0, width)]
        new_im = w_re * h_im + w_im * h_re + x_ref[pl.ds(row, 1), pl.ds(width, width)]
        return new_re, new_im

    def step(i, carry):
        a_re, a_im, b_re, b_im = carry
        up = i
        down = count - 1 - i
        a_re, a_im = advance(a_re, a_im, ma_ref[up], xa_ref, up)
        b_re, b_im = advance(b_re, b_im, mb_ref[down], xb_ref, down)
        out_ref[pl.ds(up, 1), pl.ds(0, width)] = a_re
        out_ref[pl.ds(up, 1), pl.ds(width, width)] = a_im
        out_ref[pl.ds(down, 1), pl.ds(2 * width, width)] = b_re
        out_ref[pl.ds(down, 1), pl.ds(3 * width, width)] = b_im
        return (a_re, a_im, b_re, b_im)

    zeros = jnp.zeros((1, width), jnp.float32)
    lax.fori_loop(0, count, step, (zeros, zeros, zeros, zeros), unroll=8)


def recurrence(ma, mb, w, xa, xb):
    count, double = xa.shape
    return pl.pallas_call(
        recurrence_kernel,
        out_shape=jax.ShapeDtypeStruct((count, 2 * double), jnp.float32),
        in_specs=[
            pl.BlockSpec(memory_space=pltpu.SMEM),
            pl.BlockSpec(memory_space=pltpu.SMEM),
            pl.BlockSpec(memory_space=pltpu.VMEM),
            pl.BlockSpec(memory_space=pltpu.VMEM),
            pl.BlockSpec(memory_space=pltpu.VMEM),
        ],
        out_specs=pl.BlockSpec(memory_space=pltpu.VMEM),
        cost_estimate=pl.CostEstimate(
            flops=20 * count * double, transcendentals=0, bytes_accessed=16 * count * double
        ),
    )(ma, mb, w, xa, xb)


def update(weight, gradient, velocity, average, rate, decay):
    adjusted = gradient + decay * weight
    velocity_new = momentum * velocity + adjusted
    change = -rate * (adjusted + momentum * velocity_new)
    weight_new = weight + change
    average_new = smoothing * average + (1.0 - smoothing) * weight_new
    return (weight_new, velocity_new, average_new, change)


def contract_rows(left, right):
    return lax.dot_general(
        left, right, (((0,), (0,)), ((), ())), preferred_element_type=jnp.float32
    )


def contract_cols(left, right):
    return lax.dot_general(
        left, right, (((1,), (1,)), ((), ())), preferred_element_type=jnp.float32
    )


def gather_feat(value, axis):
    return lax.all_gather(value, "feat", axis=axis, tiled=True)


def reduce_seq(parts, earlier):
    flat = jnp.concatenate([part.reshape(-1) for part in parts]).astype(jnp.bfloat16)
    if earlier is not None:
        earlier, flat = lax.optimization_barrier((earlier, flat))
    total = lax.psum(flat, "seq")
    pieces = [total]
    total = total.astype(jnp.float32)
    start = 0
    for part in parts:
        pieces.append(total[start : start + part.size].reshape(part.shape))
        start += part.size
    return pieces


def body(
    activations_in,
    cotangent,
    seq_start,
    seq_length,
    input_matrix,
    output_matrix,
    gate_matrix,
    feature_vectors,
    state_vectors,
    velocity_input,
    velocity_output,
    velocity_gate,
    velocity_feature,
    velocity_state,
    average_input,
    average_output,
    average_gate,
    average_feature,
    average_state,
):
    count = activations_in.shape[0]
    shard = activations_in.shape[1]
    layers = input_matrix.shape[0]
    width = state_vectors.shape[2]
    me = lax.axis_index("feat")
    offset = me * shard

    def mine(value):
        return lax.dynamic_slice_in_dim(value, offset, shard, axis=value.ndim - 1)

    alive, carry_prev, carry_next = masks_of(seq_start, seq_length, count)
    zero = jnp.zeros((1,), jnp.float32)
    after_next = jnp.concatenate([zero, carry_next[:-1]])
    before_prev = jnp.concatenate([carry_prev[1:], zero])

    in_all = gather_feat(input_matrix.astype(jnp.bfloat16), 1)
    out_all = gather_feat(output_matrix.astype(jnp.bfloat16), 2)
    gate_all = gather_feat(gate_matrix.astype(jnp.bfloat16), 2)
    feature_all = gather_feat(feature_vectors, 2)
    stream = gather_feat(activations_in, 1).astype(jnp.float32)

    saved = []
    for layer in range(layers):
        in_low = in_all[layer]
        out_low = out_all[layer]
        gate_low = gate_all[layer]
        feature_row = feature_all[layer]
        pole_re, pole_im, factor_re, factor_im = coefficients(state_vectors[layer])
        center = jnp.mean(stream, 1, keepdims=True)
        spread = stream - center
        scale = lax.rsqrt(jnp.mean(spread * spread, 1, keepdims=True) + epsilon)
        unit = spread * scale
        normed = unit * feature_row[0] + feature_row[1]
        normed_low = normed.astype(jnp.bfloat16)
        drive = jnp.dot(normed_low, in_low, preferred_element_type=jnp.float32)
        drive_re = drive[:, :width]
        drive_im = drive[:, width:]
        source = jnp.concatenate(
            [
                (drive_re * factor_re - drive_im * factor_im) * alive[:, None],
                (drive_re * factor_im + drive_im * factor_re) * alive[:, None],
            ],
            1,
        )
        poles = jnp.stack([pole_re, pole_im])
        states = recurrence(carry_prev, carry_next, poles, source, source)
        states_low = states.astype(jnp.bfloat16)
        mixed = (
            jnp.dot(states_low, out_low, preferred_element_type=jnp.float32)
            + feature_row[2] * normed
        )
        act = smooth(mixed)
        act_low = act.astype(jnp.bfloat16)
        pre = jnp.dot(act_low, gate_low, preferred_element_type=jnp.float32) + feature_row[3]
        saved.append((scale, unit, normed_low, drive, states, states_low, mixed, act, act_low, pre))
        stream = stream + act * jax.nn.sigmoid(pre)

    grad = gather_feat(cotangent, 1).astype(jnp.float32) * alive[:, None]
    layer_grads = [None] * layers
    previous = None
    for layer in reversed(range(layers)):
        scale, unit, normed_low, drive, states, states_low, mixed, act, act_low, pre = saved[layer]
        in_low = in_all[layer]
        out_low = out_all[layer]
        gate_low = gate_all[layer]
        feature_row = feature_all[layer]
        state_row = state_vectors[layer]
        pole_re, pole_im, factor_re, factor_im = coefficients(state_row)
        gate = jax.nn.sigmoid(pre)
        pre_grad = (grad * act * gate * (1.0 - gate)).astype(jnp.bfloat16)
        gate_grad = contract_rows(act_low, mine(pre_grad))
        gate_bias_grad = jnp.sum(pre_grad.astype(jnp.float32), 0)
        act_grad = grad * gate + contract_cols(pre_grad, gate_low)
        mixed_grad = jax.vjp(smooth, mixed)[1](act_grad)[0]
        normed = unit * feature_row[0] + feature_row[1]
        skip_grad = jnp.sum(mixed_grad * normed, 0)
        mixed_low = mixed_grad.astype(jnp.bfloat16)
        out_grad = contract_rows(states_low, mine(mixed_low))
        states_grad = contract_cols(mixed_low, out_low)
        conj = jnp.stack([pole_re, -pole_im])
        lambdas = recurrence(
            after_next, before_prev, conj, states_grad[:, 2 * width :], states_grad[:, : 2 * width]
        )
        lb_re = lambdas[:, :width]
        lb_im = lambdas[:, width : 2 * width]
        la_re = lambdas[:, 2 * width : 3 * width]
        la_im = lambdas[:, 3 * width :]
        gu_re = la_re + lb_re
        gu_im = la_im + lb_im
        live = alive[:, None]
        dg_re = (factor_re * gu_re + factor_im * gu_im) * live
        dg_im = (factor_re * gu_im - factor_im * gu_re) * live
        drive_low = jnp.concatenate([dg_re, dg_im], 1).astype(jnp.bfloat16)
        d_re = drive[:, :width] * live
        d_im = drive[:, width:] * live
        gf_re = jnp.sum(d_re * gu_re + d_im * gu_im, 0)
        gf_im = jnp.sum(d_re * gu_im - d_im * gu_re, 0)
        zero_row = jnp.zeros((1, width), jnp.float32)
        a_re = jnp.concatenate([zero_row, states[:-1, :width]], 0) * carry_prev[:, None]
        a_im = jnp.concatenate([zero_row, states[:-1, width : 2 * width]], 0) * carry_prev[:, None]
        b_re = jnp.concatenate([states[1:, 2 * width : 3 * width], zero_row], 0) * carry_next[:, None]
        b_im = jnp.concatenate([states[1:, 3 * width :], zero_row], 0) * carry_next[:, None]
        gp_re = jnp.sum(a_re * la_re + a_im * la_im + b_re * lb_re + b_im * lb_im, 0)
        gp_im = jnp.sum(a_re * la_im - a_im * la_re + b_re * lb_im - b_im * lb_re, 0)
        row_grad = jax.vjp(coefficients, state_row)[1]((gp_re, gp_im, gf_re, gf_im))[0]
        in_grad = contract_rows(mine(normed_low), drive_low)
        normed_grad = mixed_grad * feature_row[2] + jnp.dot(
            drive_low, in_low.T, preferred_element_type=jnp.float32
        )
        gain_grad = jnp.sum(normed_grad * unit, 0)
        bias_grad = jnp.sum(normed_grad, 0)
        unit_grad = normed_grad * feature_row[0]
        first_mean = jnp.mean(unit_grad, 1, keepdims=True)
        second_mean = jnp.mean(unit_grad * unit, 1, keepdims=True)
        grad = grad + scale * (unit_grad - first_mean - unit * second_mean)
        feature_grad = mine(jnp.stack([gain_grad, bias_grad, skip_grad, gate_bias_grad]))
        layer_grads[layer] = reduce_seq(
            (in_grad, out_grad, gate_grad, feature_grad, row_grad), previous
        )
        previous = layer_grads[layer].pop(0)
    factor = 1.0 / math.sqrt(count * lax.axis_size("seq"))
    grad_in, grad_out, grad_gate, grad_feature, grad_state = (
        jnp.stack([entry[k] for entry in layer_grads]) * factor for k in range(5)
    )
    new_in = update(input_matrix, grad_in, velocity_input, average_input, slow_rate, 0.0)
    new_out = update(output_matrix, grad_out, velocity_output, average_output, slow_rate, 0.0)
    new_gate = update(gate_matrix, grad_gate, velocity_gate, average_gate, main_rate, weight_decay)
    new_feature = update(
        feature_vectors, grad_feature, velocity_feature, average_feature, main_rate, weight_decay
    )
    new_state = update(state_vectors, grad_state, velocity_state, average_state, slow_rate, 0.0)
    return (
        mine(stream),
        mine(grad),
        grad_in,
        grad_out,
        grad_gate,
        grad_feature,
        grad_state,
        new_in[0],
        new_out[0],
        new_gate[0],
        new_feature[0],
        new_state[3],
        new_in[1],
        new_out[1],
        new_gate[1],
        new_feature[1],
        new_state[1],
        new_in[2],
        new_out[2],
        new_gate[2],
        new_feature[2],
        new_state[2],
    )


def solution(mesh):
    feat = P(None, None, "feat")
    rows = P(None, "feat", None)
    tokens = P("seq", "feat")
    return jax.shard_map(
        body,
        mesh=mesh,
        in_specs=(
            tokens,
            tokens,
            P("seq"),
            P("seq"),
            rows,
            feat,
            feat,
            feat,
            P(),
            rows,
            feat,
            feat,
            feat,
            P(),
            rows,
            feat,
            feat,
            feat,
            P(),
        ),
        out_specs=(
            tokens,
            tokens,
            rows,
            feat,
            feat,
            feat,
            P(),
            rows,
            feat,
            feat,
            feat,
            P(),
            rows,
            feat,
            feat,
            feat,
            P(),
            rows,
            feat,
            feat,
            feat,
            P(),
        ),
        check_vma=False,
    )
```

```python
import math

import jax
import jax.numpy as jnp
from jax import lax
from jax.experimental import pallas as pl
from jax.experimental.pallas import tpu as pltpu
from jax.sharding import PartitionSpec as P

epsilon = 1e-05
momentum = 0.9
smoothing = 0.5
slow_rate = 0.02
main_rate = 0.05
weight_decay = 0.1


def smooth(value):
    return jax.nn.gelu(value, approximate=False)


def masks_of(starts, lengths, count):
    position = jnp.arange(count, dtype=jnp.int32)[:, None]
    begin = starts[None, :]
    finish = begin + lengths[None, :]
    inside = (position >= begin) & (position < finish)
    alive = jnp.any(inside, 1)
    opening = jnp.any(inside & (position == begin), 1)
    closing = jnp.any(inside & (position == finish - 1), 1)
    return (
        alive.astype(jnp.float32),
        (alive & ~opening).astype(jnp.float32),
        (alive & ~closing).astype(jnp.float32),
    )


def coefficients(state_row):
    rate = -jnp.exp(state_row[0])
    frequency = state_row[1]
    timestep = jnp.exp(state_row[2])
    decay = jnp.exp(rate * timestep)
    angle = frequency * timestep
    pole_real = decay * jnp.cos(angle)
    pole_imag = decay * jnp.sin(angle)
    denom = rate * rate + frequency * frequency
    factor_real = ((pole_real - 1.0) * rate + pole_imag * frequency) / denom
    factor_imag = (pole_imag * rate - (pole_real - 1.0) * frequency) / denom
    return (pole_real, pole_imag, factor_real, factor_imag)


def recurrence_kernel(ma_ref, mb_ref, w_ref, xa_ref, xb_ref, out_ref):
    count = xa_ref.shape[0]
    width = w_ref.shape[1]
    w_re = w_ref[0:1, :]
    w_im = w_ref[1:2, :]

    def advance(h_re, h_im, keep, x_ref, row):
        h_re = h_re * keep
        h_im = h_im * keep
        new_re = w_re * h_re - w_im * h_im + x_ref[pl.ds(row, 1), pl.ds(0, width)]
        new_im = w_re * h_im + w_im * h_re + x_ref[pl.ds(row, 1), pl.ds(width, width)]
        return new_re, new_im

    def step(i, carry):
        a_re, a_im, b_re, b_im = carry
        up = i
        down = count - 1 - i
        a_re, a_im = advance(a_re, a_im, ma_ref[up], xa_ref, up)
        b_re, b_im = advance(b_re, b_im, mb_ref[down], xb_ref, down)
        out_ref[pl.ds(up, 1), pl.ds(0, width)] = a_re
        out_ref[pl.ds(up, 1), pl.ds(width, width)] = a_im
        out_ref[pl.ds(down, 1), pl.ds(2 * width, width)] = b_re
        out_ref[pl.ds(down, 1), pl.ds(3 * width, width)] = b_im
        return (a_re, a_im, b_re, b_im)

    zeros = jnp.zeros((1, width), jnp.float32)
    lax.fori_loop(0, count, step, (zeros, zeros, zeros, zeros), unroll=8)


def recurrence(ma, mb, w, xa, xb):
    count, double = xa.shape
    return pl.pallas_call(
        recurrence_kernel,
        out_shape=jax.ShapeDtypeStruct((count, 2 * double), jnp.float32),
        in_specs=[
            pl.BlockSpec(memory_space=pltpu.SMEM),
            pl.BlockSpec(memory_space=pltpu.SMEM),
            pl.BlockSpec(memory_space=pltpu.VMEM),
            pl.BlockSpec(memory_space=pltpu.VMEM),
            pl.BlockSpec(memory_space=pltpu.VMEM),
        ],
        out_specs=pl.BlockSpec(memory_space=pltpu.VMEM),
        cost_estimate=pl.CostEstimate(
            flops=20 * count * double, transcendentals=0, bytes_accessed=16 * count * double
        ),
    )(ma, mb, w, xa, xb)


MESH = pl.DeviceIdType.MESH


def ring_place(position, n):
    upper = position // (n // 2)
    return (1 - upper) * (2 * position) + upper * (2 * (n - 1 - position) + 1)


def ring_position(index, n):
    odd = index % 2
    return (1 - odd) * (index // 2) + odd * (n - 1 - index // 2)


def ring_sum_kernel(n, x_ref, o_ref, slots, rs_send, rs_recv, credit, done, ag_send, ag_recv):
    rows = x_ref.shape[0]
    half = rows // 2
    size = half // n
    me = ring_position(lax.axis_index("seq"), n)
    right = ring_place((me + 1) % n, n)
    left = ring_place((me + n - 1) % n, n)
    rings = ((0, me, right, left), (1, (n - me) % n, left, right))

    barrier = pltpu.get_barrier_semaphore()
    for neighbour in (left, right):
        pl.semaphore_signal(barrier, 1, device_id={"seq": neighbour}, device_id_type=MESH)
    pl.semaphore_wait(barrier, 2)
    o_ref[...] = x_ref[...]

    def block(ring, k):
        return pl.ds(pl.multiple_of(ring * half + k * size, 8), size)

    def scatter_copy(ring, place, target, s):
        return pltpu.make_async_remote_copy(
            src_ref=o_ref.at[block(ring, (place - s + n) % n)],
            dst_ref=slots.at[ring, s % 2],
            send_sem=rs_send.at[ring, s % 2],
            recv_sem=rs_recv.at[ring, s % 2],
            device_id={"seq": target},
            device_id_type=MESH,
        )

    def scatter_step(s, carry):
        copies = []
        for ring, place, target, source in rings:

            @pl.when(s >= 2)
            def _():
                pl.semaphore_wait(credit.at[ring], 1)

            copy = scatter_copy(ring, place, target, s)
            copy.start()
            copies.append(copy)
        for (ring, place, target, source), copy in zip(rings, copies):
            copy.wait_recv()
            into = block(ring, (place - s - 1 + 2 * n) % n)
            o_ref[into] = o_ref[into] + slots[ring, s % 2]
            copy.wait_send()

            @pl.when(s <= n - 4)
            def _():
                pl.semaphore_signal(credit.at[ring], 1, device_id={"seq": source}, device_id_type=MESH)

        return carry

    lax.fori_loop(0, n - 1, scatter_step, 0)
    for ring, place, target, source in rings:
        pl.semaphore_signal(done.at[ring], 1, device_id={"seq": source}, device_id_type=MESH)
    for ring, place, target, source in rings:
        pl.semaphore_wait(done.at[ring], 1)

    def gather_copy(ring, place, target, s):
        where = block(ring, (place + 1 - s + n) % n)
        return pltpu.make_async_remote_copy(
            src_ref=o_ref.at[where],
            dst_ref=o_ref.at[where],
            send_sem=ag_send.at[ring, s],
            recv_sem=ag_recv.at[ring, s],
            device_id={"seq": target},
            device_id_type=MESH,
        )

    def gather_step(s, carry):
        for ring, place, target, source in rings:

            @pl.when(s >= 1)
            def _():
                gather_copy(ring, place, target, s - 1).wait_recv()

            gather_copy(ring, place, target, s).start()

            @pl.when(s >= 1)
            def _():
                gather_copy(ring, place, target, s - 1).wait_send()

        return carry

    lax.fori_loop(0, n - 1, gather_step, 0)
    for ring, place, target, source in rings:
        last = gather_copy(ring, place, target, n - 2)
        last.wait_recv()
        last.wait_send()


def ring_sum(x, n):
    rows, lanes = x.shape
    size = rows // (2 * n)
    return pl.pallas_call(
        lambda *refs: ring_sum_kernel(n, *refs),
        out_shape=jax.ShapeDtypeStruct((rows, lanes), jnp.float32),
        in_specs=[pl.BlockSpec(memory_space=pltpu.VMEM)],
        out_specs=pl.BlockSpec(memory_space=pltpu.VMEM),
        scratch_shapes=[
            pltpu.VMEM((2, 2, size, lanes), jnp.float32),
            pltpu.SemaphoreType.DMA((2, 2)),
            pltpu.SemaphoreType.DMA((2, 2)),
            pltpu.SemaphoreType.REGULAR((2,)),
            pltpu.SemaphoreType.REGULAR((2,)),
            pltpu.SemaphoreType.DMA((2, n - 1)),
            pltpu.SemaphoreType.DMA((2, n - 1)),
        ],
        compiler_params=pltpu.CompilerParams(collective_id=0, has_side_effects=True),
    )(x)


def sum_over_seq(parts):
    n = lax.axis_size("seq")
    flat = jnp.concatenate([part.reshape(-1) for part in parts])
    grain = 2 * n * 8 * 128
    padded = -(-flat.size // grain) * grain
    flat = jnp.pad(flat, (0, padded - flat.size)).reshape(padded // 128, 128)
    total = ring_sum(flat, n).reshape(-1)
    pieces = []
    start = 0
    for part in parts:
        pieces.append(total[start : start + part.size].reshape(part.shape))
        start += part.size
    return pieces


def update(weight, gradient, velocity, average, rate, decay):
    adjusted = gradient + decay * weight
    velocity_new = momentum * velocity + adjusted
    change = -rate * (adjusted + momentum * velocity_new)
    weight_new = weight + change
    average_new = smoothing * average + (1.0 - smoothing) * weight_new
    return (weight_new, velocity_new, average_new, change)


def contract_rows(left, right):
    return lax.dot_general(
        left, right, (((0,), (0,)), ((), ())), preferred_element_type=jnp.float32
    )


def contract_cols(left, right):
    return lax.dot_general(
        left, right, (((1,), (1,)), ((), ())), preferred_element_type=jnp.float32
    )


def gather_feat(value, axis):
    return lax.all_gather(value, "feat", axis=axis, tiled=True)


def body(
    activations_in,
    cotangent,
    seq_start,
    seq_length,
    input_matrix,
    output_matrix,
    gate_matrix,
    feature_vectors,
    state_vectors,
    velocity_input,
    velocity_output,
    velocity_gate,
    velocity_feature,
    velocity_state,
    average_input,
    average_output,
    average_gate,
    average_feature,
    average_state,
):
    count = activations_in.shape[0]
    shard = activations_in.shape[1]
    layers = input_matrix.shape[0]
    width = state_vectors.shape[2]
    me = lax.axis_index("feat")
    offset = me * shard

    def mine(value):
        return lax.dynamic_slice_in_dim(value, offset, shard, axis=value.ndim - 1)

    alive, carry_prev, carry_next = masks_of(seq_start, seq_length, count)
    zero = jnp.zeros((1,), jnp.float32)
    after_next = jnp.concatenate([zero, carry_next[:-1]])
    before_prev = jnp.concatenate([carry_prev[1:], zero])

    in_all = gather_feat(input_matrix.astype(jnp.bfloat16), 1)
    out_all = gather_feat(output_matrix.astype(jnp.bfloat16), 2)
    gate_all = gather_feat(gate_matrix.astype(jnp.bfloat16), 2)
    feature_all = gather_feat(feature_vectors, 2)
    stream = gather_feat(activations_in, 1).astype(jnp.float32)

    saved = []
    for layer in range(layers):
        in_low = in_all[layer]
        out_low = out_all[layer]
        gate_low = gate_all[layer]
        feature_row = feature_all[layer]
        pole_re, pole_im, factor_re, factor_im = coefficients(state_vectors[layer])
        center = jnp.mean(stream, 1, keepdims=True)
        spread = stream - center
        scale = lax.rsqrt(jnp.mean(spread * spread, 1, keepdims=True) + epsilon)
        unit = spread * scale
        normed = unit * feature_row[0] + feature_row[1]
        normed_low = normed.astype(jnp.bfloat16)
        drive = jnp.dot(normed_low, in_low, preferred_element_type=jnp.float32)
        drive_re = drive[:, :width]
        drive_im = drive[:, width:]
        source = jnp.concatenate(
            [
                (drive_re * factor_re - drive_im * factor_im) * alive[:, None],
                (drive_re * factor_im + drive_im * factor_re) * alive[:, None],
            ],
            1,
        )
        poles = jnp.stack([pole_re, pole_im])
        states = recurrence(carry_prev, carry_next, poles, source, source)
        states_low = states.astype(jnp.bfloat16)
        mixed = (
            jnp.dot(states_low, out_low, preferred_element_type=jnp.float32)
            + feature_row[2] * normed
        )
        act = smooth(mixed)
        act_low = act.astype(jnp.bfloat16)
        pre = jnp.dot(act_low, gate_low, preferred_element_type=jnp.float32) + feature_row[3]
        saved.append((scale, unit, normed_low, drive, states, states_low, mixed, act, act_low, pre))
        stream = stream + act * jax.nn.sigmoid(pre)

    grad = gather_feat(cotangent, 1).astype(jnp.float32) * alive[:, None]
    layer_grads = [None] * layers
    for layer in reversed(range(layers)):
        scale, unit, normed_low, drive, states, states_low, mixed, act, act_low, pre = saved[layer]
        in_low = in_all[layer]
        out_low = out_all[layer]
        gate_low = gate_all[layer]
        feature_row = feature_all[layer]
        state_row = state_vectors[layer]
        pole_re, pole_im, factor_re, factor_im = coefficients(state_row)
        gate = jax.nn.sigmoid(pre)
        pre_grad = (grad * act * gate * (1.0 - gate)).astype(jnp.bfloat16)
        gate_grad = contract_rows(act_low, mine(pre_grad))
        gate_bias_grad = jnp.sum(pre_grad.astype(jnp.float32), 0)
        act_grad = grad * gate + contract_cols(pre_grad, gate_low)
        mixed_grad = jax.vjp(smooth, mixed)[1](act_grad)[0]
        normed = unit * feature_row[0] + feature_row[1]
        skip_grad = jnp.sum(mixed_grad * normed, 0)
        mixed_low = mixed_grad.astype(jnp.bfloat16)
        out_grad = contract_rows(states_low, mine(mixed_low))
        states_grad = contract_cols(mixed_low, out_low)
        conj = jnp.stack([pole_re, -pole_im])
        lambdas = recurrence(
            after_next, before_prev, conj, states_grad[:, 2 * width :], states_grad[:, : 2 * width]
        )
        lb_re = lambdas[:, :width]
        lb_im = lambdas[:, width : 2 * width]
        la_re = lambdas[:, 2 * width : 3 * width]
        la_im = lambdas[:, 3 * width :]
        gu_re = la_re + lb_re
        gu_im = la_im + lb_im
        live = alive[:, None]
        dg_re = (factor_re * gu_re + factor_im * gu_im) * live
        dg_im = (factor_re * gu_im - factor_im * gu_re) * live
        drive_low = jnp.concatenate([dg_re, dg_im], 1).astype(jnp.bfloat16)
        d_re = drive[:, :width] * live
        d_im = drive[:, width:] * live
        gf_re = jnp.sum(d_re * gu_re + d_im * gu_im, 0)
        gf_im = jnp.sum(d_re * gu_im - d_im * gu_re, 0)
        zero_row = jnp.zeros((1, width), jnp.float32)
        a_re = jnp.concatenate([zero_row, states[:-1, :width]], 0) * carry_prev[:, None]
        a_im = jnp.concatenate([zero_row, states[:-1, width : 2 * width]], 0) * carry_prev[:, None]
        b_re = jnp.concatenate([states[1:, 2 * width : 3 * width], zero_row], 0) * carry_next[:, None]
        b_im = jnp.concatenate([states[1:, 3 * width :], zero_row], 0) * carry_next[:, None]
        gp_re = jnp.sum(a_re * la_re + a_im * la_im + b_re * lb_re + b_im * lb_im, 0)
        gp_im = jnp.sum(a_re * la_im - a_im * la_re + b_re * lb_im - b_im * lb_re, 0)
        row_grad = jax.vjp(coefficients, state_row)[1]((gp_re, gp_im, gf_re, gf_im))[0]
        in_grad = contract_rows(mine(normed_low), drive_low)
        normed_grad = mixed_grad * feature_row[2] + jnp.dot(
            drive_low, in_low.T, preferred_element_type=jnp.float32
        )
        gain_grad = jnp.sum(normed_grad * unit, 0)
        bias_grad = jnp.sum(normed_grad, 0)
        unit_grad = normed_grad * feature_row[0]
        first_mean = jnp.mean(unit_grad, 1, keepdims=True)
        second_mean = jnp.mean(unit_grad * unit, 1, keepdims=True)
        grad = grad + scale * (unit_grad - first_mean - unit * second_mean)
        feature_grad = mine(jnp.stack([gain_grad, bias_grad, skip_grad, gate_bias_grad]))
        layer_grads[layer] = (in_grad, out_grad, gate_grad, feature_grad, row_grad)
    stacked_in = jnp.stack([entry[0] for entry in layer_grads])
    stacked_out = jnp.stack([entry[1] for entry in layer_grads])
    stacked_gate = jnp.stack([entry[2] for entry in layer_grads])
    stacked_feature = jnp.stack([entry[3] for entry in layer_grads])
    stacked_state = jnp.stack([entry[4] for entry in layer_grads])
    summed = sum_over_seq((stacked_in, stacked_out, stacked_gate, stacked_feature, stacked_state))
    factor = 1.0 / math.sqrt(count * lax.axis_size("seq"))
    grad_in = summed[0] * factor
    grad_out = summed[1] * factor
    grad_gate = summed[2] * factor
    grad_feature = summed[3] * factor
    grad_state = summed[4] * factor
    new_in = update(input_matrix, grad_in, velocity_input, average_input, slow_rate, 0.0)
    new_out = update(output_matrix, grad_out, velocity_output, average_output, slow_rate, 0.0)
    new_gate = update(gate_matrix, grad_gate, velocity_gate, average_gate, main_rate, weight_decay)
    new_feature = update(
        feature_vectors, grad_feature, velocity_feature, average_feature, main_rate, weight_decay
    )
    new_state = update(state_vectors, grad_state, velocity_state, average_state, slow_rate, 0.0)
    return (
        mine(stream),
        mine(grad),
        grad_in,
        grad_out,
        grad_gate,
        grad_feature,
        grad_state,
        new_in[0],
        new_out[0],
        new_gate[0],
        new_feature[0],
        new_state[3],
        new_in[1],
        new_out[1],
        new_gate[1],
        new_feature[1],
        new_state[1],
        new_in[2],
        new_out[2],
        new_gate[2],
        new_feature[2],
        new_state[2],
    )


def solution(mesh):
    feat = P(None, None, "feat")
    rows = P(None, "feat", None)
    tokens = P("seq", "feat")
    return jax.shard_map(
        body,
        mesh=mesh,
        in_specs=(
            tokens,
            tokens,
            P("seq"),
            P("seq"),
            rows,
            feat,
            feat,
            feat,
            P(),
            rows,
            feat,
            feat,
            feat,
            P(),
            rows,
            feat,
            feat,
            feat,
            P(),
        ),
        out_specs=(
            tokens,
            tokens,
            rows,
            feat,
            feat,
            feat,
            P(),
            rows,
            feat,
            feat,
            feat,
            P(),
            rows,
            feat,
            feat,
            feat,
            P(),
            rows,
            feat,
            feat,
            feat,
            P(),
        ),
        check_vma=False,
    )
```

```python
import math

import jax
import jax.numpy as jnp
from jax import lax
from jax.experimental import pallas as pl
from jax.experimental.pallas import tpu as pltpu
from jax.sharding import PartitionSpec as P

epsilon = 1e-05
momentum = 0.9
smoothing = 0.5
slow_rate = 0.02
main_rate = 0.05
weight_decay = 0.1


def smooth(value):
    return jax.nn.gelu(value, approximate=False)


def masks_of(starts, lengths, count):
    position = jnp.arange(count, dtype=jnp.int32)[:, None]
    begin = starts[None, :]
    finish = begin + lengths[None, :]
    inside = (position >= begin) & (position < finish)
    alive = jnp.any(inside, 1)
    opening = jnp.any(inside & (position == begin), 1)
    closing = jnp.any(inside & (position == finish - 1), 1)
    return (
        alive.astype(jnp.float32),
        (alive & ~opening).astype(jnp.float32),
        (alive & ~closing).astype(jnp.float32),
    )


def coefficients(state_row):
    rate = -jnp.exp(state_row[0])
    frequency = state_row[1]
    timestep = jnp.exp(state_row[2])
    decay = jnp.exp(rate * timestep)
    angle = frequency * timestep
    pole_real = decay * jnp.cos(angle)
    pole_imag = decay * jnp.sin(angle)
    denom = rate * rate + frequency * frequency
    factor_real = ((pole_real - 1.0) * rate + pole_imag * frequency) / denom
    factor_imag = (pole_imag * rate - (pole_real - 1.0) * frequency) / denom
    return (pole_real, pole_imag, factor_real, factor_imag)


def recurrence_kernel(ma_ref, mb_ref, w_ref, xa_ref, xb_ref, out_ref):
    count = xa_ref.shape[0]
    width = w_ref.shape[1]
    w_re = w_ref[0:1, :]
    w_im = w_ref[1:2, :]

    def advance(h_re, h_im, keep, x_ref, row):
        h_re = h_re * keep
        h_im = h_im * keep
        new_re = w_re * h_re - w_im * h_im + x_ref[pl.ds(row, 1), pl.ds(0, width)]
        new_im = w_re * h_im + w_im * h_re + x_ref[pl.ds(row, 1), pl.ds(width, width)]
        return new_re, new_im

    def step(i, carry):
        a_re, a_im, b_re, b_im = carry
        up = i
        down = count - 1 - i
        a_re, a_im = advance(a_re, a_im, ma_ref[up], xa_ref, up)
        b_re, b_im = advance(b_re, b_im, mb_ref[down], xb_ref, down)
        out_ref[pl.ds(up, 1), pl.ds(0, width)] = a_re
        out_ref[pl.ds(up, 1), pl.ds(width, width)] = a_im
        out_ref[pl.ds(down, 1), pl.ds(2 * width, width)] = b_re
        out_ref[pl.ds(down, 1), pl.ds(3 * width, width)] = b_im
        return (a_re, a_im, b_re, b_im)

    zeros = jnp.zeros((1, width), jnp.float32)
    lax.fori_loop(0, count, step, (zeros, zeros, zeros, zeros), unroll=8)


def recurrence(ma, mb, w, xa, xb):
    count, double = xa.shape
    return pl.pallas_call(
        recurrence_kernel,
        out_shape=jax.ShapeDtypeStruct((count, 2 * double), jnp.float32),
        in_specs=[
            pl.BlockSpec(memory_space=pltpu.SMEM),
            pl.BlockSpec(memory_space=pltpu.SMEM),
            pl.BlockSpec(memory_space=pltpu.VMEM),
            pl.BlockSpec(memory_space=pltpu.VMEM),
            pl.BlockSpec(memory_space=pltpu.VMEM),
        ],
        out_specs=pl.BlockSpec(memory_space=pltpu.VMEM),
        cost_estimate=pl.CostEstimate(
            flops=20 * count * double, transcendentals=0, bytes_accessed=16 * count * double
        ),
    )(ma, mb, w, xa, xb)


MESH = pl.DeviceIdType.MESH


def ring_place(position, n):
    upper = position // (n // 2)
    return (1 - upper) * (2 * position) + upper * (2 * (n - 1 - position) + 1)


def ring_position(index, n):
    odd = index % 2
    return (1 - odd) * (index // 2) + odd * (n - 1 - index // 2)


def ring_sum_kernel(n, x_ref, r_ref, o_ref, slots, rs_send, rs_recv, credit, done, ag_send, ag_recv):
    rows = x_ref.shape[0]
    half = rows // 2
    size = half // n
    me = ring_position(lax.axis_index("seq"), n)
    right = ring_place((me + 1) % n, n)
    left = ring_place((me + n - 1) % n, n)
    rings = ((0, me, right, left), (1, (n - me) % n, left, right))

    barrier = pltpu.get_barrier_semaphore()
    for neighbour in (left, right):
        pl.semaphore_signal(barrier, 1, device_id={"seq": neighbour}, device_id_type=MESH)
    pl.semaphore_wait(barrier, 2)
    o_ref[...] = x_ref[...]

    def block(ring, k):
        return pl.ds(pl.multiple_of(ring * half + k * size, 8), size)

    def scatter_copy(ring, place, target, s):
        return pltpu.make_async_remote_copy(
            src_ref=o_ref.at[block(ring, (place - s + n) % n)],
            dst_ref=slots.at[ring, s % 2],
            send_sem=rs_send.at[ring, s % 2],
            recv_sem=rs_recv.at[ring, s % 2],
            device_id={"seq": target},
            device_id_type=MESH,
        )

    def scatter_step(s, carry):
        copies = []
        for ring, place, target, source in rings:

            @pl.when(s >= 2)
            def _():
                pl.semaphore_wait(credit.at[ring], 1)

            copy = scatter_copy(ring, place, target, s)
            copy.start()
            copies.append(copy)
        for (ring, place, target, source), copy in zip(rings, copies):
            copy.wait_recv()
            into = block(ring, (place - s - 1 + 2 * n) % n)
            o_ref[into] = o_ref[into] + slots[ring, s % 2]
            copy.wait_send()

            @pl.when(s <= n - 4)
            def _():
                pl.semaphore_signal(credit.at[ring], 1, device_id={"seq": source}, device_id_type=MESH)

        return carry

    lax.fori_loop(0, n - 1, scatter_step, 0)
    for ring, place, target, source in rings:
        pl.semaphore_signal(done.at[ring], 1, device_id={"seq": source}, device_id_type=MESH)
    for ring, place, target, source in rings:
        final = block(ring, (place + 1) % n)
        r_ref[final] = o_ref[final].astype(r_ref.dtype)
    for ring, place, target, source in rings:
        pl.semaphore_wait(done.at[ring], 1)

    def gather_copy(ring, place, target, s):
        where = block(ring, (place + 1 - s + n) % n)
        return pltpu.make_async_remote_copy(
            src_ref=r_ref.at[where],
            dst_ref=r_ref.at[where],
            send_sem=ag_send.at[ring, s],
            recv_sem=ag_recv.at[ring, s],
            device_id={"seq": target},
            device_id_type=MESH,
        )

    def gather_step(s, carry):
        for ring, place, target, source in rings:

            @pl.when(s >= 1)
            def _():
                gather_copy(ring, place, target, s - 1).wait_recv()

            gather_copy(ring, place, target, s).start()

            @pl.when(s >= 1)
            def _():
                gather_copy(ring, place, target, s - 1).wait_send()

        return carry

    lax.fori_loop(0, n - 1, gather_step, 0)
    for ring, place, target, source in rings:
        last = gather_copy(ring, place, target, n - 2)
        last.wait_recv()
        last.wait_send()


def ring_sum(x, n):
    rows, lanes = x.shape
    size = rows // (2 * n)
    return pl.pallas_call(
        lambda *refs: ring_sum_kernel(n, *refs),
        out_shape=jax.ShapeDtypeStruct((rows, lanes), jnp.bfloat16),
        in_specs=[pl.BlockSpec(memory_space=pltpu.VMEM)],
        out_specs=pl.BlockSpec(memory_space=pltpu.VMEM),
        scratch_shapes=[
            pltpu.VMEM((rows, lanes), jnp.float32),
            pltpu.VMEM((2, 2, size, lanes), jnp.float32),
            pltpu.SemaphoreType.DMA((2, 2)),
            pltpu.SemaphoreType.DMA((2, 2)),
            pltpu.SemaphoreType.REGULAR((2,)),
            pltpu.SemaphoreType.REGULAR((2,)),
            pltpu.SemaphoreType.DMA((2, n - 1)),
            pltpu.SemaphoreType.DMA((2, n - 1)),
        ],
        compiler_params=pltpu.CompilerParams(collective_id=0, has_side_effects=True),
    )(x)


def sum_over_seq(parts):
    n = lax.axis_size("seq")
    flat = jnp.concatenate([part.reshape(-1) for part in parts])
    grain = 2 * n * 16 * 128
    padded = -(-flat.size // grain) * grain
    flat = jnp.pad(flat, (0, padded - flat.size)).reshape(padded // 128, 128)
    total = ring_sum(flat, n).astype(jnp.float32).reshape(-1)
    pieces = []
    start = 0
    for part in parts:
        pieces.append(total[start : start + part.size].reshape(part.shape))
        start += part.size
    return pieces


def update(weight, gradient, velocity, average, rate, decay):
    adjusted = gradient + decay * weight
    velocity_new = momentum * velocity + adjusted
    change = -rate * (adjusted + momentum * velocity_new)
    weight_new = weight + change
    average_new = smoothing * average + (1.0 - smoothing) * weight_new
    return (weight_new, velocity_new, average_new, change)


def contract_rows(left, right):
    return lax.dot_general(
        left, right, (((0,), (0,)), ((), ())), preferred_element_type=jnp.float32
    )


def contract_cols(left, right):
    return lax.dot_general(
        left, right, (((1,), (1,)), ((), ())), preferred_element_type=jnp.float32
    )


def gather_feat(value, axis):
    return lax.all_gather(value, "feat", axis=axis, tiled=True)


def body(
    activations_in,
    cotangent,
    seq_start,
    seq_length,
    input_matrix,
    output_matrix,
    gate_matrix,
    feature_vectors,
    state_vectors,
    velocity_input,
    velocity_output,
    velocity_gate,
    velocity_feature,
    velocity_state,
    average_input,
    average_output,
    average_gate,
    average_feature,
    average_state,
):
    count = activations_in.shape[0]
    shard = activations_in.shape[1]
    layers = input_matrix.shape[0]
    width = state_vectors.shape[2]
    me = lax.axis_index("feat")
    offset = me * shard

    def mine(value):
        return lax.dynamic_slice_in_dim(value, offset, shard, axis=value.ndim - 1)

    alive, carry_prev, carry_next = masks_of(seq_start, seq_length, count)
    zero = jnp.zeros((1,), jnp.float32)
    after_next = jnp.concatenate([zero, carry_next[:-1]])
    before_prev = jnp.concatenate([carry_prev[1:], zero])

    in_all = gather_feat(input_matrix.astype(jnp.bfloat16), 1)
    out_all = gather_feat(output_matrix.astype(jnp.bfloat16), 2)
    gate_all = gather_feat(gate_matrix.astype(jnp.bfloat16), 2)
    feature_all = gather_feat(feature_vectors, 2)
    stream = gather_feat(activations_in, 1).astype(jnp.float32)

    saved = []
    for layer in range(layers):
        in_low = in_all[layer]
        out_low = out_all[layer]
        gate_low = gate_all[layer]
        feature_row = feature_all[layer]
        pole_re, pole_im, factor_re, factor_im = coefficients(state_vectors[layer])
        center = jnp.mean(stream, 1, keepdims=True)
        spread = stream - center
        scale = lax.rsqrt(jnp.mean(spread * spread, 1, keepdims=True) + epsilon)
        unit = spread * scale
        normed = unit * feature_row[0] + feature_row[1]
        normed_low = normed.astype(jnp.bfloat16)
        drive = jnp.dot(normed_low, in_low, preferred_element_type=jnp.float32)
        drive_re = drive[:, :width]
        drive_im = drive[:, width:]
        source = jnp.concatenate(
            [
                (drive_re * factor_re - drive_im * factor_im) * alive[:, None],
                (drive_re * factor_im + drive_im * factor_re) * alive[:, None],
            ],
            1,
        )
        poles = jnp.stack([pole_re, pole_im])
        states = recurrence(carry_prev, carry_next, poles, source, source)
        states_low = states.astype(jnp.bfloat16)
        mixed = (
            jnp.dot(states_low, out_low, preferred_element_type=jnp.float32)
            + feature_row[2] * normed
        )
        act = smooth(mixed)
        act_low = act.astype(jnp.bfloat16)
        pre = jnp.dot(act_low, gate_low, preferred_element_type=jnp.float32) + feature_row[3]
        saved.append((scale, unit, normed_low, drive, states, states_low, mixed, act, act_low, pre))
        stream = stream + act * jax.nn.sigmoid(pre)

    grad = gather_feat(cotangent, 1).astype(jnp.float32) * alive[:, None]
    layer_grads = [None] * layers
    for layer in reversed(range(layers)):
        scale, unit, normed_low, drive, states, states_low, mixed, act, act_low, pre = saved[layer]
        in_low = in_all[layer]
        out_low = out_all[layer]
        gate_low = gate_all[layer]
        feature_row = feature_all[layer]
        state_row = state_vectors[layer]
        pole_re, pole_im, factor_re, factor_im = coefficients(state_row)
        gate = jax.nn.sigmoid(pre)
        pre_grad = (grad * act * gate * (1.0 - gate)).astype(jnp.bfloat16)
        gate_grad = contract_rows(act_low, mine(pre_grad))
        gate_bias_grad = jnp.sum(pre_grad.astype(jnp.float32), 0)
        act_grad = grad * gate + contract_cols(pre_grad, gate_low)
        mixed_grad = jax.vjp(smooth, mixed)[1](act_grad)[0]
        normed = unit * feature_row[0] + feature_row[1]
        skip_grad = jnp.sum(mixed_grad * normed, 0)
        mixed_low = mixed_grad.astype(jnp.bfloat16)
        out_grad = contract_rows(states_low, mine(mixed_low))
        states_grad = contract_cols(mixed_low, out_low)
        conj = jnp.stack([pole_re, -pole_im])
        lambdas = recurrence(
            after_next, before_prev, conj, states_grad[:, 2 * width :], states_grad[:, : 2 * width]
        )
        lb_re = lambdas[:, :width]
        lb_im = lambdas[:, width : 2 * width]
        la_re = lambdas[:, 2 * width : 3 * width]
        la_im = lambdas[:, 3 * width :]
        gu_re = la_re + lb_re
        gu_im = la_im + lb_im
        live = alive[:, None]
        dg_re = (factor_re * gu_re + factor_im * gu_im) * live
        dg_im = (factor_re * gu_im - factor_im * gu_re) * live
        drive_low = jnp.concatenate([dg_re, dg_im], 1).astype(jnp.bfloat16)
        d_re = drive[:, :width] * live
        d_im = drive[:, width:] * live
        gf_re = jnp.sum(d_re * gu_re + d_im * gu_im, 0)
        gf_im = jnp.sum(d_re * gu_im - d_im * gu_re, 0)
        zero_row = jnp.zeros((1, width), jnp.float32)
        a_re = jnp.concatenate([zero_row, states[:-1, :width]], 0) * carry_prev[:, None]
        a_im = jnp.concatenate([zero_row, states[:-1, width : 2 * width]], 0) * carry_prev[:, None]
        b_re = jnp.concatenate([states[1:, 2 * width : 3 * width], zero_row], 0) * carry_next[:, None]
        b_im = jnp.concatenate([states[1:, 3 * width :], zero_row], 0) * carry_next[:, None]
        gp_re = jnp.sum(a_re * la_re + a_im * la_im + b_re * lb_re + b_im * lb_im, 0)
        gp_im = jnp.sum(a_re * la_im - a_im * la_re + b_re * lb_im - b_im * lb_re, 0)
        row_grad = jax.vjp(coefficients, state_row)[1]((gp_re, gp_im, gf_re, gf_im))[0]
        in_grad = contract_rows(mine(normed_low), drive_low)
        normed_grad = mixed_grad * feature_row[2] + jnp.dot(
            drive_low, in_low.T, preferred_element_type=jnp.float32
        )
        gain_grad = jnp.sum(normed_grad * unit, 0)
        bias_grad = jnp.sum(normed_grad, 0)
        unit_grad = normed_grad * feature_row[0]
        first_mean = jnp.mean(unit_grad, 1, keepdims=True)
        second_mean = jnp.mean(unit_grad * unit, 1, keepdims=True)
        grad = grad + scale * (unit_grad - first_mean - unit * second_mean)
        feature_grad = mine(jnp.stack([gain_grad, bias_grad, skip_grad, gate_bias_grad]))
        layer_grads[layer] = (in_grad, out_grad, gate_grad, feature_grad, row_grad)
    stacked_in = jnp.stack([entry[0] for entry in layer_grads])
    stacked_out = jnp.stack([entry[1] for entry in layer_grads])
    stacked_gate = jnp.stack([entry[2] for entry in layer_grads])
    stacked_feature = jnp.stack([entry[3] for entry in layer_grads])
    stacked_state = jnp.stack([entry[4] for entry in layer_grads])
    summed = sum_over_seq((stacked_in, stacked_out, stacked_gate, stacked_feature, stacked_state))
    factor = 1.0 / math.sqrt(count * lax.axis_size("seq"))
    grad_in = summed[0] * factor
    grad_out = summed[1] * factor
    grad_gate = summed[2] * factor
    grad_feature = summed[3] * factor
    grad_state = summed[4] * factor
    new_in = update(input_matrix, grad_in, velocity_input, average_input, slow_rate, 0.0)
    new_out = update(output_matrix, grad_out, velocity_output, average_output, slow_rate, 0.0)
    new_gate = update(gate_matrix, grad_gate, velocity_gate, average_gate, main_rate, weight_decay)
    new_feature = update(
        feature_vectors, grad_feature, velocity_feature, average_feature, main_rate, weight_decay
    )
    new_state = update(state_vectors, grad_state, velocity_state, average_state, slow_rate, 0.0)
    return (
        mine(stream),
        mine(grad),
        grad_in,
        grad_out,
        grad_gate,
        grad_feature,
        grad_state,
        new_in[0],
        new_out[0],
        new_gate[0],
        new_feature[0],
        new_state[3],
        new_in[1],
        new_out[1],
        new_gate[1],
        new_feature[1],
        new_state[1],
        new_in[2],
        new_out[2],
        new_gate[2],
        new_feature[2],
        new_state[2],
    )


def solution(mesh):
    feat = P(None, None, "feat")
    rows = P(None, "feat", None)
    tokens = P("seq", "feat")
    return jax.shard_map(
        body,
        mesh=mesh,
        in_specs=(
            tokens,
            tokens,
            P("seq"),
            P("seq"),
            rows,
            feat,
            feat,
            feat,
            P(),
            rows,
            feat,
            feat,
            feat,
            P(),
            rows,
            feat,
            feat,
            feat,
            P(),
        ),
        out_specs=(
            tokens,
            tokens,
            rows,
            feat,
            feat,
            feat,
            P(),
            rows,
            feat,
            feat,
            feat,
            P(),
            rows,
            feat,
            feat,
            feat,
            P(),
            rows,
            feat,
            feat,
            feat,
            P(),
        ),
        check_vma=False,
    )
```

```python
import math

import jax
import jax.numpy as jnp
from jax import lax
from jax.experimental import pallas as pl
from jax.experimental.pallas import tpu as pltpu
from jax.sharding import PartitionSpec as P

epsilon = 1e-05
momentum = 0.9
smoothing = 0.5
slow_rate = 0.02
main_rate = 0.05
weight_decay = 0.1


def smooth(value):
    return jax.nn.gelu(value, approximate=False)


def masks_of(starts, lengths, count):
    position = jnp.arange(count, dtype=jnp.int32)[:, None]
    begin = starts[None, :]
    finish = begin + lengths[None, :]
    inside = (position >= begin) & (position < finish)
    alive = jnp.any(inside, 1)
    opening = jnp.any(inside & (position == begin), 1)
    closing = jnp.any(inside & (position == finish - 1), 1)
    return (
        alive.astype(jnp.float32),
        (alive & ~opening).astype(jnp.float32),
        (alive & ~closing).astype(jnp.float32),
    )


def coefficients(state_row):
    rate = -jnp.exp(state_row[0])
    frequency = state_row[1]
    timestep = jnp.exp(state_row[2])
    decay = jnp.exp(rate * timestep)
    angle = frequency * timestep
    pole_real = decay * jnp.cos(angle)
    pole_imag = decay * jnp.sin(angle)
    denom = rate * rate + frequency * frequency
    factor_real = ((pole_real - 1.0) * rate + pole_imag * frequency) / denom
    factor_imag = (pole_imag * rate - (pole_real - 1.0) * frequency) / denom
    return (pole_real, pole_imag, factor_real, factor_imag)


def recurrence_kernel(ma_ref, mb_ref, w_ref, xa_ref, xb_ref, out_ref):
    count = xa_ref.shape[0]
    width = w_ref.shape[1]
    w_re = w_ref[0:1, :]
    w_im = w_ref[1:2, :]

    def advance(h_re, h_im, keep, x_ref, row):
        h_re = h_re * keep
        h_im = h_im * keep
        new_re = w_re * h_re - w_im * h_im + x_ref[pl.ds(row, 1), pl.ds(0, width)]
        new_im = w_re * h_im + w_im * h_re + x_ref[pl.ds(row, 1), pl.ds(width, width)]
        return new_re, new_im

    def step(i, carry):
        a_re, a_im, b_re, b_im = carry
        up = i
        down = count - 1 - i
        a_re, a_im = advance(a_re, a_im, ma_ref[up], xa_ref, up)
        b_re, b_im = advance(b_re, b_im, mb_ref[down], xb_ref, down)
        out_ref[pl.ds(up, 1), pl.ds(0, width)] = a_re
        out_ref[pl.ds(up, 1), pl.ds(width, width)] = a_im
        out_ref[pl.ds(down, 1), pl.ds(2 * width, width)] = b_re
        out_ref[pl.ds(down, 1), pl.ds(3 * width, width)] = b_im
        return (a_re, a_im, b_re, b_im)

    zeros = jnp.zeros((1, width), jnp.float32)
    lax.fori_loop(0, count, step, (zeros, zeros, zeros, zeros), unroll=8)


def recurrence(ma, mb, w, xa, xb):
    count, double = xa.shape
    return pl.pallas_call(
        recurrence_kernel,
        out_shape=jax.ShapeDtypeStruct((count, 2 * double), jnp.float32),
        in_specs=[
            pl.BlockSpec(memory_space=pltpu.SMEM),
            pl.BlockSpec(memory_space=pltpu.SMEM),
            pl.BlockSpec(memory_space=pltpu.VMEM),
            pl.BlockSpec(memory_space=pltpu.VMEM),
            pl.BlockSpec(memory_space=pltpu.VMEM),
        ],
        out_specs=pl.BlockSpec(memory_space=pltpu.VMEM),
        cost_estimate=pl.CostEstimate(
            flops=20 * count * double, transcendentals=0, bytes_accessed=16 * count * double
        ),
    )(ma, mb, w, xa, xb)


MESH = pl.DeviceIdType.MESH


def ring_place(position, n):
    upper = position // (n // 2)
    return (1 - upper) * (2 * position) + upper * (2 * (n - 1 - position) + 1)


def ring_position(index, n):
    odd = index % 2
    return (1 - odd) * (index // 2) + odd * (n - 1 - index // 2)


def ring_sum_kernel(n, x_ref, r_ref, o_ref, low, slots, rs_send, rs_recv, credit, done, ag_send, ag_recv):
    rows = x_ref.shape[0]
    half = rows // 2
    size = half // n
    me = ring_position(lax.axis_index("seq"), n)
    right = ring_place((me + 1) % n, n)
    left = ring_place((me + n - 1) % n, n)
    rings = ((0, me, right, left), (1, (n - me) % n, left, right))

    barrier = pltpu.get_barrier_semaphore()
    for neighbour in (left, right):
        pl.semaphore_signal(barrier, 1, device_id={"seq": neighbour}, device_id_type=MESH)
    pl.semaphore_wait(barrier, 2)
    o_ref[...] = x_ref[...]
    low[...] = x_ref[...].astype(low.dtype)

    def block(ring, k):
        return pl.ds(pl.multiple_of(ring * half + k * size, 8), size)

    def scatter_copy(ring, place, target, s):
        return pltpu.make_async_remote_copy(
            src_ref=low.at[block(ring, (place - s + n) % n)],
            dst_ref=slots.at[ring, s % 2],
            send_sem=rs_send.at[ring, s % 2],
            recv_sem=rs_recv.at[ring, s % 2],
            device_id={"seq": target},
            device_id_type=MESH,
        )

    def scatter_step(s, carry):
        copies = []
        for ring, place, target, source in rings:

            @pl.when(s >= 2)
            def _():
                pl.semaphore_wait(credit.at[ring], 1)

            copy = scatter_copy(ring, place, target, s)
            copy.start()
            copies.append(copy)
        for (ring, place, target, source), copy in zip(rings, copies):
            copy.wait_recv()
            into = block(ring, (place - s - 1 + 2 * n) % n)
            total = o_ref[into] + slots[ring, s % 2].astype(jnp.float32)
            o_ref[into] = total
            low[into] = total.astype(low.dtype)
            copy.wait_send()

            @pl.when(s <= n - 4)
            def _():
                pl.semaphore_signal(credit.at[ring], 1, device_id={"seq": source}, device_id_type=MESH)

        return carry

    lax.fori_loop(0, n - 1, scatter_step, 0)
    for ring, place, target, source in rings:
        pl.semaphore_signal(done.at[ring], 1, device_id={"seq": source}, device_id_type=MESH)
    for ring, place, target, source in rings:
        final = block(ring, (place + 1) % n)
        r_ref[final] = o_ref[final].astype(r_ref.dtype)
    for ring, place, target, source in rings:
        pl.semaphore_wait(done.at[ring], 1)

    def gather_copy(ring, place, target, s):
        where = block(ring, (place + 1 - s + n) % n)
        return pltpu.make_async_remote_copy(
            src_ref=r_ref.at[where],
            dst_ref=r_ref.at[where],
            send_sem=ag_send.at[ring, s],
            recv_sem=ag_recv.at[ring, s],
            device_id={"seq": target},
            device_id_type=MESH,
        )

    def gather_step(s, carry):
        for ring, place, target, source in rings:

            @pl.when(s >= 1)
            def _():
                gather_copy(ring, place, target, s - 1).wait_recv()

            gather_copy(ring, place, target, s).start()

            @pl.when(s >= 1)
            def _():
                gather_copy(ring, place, target, s - 1).wait_send()

        return carry

    lax.fori_loop(0, n - 1, gather_step, 0)
    for ring, place, target, source in rings:
        last = gather_copy(ring, place, target, n - 2)
        last.wait_recv()
        last.wait_send()


def ring_sum(x, n):
    rows, lanes = x.shape
    size = rows // (2 * n)
    return pl.pallas_call(
        lambda *refs: ring_sum_kernel(n, *refs),
        out_shape=jax.ShapeDtypeStruct((rows, lanes), jnp.bfloat16),
        in_specs=[pl.BlockSpec(memory_space=pltpu.VMEM)],
        out_specs=pl.BlockSpec(memory_space=pltpu.VMEM),
        scratch_shapes=[
            pltpu.VMEM((rows, lanes), jnp.float32),
            pltpu.VMEM((rows, lanes), jnp.bfloat16),
            pltpu.VMEM((2, 2, size, lanes), jnp.bfloat16),
            pltpu.SemaphoreType.DMA((2, 2)),
            pltpu.SemaphoreType.DMA((2, 2)),
            pltpu.SemaphoreType.REGULAR((2,)),
            pltpu.SemaphoreType.REGULAR((2,)),
            pltpu.SemaphoreType.DMA((2, n - 1)),
            pltpu.SemaphoreType.DMA((2, n - 1)),
        ],
        compiler_params=pltpu.CompilerParams(collective_id=0, has_side_effects=True),
    )(x)


def sum_over_seq(parts):
    n = lax.axis_size("seq")
    flat = jnp.concatenate([part.reshape(-1) for part in parts])
    grain = 2 * n * 16 * 128
    padded = -(-flat.size // grain) * grain
    flat = jnp.pad(flat, (0, padded - flat.size)).reshape(padded // 128, 128)
    total = ring_sum(flat, n).astype(jnp.float32).reshape(-1)
    pieces = []
    start = 0
    for part in parts:
        pieces.append(total[start : start + part.size].reshape(part.shape))
        start += part.size
    return pieces


def update(weight, gradient, velocity, average, rate, decay):
    adjusted = gradient + decay * weight
    velocity_new = momentum * velocity + adjusted
    change = -rate * (adjusted + momentum * velocity_new)
    weight_new = weight + change
    average_new = smoothing * average + (1.0 - smoothing) * weight_new
    return (weight_new, velocity_new, average_new, change)


def contract_rows(left, right):
    return lax.dot_general(
        left, right, (((0,), (0,)), ((), ())), preferred_element_type=jnp.float32
    )


def contract_cols(left, right):
    return lax.dot_general(
        left, right, (((1,), (1,)), ((), ())), preferred_element_type=jnp.float32
    )


def gather_feat(value, axis):
    return lax.all_gather(value, "feat", axis=axis, tiled=True)


def body(
    activations_in,
    cotangent,
    seq_start,
    seq_length,
    input_matrix,
    output_matrix,
    gate_matrix,
    feature_vectors,
    state_vectors,
    velocity_input,
    velocity_output,
    velocity_gate,
    velocity_feature,
    velocity_state,
    average_input,
    average_output,
    average_gate,
    average_feature,
    average_state,
):
    count = activations_in.shape[0]
    shard = activations_in.shape[1]
    layers = input_matrix.shape[0]
    width = state_vectors.shape[2]
    me = lax.axis_index("feat")
    offset = me * shard

    def mine(value):
        return lax.dynamic_slice_in_dim(value, offset, shard, axis=value.ndim - 1)

    alive, carry_prev, carry_next = masks_of(seq_start, seq_length, count)
    zero = jnp.zeros((1,), jnp.float32)
    after_next = jnp.concatenate([zero, carry_next[:-1]])
    before_prev = jnp.concatenate([carry_prev[1:], zero])

    in_all = gather_feat(input_matrix.astype(jnp.bfloat16), 1)
    out_all = gather_feat(output_matrix.astype(jnp.bfloat16), 2)
    gate_all = gather_feat(gate_matrix.astype(jnp.bfloat16), 2)
    feature_all = gather_feat(feature_vectors, 2)
    stream = gather_feat(activations_in, 1).astype(jnp.float32)

    saved = []
    for layer in range(layers):
        in_low = in_all[layer]
        out_low = out_all[layer]
        gate_low = gate_all[layer]
        feature_row = feature_all[layer]
        pole_re, pole_im, factor_re, factor_im = coefficients(state_vectors[layer])
        center = jnp.mean(stream, 1, keepdims=True)
        spread = stream - center
        scale = lax.rsqrt(jnp.mean(spread * spread, 1, keepdims=True) + epsilon)
        unit = spread * scale
        normed = unit * feature_row[0] + feature_row[1]
        normed_low = normed.astype(jnp.bfloat16)
        drive = jnp.dot(normed_low, in_low, preferred_element_type=jnp.float32)
        drive_re = drive[:, :width]
        drive_im = drive[:, width:]
        source = jnp.concatenate(
            [
                (drive_re * factor_re - drive_im * factor_im) * alive[:, None],
                (drive_re * factor_im + drive_im * factor_re) * alive[:, None],
            ],
            1,
        )
        poles = jnp.stack([pole_re, pole_im])
        states = recurrence(carry_prev, carry_next, poles, source, source)
        states_low = states.astype(jnp.bfloat16)
        mixed = (
            jnp.dot(states_low, out_low, preferred_element_type=jnp.float32)
            + feature_row[2] * normed
        )
        act = smooth(mixed)
        act_low = act.astype(jnp.bfloat16)
        pre = jnp.dot(act_low, gate_low, preferred_element_type=jnp.float32) + feature_row[3]
        saved.append((scale, unit, normed_low, drive, states, states_low, mixed, act, act_low, pre))
        stream = stream + act * jax.nn.sigmoid(pre)

    grad = gather_feat(cotangent, 1).astype(jnp.float32) * alive[:, None]
    layer_grads = [None] * layers
    for layer in reversed(range(layers)):
        scale, unit, normed_low, drive, states, states_low, mixed, act, act_low, pre = saved[layer]
        in_low = in_all[layer]
        out_low = out_all[layer]
        gate_low = gate_all[layer]
        feature_row = feature_all[layer]
        state_row = state_vectors[layer]
        pole_re, pole_im, factor_re, factor_im = coefficients(state_row)
        gate = jax.nn.sigmoid(pre)
        pre_grad = (grad * act * gate * (1.0 - gate)).astype(jnp.bfloat16)
        gate_grad = contract_rows(act_low, mine(pre_grad))
        gate_bias_grad = jnp.sum(pre_grad.astype(jnp.float32), 0)
        act_grad = grad * gate + contract_cols(pre_grad, gate_low)
        mixed_grad = jax.vjp(smooth, mixed)[1](act_grad)[0]
        normed = unit * feature_row[0] + feature_row[1]
        skip_grad = jnp.sum(mixed_grad * normed, 0)
        mixed_low = mixed_grad.astype(jnp.bfloat16)
        out_grad = contract_rows(states_low, mine(mixed_low))
        states_grad = contract_cols(mixed_low, out_low)
        conj = jnp.stack([pole_re, -pole_im])
        lambdas = recurrence(
            after_next, before_prev, conj, states_grad[:, 2 * width :], states_grad[:, : 2 * width]
        )
        lb_re = lambdas[:, :width]
        lb_im = lambdas[:, width : 2 * width]
        la_re = lambdas[:, 2 * width : 3 * width]
        la_im = lambdas[:, 3 * width :]
        gu_re = la_re + lb_re
        gu_im = la_im + lb_im
        live = alive[:, None]
        dg_re = (factor_re * gu_re + factor_im * gu_im) * live
        dg_im = (factor_re * gu_im - factor_im * gu_re) * live
        drive_low = jnp.concatenate([dg_re, dg_im], 1).astype(jnp.bfloat16)
        d_re = drive[:, :width] * live
        d_im = drive[:, width:] * live
        gf_re = jnp.sum(d_re * gu_re + d_im * gu_im, 0)
        gf_im = jnp.sum(d_re * gu_im - d_im * gu_re, 0)
        zero_row = jnp.zeros((1, width), jnp.float32)
        a_re = jnp.concatenate([zero_row, states[:-1, :width]], 0) * carry_prev[:, None]
        a_im = jnp.concatenate([zero_row, states[:-1, width : 2 * width]], 0) * carry_prev[:, None]
        b_re = jnp.concatenate([states[1:, 2 * width : 3 * width], zero_row], 0) * carry_next[:, None]
        b_im = jnp.concatenate([states[1:, 3 * width :], zero_row], 0) * carry_next[:, None]
        gp_re = jnp.sum(a_re * la_re + a_im * la_im + b_re * lb_re + b_im * lb_im, 0)
        gp_im = jnp.sum(a_re * la_im - a_im * la_re + b_re * lb_im - b_im * lb_re, 0)
        row_grad = jax.vjp(coefficients, state_row)[1]((gp_re, gp_im, gf_re, gf_im))[0]
        in_grad = contract_rows(mine(normed_low), drive_low)
        normed_grad = mixed_grad * feature_row[2] + jnp.dot(
            drive_low, in_low.T, preferred_element_type=jnp.float32
        )
        gain_grad = jnp.sum(normed_grad * unit, 0)
        bias_grad = jnp.sum(normed_grad, 0)
        unit_grad = normed_grad * feature_row[0]
        first_mean = jnp.mean(unit_grad, 1, keepdims=True)
        second_mean = jnp.mean(unit_grad * unit, 1, keepdims=True)
        grad = grad + scale * (unit_grad - first_mean - unit * second_mean)
        feature_grad = mine(jnp.stack([gain_grad, bias_grad, skip_grad, gate_bias_grad]))
        layer_grads[layer] = (in_grad, out_grad, gate_grad, feature_grad, row_grad)
    stacked_in = jnp.stack([entry[0] for entry in layer_grads])
    stacked_out = jnp.stack([entry[1] for entry in layer_grads])
    stacked_gate = jnp.stack([entry[2] for entry in layer_grads])
    stacked_feature = jnp.stack([entry[3] for entry in layer_grads])
    stacked_state = jnp.stack([entry[4] for entry in layer_grads])
    summed = sum_over_seq((stacked_in, stacked_out, stacked_gate, stacked_feature, stacked_state))
    factor = 1.0 / math.sqrt(count * lax.axis_size("seq"))
    grad_in = summed[0] * factor
    grad_out = summed[1] * factor
    grad_gate = summed[2] * factor
    grad_feature = summed[3] * factor
    grad_state = summed[4] * factor
    new_in = update(input_matrix, grad_in, velocity_input, average_input, slow_rate, 0.0)
    new_out = update(output_matrix, grad_out, velocity_output, average_output, slow_rate, 0.0)
    new_gate = update(gate_matrix, grad_gate, velocity_gate, average_gate, main_rate, weight_decay)
    new_feature = update(
        feature_vectors, grad_feature, velocity_feature, average_feature, main_rate, weight_decay
    )
    new_state = update(state_vectors, grad_state, velocity_state, average_state, slow_rate, 0.0)
    return (
        mine(stream),
        mine(grad),
        grad_in,
        grad_out,
        grad_gate,
        grad_feature,
        grad_state,
        new_in[0],
        new_out[0],
        new_gate[0],
        new_feature[0],
        new_state[3],
        new_in[1],
        new_out[1],
        new_gate[1],
        new_feature[1],
        new_state[1],
        new_in[2],
        new_out[2],
        new_gate[2],
        new_feature[2],
        new_state[2],
    )


def solution(mesh):
    feat = P(None, None, "feat")
    rows = P(None, "feat", None)
    tokens = P("seq", "feat")
    return jax.shard_map(
        body,
        mesh=mesh,
        in_specs=(
            tokens,
            tokens,
            P("seq"),
            P("seq"),
            rows,
            feat,
            feat,
            feat,
            P(),
            rows,
            feat,
            feat,
            feat,
            P(),
            rows,
            feat,
            feat,
            feat,
            P(),
        ),
        out_specs=(
            tokens,
            tokens,
            rows,
            feat,
            feat,
            feat,
            P(),
            rows,
            feat,
            feat,
            feat,
            P(),
            rows,
            feat,
            feat,
            feat,
            P(),
            rows,
            feat,
            feat,
            feat,
            P(),
        ),
        check_vma=False,
    )
```

```python
import math

import jax
import jax.numpy as jnp
from jax import lax
from jax.experimental import pallas as pl
from jax.experimental.pallas import tpu as pltpu
from jax.sharding import PartitionSpec as P

epsilon = 1e-05
momentum = 0.9
smoothing = 0.5
slow_rate = 0.02
main_rate = 0.05
weight_decay = 0.1


def smooth(value):
    return jax.nn.gelu(value, approximate=False)


def masks_of(starts, lengths, count):
    position = jnp.arange(count, dtype=jnp.int32)[:, None]
    begin = starts[None, :]
    finish = begin + lengths[None, :]
    inside = (position >= begin) & (position < finish)
    alive = jnp.any(inside, 1)
    opening = jnp.any(inside & (position == begin), 1)
    closing = jnp.any(inside & (position == finish - 1), 1)
    return (
        alive.astype(jnp.float32),
        (alive & ~opening).astype(jnp.float32),
        (alive & ~closing).astype(jnp.float32),
    )


def coefficients(state_row):
    rate = -jnp.exp(state_row[0])
    frequency = state_row[1]
    timestep = jnp.exp(state_row[2])
    decay = jnp.exp(rate * timestep)
    angle = frequency * timestep
    pole_real = decay * jnp.cos(angle)
    pole_imag = decay * jnp.sin(angle)
    denom = rate * rate + frequency * frequency
    factor_real = ((pole_real - 1.0) * rate + pole_imag * frequency) / denom
    factor_imag = (pole_imag * rate - (pole_real - 1.0) * frequency) / denom
    return (pole_real, pole_imag, factor_real, factor_imag)


def recurrence_kernel(ma_ref, mb_ref, w_ref, xa_ref, xb_ref, out_ref):
    count = xa_ref.shape[0]
    width = w_ref.shape[1]
    w_re = w_ref[0:1, :]
    w_im = w_ref[1:2, :]

    def advance(h_re, h_im, keep, x_ref, row):
        h_re = h_re * keep
        h_im = h_im * keep
        new_re = w_re * h_re - w_im * h_im + x_ref[pl.ds(row, 1), pl.ds(0, width)]
        new_im = w_re * h_im + w_im * h_re + x_ref[pl.ds(row, 1), pl.ds(width, width)]
        return new_re, new_im

    def step(i, carry):
        a_re, a_im, b_re, b_im = carry
        up = i
        down = count - 1 - i
        a_re, a_im = advance(a_re, a_im, ma_ref[up], xa_ref, up)
        b_re, b_im = advance(b_re, b_im, mb_ref[down], xb_ref, down)
        out_ref[pl.ds(up, 1), pl.ds(0, width)] = a_re
        out_ref[pl.ds(up, 1), pl.ds(width, width)] = a_im
        out_ref[pl.ds(down, 1), pl.ds(2 * width, width)] = b_re
        out_ref[pl.ds(down, 1), pl.ds(3 * width, width)] = b_im
        return (a_re, a_im, b_re, b_im)

    zeros = jnp.zeros((1, width), jnp.float32)
    lax.fori_loop(0, count, step, (zeros, zeros, zeros, zeros), unroll=8)


def recurrence(ma, mb, w, xa, xb):
    count, double = xa.shape
    return pl.pallas_call(
        recurrence_kernel,
        out_shape=jax.ShapeDtypeStruct((count, 2 * double), jnp.float32),
        in_specs=[
            pl.BlockSpec(memory_space=pltpu.SMEM),
            pl.BlockSpec(memory_space=pltpu.SMEM),
            pl.BlockSpec(memory_space=pltpu.VMEM),
            pl.BlockSpec(memory_space=pltpu.VMEM),
            pl.BlockSpec(memory_space=pltpu.VMEM),
        ],
        out_specs=pl.BlockSpec(memory_space=pltpu.VMEM),
        cost_estimate=pl.CostEstimate(
            flops=20 * count * double, transcendentals=0, bytes_accessed=16 * count * double
        ),
    )(ma, mb, w, xa, xb)


MESH = pl.DeviceIdType.MESH


def ring_place(position, n):
    upper = position // (n // 2)
    return (1 - upper) * (2 * position) + upper * (2 * (n - 1 - position) + 1)


def ring_position(index, n):
    odd = index % 2
    return (1 - odd) * (index // 2) + odd * (n - 1 - index // 2)


def ring_sum_kernel(n, x_ref, r_ref, o_ref, low, slots, rs_send, rs_recv, credit, done, ag_send, ag_recv):
    rows = x_ref.shape[0]
    half = rows // 2
    size = half // n
    me = ring_position(lax.axis_index("seq"), n)
    right = ring_place((me + 1) % n, n)
    left = ring_place((me + n - 1) % n, n)
    rings = ((0, me, right, left), (1, (n - me) % n, left, right))

    barrier = pltpu.get_barrier_semaphore()
    for neighbour in (left, right):
        pl.semaphore_signal(barrier, 1, device_id={"seq": neighbour}, device_id_type=MESH)
    pl.semaphore_wait(barrier, 2)
    o_ref[...] = x_ref[...]
    low[...] = x_ref[...].astype(low.dtype)

    def block(ring, k):
        return pl.ds(pl.multiple_of(ring * half + k * size, 8), size)

    def scatter_copy(ring, place, target, s):
        return pltpu.make_async_remote_copy(
            src_ref=low.at[block(ring, (place - s + n) % n)],
            dst_ref=slots.at[ring, s % 2],
            send_sem=rs_send.at[ring, s % 2],
            recv_sem=rs_recv.at[ring, s % 2],
            device_id={"seq": target},
            device_id_type=MESH,
        )

    def scatter_step(s, carry):
        copies = []
        for ring, place, target, source in rings:

            @pl.when(s >= 2)
            def _():
                pl.semaphore_wait(credit.at[ring], 1)

            copy = scatter_copy(ring, place, target, s)
            copy.start()
            copies.append(copy)
        for (ring, place, target, source), copy in zip(rings, copies):
            copy.wait_recv()
            into = block(ring, (place - s - 1 + 2 * n) % n)
            total = o_ref[into] + slots[ring, s % 2].astype(jnp.float32)
            o_ref[into] = total
            low[into] = total.astype(low.dtype)
            copy.wait_send()

            @pl.when(s <= n - 4)
            def _():
                pl.semaphore_signal(credit.at[ring], 1, device_id={"seq": source}, device_id_type=MESH)

        return carry

    lax.fori_loop(0, n - 1, scatter_step, 0)
    for ring, place, target, source in rings:
        pl.semaphore_signal(done.at[ring], 1, device_id={"seq": source}, device_id_type=MESH)
    for ring, place, target, source in rings:
        final = block(ring, (place + 1) % n)
        r_ref[final] = o_ref[final].astype(r_ref.dtype)
    for ring, place, target, source in rings:
        pl.semaphore_wait(done.at[ring], 1)

    def gather_copy(ring, place, target, s):
        where = block(ring, (place + 1 - s + n) % n)
        return pltpu.make_async_remote_copy(
            src_ref=r_ref.at[where],
            dst_ref=r_ref.at[where],
            send_sem=ag_send.at[ring, s],
            recv_sem=ag_recv.at[ring, s],
            device_id={"seq": target},
            device_id_type=MESH,
        )

    def gather_step(s, carry):
        for ring, place, target, source in rings:

            @pl.when(s >= 1)
            def _():
                gather_copy(ring, place, target, s - 1).wait_recv()

            gather_copy(ring, place, target, s).start()

            @pl.when(s >= 1)
            def _():
                gather_copy(ring, place, target, s - 1).wait_send()

        return carry

    lax.fori_loop(0, n - 1, gather_step, 0)
    for ring, place, target, source in rings:
        last = gather_copy(ring, place, target, n - 2)
        last.wait_recv()
        last.wait_send()


def ring_sum(x, n):
    rows, lanes = x.shape
    size = rows // (2 * n)
    return pl.pallas_call(
        lambda *refs: ring_sum_kernel(n, *refs),
        out_shape=jax.ShapeDtypeStruct((rows, lanes), jnp.bfloat16),
        in_specs=[pl.BlockSpec(memory_space=pltpu.VMEM)],
        out_specs=pl.BlockSpec(memory_space=pltpu.VMEM),
        scratch_shapes=[
            pltpu.VMEM((rows, lanes), jnp.float32),
            pltpu.VMEM((rows, lanes), jnp.bfloat16),
            pltpu.VMEM((2, 2, size, lanes), jnp.bfloat16),
            pltpu.SemaphoreType.DMA((2, 2)),
            pltpu.SemaphoreType.DMA((2, 2)),
            pltpu.SemaphoreType.REGULAR((2,)),
            pltpu.SemaphoreType.REGULAR((2,)),
            pltpu.SemaphoreType.DMA((2, n - 1)),
            pltpu.SemaphoreType.DMA((2, n - 1)),
        ],
        compiler_params=pltpu.CompilerParams(collective_id=0, has_side_effects=True),
    )(x)


def sum_over_seq(parts):
    n = lax.axis_size("seq")
    flat = jnp.concatenate([part.reshape(-1) for part in parts])
    grain = 2 * n * 16 * 128
    padded = -(-flat.size // grain) * grain
    flat = jnp.pad(flat, (0, padded - flat.size)).reshape(padded // 128, 128)
    total = ring_sum(flat, n).astype(jnp.float32).reshape(-1)
    pieces = []
    start = 0
    for part in parts:
        pieces.append(total[start : start + part.size].reshape(part.shape))
        start += part.size
    return pieces


def adjoint_kernel(ma_ref, mb_ref, coef_ref, masks_ref, g_ref, states_ref, drive_ref, dg_ref, sums_ref, lam):
    count = g_ref.shape[0]
    width = coef_ref.shape[1]
    pad = 8
    w_re = coef_ref[0:1, :]
    w_im = -coef_ref[1:2, :]
    f_re = coef_ref[2:3, :]
    f_im = coef_ref[3:4, :]
    zero_rows = jnp.zeros((pad, 4 * width), jnp.float32)
    lam[0:pad, :] = zero_rows
    lam[pad + count : 2 * pad + count, :] = zero_rows

    def advance(h_re, h_im, keep, column, row):
        h_re = h_re * keep
        h_im = h_im * keep
        new_re = w_re * h_re - w_im * h_im + g_ref[pl.ds(row, 1), pl.ds(column, width)]
        new_im = w_re * h_im + w_im * h_re + g_ref[pl.ds(row, 1), pl.ds(column + width, width)]
        return new_re, new_im

    def step(i, carry):
        b_re, b_im, a_re, a_im = carry
        up = i
        down = count - 1 - i
        b_re, b_im = advance(b_re, b_im, ma_ref[up], 2 * width, up)
        a_re, a_im = advance(a_re, a_im, mb_ref[down], 0, down)
        lam[pl.ds(pad + up, 1), pl.ds(0, width)] = b_re
        lam[pl.ds(pad + up, 1), pl.ds(width, width)] = b_im
        lam[pl.ds(pad + down, 1), pl.ds(2 * width, width)] = a_re
        lam[pl.ds(pad + down, 1), pl.ds(3 * width, width)] = a_im
        return (b_re, b_im, a_re, a_im)

    zeros = jnp.zeros((1, width), jnp.float32)
    lax.fori_loop(0, count, step, (zeros, zeros, zeros, zeros), unroll=8)

    rows = 16

    def part(ref, start, column):
        return ref[pl.ds(start, rows), pl.ds(column, width)]

    def epilogue(k, sums):
        gp_re, gp_im, gf_re, gf_im = sums
        r0 = pl.multiple_of(k * rows, rows)
        live = masks_ref[pl.ds(r0, rows), 0:1]
        keep_prev = masks_ref[pl.ds(r0, rows), 1:2]
        keep_next = masks_ref[pl.ds(r0, rows), 2:3]
        lb_re = part(lam, pad + r0, 0)
        lb_im = part(lam, pad + r0, width)
        la_re = part(lam, pad + r0, 2 * width)
        la_im = part(lam, pad + r0, 3 * width)
        gu_re = la_re + lb_re
        gu_im = la_im + lb_im
        dg_ref[pl.ds(r0, rows), pl.ds(0, width)] = ((f_re * gu_re + f_im * gu_im) * live).astype(dg_ref.dtype)
        dg_ref[pl.ds(r0, rows), pl.ds(width, width)] = ((f_re * gu_im - f_im * gu_re) * live).astype(dg_ref.dtype)
        d_re = part(drive_ref, r0, 0) * live
        d_im = part(drive_ref, r0, width) * live
        gf_re = gf_re + d_re * gu_re + d_im * gu_im
        gf_im = gf_im + d_re * gu_im - d_im * gu_re
        a_re = part(states_ref, r0, 0) * keep_next
        a_im = part(states_ref, r0, width) * keep_next
        b_re = part(states_ref, r0, 2 * width) * keep_prev
        b_im = part(states_ref, r0, 3 * width) * keep_prev
        ahead_rows = lam[pl.ds(pad + r0, rows + 8), pl.ds(2 * width, 2 * width)][1 : rows + 1]
        behind_rows = lam[pl.ds(r0, rows + 8), pl.ds(0, 2 * width)][pad - 1 : pad - 1 + rows]
        na_re = ahead_rows[:, :width]
        na_im = ahead_rows[:, width:]
        pb_re = behind_rows[:, :width]
        pb_im = behind_rows[:, width:]
        gp_re = gp_re + a_re * na_re + a_im * na_im + b_re * pb_re + b_im * pb_im
        gp_im = gp_im + a_re * na_im - a_im * na_re + b_re * pb_im - b_im * pb_re
        return (gp_re, gp_im, gf_re, gf_im)

    block = jnp.zeros((rows, width), jnp.float32)
    sums = lax.fori_loop(0, count // rows, epilogue, (block, block, block, block))
    for k, value in enumerate(sums):
        sums_ref[k : k + 1, :] = jnp.sum(value, 0, keepdims=True)


def adjoint(ma, mb, coef, masks, states_grad, states, drive):
    count, quad = states_grad.shape
    width = quad // 4
    vmem = pl.BlockSpec(memory_space=pltpu.VMEM)
    smem = pl.BlockSpec(memory_space=pltpu.SMEM)
    return pl.pallas_call(
        adjoint_kernel,
        out_shape=(
            jax.ShapeDtypeStruct((count, 2 * width), jnp.bfloat16),
            jax.ShapeDtypeStruct((4, width), jnp.float32),
        ),
        in_specs=[smem, smem, vmem, vmem, vmem, vmem, vmem],
        out_specs=(vmem, vmem),
        scratch_shapes=[pltpu.VMEM((count + 16, 4 * width), jnp.float32)],
        cost_estimate=pl.CostEstimate(
            flops=60 * count * width, transcendentals=0, bytes_accessed=48 * count * width
        ),
    )(ma, mb, coef, masks, states_grad, states, drive)


def update(weight, gradient, velocity, average, rate, decay):
    adjusted = gradient + decay * weight
    velocity_new = momentum * velocity + adjusted
    change = -rate * (adjusted + momentum * velocity_new)
    weight_new = weight + change
    average_new = smoothing * average + (1.0 - smoothing) * weight_new
    return (weight_new, velocity_new, average_new, change)


def contract_rows(left, right):
    return lax.dot_general(
        left, right, (((0,), (0,)), ((), ())), preferred_element_type=jnp.float32
    )


def contract_cols(left, right):
    return lax.dot_general(
        left, right, (((1,), (1,)), ((), ())), preferred_element_type=jnp.float32
    )


def gather_feat(value, axis):
    return lax.all_gather(value, "feat", axis=axis, tiled=True)


def body(
    activations_in,
    cotangent,
    seq_start,
    seq_length,
    input_matrix,
    output_matrix,
    gate_matrix,
    feature_vectors,
    state_vectors,
    velocity_input,
    velocity_output,
    velocity_gate,
    velocity_feature,
    velocity_state,
    average_input,
    average_output,
    average_gate,
    average_feature,
    average_state,
):
    count = activations_in.shape[0]
    shard = activations_in.shape[1]
    layers = input_matrix.shape[0]
    width = state_vectors.shape[2]
    me = lax.axis_index("feat")
    offset = me * shard

    def mine(value):
        return lax.dynamic_slice_in_dim(value, offset, shard, axis=value.ndim - 1)

    alive, carry_prev, carry_next = masks_of(seq_start, seq_length, count)
    zero = jnp.zeros((1,), jnp.float32)
    after_next = jnp.concatenate([zero, carry_next[:-1]])
    before_prev = jnp.concatenate([carry_prev[1:], zero])
    mask_columns = jnp.stack([alive, carry_prev, carry_next, jnp.zeros_like(alive)], 1)

    in_all = gather_feat(input_matrix.astype(jnp.bfloat16), 1)
    out_all = gather_feat(output_matrix.astype(jnp.bfloat16), 2)
    gate_all = gather_feat(gate_matrix.astype(jnp.bfloat16), 2)
    feature_all = gather_feat(feature_vectors, 2)
    stream = gather_feat(activations_in, 1).astype(jnp.float32)

    saved = []
    for layer in range(layers):
        in_low = in_all[layer]
        out_low = out_all[layer]
        gate_low = gate_all[layer]
        feature_row = feature_all[layer]
        pole_re, pole_im, factor_re, factor_im = coefficients(state_vectors[layer])
        center = jnp.mean(stream, 1, keepdims=True)
        spread = stream - center
        scale = lax.rsqrt(jnp.mean(spread * spread, 1, keepdims=True) + epsilon)
        unit = spread * scale
        normed = unit * feature_row[0] + feature_row[1]
        normed_low = normed.astype(jnp.bfloat16)
        drive = jnp.dot(normed_low, in_low, preferred_element_type=jnp.float32)
        drive_re = drive[:, :width]
        drive_im = drive[:, width:]
        source = jnp.concatenate(
            [
                (drive_re * factor_re - drive_im * factor_im) * alive[:, None],
                (drive_re * factor_im + drive_im * factor_re) * alive[:, None],
            ],
            1,
        )
        poles = jnp.stack([pole_re, pole_im])
        states = recurrence(carry_prev, carry_next, poles, source, source)
        states_low = states.astype(jnp.bfloat16)
        mixed = (
            jnp.dot(states_low, out_low, preferred_element_type=jnp.float32)
            + feature_row[2] * normed
        )
        act = smooth(mixed)
        act_low = act.astype(jnp.bfloat16)
        pre = jnp.dot(act_low, gate_low, preferred_element_type=jnp.float32) + feature_row[3]
        saved.append((scale, unit, normed_low, drive, states, states_low, mixed, act, act_low, pre))
        stream = stream + act * jax.nn.sigmoid(pre)

    grad = gather_feat(cotangent, 1).astype(jnp.float32) * alive[:, None]
    layer_grads = [None] * layers
    for layer in reversed(range(layers)):
        scale, unit, normed_low, drive, states, states_low, mixed, act, act_low, pre = saved[layer]
        in_low = in_all[layer]
        out_low = out_all[layer]
        gate_low = gate_all[layer]
        feature_row = feature_all[layer]
        state_row = state_vectors[layer]
        pole_re, pole_im, factor_re, factor_im = coefficients(state_row)
        gate = jax.nn.sigmoid(pre)
        pre_grad = (grad * act * gate * (1.0 - gate)).astype(jnp.bfloat16)
        gate_grad = contract_rows(act_low, mine(pre_grad))
        gate_bias_grad = jnp.sum(pre_grad.astype(jnp.float32), 0)
        act_grad = grad * gate + contract_cols(pre_grad, gate_low)
        mixed_grad = jax.vjp(smooth, mixed)[1](act_grad)[0]
        normed = unit * feature_row[0] + feature_row[1]
        skip_grad = jnp.sum(mixed_grad * normed, 0)
        mixed_low = mixed_grad.astype(jnp.bfloat16)
        out_grad = contract_rows(states_low, mine(mixed_low))
        states_grad = contract_cols(mixed_low, out_low)
        coef = jnp.stack([pole_re, pole_im, factor_re, factor_im])
        drive_low, sums = adjoint(after_next, before_prev, coef, mask_columns, states_grad, states, drive)
        gp_re, gp_im, gf_re, gf_im = sums[0], sums[1], sums[2], sums[3]
        row_grad = jax.vjp(coefficients, state_row)[1]((gp_re, gp_im, gf_re, gf_im))[0]
        in_grad = contract_rows(mine(normed_low), drive_low)
        normed_grad = mixed_grad * feature_row[2] + jnp.dot(
            drive_low, in_low.T, preferred_element_type=jnp.float32
        )
        gain_grad = jnp.sum(normed_grad * unit, 0)
        bias_grad = jnp.sum(normed_grad, 0)
        unit_grad = normed_grad * feature_row[0]
        first_mean = jnp.mean(unit_grad, 1, keepdims=True)
        second_mean = jnp.mean(unit_grad * unit, 1, keepdims=True)
        grad = grad + scale * (unit_grad - first_mean - unit * second_mean)
        feature_grad = mine(jnp.stack([gain_grad, bias_grad, skip_grad, gate_bias_grad]))
        layer_grads[layer] = (in_grad, out_grad, gate_grad, feature_grad, row_grad)
    stacked_in = jnp.stack([entry[0] for entry in layer_grads])
    stacked_out = jnp.stack([entry[1] for entry in layer_grads])
    stacked_gate = jnp.stack([entry[2] for entry in layer_grads])
    stacked_feature = jnp.stack([entry[3] for entry in layer_grads])
    stacked_state = jnp.stack([entry[4] for entry in layer_grads])
    summed = sum_over_seq((stacked_in, stacked_out, stacked_gate, stacked_feature, stacked_state))
    factor = 1.0 / math.sqrt(count * lax.axis_size("seq"))
    grad_in = summed[0] * factor
    grad_out = summed[1] * factor
    grad_gate = summed[2] * factor
    grad_feature = summed[3] * factor
    grad_state = summed[4] * factor
    new_in = update(input_matrix, grad_in, velocity_input, average_input, slow_rate, 0.0)
    new_out = update(output_matrix, grad_out, velocity_output, average_output, slow_rate, 0.0)
    new_gate = update(gate_matrix, grad_gate, velocity_gate, average_gate, main_rate, weight_decay)
    new_feature = update(
        feature_vectors, grad_feature, velocity_feature, average_feature, main_rate, weight_decay
    )
    new_state = update(state_vectors, grad_state, velocity_state, average_state, slow_rate, 0.0)
    return (
        mine(stream),
        mine(grad),
        grad_in,
        grad_out,
        grad_gate,
        grad_feature,
        grad_state,
        new_in[0],
        new_out[0],
        new_gate[0],
        new_feature[0],
        new_state[3],
        new_in[1],
        new_out[1],
        new_gate[1],
        new_feature[1],
        new_state[1],
        new_in[2],
        new_out[2],
        new_gate[2],
        new_feature[2],
        new_state[2],
    )


def solution(mesh):
    feat = P(None, None, "feat")
    rows = P(None, "feat", None)
    tokens = P("seq", "feat")
    return jax.shard_map(
        body,
        mesh=mesh,
        in_specs=(
            tokens,
            tokens,
            P("seq"),
            P("seq"),
            rows,
            feat,
            feat,
            feat,
            P(),
            rows,
            feat,
            feat,
            feat,
            P(),
            rows,
            feat,
            feat,
            feat,
            P(),
        ),
        out_specs=(
            tokens,
            tokens,
            rows,
            feat,
            feat,
            feat,
            P(),
            rows,
            feat,
            feat,
            feat,
            P(),
            rows,
            feat,
            feat,
            feat,
            P(),
            rows,
            feat,
            feat,
            feat,
            P(),
        ),
        check_vma=False,
    )
```

```python
import math

import jax
import jax.numpy as jnp
from jax import lax
from jax.experimental import pallas as pl
from jax.experimental.pallas import tpu as pltpu
from jax.sharding import PartitionSpec as P

epsilon = 1e-05
momentum = 0.9
smoothing = 0.5
slow_rate = 0.02
main_rate = 0.05
weight_decay = 0.1


def smooth(value):
    return jax.nn.gelu(value, approximate=False)


def masks_of(starts, lengths, count):
    position = jnp.arange(count, dtype=jnp.int32)[:, None]
    begin = starts[None, :]
    finish = begin + lengths[None, :]
    inside = (position >= begin) & (position < finish)
    alive = jnp.any(inside, 1)
    opening = jnp.any(inside & (position == begin), 1)
    closing = jnp.any(inside & (position == finish - 1), 1)
    return (
        alive.astype(jnp.float32),
        (alive & ~opening).astype(jnp.float32),
        (alive & ~closing).astype(jnp.float32),
    )


def coefficients(state_row):
    rate = -jnp.exp(state_row[0])
    frequency = state_row[1]
    timestep = jnp.exp(state_row[2])
    decay = jnp.exp(rate * timestep)
    angle = frequency * timestep
    pole_real = decay * jnp.cos(angle)
    pole_imag = decay * jnp.sin(angle)
    denom = rate * rate + frequency * frequency
    factor_real = ((pole_real - 1.0) * rate + pole_imag * frequency) / denom
    factor_imag = (pole_imag * rate - (pole_real - 1.0) * frequency) / denom
    return (pole_real, pole_imag, factor_real, factor_imag)


def recurrence_kernel(ma_ref, mb_ref, w_ref, xa_ref, xb_ref, out_ref):
    count = xa_ref.shape[0]
    width = w_ref.shape[1]
    w_re = w_ref[0:1, :]
    w_im = w_ref[1:2, :]

    def advance(h_re, h_im, keep, x_ref, row):
        h_re = h_re * keep
        h_im = h_im * keep
        new_re = w_re * h_re - w_im * h_im + x_ref[pl.ds(row, 1), pl.ds(0, width)]
        new_im = w_re * h_im + w_im * h_re + x_ref[pl.ds(row, 1), pl.ds(width, width)]
        return new_re, new_im

    def step(i, carry):
        a_re, a_im, b_re, b_im = carry
        up = i
        down = count - 1 - i
        a_re, a_im = advance(a_re, a_im, ma_ref[up], xa_ref, up)
        b_re, b_im = advance(b_re, b_im, mb_ref[down], xb_ref, down)
        out_ref[pl.ds(up, 1), pl.ds(0, width)] = a_re
        out_ref[pl.ds(up, 1), pl.ds(width, width)] = a_im
        out_ref[pl.ds(down, 1), pl.ds(2 * width, width)] = b_re
        out_ref[pl.ds(down, 1), pl.ds(3 * width, width)] = b_im
        return (a_re, a_im, b_re, b_im)

    zeros = jnp.zeros((1, width), jnp.float32)
    lax.fori_loop(0, count, step, (zeros, zeros, zeros, zeros), unroll=8)


def recurrence(ma, mb, w, xa, xb):
    count, double = xa.shape
    return pl.pallas_call(
        recurrence_kernel,
        out_shape=jax.ShapeDtypeStruct((count, 2 * double), jnp.float32),
        in_specs=[
            pl.BlockSpec(memory_space=pltpu.SMEM),
            pl.BlockSpec(memory_space=pltpu.SMEM),
            pl.BlockSpec(memory_space=pltpu.VMEM),
            pl.BlockSpec(memory_space=pltpu.VMEM),
            pl.BlockSpec(memory_space=pltpu.VMEM),
        ],
        out_specs=pl.BlockSpec(memory_space=pltpu.VMEM),
        cost_estimate=pl.CostEstimate(
            flops=20 * count * double, transcendentals=0, bytes_accessed=16 * count * double
        ),
    )(ma, mb, w, xa, xb)


MESH = pl.DeviceIdType.MESH


def ring_place(position, n):
    upper = position // (n // 2)
    return (1 - upper) * (2 * position) + upper * (2 * (n - 1 - position) + 1)


def ring_position(index, n):
    odd = index % 2
    return (1 - odd) * (index // 2) + odd * (n - 1 - index // 2)


def ring_sum_kernel(n, x_ref, r_ref, o_ref, low, slots, rs_send, rs_recv, credit, done, ag_send, ag_recv):
    rows = x_ref.shape[0]
    half = rows // 2
    size = half // n
    me = ring_position(lax.axis_index("seq"), n)
    right = ring_place((me + 1) % n, n)
    left = ring_place((me + n - 1) % n, n)
    rings = ((0, me, right, left), (1, (n - me) % n, left, right))

    barrier = pltpu.get_barrier_semaphore()
    for neighbour in (left, right):
        pl.semaphore_signal(barrier, 1, device_id={"seq": neighbour}, device_id_type=MESH)
    pl.semaphore_wait(barrier, 2)
    o_ref[...] = x_ref[...]
    low[...] = x_ref[...].astype(low.dtype)

    def block(ring, k):
        return pl.ds(pl.multiple_of(ring * half + k * size, 8), size)

    def scatter_copy(ring, place, target, s):
        return pltpu.make_async_remote_copy(
            src_ref=low.at[block(ring, (place - s + n) % n)],
            dst_ref=slots.at[ring, s % 2],
            send_sem=rs_send.at[ring, s % 2],
            recv_sem=rs_recv.at[ring, s % 2],
            device_id={"seq": target},
            device_id_type=MESH,
        )

    def scatter_step(s, carry):
        copies = []
        for ring, place, target, source in rings:

            @pl.when(s >= 2)
            def _():
                pl.semaphore_wait(credit.at[ring], 1)

            copy = scatter_copy(ring, place, target, s)
            copy.start()
            copies.append(copy)
        for (ring, place, target, source), copy in zip(rings, copies):
            copy.wait_recv()
            into = block(ring, (place - s - 1 + 2 * n) % n)
            total = o_ref[into] + slots[ring, s % 2].astype(jnp.float32)
            o_ref[into] = total
            low[into] = total.astype(low.dtype)
            copy.wait_send()

            @pl.when(s <= n - 4)
            def _():
                pl.semaphore_signal(credit.at[ring], 1, device_id={"seq": source}, device_id_type=MESH)

        return carry

    lax.fori_loop(0, n - 1, scatter_step, 0)
    for ring, place, target, source in rings:
        pl.semaphore_signal(done.at[ring], 1, device_id={"seq": source}, device_id_type=MESH)
    for ring, place, target, source in rings:
        final = block(ring, (place + 1) % n)
        r_ref[final] = o_ref[final].astype(r_ref.dtype)
    for ring, place, target, source in rings:
        pl.semaphore_wait(done.at[ring], 1)

    def gather_copy(ring, place, target, s):
        where = block(ring, (place + 1 - s + n) % n)
        return pltpu.make_async_remote_copy(
            src_ref=r_ref.at[where],
            dst_ref=r_ref.at[where],
            send_sem=ag_send.at[ring, s],
            recv_sem=ag_recv.at[ring, s],
            device_id={"seq": target},
            device_id_type=MESH,
        )

    def gather_step(s, carry):
        for ring, place, target, source in rings:

            @pl.when(s >= 1)
            def _():
                gather_copy(ring, place, target, s - 1).wait_recv()

            gather_copy(ring, place, target, s).start()

            @pl.when(s >= 1)
            def _():
                gather_copy(ring, place, target, s - 1).wait_send()

        return carry

    lax.fori_loop(0, n - 1, gather_step, 0)
    for ring, place, target, source in rings:
        last = gather_copy(ring, place, target, n - 2)
        last.wait_recv()
        last.wait_send()


def ring_sum(x, n):
    rows, lanes = x.shape
    size = rows // (2 * n)
    return pl.pallas_call(
        lambda *refs: ring_sum_kernel(n, *refs),
        out_shape=jax.ShapeDtypeStruct((rows, lanes), jnp.bfloat16),
        in_specs=[pl.BlockSpec(memory_space=pltpu.VMEM)],
        out_specs=pl.BlockSpec(memory_space=pltpu.VMEM),
        scratch_shapes=[
            pltpu.VMEM((rows, lanes), jnp.float32),
            pltpu.VMEM((rows, lanes), jnp.bfloat16),
            pltpu.VMEM((2, 2, size, lanes), jnp.bfloat16),
            pltpu.SemaphoreType.DMA((2, 2)),
            pltpu.SemaphoreType.DMA((2, 2)),
            pltpu.SemaphoreType.REGULAR((2,)),
            pltpu.SemaphoreType.REGULAR((2,)),
            pltpu.SemaphoreType.DMA((2, n - 1)),
            pltpu.SemaphoreType.DMA((2, n - 1)),
        ],
        compiler_params=pltpu.CompilerParams(collective_id=0, has_side_effects=True),
    )(x)


def sum_over_seq(parts):
    n = lax.axis_size("seq")
    flat = jnp.concatenate([part.reshape(-1) for part in parts])
    grain = 2 * n * 16 * 128
    padded = -(-flat.size // grain) * grain
    flat = jnp.pad(flat, (0, padded - flat.size)).reshape(padded // 128, 128)
    total = ring_sum(flat, n).astype(jnp.float32).reshape(-1)
    pieces = []
    start = 0
    for part in parts:
        pieces.append(total[start : start + part.size].reshape(part.shape))
        start += part.size
    return pieces


def adjoint_kernel(ma_ref, mb_ref, coef_ref, masks_ref, g_ref, states_ref, drive_ref, dg_ref, sums_ref, lam):
    count = g_ref.shape[0]
    width = coef_ref.shape[1]
    pad = 8
    w_re = coef_ref[0:1, :]
    w_im = -coef_ref[1:2, :]
    f_re = coef_ref[2:3, :]
    f_im = coef_ref[3:4, :]
    zero_rows = jnp.zeros((pad, 4 * width), jnp.float32)
    lam[0:pad, :] = zero_rows
    lam[pad + count : 2 * pad + count, :] = zero_rows

    def advance(h_re, h_im, keep, column, row):
        h_re = h_re * keep
        h_im = h_im * keep
        new_re = w_re * h_re - w_im * h_im + g_ref[pl.ds(row, 1), pl.ds(column, width)]
        new_im = w_re * h_im + w_im * h_re + g_ref[pl.ds(row, 1), pl.ds(column + width, width)]
        return new_re, new_im

    def step(i, carry):
        b_re, b_im, a_re, a_im = carry
        up = i
        down = count - 1 - i
        b_re, b_im = advance(b_re, b_im, ma_ref[up], 2 * width, up)
        a_re, a_im = advance(a_re, a_im, mb_ref[down], 0, down)
        lam[pl.ds(pad + up, 1), pl.ds(0, width)] = b_re
        lam[pl.ds(pad + up, 1), pl.ds(width, width)] = b_im
        lam[pl.ds(pad + down, 1), pl.ds(2 * width, width)] = a_re
        lam[pl.ds(pad + down, 1), pl.ds(3 * width, width)] = a_im
        return (b_re, b_im, a_re, a_im)

    zeros = jnp.zeros((1, width), jnp.float32)
    lax.fori_loop(0, count, step, (zeros, zeros, zeros, zeros), unroll=8)

    rows = 16

    def part(ref, start, column):
        return ref[pl.ds(start, rows), pl.ds(column, width)]

    def epilogue(k, sums):
        gp_re, gp_im, gf_re, gf_im = sums
        r0 = pl.multiple_of(k * rows, rows)
        live = masks_ref[pl.ds(r0, rows), 0:1]
        keep_prev = masks_ref[pl.ds(r0, rows), 1:2]
        keep_next = masks_ref[pl.ds(r0, rows), 2:3]
        lb_re = part(lam, pad + r0, 0)
        lb_im = part(lam, pad + r0, width)
        la_re = part(lam, pad + r0, 2 * width)
        la_im = part(lam, pad + r0, 3 * width)
        gu_re = la_re + lb_re
        gu_im = la_im + lb_im
        dg_ref[pl.ds(r0, rows), pl.ds(0, width)] = ((f_re * gu_re + f_im * gu_im) * live).astype(dg_ref.dtype)
        dg_ref[pl.ds(r0, rows), pl.ds(width, width)] = ((f_re * gu_im - f_im * gu_re) * live).astype(dg_ref.dtype)
        d_re = part(drive_ref, r0, 0) * live
        d_im = part(drive_ref, r0, width) * live
        gf_re = gf_re + d_re * gu_re + d_im * gu_im
        gf_im = gf_im + d_re * gu_im - d_im * gu_re
        a_re = part(states_ref, r0, 0) * keep_next
        a_im = part(states_ref, r0, width) * keep_next
        b_re = part(states_ref, r0, 2 * width) * keep_prev
        b_im = part(states_ref, r0, 3 * width) * keep_prev
        ahead_rows = lam[pl.ds(pad + r0, rows + 8), pl.ds(2 * width, 2 * width)][1 : rows + 1]
        behind_rows = lam[pl.ds(r0, rows + 8), pl.ds(0, 2 * width)][pad - 1 : pad - 1 + rows]
        na_re = ahead_rows[:, :width]
        na_im = ahead_rows[:, width:]
        pb_re = behind_rows[:, :width]
        pb_im = behind_rows[:, width:]
        gp_re = gp_re + a_re * na_re + a_im * na_im + b_re * pb_re + b_im * pb_im
        gp_im = gp_im + a_re * na_im - a_im * na_re + b_re * pb_im - b_im * pb_re
        return (gp_re, gp_im, gf_re, gf_im)

    block = jnp.zeros((rows, width), jnp.float32)
    sums = lax.fori_loop(0, count // rows, epilogue, (block, block, block, block))
    for k, value in enumerate(sums):
        sums_ref[k : k + 1, :] = jnp.sum(value, 0, keepdims=True)


def adjoint(ma, mb, coef, masks, states_grad, states, drive):
    count, quad = states_grad.shape
    width = quad // 4
    vmem = pl.BlockSpec(memory_space=pltpu.VMEM)
    smem = pl.BlockSpec(memory_space=pltpu.SMEM)
    return pl.pallas_call(
        adjoint_kernel,
        out_shape=(
            jax.ShapeDtypeStruct((count, 2 * width), jnp.bfloat16),
            jax.ShapeDtypeStruct((4, width), jnp.float32),
        ),
        in_specs=[smem, smem, vmem, vmem, vmem, vmem, vmem],
        out_specs=(vmem, vmem),
        scratch_shapes=[pltpu.VMEM((count + 16, 4 * width), jnp.float32)],
        cost_estimate=pl.CostEstimate(
            flops=60 * count * width, transcendentals=0, bytes_accessed=48 * count * width
        ),
    )(ma, mb, coef, masks, states_grad, states, drive)


def update(weight, gradient, velocity, average, rate, decay):
    adjusted = gradient + decay * weight
    velocity_new = momentum * velocity + adjusted
    change = -rate * (adjusted + momentum * velocity_new)
    weight_new = weight + change
    average_new = smoothing * average + (1.0 - smoothing) * weight_new
    return (weight_new, velocity_new, average_new, change)


def contract_rows(left, right):
    return lax.dot_general(
        left, right, (((0,), (0,)), ((), ())), preferred_element_type=jnp.float32
    )


def contract_cols(left, right):
    return lax.dot_general(
        left, right, (((1,), (1,)), ((), ())), preferred_element_type=jnp.float32
    )


def gather_feat(value, axis):
    return lax.all_gather(value, "feat", axis=axis, tiled=True)


def gather_layer_weights(in_shard, out_shard, gate_shard, after=None):
    pieces = (in_shard.T, out_shard, gate_shard)
    packed = jnp.concatenate([piece.astype(jnp.bfloat16) for piece in pieces], 0)
    if after is not None:
        packed, after = lax.optimization_barrier((packed, after))
    stacked = lax.all_gather(packed, "feat", axis=0, tiled=False)
    result = []
    start = 0
    for piece in pieces:
        result.append(stacked[:, start : start + piece.shape[0]])
        start += piece.shape[0]
    return result


def lanes_of(value, parts):
    return value.reshape(value.shape[0], parts, value.shape[1] // parts)


def body(
    activations_in,
    cotangent,
    seq_start,
    seq_length,
    input_matrix,
    output_matrix,
    gate_matrix,
    feature_vectors,
    state_vectors,
    velocity_input,
    velocity_output,
    velocity_gate,
    velocity_feature,
    velocity_state,
    average_input,
    average_output,
    average_gate,
    average_feature,
    average_state,
):
    count = activations_in.shape[0]
    shard = activations_in.shape[1]
    layers = input_matrix.shape[0]
    width = state_vectors.shape[2]
    me = lax.axis_index("feat")
    offset = me * shard

    def mine(value):
        return lax.dynamic_slice_in_dim(value, offset, shard, axis=value.ndim - 1)

    alive, carry_prev, carry_next = masks_of(seq_start, seq_length, count)
    zero = jnp.zeros((1,), jnp.float32)
    after_next = jnp.concatenate([zero, carry_next[:-1]])
    before_prev = jnp.concatenate([carry_prev[1:], zero])
    mask_columns = jnp.stack([alive, carry_prev, carry_next, jnp.zeros_like(alive)], 1)

    weights = [gather_layer_weights(input_matrix[0], output_matrix[0], gate_matrix[0])]
    parts = lax.axis_size("feat")
    feature_all = gather_feat(feature_vectors, 2)
    stream = gather_feat(activations_in, 1).astype(jnp.float32)

    saved = []
    for layer in range(layers):
        in_t, out_w, gate_w = weights[layer]
        feature_row = feature_all[layer]
        pole_re, pole_im, factor_re, factor_im = coefficients(state_vectors[layer])
        center = jnp.mean(stream, 1, keepdims=True)
        spread = stream - center
        scale = lax.rsqrt(jnp.mean(spread * spread, 1, keepdims=True) + epsilon)
        unit = spread * scale
        normed = unit * feature_row[0] + feature_row[1]
        normed_low = normed.astype(jnp.bfloat16)
        drive = jnp.einsum(
            "tfk,fck->tc", lanes_of(normed_low, parts), in_t, preferred_element_type=jnp.float32
        )
        drive_re = drive[:, :width]
        drive_im = drive[:, width:]
        source = jnp.concatenate(
            [
                (drive_re * factor_re - drive_im * factor_im) * alive[:, None],
                (drive_re * factor_im + drive_im * factor_re) * alive[:, None],
            ],
            1,
        )
        poles = jnp.stack([pole_re, pole_im])
        states = recurrence(carry_prev, carry_next, poles, source, source)
        if layer + 1 < layers:
            weights.append(
                gather_layer_weights(
                    input_matrix[layer + 1], output_matrix[layer + 1], gate_matrix[layer + 1], states
                )
            )
        states_low = states.astype(jnp.bfloat16)
        mixed = (
            jnp.einsum("tk,fkc->tfc", states_low, out_w, preferred_element_type=jnp.float32).reshape(
                count, -1
            )
            + feature_row[2] * normed
        )
        act = smooth(mixed)
        act_low = act.astype(jnp.bfloat16)
        pre = (
            jnp.einsum("tk,fkc->tfc", act_low, gate_w, preferred_element_type=jnp.float32).reshape(
                count, -1
            )
            + feature_row[3]
        )
        saved.append((scale, unit, normed_low, drive, states, states_low, mixed, act, act_low, pre))
        stream = stream + act * jax.nn.sigmoid(pre)

    first_stream, cotangent = lax.optimization_barrier((saved[0][7], cotangent))
    grad = gather_feat(cotangent, 1).astype(jnp.float32) * alive[:, None]
    layer_grads = [None] * layers
    for layer in reversed(range(layers)):
        scale, unit, normed_low, drive, states, states_low, mixed, act, act_low, pre = saved[layer]
        in_t, out_w, gate_w = weights[layer]
        feature_row = feature_all[layer]
        state_row = state_vectors[layer]
        pole_re, pole_im, factor_re, factor_im = coefficients(state_row)
        gate = jax.nn.sigmoid(pre)
        pre_grad = (grad * act * gate * (1.0 - gate)).astype(jnp.bfloat16)
        gate_grad = contract_rows(act_low, mine(pre_grad))
        gate_bias_grad = jnp.sum(pre_grad.astype(jnp.float32), 0)
        act_grad = grad * gate + jnp.einsum(
            "tfc,fkc->tk", lanes_of(pre_grad, parts), gate_w, preferred_element_type=jnp.float32
        )
        mixed_grad = jax.vjp(smooth, mixed)[1](act_grad)[0]
        normed = unit * feature_row[0] + feature_row[1]
        skip_grad = jnp.sum(mixed_grad * normed, 0)
        mixed_low = mixed_grad.astype(jnp.bfloat16)
        out_grad = contract_rows(states_low, mine(mixed_low))
        states_grad = jnp.einsum(
            "tfc,fkc->tk", lanes_of(mixed_low, parts), out_w, preferred_element_type=jnp.float32
        )
        coef = jnp.stack([pole_re, pole_im, factor_re, factor_im])
        drive_low, sums = adjoint(after_next, before_prev, coef, mask_columns, states_grad, states, drive)
        gp_re, gp_im, gf_re, gf_im = sums[0], sums[1], sums[2], sums[3]
        row_grad = jax.vjp(coefficients, state_row)[1]((gp_re, gp_im, gf_re, gf_im))[0]
        in_grad = contract_rows(mine(normed_low), drive_low)
        normed_grad = mixed_grad * feature_row[2] + jnp.einsum(
            "tc,fck->tfk", drive_low, in_t, preferred_element_type=jnp.float32
        ).reshape(count, -1)
        gain_grad = jnp.sum(normed_grad * unit, 0)
        bias_grad = jnp.sum(normed_grad, 0)
        unit_grad = normed_grad * feature_row[0]
        first_mean = jnp.mean(unit_grad, 1, keepdims=True)
        second_mean = jnp.mean(unit_grad * unit, 1, keepdims=True)
        grad = grad + scale * (unit_grad - first_mean - unit * second_mean)
        feature_grad = mine(jnp.stack([gain_grad, bias_grad, skip_grad, gate_bias_grad]))
        layer_grads[layer] = (in_grad, out_grad, gate_grad, feature_grad, row_grad)
    stacked_in = jnp.stack([entry[0] for entry in layer_grads])
    stacked_out = jnp.stack([entry[1] for entry in layer_grads])
    stacked_gate = jnp.stack([entry[2] for entry in layer_grads])
    stacked_feature = jnp.stack([entry[3] for entry in layer_grads])
    stacked_state = jnp.stack([entry[4] for entry in layer_grads])
    summed = sum_over_seq((stacked_in, stacked_out, stacked_gate, stacked_feature, stacked_state))
    factor = 1.0 / math.sqrt(count * lax.axis_size("seq"))
    grad_in = summed[0] * factor
    grad_out = summed[1] * factor
    grad_gate = summed[2] * factor
    grad_feature = summed[3] * factor
    grad_state = summed[4] * factor
    new_in = update(input_matrix, grad_in, velocity_input, average_input, slow_rate, 0.0)
    new_out = update(output_matrix, grad_out, velocity_output, average_output, slow_rate, 0.0)
    new_gate = update(gate_matrix, grad_gate, velocity_gate, average_gate, main_rate, weight_decay)
    new_feature = update(
        feature_vectors, grad_feature, velocity_feature, average_feature, main_rate, weight_decay
    )
    new_state = update(state_vectors, grad_state, velocity_state, average_state, slow_rate, 0.0)
    return (
        mine(stream),
        mine(grad),
        grad_in,
        grad_out,
        grad_gate,
        grad_feature,
        grad_state,
        new_in[0],
        new_out[0],
        new_gate[0],
        new_feature[0],
        new_state[3],
        new_in[1],
        new_out[1],
        new_gate[1],
        new_feature[1],
        new_state[1],
        new_in[2],
        new_out[2],
        new_gate[2],
        new_feature[2],
        new_state[2],
    )


def solution(mesh):
    feat = P(None, None, "feat")
    rows = P(None, "feat", None)
    tokens = P("seq", "feat")
    return jax.shard_map(
        body,
        mesh=mesh,
        in_specs=(
            tokens,
            tokens,
            P("seq"),
            P("seq"),
            rows,
            feat,
            feat,
            feat,
            P(),
            rows,
            feat,
            feat,
            feat,
            P(),
            rows,
            feat,
            feat,
            feat,
            P(),
        ),
        out_specs=(
            tokens,
            tokens,
            rows,
            feat,
            feat,
            feat,
            P(),
            rows,
            feat,
            feat,
            feat,
            P(),
            rows,
            feat,
            feat,
            feat,
            P(),
            rows,
            feat,
            feat,
            feat,
            P(),
        ),
        check_vma=False,
    )
```

```python
import math

import jax
import jax.numpy as jnp
from jax import lax
from jax.experimental import pallas as pl
from jax.experimental.pallas import tpu as pltpu
from jax.sharding import PartitionSpec as P

epsilon = 1e-05
momentum = 0.9
smoothing = 0.5
slow_rate = 0.02
main_rate = 0.05
weight_decay = 0.1


def smooth(value):
    return jax.nn.gelu(value, approximate=False)


def masks_of(starts, lengths, count):
    position = jnp.arange(count, dtype=jnp.int32)[:, None]
    begin = starts[None, :]
    finish = begin + lengths[None, :]
    inside = (position >= begin) & (position < finish)
    alive = jnp.any(inside, 1)
    opening = jnp.any(inside & (position == begin), 1)
    closing = jnp.any(inside & (position == finish - 1), 1)
    return (
        alive.astype(jnp.float32),
        (alive & ~opening).astype(jnp.float32),
        (alive & ~closing).astype(jnp.float32),
    )


def coefficients(state_row):
    rate = -jnp.exp(state_row[0])
    frequency = state_row[1]
    timestep = jnp.exp(state_row[2])
    decay = jnp.exp(rate * timestep)
    angle = frequency * timestep
    pole_real = decay * jnp.cos(angle)
    pole_imag = decay * jnp.sin(angle)
    denom = rate * rate + frequency * frequency
    factor_real = ((pole_real - 1.0) * rate + pole_imag * frequency) / denom
    factor_imag = (pole_imag * rate - (pole_real - 1.0) * frequency) / denom
    return (pole_real, pole_imag, factor_real, factor_imag)


def recurrence_kernel(ma_ref, mb_ref, w_ref, xa_ref, xb_ref, out_ref):
    count = xa_ref.shape[0]
    width = w_ref.shape[1]
    w_re = w_ref[0:1, :]
    w_im = w_ref[1:2, :]

    def advance(h_re, h_im, keep, x_ref, row):
        h_re = h_re * keep
        h_im = h_im * keep
        new_re = w_re * h_re - w_im * h_im + x_ref[pl.ds(row, 1), pl.ds(0, width)]
        new_im = w_re * h_im + w_im * h_re + x_ref[pl.ds(row, 1), pl.ds(width, width)]
        return new_re, new_im

    def step(i, carry):
        a_re, a_im, b_re, b_im = carry
        up = i
        down = count - 1 - i
        a_re, a_im = advance(a_re, a_im, ma_ref[up], xa_ref, up)
        b_re, b_im = advance(b_re, b_im, mb_ref[down], xb_ref, down)
        out_ref[pl.ds(up, 1), pl.ds(0, width)] = a_re
        out_ref[pl.ds(up, 1), pl.ds(width, width)] = a_im
        out_ref[pl.ds(down, 1), pl.ds(2 * width, width)] = b_re
        out_ref[pl.ds(down, 1), pl.ds(3 * width, width)] = b_im
        return (a_re, a_im, b_re, b_im)

    zeros = jnp.zeros((1, width), jnp.float32)
    lax.fori_loop(0, count, step, (zeros, zeros, zeros, zeros), unroll=8)


def recurrence(ma, mb, w, xa, xb):
    count, double = xa.shape
    return pl.pallas_call(
        recurrence_kernel,
        out_shape=jax.ShapeDtypeStruct((count, 2 * double), jnp.float32),
        in_specs=[
            pl.BlockSpec(memory_space=pltpu.SMEM),
            pl.BlockSpec(memory_space=pltpu.SMEM),
            pl.BlockSpec(memory_space=pltpu.VMEM),
            pl.BlockSpec(memory_space=pltpu.VMEM),
            pl.BlockSpec(memory_space=pltpu.VMEM),
        ],
        out_specs=pl.BlockSpec(memory_space=pltpu.VMEM),
        cost_estimate=pl.CostEstimate(
            flops=20 * count * double, transcendentals=0, bytes_accessed=16 * count * double
        ),
    )(ma, mb, w, xa, xb)


MESH = pl.DeviceIdType.MESH


def ring_place(position, n):
    upper = position // (n // 2)
    return (1 - upper) * (2 * position) + upper * (2 * (n - 1 - position) + 1)


def ring_position(index, n):
    odd = index % 2
    return (1 - odd) * (index // 2) + odd * (n - 1 - index // 2)


def ring_sum_kernel(n, x_ref, r_ref, o_ref, low, slots, rs_send, rs_recv, credit, done, ag_send, ag_recv):
    rows = x_ref.shape[0]
    half = rows // 2
    size = half // n
    me = ring_position(lax.axis_index("seq"), n)
    right = ring_place((me + 1) % n, n)
    left = ring_place((me + n - 1) % n, n)
    rings = ((0, me, right, left), (1, (n - me) % n, left, right))

    barrier = pltpu.get_barrier_semaphore()
    for neighbour in (left, right):
        pl.semaphore_signal(barrier, 1, device_id={"seq": neighbour}, device_id_type=MESH)
    pl.semaphore_wait(barrier, 2)
    o_ref[...] = x_ref[...]
    low[...] = x_ref[...].astype(low.dtype)

    def block(ring, k):
        return pl.ds(pl.multiple_of(ring * half + k * size, 8), size)

    def scatter_copy(ring, place, target, s):
        return pltpu.make_async_remote_copy(
            src_ref=low.at[block(ring, (place - s + n) % n)],
            dst_ref=slots.at[ring, s % 2],
            send_sem=rs_send.at[ring, s % 2],
            recv_sem=rs_recv.at[ring, s % 2],
            device_id={"seq": target},
            device_id_type=MESH,
        )

    def scatter_step(s, carry):
        copies = []
        for ring, place, target, source in rings:

            @pl.when(s >= 2)
            def _():
                pl.semaphore_wait(credit.at[ring], 1)

            copy = scatter_copy(ring, place, target, s)
            copy.start()
            copies.append(copy)
        for (ring, place, target, source), copy in zip(rings, copies):
            copy.wait_recv()
            into = block(ring, (place - s - 1 + 2 * n) % n)
            total = o_ref[into] + slots[ring, s % 2].astype(jnp.float32)
            o_ref[into] = total
            low[into] = total.astype(low.dtype)
            copy.wait_send()

            @pl.when(s <= n - 4)
            def _():
                pl.semaphore_signal(credit.at[ring], 1, device_id={"seq": source}, device_id_type=MESH)

        return carry

    lax.fori_loop(0, n - 1, scatter_step, 0)
    for ring, place, target, source in rings:
        pl.semaphore_signal(done.at[ring], 1, device_id={"seq": source}, device_id_type=MESH)
    for ring, place, target, source in rings:
        final = block(ring, (place + 1) % n)
        r_ref[final] = o_ref[final].astype(r_ref.dtype)
    for ring, place, target, source in rings:
        pl.semaphore_wait(done.at[ring], 1)

    def gather_copy(ring, place, target, s):
        where = block(ring, (place + 1 - s + n) % n)
        return pltpu.make_async_remote_copy(
            src_ref=r_ref.at[where],
            dst_ref=r_ref.at[where],
            send_sem=ag_send.at[ring, s],
            recv_sem=ag_recv.at[ring, s],
            device_id={"seq": target},
            device_id_type=MESH,
        )

    def gather_step(s, carry):
        for ring, place, target, source in rings:

            @pl.when(s >= 1)
            def _():
                gather_copy(ring, place, target, s - 1).wait_recv()

            gather_copy(ring, place, target, s).start()

            @pl.when(s >= 1)
            def _():
                gather_copy(ring, place, target, s - 1).wait_send()

        return carry

    lax.fori_loop(0, n - 1, gather_step, 0)
    for ring, place, target, source in rings:
        last = gather_copy(ring, place, target, n - 2)
        last.wait_recv()
        last.wait_send()


def ring_sum(x, n):
    rows, lanes = x.shape
    size = rows // (2 * n)
    return pl.pallas_call(
        lambda *refs: ring_sum_kernel(n, *refs),
        out_shape=jax.ShapeDtypeStruct((rows, lanes), jnp.bfloat16),
        in_specs=[pl.BlockSpec(memory_space=pltpu.VMEM)],
        out_specs=pl.BlockSpec(memory_space=pltpu.VMEM),
        scratch_shapes=[
            pltpu.VMEM((rows, lanes), jnp.float32),
            pltpu.VMEM((rows, lanes), jnp.bfloat16),
            pltpu.VMEM((2, 2, size, lanes), jnp.bfloat16),
            pltpu.SemaphoreType.DMA((2, 2)),
            pltpu.SemaphoreType.DMA((2, 2)),
            pltpu.SemaphoreType.REGULAR((2,)),
            pltpu.SemaphoreType.REGULAR((2,)),
            pltpu.SemaphoreType.DMA((2, n - 1)),
            pltpu.SemaphoreType.DMA((2, n - 1)),
        ],
        compiler_params=pltpu.CompilerParams(collective_id=0, has_side_effects=True),
    )(x)


def sum_over_seq(parts):
    n = lax.axis_size("seq")
    flat = jnp.concatenate([part.reshape(-1) for part in parts])
    grain = 2 * n * 16 * 128
    padded = -(-flat.size // grain) * grain
    flat = jnp.pad(flat, (0, padded - flat.size)).reshape(padded // 128, 128)
    total = ring_sum(flat, n).astype(jnp.float32).reshape(-1)
    pieces = []
    start = 0
    for part in parts:
        pieces.append(total[start : start + part.size].reshape(part.shape))
        start += part.size
    return pieces


def adjoint_kernel(ma_ref, mb_ref, coef_ref, masks_ref, g_ref, states_ref, drive_ref, dg_ref, sums_ref, lam):
    count = g_ref.shape[0]
    width = coef_ref.shape[1]
    pad = 8
    w_re = coef_ref[0:1, :]
    w_im = -coef_ref[1:2, :]
    f_re = coef_ref[2:3, :]
    f_im = coef_ref[3:4, :]
    zero_rows = jnp.zeros((pad, 4 * width), jnp.float32)
    lam[0:pad, :] = zero_rows
    lam[pad + count : 2 * pad + count, :] = zero_rows

    def advance(h_re, h_im, keep, column, row):
        h_re = h_re * keep
        h_im = h_im * keep
        new_re = w_re * h_re - w_im * h_im + g_ref[pl.ds(row, 1), pl.ds(column, width)]
        new_im = w_re * h_im + w_im * h_re + g_ref[pl.ds(row, 1), pl.ds(column + width, width)]
        return new_re, new_im

    def step(i, carry):
        b_re, b_im, a_re, a_im = carry
        up = i
        down = count - 1 - i
        b_re, b_im = advance(b_re, b_im, ma_ref[up], 2 * width, up)
        a_re, a_im = advance(a_re, a_im, mb_ref[down], 0, down)
        lam[pl.ds(pad + up, 1), pl.ds(0, width)] = b_re
        lam[pl.ds(pad + up, 1), pl.ds(width, width)] = b_im
        lam[pl.ds(pad + down, 1), pl.ds(2 * width, width)] = a_re
        lam[pl.ds(pad + down, 1), pl.ds(3 * width, width)] = a_im
        return (b_re, b_im, a_re, a_im)

    zeros = jnp.zeros((1, width), jnp.float32)
    lax.fori_loop(0, count, step, (zeros, zeros, zeros, zeros), unroll=8)

    rows = 16

    def part(ref, start, column):
        return ref[pl.ds(start, rows), pl.ds(column, width)]

    def epilogue(k, sums):
        gp_re, gp_im, gf_re, gf_im = sums
        r0 = pl.multiple_of(k * rows, rows)
        live = masks_ref[pl.ds(r0, rows), 0:1]
        keep_prev = masks_ref[pl.ds(r0, rows), 1:2]
        keep_next = masks_ref[pl.ds(r0, rows), 2:3]
        lb_re = part(lam, pad + r0, 0)
        lb_im = part(lam, pad + r0, width)
        la_re = part(lam, pad + r0, 2 * width)
        la_im = part(lam, pad + r0, 3 * width)
        gu_re = la_re + lb_re
        gu_im = la_im + lb_im
        dg_ref[pl.ds(r0, rows), pl.ds(0, width)] = ((f_re * gu_re + f_im * gu_im) * live).astype(dg_ref.dtype)
        dg_ref[pl.ds(r0, rows), pl.ds(width, width)] = ((f_re * gu_im - f_im * gu_re) * live).astype(dg_ref.dtype)
        d_re = part(drive_ref, r0, 0) * live
        d_im = part(drive_ref, r0, width) * live
        gf_re = gf_re + d_re * gu_re + d_im * gu_im
        gf_im = gf_im + d_re * gu_im - d_im * gu_re
        a_re = part(states_ref, r0, 0) * keep_next
        a_im = part(states_ref, r0, width) * keep_next
        b_re = part(states_ref, r0, 2 * width) * keep_prev
        b_im = part(states_ref, r0, 3 * width) * keep_prev
        ahead_rows = lam[pl.ds(pad + r0, rows + 8), pl.ds(2 * width, 2 * width)][1 : rows + 1]
        behind_rows = lam[pl.ds(r0, rows + 8), pl.ds(0, 2 * width)][pad - 1 : pad - 1 + rows]
        na_re = ahead_rows[:, :width]
        na_im = ahead_rows[:, width:]
        pb_re = behind_rows[:, :width]
        pb_im = behind_rows[:, width:]
        gp_re = gp_re + a_re * na_re + a_im * na_im + b_re * pb_re + b_im * pb_im
        gp_im = gp_im + a_re * na_im - a_im * na_re + b_re * pb_im - b_im * pb_re
        return (gp_re, gp_im, gf_re, gf_im)

    block = jnp.zeros((rows, width), jnp.float32)
    sums = lax.fori_loop(0, count // rows, epilogue, (block, block, block, block))
    for k, value in enumerate(sums):
        sums_ref[k : k + 1, :] = jnp.sum(value, 0, keepdims=True)


def adjoint(ma, mb, coef, masks, states_grad, states, drive):
    count, quad = states_grad.shape
    width = quad // 4
    vmem = pl.BlockSpec(memory_space=pltpu.VMEM)
    smem = pl.BlockSpec(memory_space=pltpu.SMEM)
    return pl.pallas_call(
        adjoint_kernel,
        out_shape=(
            jax.ShapeDtypeStruct((count, 2 * width), jnp.bfloat16),
            jax.ShapeDtypeStruct((4, width), jnp.float32),
        ),
        in_specs=[smem, smem, vmem, vmem, vmem, vmem, vmem],
        out_specs=(vmem, vmem),
        scratch_shapes=[pltpu.VMEM((count + 16, 4 * width), jnp.float32)],
        cost_estimate=pl.CostEstimate(
            flops=60 * count * width, transcendentals=0, bytes_accessed=48 * count * width
        ),
    )(ma, mb, coef, masks, states_grad, states, drive)


def update(weight, gradient, velocity, average, rate, decay):
    adjusted = gradient + decay * weight
    velocity_new = momentum * velocity + adjusted
    change = -rate * (adjusted + momentum * velocity_new)
    weight_new = weight + change
    average_new = smoothing * average + (1.0 - smoothing) * weight_new
    return (weight_new, velocity_new, average_new, change)


def contract_rows(left, right):
    return lax.dot_general(
        left, right, (((0,), (0,)), ((), ())), preferred_element_type=jnp.float32
    )


def contract_cols(left, right):
    return lax.dot_general(
        left, right, (((1,), (1,)), ((), ())), preferred_element_type=jnp.float32
    )


def gather_feat(value, axis):
    return lax.all_gather(value, "feat", axis=axis, tiled=True)


def gather_layer_weights(in_shard, out_shard, gate_shard, after=None):
    pieces = (in_shard.T, out_shard, gate_shard)
    packed = jnp.concatenate([piece.astype(jnp.bfloat16) for piece in pieces], 0)
    if after is not None:
        packed, after = lax.optimization_barrier((packed, after))
    stacked = lax.all_gather(packed, "feat", axis=0, tiled=False)
    result = []
    start = 0
    for piece in pieces:
        result.append(stacked[:, start : start + piece.shape[0]])
        start += piece.shape[0]
    in_t, out_w, gate_w = result
    in_full = jnp.transpose(in_t, (0, 2, 1)).reshape(-1, in_t.shape[1])
    return [in_full, lanes_joined(out_w), lanes_joined(gate_w), stacked]


def lanes_joined(stacked):
    moved = jnp.moveaxis(stacked, 0, 1)
    return moved.reshape(moved.shape[0], -1)


def lanes_of(value, parts):
    return value.reshape(value.shape[0], parts, value.shape[1] // parts)


def body(
    activations_in,
    cotangent,
    seq_start,
    seq_length,
    input_matrix,
    output_matrix,
    gate_matrix,
    feature_vectors,
    state_vectors,
    velocity_input,
    velocity_output,
    velocity_gate,
    velocity_feature,
    velocity_state,
    average_input,
    average_output,
    average_gate,
    average_feature,
    average_state,
):
    count = activations_in.shape[0]
    shard = activations_in.shape[1]
    layers = input_matrix.shape[0]
    width = state_vectors.shape[2]
    me = lax.axis_index("feat")
    offset = me * shard

    def mine(value):
        return lax.dynamic_slice_in_dim(value, offset, shard, axis=value.ndim - 1)

    alive, carry_prev, carry_next = masks_of(seq_start, seq_length, count)
    zero = jnp.zeros((1,), jnp.float32)
    after_next = jnp.concatenate([zero, carry_next[:-1]])
    before_prev = jnp.concatenate([carry_prev[1:], zero])
    mask_columns = jnp.stack([alive, carry_prev, carry_next, jnp.zeros_like(alive)], 1)

    weights = [gather_layer_weights(input_matrix[0], output_matrix[0], gate_matrix[0])]
    for k in range(1, layers):
        weights.append(
            gather_layer_weights(input_matrix[k], output_matrix[k], gate_matrix[k], weights[-1][3])
        )
    feature_all = gather_feat(feature_vectors, 2)
    stream = gather_feat(activations_in, 1).astype(jnp.float32)

    saved = []
    for layer in range(layers):
        in_low, out_low, gate_low, _ = weights[layer]
        feature_row = feature_all[layer]
        pole_re, pole_im, factor_re, factor_im = coefficients(state_vectors[layer])
        center = jnp.mean(stream, 1, keepdims=True)
        spread = stream - center
        scale = lax.rsqrt(jnp.mean(spread * spread, 1, keepdims=True) + epsilon)
        unit = spread * scale
        normed = unit * feature_row[0] + feature_row[1]
        normed_low = normed.astype(jnp.bfloat16)
        drive = jnp.dot(normed_low, in_low, preferred_element_type=jnp.float32)
        drive_re = drive[:, :width]
        drive_im = drive[:, width:]
        source = jnp.concatenate(
            [
                (drive_re * factor_re - drive_im * factor_im) * alive[:, None],
                (drive_re * factor_im + drive_im * factor_re) * alive[:, None],
            ],
            1,
        )
        poles = jnp.stack([pole_re, pole_im])
        states = recurrence(carry_prev, carry_next, poles, source, source)
        states_low = states.astype(jnp.bfloat16)
        mixed = (
            jnp.dot(states_low, out_low, preferred_element_type=jnp.float32)
            + feature_row[2] * normed
        )
        act = smooth(mixed)
        act_low = act.astype(jnp.bfloat16)
        pre = jnp.dot(act_low, gate_low, preferred_element_type=jnp.float32) + feature_row[3]
        saved.append((scale, unit, normed_low, drive, states, states_low, mixed, act, act_low, pre))
        stream = stream + act * jax.nn.sigmoid(pre)

    stream, cotangent = lax.optimization_barrier((stream, cotangent))
    grad = gather_feat(cotangent, 1).astype(jnp.float32) * alive[:, None]
    layer_grads = [None] * layers
    for layer in reversed(range(layers)):
        scale, unit, normed_low, drive, states, states_low, mixed, act, act_low, pre = saved[layer]
        in_low, out_low, gate_low, _ = weights[layer]
        feature_row = feature_all[layer]
        state_row = state_vectors[layer]
        pole_re, pole_im, factor_re, factor_im = coefficients(state_row)
        gate = jax.nn.sigmoid(pre)
        pre_grad = (grad * act * gate * (1.0 - gate)).astype(jnp.bfloat16)
        gate_grad = contract_rows(act_low, mine(pre_grad))
        gate_bias_grad = jnp.sum(pre_grad.astype(jnp.float32), 0)
        act_grad = grad * gate + contract_cols(pre_grad, gate_low)
        mixed_grad = jax.vjp(smooth, mixed)[1](act_grad)[0]
        normed = unit * feature_row[0] + feature_row[1]
        skip_grad = jnp.sum(mixed_grad * normed, 0)
        mixed_low = mixed_grad.astype(jnp.bfloat16)
        out_grad = contract_rows(states_low, mine(mixed_low))
        states_grad = contract_cols(mixed_low, out_low)
        coef = jnp.stack([pole_re, pole_im, factor_re, factor_im])
        drive_low, sums = adjoint(after_next, before_prev, coef, mask_columns, states_grad, states, drive)
        gp_re, gp_im, gf_re, gf_im = sums[0], sums[1], sums[2], sums[3]
        row_grad = jax.vjp(coefficients, state_row)[1]((gp_re, gp_im, gf_re, gf_im))[0]
        in_grad = contract_rows(mine(normed_low), drive_low)
        normed_grad = mixed_grad * feature_row[2] + jnp.dot(
            drive_low, in_low.T, preferred_element_type=jnp.float32
        )
        gain_grad = jnp.sum(normed_grad * unit, 0)
        bias_grad = jnp.sum(normed_grad, 0)
        unit_grad = normed_grad * feature_row[0]
        first_mean = jnp.mean(unit_grad, 1, keepdims=True)
        second_mean = jnp.mean(unit_grad * unit, 1, keepdims=True)
        grad = grad + scale * (unit_grad - first_mean - unit * second_mean)
        feature_grad = mine(jnp.stack([gain_grad, bias_grad, skip_grad, gate_bias_grad]))
        layer_grads[layer] = (in_grad, out_grad, gate_grad, feature_grad, row_grad)
    stacked_in = jnp.stack([entry[0] for entry in layer_grads])
    stacked_out = jnp.stack([entry[1] for entry in layer_grads])
    stacked_gate = jnp.stack([entry[2] for entry in layer_grads])
    stacked_feature = jnp.stack([entry[3] for entry in layer_grads])
    stacked_state = jnp.stack([entry[4] for entry in layer_grads])
    summed = sum_over_seq((stacked_in, stacked_out, stacked_gate, stacked_feature, stacked_state))
    factor = 1.0 / math.sqrt(count * lax.axis_size("seq"))
    grad_in = summed[0] * factor
    grad_out = summed[1] * factor
    grad_gate = summed[2] * factor
    grad_feature = summed[3] * factor
    grad_state = summed[4] * factor
    new_in = update(input_matrix, grad_in, velocity_input, average_input, slow_rate, 0.0)
    new_out = update(output_matrix, grad_out, velocity_output, average_output, slow_rate, 0.0)
    new_gate = update(gate_matrix, grad_gate, velocity_gate, average_gate, main_rate, weight_decay)
    new_feature = update(
        feature_vectors, grad_feature, velocity_feature, average_feature, main_rate, weight_decay
    )
    new_state = update(state_vectors, grad_state, velocity_state, average_state, slow_rate, 0.0)
    return (
        mine(stream),
        mine(grad),
        grad_in,
        grad_out,
        grad_gate,
        grad_feature,
        grad_state,
        new_in[0],
        new_out[0],
        new_gate[0],
        new_feature[0],
        new_state[3],
        new_in[1],
        new_out[1],
        new_gate[1],
        new_feature[1],
        new_state[1],
        new_in[2],
        new_out[2],
        new_gate[2],
        new_feature[2],
        new_state[2],
    )


def solution(mesh):
    feat = P(None, None, "feat")
    rows = P(None, "feat", None)
    tokens = P("seq", "feat")
    return jax.shard_map(
        body,
        mesh=mesh,
        in_specs=(
            tokens,
            tokens,
            P("seq"),
            P("seq"),
            rows,
            feat,
            feat,
            feat,
            P(),
            rows,
            feat,
            feat,
            feat,
            P(),
            rows,
            feat,
            feat,
            feat,
            P(),
        ),
        out_specs=(
            tokens,
            tokens,
            rows,
            feat,
            feat,
            feat,
            P(),
            rows,
            feat,
            feat,
            feat,
            P(),
            rows,
            feat,
            feat,
            feat,
            P(),
            rows,
            feat,
            feat,
            feat,
            P(),
        ),
        check_vma=False,
    )
```

```python
import math

import jax
import jax.numpy as jnp
from jax import lax
from jax.experimental import pallas as pl
from jax.experimental.pallas import tpu as pltpu
from jax.sharding import PartitionSpec as P

epsilon = 1e-05
momentum = 0.9
smoothing = 0.5
slow_rate = 0.02
main_rate = 0.05
weight_decay = 0.1


def smooth(value):
    return jax.nn.gelu(value, approximate=False)


def masks_of(starts, lengths, count):
    position = jnp.arange(count, dtype=jnp.int32)[:, None]
    begin = starts[None, :]
    finish = begin + lengths[None, :]
    inside = (position >= begin) & (position < finish)
    alive = jnp.any(inside, 1)
    opening = jnp.any(inside & (position == begin), 1)
    closing = jnp.any(inside & (position == finish - 1), 1)
    return (
        alive.astype(jnp.float32),
        (alive & ~opening).astype(jnp.float32),
        (alive & ~closing).astype(jnp.float32),
    )


def coefficients(state_row):
    rate = -jnp.exp(state_row[0])
    frequency = state_row[1]
    timestep = jnp.exp(state_row[2])
    decay = jnp.exp(rate * timestep)
    angle = frequency * timestep
    pole_real = decay * jnp.cos(angle)
    pole_imag = decay * jnp.sin(angle)
    denom = rate * rate + frequency * frequency
    factor_real = ((pole_real - 1.0) * rate + pole_imag * frequency) / denom
    factor_imag = (pole_imag * rate - (pole_real - 1.0) * frequency) / denom
    return (pole_real, pole_imag, factor_real, factor_imag)


def recurrence_kernel(ma_ref, mb_ref, w_ref, xa_ref, xb_ref, out_ref):
    count = xa_ref.shape[0]
    width = w_ref.shape[1]
    w_re = w_ref[0:1, :]
    w_im = w_ref[1:2, :]

    def advance(h_re, h_im, keep, x_ref, row):
        h_re = h_re * keep
        h_im = h_im * keep
        new_re = w_re * h_re - w_im * h_im + x_ref[pl.ds(row, 1), pl.ds(0, width)]
        new_im = w_re * h_im + w_im * h_re + x_ref[pl.ds(row, 1), pl.ds(width, width)]
        return new_re, new_im

    def step(i, carry):
        a_re, a_im, b_re, b_im = carry
        up = i
        down = count - 1 - i
        a_re, a_im = advance(a_re, a_im, ma_ref[up], xa_ref, up)
        b_re, b_im = advance(b_re, b_im, mb_ref[down], xb_ref, down)
        out_ref[pl.ds(up, 1), pl.ds(0, width)] = a_re
        out_ref[pl.ds(up, 1), pl.ds(width, width)] = a_im
        out_ref[pl.ds(down, 1), pl.ds(2 * width, width)] = b_re
        out_ref[pl.ds(down, 1), pl.ds(3 * width, width)] = b_im
        return (a_re, a_im, b_re, b_im)

    zeros = jnp.zeros((1, width), jnp.float32)
    lax.fori_loop(0, count, step, (zeros, zeros, zeros, zeros), unroll=8)


def recurrence(ma, mb, w, xa, xb):
    count, double = xa.shape
    return pl.pallas_call(
        recurrence_kernel,
        out_shape=jax.ShapeDtypeStruct((count, 2 * double), jnp.float32),
        in_specs=[
            pl.BlockSpec(memory_space=pltpu.SMEM),
            pl.BlockSpec(memory_space=pltpu.SMEM),
            pl.BlockSpec(memory_space=pltpu.VMEM),
            pl.BlockSpec(memory_space=pltpu.VMEM),
            pl.BlockSpec(memory_space=pltpu.VMEM),
        ],
        out_specs=pl.BlockSpec(memory_space=pltpu.VMEM),
        cost_estimate=pl.CostEstimate(
            flops=20 * count * double, transcendentals=0, bytes_accessed=16 * count * double
        ),
    )(ma, mb, w, xa, xb)


MESH = pl.DeviceIdType.MESH


def ring_place(position, n):
    upper = position // (n // 2)
    return (1 - upper) * (2 * position) + upper * (2 * (n - 1 - position) + 1)


def ring_position(index, n):
    odd = index % 2
    return (1 - odd) * (index // 2) + odd * (n - 1 - index // 2)


def ring_sum_kernel(n, x_ref, r_ref, o_ref, low, slots, rs_send, rs_recv, credit, done, ag_send, ag_recv):
    rows = x_ref.shape[0]
    half = rows // 2
    size = half // n
    me = ring_position(lax.axis_index("seq"), n)
    right = ring_place((me + 1) % n, n)
    left = ring_place((me + n - 1) % n, n)
    rings = ((0, me, right, left), (1, (n - me) % n, left, right))

    barrier = pltpu.get_barrier_semaphore()
    for neighbour in (left, right):
        pl.semaphore_signal(barrier, 1, device_id={"seq": neighbour}, device_id_type=MESH)
    pl.semaphore_wait(barrier, 2)
    o_ref[...] = x_ref[...]
    low[...] = x_ref[...].astype(low.dtype)

    def block(ring, k):
        return pl.ds(pl.multiple_of(ring * half + k * size, 8), size)

    def scatter_copy(ring, place, target, s):
        return pltpu.make_async_remote_copy(
            src_ref=low.at[block(ring, (place - s + n) % n)],
            dst_ref=slots.at[ring, s % 2],
            send_sem=rs_send.at[ring, s % 2],
            recv_sem=rs_recv.at[ring, s % 2],
            device_id={"seq": target},
            device_id_type=MESH,
        )

    def scatter_step(s, carry):
        copies = []
        for ring, place, target, source in rings:

            @pl.when(s >= 2)
            def _():
                pl.semaphore_wait(credit.at[ring], 1)

            copy = scatter_copy(ring, place, target, s)
            copy.start()
            copies.append(copy)
        for (ring, place, target, source), copy in zip(rings, copies):
            copy.wait_recv()
            into = block(ring, (place - s - 1 + 2 * n) % n)
            total = o_ref[into] + slots[ring, s % 2].astype(jnp.float32)
            o_ref[into] = total
            low[into] = total.astype(low.dtype)
            copy.wait_send()

            @pl.when(s <= n - 4)
            def _():
                pl.semaphore_signal(credit.at[ring], 1, device_id={"seq": source}, device_id_type=MESH)

        return carry

    lax.fori_loop(0, n - 1, scatter_step, 0)
    for ring, place, target, source in rings:
        pl.semaphore_signal(done.at[ring], 1, device_id={"seq": source}, device_id_type=MESH)
    for ring, place, target, source in rings:
        final = block(ring, (place + 1) % n)
        r_ref[final] = o_ref[final].astype(r_ref.dtype)
    for ring, place, target, source in rings:
        pl.semaphore_wait(done.at[ring], 1)

    def gather_copy(ring, place, target, s):
        where = block(ring, (place + 1 - s + n) % n)
        return pltpu.make_async_remote_copy(
            src_ref=r_ref.at[where],
            dst_ref=r_ref.at[where],
            send_sem=ag_send.at[ring, s],
            recv_sem=ag_recv.at[ring, s],
            device_id={"seq": target},
            device_id_type=MESH,
        )

    def gather_step(s, carry):
        for ring, place, target, source in rings:

            @pl.when(s >= 1)
            def _():
                gather_copy(ring, place, target, s - 1).wait_recv()

            gather_copy(ring, place, target, s).start()

            @pl.when(s >= 1)
            def _():
                gather_copy(ring, place, target, s - 1).wait_send()

        return carry

    lax.fori_loop(0, n - 1, gather_step, 0)
    for ring, place, target, source in rings:
        last = gather_copy(ring, place, target, n - 2)
        last.wait_recv()
        last.wait_send()


def ring_sum(x, n):
    rows, lanes = x.shape
    size = rows // (2 * n)
    return pl.pallas_call(
        lambda *refs: ring_sum_kernel(n, *refs),
        out_shape=jax.ShapeDtypeStruct((rows, lanes), jnp.bfloat16),
        in_specs=[pl.BlockSpec(memory_space=pltpu.VMEM)],
        out_specs=pl.BlockSpec(memory_space=pltpu.VMEM),
        scratch_shapes=[
            pltpu.VMEM((rows, lanes), jnp.float32),
            pltpu.VMEM((rows, lanes), jnp.bfloat16),
            pltpu.VMEM((2, 2, size, lanes), jnp.bfloat16),
            pltpu.SemaphoreType.DMA((2, 2)),
            pltpu.SemaphoreType.DMA((2, 2)),
            pltpu.SemaphoreType.REGULAR((2,)),
            pltpu.SemaphoreType.REGULAR((2,)),
            pltpu.SemaphoreType.DMA((2, n - 1)),
            pltpu.SemaphoreType.DMA((2, n - 1)),
        ],
        compiler_params=pltpu.CompilerParams(collective_id=0, has_side_effects=True),
    )(x)


def sum_over_seq(parts):
    n = lax.axis_size("seq")
    flat = jnp.concatenate([part.reshape(-1) for part in parts])
    grain = 2 * n * 16 * 128
    padded = -(-flat.size // grain) * grain
    flat = jnp.pad(flat, (0, padded - flat.size)).reshape(padded // 128, 128)
    total = ring_sum(flat, n).astype(jnp.float32).reshape(-1)
    pieces = []
    start = 0
    for part in parts:
        pieces.append(total[start : start + part.size].reshape(part.shape))
        start += part.size
    return pieces


def adjoint_kernel(ma_ref, mb_ref, coef_ref, masks_ref, g_ref, states_ref, drive_ref, dg_ref, sums_ref, lam):
    count = g_ref.shape[0]
    width = coef_ref.shape[1]
    pad = 8
    w_re = coef_ref[0:1, :]
    w_im = -coef_ref[1:2, :]
    f_re = coef_ref[2:3, :]
    f_im = coef_ref[3:4, :]
    zero_rows = jnp.zeros((pad, 4 * width), jnp.float32)
    lam[0:pad, :] = zero_rows
    lam[pad + count : 2 * pad + count, :] = zero_rows

    def advance(h_re, h_im, keep, column, row):
        h_re = h_re * keep
        h_im = h_im * keep
        new_re = w_re * h_re - w_im * h_im + g_ref[pl.ds(row, 1), pl.ds(column, width)]
        new_im = w_re * h_im + w_im * h_re + g_ref[pl.ds(row, 1), pl.ds(column + width, width)]
        return new_re, new_im

    def step(i, carry):
        b_re, b_im, a_re, a_im = carry
        up = i
        down = count - 1 - i
        b_re, b_im = advance(b_re, b_im, ma_ref[up], 2 * width, up)
        a_re, a_im = advance(a_re, a_im, mb_ref[down], 0, down)
        lam[pl.ds(pad + up, 1), pl.ds(0, width)] = b_re
        lam[pl.ds(pad + up, 1), pl.ds(width, width)] = b_im
        lam[pl.ds(pad + down, 1), pl.ds(2 * width, width)] = a_re
        lam[pl.ds(pad + down, 1), pl.ds(3 * width, width)] = a_im
        return (b_re, b_im, a_re, a_im)

    zeros = jnp.zeros((1, width), jnp.float32)
    lax.fori_loop(0, count, step, (zeros, zeros, zeros, zeros), unroll=8)

    rows = 16

    def part(ref, start, column):
        return ref[pl.ds(start, rows), pl.ds(column, width)]

    def epilogue(k, sums):
        gp_re, gp_im, gf_re, gf_im = sums
        r0 = pl.multiple_of(k * rows, rows)
        live = masks_ref[pl.ds(r0, rows), 0:1]
        keep_prev = masks_ref[pl.ds(r0, rows), 1:2]
        keep_next = masks_ref[pl.ds(r0, rows), 2:3]
        lb_re = part(lam, pad + r0, 0)
        lb_im = part(lam, pad + r0, width)
        la_re = part(lam, pad + r0, 2 * width)
        la_im = part(lam, pad + r0, 3 * width)
        gu_re = la_re + lb_re
        gu_im = la_im + lb_im
        dg_ref[pl.ds(r0, rows), pl.ds(0, width)] = ((f_re * gu_re + f_im * gu_im) * live).astype(dg_ref.dtype)
        dg_ref[pl.ds(r0, rows), pl.ds(width, width)] = ((f_re * gu_im - f_im * gu_re) * live).astype(dg_ref.dtype)
        d_re = part(drive_ref, r0, 0) * live
        d_im = part(drive_ref, r0, width) * live
        gf_re = gf_re + d_re * gu_re + d_im * gu_im
        gf_im = gf_im + d_re * gu_im - d_im * gu_re
        a_re = part(states_ref, r0, 0) * keep_next
        a_im = part(states_ref, r0, width) * keep_next
        b_re = part(states_ref, r0, 2 * width) * keep_prev
        b_im = part(states_ref, r0, 3 * width) * keep_prev
        ahead_rows = lam[pl.ds(pad + r0, rows + 8), pl.ds(2 * width, 2 * width)][1 : rows + 1]
        behind_rows = lam[pl.ds(r0, rows + 8), pl.ds(0, 2 * width)][pad - 1 : pad - 1 + rows]
        na_re = ahead_rows[:, :width]
        na_im = ahead_rows[:, width:]
        pb_re = behind_rows[:, :width]
        pb_im = behind_rows[:, width:]
        gp_re = gp_re + a_re * na_re + a_im * na_im + b_re * pb_re + b_im * pb_im
        gp_im = gp_im + a_re * na_im - a_im * na_re + b_re * pb_im - b_im * pb_re
        return (gp_re, gp_im, gf_re, gf_im)

    block = jnp.zeros((rows, width), jnp.float32)
    sums = lax.fori_loop(0, count // rows, epilogue, (block, block, block, block))
    for k, value in enumerate(sums):
        sums_ref[k : k + 1, :] = jnp.sum(value, 0, keepdims=True)


def adjoint(ma, mb, coef, masks, states_grad, states, drive):
    count, quad = states_grad.shape
    width = quad // 4
    vmem = pl.BlockSpec(memory_space=pltpu.VMEM)
    smem = pl.BlockSpec(memory_space=pltpu.SMEM)
    return pl.pallas_call(
        adjoint_kernel,
        out_shape=(
            jax.ShapeDtypeStruct((count, 2 * width), jnp.bfloat16),
            jax.ShapeDtypeStruct((4, width), jnp.float32),
        ),
        in_specs=[smem, smem, vmem, vmem, vmem, vmem, vmem],
        out_specs=(vmem, vmem),
        scratch_shapes=[pltpu.VMEM((count + 16, 4 * width), jnp.float32)],
        cost_estimate=pl.CostEstimate(
            flops=60 * count * width, transcendentals=0, bytes_accessed=48 * count * width
        ),
    )(ma, mb, coef, masks, states_grad, states, drive)


def update(weight, gradient, velocity, average, rate, decay):
    adjusted = gradient + decay * weight
    velocity_new = momentum * velocity + adjusted
    change = -rate * (adjusted + momentum * velocity_new)
    weight_new = weight + change
    average_new = smoothing * average + (1.0 - smoothing) * weight_new
    return (weight_new, velocity_new, average_new, change)


def contract_rows(left, right):
    return lax.dot_general(
        left, right, (((0,), (0,)), ((), ())), preferred_element_type=jnp.float32
    )


def contract_cols(left, right):
    return lax.dot_general(
        left, right, (((1,), (1,)), ((), ())), preferred_element_type=jnp.float32
    )


def gather_feat(value, axis):
    return lax.all_gather(value, "feat", axis=axis, tiled=True)


def split_exact(value):
    high = lax.reduce_precision(value, exponent_bits=8, mantissa_bits=7)
    rest = value - high
    middle = lax.reduce_precision(rest, exponent_bits=8, mantissa_bits=7)
    low = rest - middle
    return jnp.concatenate([high, middle, low], 0).astype(jnp.bfloat16)


def join_exact(pieces):
    third = pieces.shape[-2] // 3
    pieces = pieces.astype(jnp.float32)
    return pieces[..., :third, :] + (pieces[..., third : 2 * third, :] + pieces[..., 2 * third :, :])


def gather_packed(pieces, after=None):
    packed = jnp.concatenate(pieces, 0)
    if after is not None:
        packed, after = lax.optimization_barrier((packed, after))
    parts = lax.axis_size("feat")
    cores = 2
    across = [[c + cores * k for k in range(parts // cores)] for c in range(cores)]
    within = [[cores * k + c for c in range(cores)] for k in range(parts // cores)]
    stage = lax.all_gather(packed, "feat", axis=0, tiled=False, axis_index_groups=across)
    stage = lax.all_gather(stage, "feat", axis=0, tiled=False, axis_index_groups=within)
    stacked = jnp.swapaxes(stage, 0, 1).reshape((parts,) + packed.shape)
    result = []
    start = 0
    for piece in pieces:
        result.append(stacked[:, start : start + piece.shape[0]])
        start += piece.shape[0]
    return result


def lanes_joined(stacked):
    moved = jnp.moveaxis(stacked, 0, 1)
    return moved.reshape(moved.shape[0], -1)


def layer_weights(in_shard, out_shard, gate_shard, extra, after=None):
    pieces = [in_shard.T.astype(jnp.bfloat16), out_shard.astype(jnp.bfloat16), gate_shard.astype(jnp.bfloat16)]
    gathered = gather_packed(pieces + list(extra), after)
    in_t, out_w, gate_w = gathered[:3]
    in_full = jnp.transpose(in_t, (0, 2, 1)).reshape(-1, in_t.shape[1])
    return [in_full, lanes_joined(out_w), lanes_joined(gate_w), gathered[3:]]


def lanes_of(value, parts):
    return value.reshape(value.shape[0], parts, value.shape[1] // parts)


def body(
    activations_in,
    cotangent,
    seq_start,
    seq_length,
    input_matrix,
    output_matrix,
    gate_matrix,
    feature_vectors,
    state_vectors,
    velocity_input,
    velocity_output,
    velocity_gate,
    velocity_feature,
    velocity_state,
    average_input,
    average_output,
    average_gate,
    average_feature,
    average_state,
):
    count = activations_in.shape[0]
    shard = activations_in.shape[1]
    layers = input_matrix.shape[0]
    width = state_vectors.shape[2]
    me = lax.axis_index("feat")
    offset = me * shard

    def mine(value):
        return lax.dynamic_slice_in_dim(value, offset, shard, axis=value.ndim - 1)

    alive, carry_prev, carry_next = masks_of(seq_start, seq_length, count)
    zero = jnp.zeros((1,), jnp.float32)
    after_next = jnp.concatenate([zero, carry_next[:-1]])
    before_prev = jnp.concatenate([carry_prev[1:], zero])
    mask_columns = jnp.stack([alive, carry_prev, carry_next, jnp.zeros_like(alive)], 1)

    feature_pieces = split_exact(feature_vectors.reshape(-1, shard))
    weights = [
        layer_weights(
            input_matrix[0],
            output_matrix[0],
            gate_matrix[0],
            (feature_pieces, activations_in) + (() if layers > 1 else (cotangent,)),
        )
    ]
    for k in range(1, layers):
        extra = (cotangent,) if k == layers - 1 else ()
        weights.append(
            layer_weights(input_matrix[k], output_matrix[k], gate_matrix[k], extra, weights[-1][3][0])
        )
    feature_all = lanes_joined(join_exact(weights[0][3][0])).reshape(feature_vectors.shape[:-1] + (-1,))
    stream = lanes_joined(weights[0][3][1]).astype(jnp.float32)
    cotangent_all = lanes_joined(weights[-1][3][-1]) if layers > 1 else lanes_joined(weights[0][3][2])

    saved = []
    for layer in range(layers):
        in_low, out_low, gate_low, _ = weights[layer]
        feature_row = feature_all[layer]
        pole_re, pole_im, factor_re, factor_im = coefficients(state_vectors[layer])
        center = jnp.mean(stream, 1, keepdims=True)
        spread = stream - center
        scale = lax.rsqrt(jnp.mean(spread * spread, 1, keepdims=True) + epsilon)
        unit = spread * scale
        normed = unit * feature_row[0] + feature_row[1]
        normed_low = normed.astype(jnp.bfloat16)
        drive = jnp.dot(normed_low, in_low, preferred_element_type=jnp.float32)
        drive_re = drive[:, :width]
        drive_im = drive[:, width:]
        source = jnp.concatenate(
            [
                (drive_re * factor_re - drive_im * factor_im) * alive[:, None],
                (drive_re * factor_im + drive_im * factor_re) * alive[:, None],
            ],
            1,
        )
        poles = jnp.stack([pole_re, pole_im])
        states = recurrence(carry_prev, carry_next, poles, source, source)
        states_low = states.astype(jnp.bfloat16)
        mixed = (
            jnp.dot(states_low, out_low, preferred_element_type=jnp.float32)
            + feature_row[2] * normed
        )
        act = smooth(mixed)
        act_low = act.astype(jnp.bfloat16)
        pre = jnp.dot(act_low, gate_low, preferred_element_type=jnp.float32) + feature_row[3]
        saved.append((scale, unit, normed_low, drive, states, states_low, mixed, act, act_low, pre))
        stream = stream + act * jax.nn.sigmoid(pre)

    grad = cotangent_all.astype(jnp.float32) * alive[:, None]
    layer_grads = [None] * layers
    for layer in reversed(range(layers)):
        scale, unit, normed_low, drive, states, states_low, mixed, act, act_low, pre = saved[layer]
        in_low, out_low, gate_low, _ = weights[layer]
        feature_row = feature_all[layer]
        state_row = state_vectors[layer]
        pole_re, pole_im, factor_re, factor_im = coefficients(state_row)
        gate = jax.nn.sigmoid(pre)
        pre_grad = (grad * act * gate * (1.0 - gate)).astype(jnp.bfloat16)
        gate_grad = contract_rows(act_low, mine(pre_grad))
        gate_bias_grad = jnp.sum(pre_grad.astype(jnp.float32), 0)
        act_grad = grad * gate + contract_cols(pre_grad, gate_low)
        mixed_grad = jax.vjp(smooth, mixed)[1](act_grad)[0]
        normed = unit * feature_row[0] + feature_row[1]
        skip_grad = jnp.sum(mixed_grad * normed, 0)
        mixed_low = mixed_grad.astype(jnp.bfloat16)
        out_grad = contract_rows(states_low, mine(mixed_low))
        states_grad = contract_cols(mixed_low, out_low)
        coef = jnp.stack([pole_re, pole_im, factor_re, factor_im])
        drive_low, sums = adjoint(after_next, before_prev, coef, mask_columns, states_grad, states, drive)
        gp_re, gp_im, gf_re, gf_im = sums[0], sums[1], sums[2], sums[3]
        row_grad = jax.vjp(coefficients, state_row)[1]((gp_re, gp_im, gf_re, gf_im))[0]
        in_grad = contract_rows(mine(normed_low), drive_low)
        normed_grad = mixed_grad * feature_row[2] + jnp.dot(
            drive_low, in_low.T, preferred_element_type=jnp.float32
        )
        gain_grad = jnp.sum(normed_grad * unit, 0)
        bias_grad = jnp.sum(normed_grad, 0)
        unit_grad = normed_grad * feature_row[0]
        first_mean = jnp.mean(unit_grad, 1, keepdims=True)
        second_mean = jnp.mean(unit_grad * unit, 1, keepdims=True)
        grad = grad + scale * (unit_grad - first_mean - unit * second_mean)
        feature_grad = mine(jnp.stack([gain_grad, bias_grad, skip_grad, gate_bias_grad]))
        layer_grads[layer] = (in_grad, out_grad, gate_grad, feature_grad, row_grad)
    stacked_in = jnp.stack([entry[0] for entry in layer_grads])
    stacked_out = jnp.stack([entry[1] for entry in layer_grads])
    stacked_gate = jnp.stack([entry[2] for entry in layer_grads])
    stacked_feature = jnp.stack([entry[3] for entry in layer_grads])
    stacked_state = jnp.stack([entry[4] for entry in layer_grads])
    summed = sum_over_seq((stacked_in, stacked_out, stacked_gate, stacked_feature, stacked_state))
    factor = 1.0 / math.sqrt(count * lax.axis_size("seq"))
    grad_in = summed[0] * factor
    grad_out = summed[1] * factor
    grad_gate = summed[2] * factor
    grad_feature = summed[3] * factor
    grad_state = summed[4] * factor
    new_in = update(input_matrix, grad_in, velocity_input, average_input, slow_rate, 0.0)
    new_out = update(output_matrix, grad_out, velocity_output, average_output, slow_rate, 0.0)
    new_gate = update(gate_matrix, grad_gate, velocity_gate, average_gate, main_rate, weight_decay)
    new_feature = update(
        feature_vectors, grad_feature, velocity_feature, average_feature, main_rate, weight_decay
    )
    new_state = update(state_vectors, grad_state, velocity_state, average_state, slow_rate, 0.0)
    return (
        mine(stream),
        mine(grad),
        grad_in,
        grad_out,
        grad_gate,
        grad_feature,
        grad_state,
        new_in[0],
        new_out[0],
        new_gate[0],
        new_feature[0],
        new_state[3],
        new_in[1],
        new_out[1],
        new_gate[1],
        new_feature[1],
        new_state[1],
        new_in[2],
        new_out[2],
        new_gate[2],
        new_feature[2],
        new_state[2],
    )


def solution(mesh):
    feat = P(None, None, "feat")
    rows = P(None, "feat", None)
    tokens = P("seq", "feat")
    return jax.shard_map(
        body,
        mesh=mesh,
        in_specs=(
            tokens,
            tokens,
            P("seq"),
            P("seq"),
            rows,
            feat,
            feat,
            feat,
            P(),
            rows,
            feat,
            feat,
            feat,
            P(),
            rows,
            feat,
            feat,
            feat,
            P(),
        ),
        out_specs=(
            tokens,
            tokens,
            rows,
            feat,
            feat,
            feat,
            P(),
            rows,
            feat,
            feat,
            feat,
            P(),
            rows,
            feat,
            feat,
            feat,
            P(),
            rows,
            feat,
            feat,
            feat,
            P(),
        ),
        check_vma=False,
    )
```

```python
import math

import jax
import jax.numpy as jnp
from jax import lax
from jax.experimental import pallas as pl
from jax.experimental.pallas import tpu as pltpu
from jax.sharding import PartitionSpec as P

epsilon = 1e-05
momentum = 0.9
smoothing = 0.5
slow_rate = 0.02
main_rate = 0.05
weight_decay = 0.1


def smooth(value):
    return jax.nn.gelu(value, approximate=False)


def masks_of(starts, lengths, count):
    position = jnp.arange(count, dtype=jnp.int32)[:, None]
    begin = starts[None, :]
    finish = begin + lengths[None, :]
    inside = (position >= begin) & (position < finish)
    alive = jnp.any(inside, 1)
    opening = jnp.any(inside & (position == begin), 1)
    closing = jnp.any(inside & (position == finish - 1), 1)
    return (
        alive.astype(jnp.float32),
        (alive & ~opening).astype(jnp.float32),
        (alive & ~closing).astype(jnp.float32),
    )


def coefficients(state_row):
    rate = -jnp.exp(state_row[0])
    frequency = state_row[1]
    timestep = jnp.exp(state_row[2])
    decay = jnp.exp(rate * timestep)
    angle = frequency * timestep
    pole_real = decay * jnp.cos(angle)
    pole_imag = decay * jnp.sin(angle)
    denom = rate * rate + frequency * frequency
    factor_real = ((pole_real - 1.0) * rate + pole_imag * frequency) / denom
    factor_imag = (pole_imag * rate - (pole_real - 1.0) * frequency) / denom
    return (pole_real, pole_imag, factor_real, factor_imag)


def tile_scan(x_re, x_im, keep, powers, down):
    reps = x_re.shape[1] // keep.shape[1]
    rows = lax.broadcasted_iota(jnp.int32, keep.shape, 0)
    b_re, b_im = x_re, x_im
    for level, k in enumerate((1, 2, 4)):
        shift = 8 - k if down else k
        valid = rows <= 7 - k if down else rows >= k
        gate = jnp.tile(jnp.where(valid, keep, 0.0), (1, reps))
        p_re = pltpu.roll(b_re, shift, 0)
        p_im = pltpu.roll(b_im, shift, 0)
        w_re = powers[0][(0, 1, 3)[level] : (0, 1, 3)[level] + 1]
        w_im = powers[1][(0, 1, 3)[level] : (0, 1, 3)[level] + 1]
        b_re = b_re + gate * (w_re * p_re - w_im * p_im)
        b_im = b_im + gate * (w_re * p_im + w_im * p_re)
        keep = keep * jnp.where(valid, pltpu.roll(keep, shift, 0), 1.0)
    return b_re, b_im, jnp.tile(keep, (1, reps))


def blocked_scan(count, width, pow_ref, up_keep, down_keep, load_up, load_down, store_up, store_down):
    tiles = count // 8
    up_powers = (pow_ref[0], pow_ref[1])
    down_powers = (pow_ref[2], pow_ref[3])

    def carry_in(b_re, b_im, reach, powers, h_re, h_im):
        q_re = powers[0] * h_re - powers[1] * h_im
        q_im = powers[0] * h_im + powers[1] * h_re
        return b_re + reach * q_re, b_im + reach * q_im

    def step(i, carry):
        u_re, u_im, d_re, d_im = carry
        tu = pl.multiple_of(i * 8, 8)
        td = pl.multiple_of((tiles - 1 - i) * 8, 8)
        xu_re, xu_im = load_up(tu)
        xd_re, xd_im = load_down(td)
        bu_re, bu_im, ru = tile_scan(xu_re, xu_im, up_keep[pl.ds(tu, 8), :], up_powers, False)
        bd_re, bd_im, rd = tile_scan(xd_re, xd_im, down_keep[pl.ds(td, 8), :], up_powers, True)
        hu_re, hu_im = carry_in(bu_re, bu_im, ru, up_powers, u_re, u_im)
        hd_re, hd_im = carry_in(bd_re, bd_im, rd, down_powers, d_re, d_im)
        store_up(tu, hu_re, hu_im)
        store_down(td, hd_re, hd_im)
        return (hu_re[7:8], hu_im[7:8], hd_re[0:1], hd_im[0:1])

    zeros = jnp.zeros((1, width), jnp.float32)
    lax.fori_loop(0, tiles, step, (zeros, zeros, zeros, zeros), unroll=2)


def pole_powers(p_re, p_im):
    rows_re = [p_re]
    rows_im = [p_im]
    for _ in range(7):
        a, b = rows_re[-1], rows_im[-1]
        rows_re.append(a * p_re - b * p_im)
        rows_im.append(a * p_im + b * p_re)
    up_re = jnp.stack(rows_re)
    up_im = jnp.stack(rows_im)
    return jnp.stack([up_re, up_im, up_re[::-1], up_im[::-1]])


def recurrence_kernel(up_ref, down_ref, pow_ref, x_ref, out_ref):
    count = x_ref.shape[0]
    width = pow_ref.shape[2]

    def load(t):
        return x_ref[pl.ds(t, 8), pl.ds(0, width)], x_ref[pl.ds(t, 8), pl.ds(width, width)]

    def store(column):
        def put(t, h_re, h_im):
            out_ref[pl.ds(t, 8), pl.ds(column, width)] = h_re
            out_ref[pl.ds(t, 8), pl.ds(column + width, width)] = h_im

        return put

    blocked_scan(count, width, pow_ref, up_ref, down_ref, load, load, store(0), store(2 * width))


def recurrence(up, down, powers, x):
    count, double = x.shape
    vmem = pl.BlockSpec(memory_space=pltpu.VMEM)
    return pl.pallas_call(
        recurrence_kernel,
        out_shape=jax.ShapeDtypeStruct((count, 2 * double), jnp.float32),
        in_specs=[vmem, vmem, vmem, vmem],
        out_specs=vmem,
        cost_estimate=pl.CostEstimate(
            flops=20 * count * double, transcendentals=0, bytes_accessed=16 * count * double
        ),
    )(up, down, powers, x)


MESH = pl.DeviceIdType.MESH


def ring_place(position, n):
    upper = position // (n // 2)
    return (1 - upper) * (2 * position) + upper * (2 * (n - 1 - position) + 1)


def ring_position(index, n):
    odd = index % 2
    return (1 - odd) * (index // 2) + odd * (n - 1 - index // 2)


def ring_sum_kernel(n, x_ref, r_ref, o_ref, low, slots, rs_send, rs_recv, credit, done, ag_send, ag_recv):
    rows = x_ref.shape[0]
    half = rows // 2
    size = half // n
    me = ring_position(lax.axis_index("seq"), n)
    right = ring_place((me + 1) % n, n)
    left = ring_place((me + n - 1) % n, n)
    rings = ((0, me, right, left), (1, (n - me) % n, left, right))

    barrier = pltpu.get_barrier_semaphore()
    for neighbour in (left, right):
        pl.semaphore_signal(barrier, 1, device_id={"seq": neighbour}, device_id_type=MESH)
    pl.semaphore_wait(barrier, 2)
    o_ref[...] = x_ref[...]
    low[...] = x_ref[...].astype(low.dtype)

    def block(ring, k):
        return pl.ds(pl.multiple_of(ring * half + k * size, 8), size)

    def scatter_copy(ring, place, target, s):
        return pltpu.make_async_remote_copy(
            src_ref=low.at[block(ring, (place - s + n) % n)],
            dst_ref=slots.at[ring, s % 2],
            send_sem=rs_send.at[ring, s % 2],
            recv_sem=rs_recv.at[ring, s % 2],
            device_id={"seq": target},
            device_id_type=MESH,
        )

    def scatter_step(s, carry):
        copies = []
        for ring, place, target, source in rings:

            @pl.when(s >= 2)
            def _():
                pl.semaphore_wait(credit.at[ring], 1)

            copy = scatter_copy(ring, place, target, s)
            copy.start()
            copies.append(copy)
        for (ring, place, target, source), copy in zip(rings, copies):
            copy.wait_recv()
            into = block(ring, (place - s - 1 + 2 * n) % n)
            total = o_ref[into] + slots[ring, s % 2].astype(jnp.float32)
            o_ref[into] = total
            low[into] = total.astype(low.dtype)
            copy.wait_send()

            @pl.when(s <= n - 4)
            def _():
                pl.semaphore_signal(credit.at[ring], 1, device_id={"seq": source}, device_id_type=MESH)

        return carry

    lax.fori_loop(0, n - 1, scatter_step, 0)
    for ring, place, target, source in rings:
        pl.semaphore_signal(done.at[ring], 1, device_id={"seq": source}, device_id_type=MESH)
    for ring, place, target, source in rings:
        final = block(ring, (place + 1) % n)
        r_ref[final] = o_ref[final].astype(r_ref.dtype)
    for ring, place, target, source in rings:
        pl.semaphore_wait(done.at[ring], 1)

    def gather_copy(ring, place, target, s):
        where = block(ring, (place + 1 - s + n) % n)
        return pltpu.make_async_remote_copy(
            src_ref=r_ref.at[where],
            dst_ref=r_ref.at[where],
            send_sem=ag_send.at[ring, s],
            recv_sem=ag_recv.at[ring, s],
            device_id={"seq": target},
            device_id_type=MESH,
        )

    def gather_step(s, carry):
        for ring, place, target, source in rings:

            @pl.when(s >= 1)
            def _():
                gather_copy(ring, place, target, s - 1).wait_recv()

            gather_copy(ring, place, target, s).start()

            @pl.when(s >= 1)
            def _():
                gather_copy(ring, place, target, s - 1).wait_send()

        return carry

    lax.fori_loop(0, n - 1, gather_step, 0)
    for ring, place, target, source in rings:
        last = gather_copy(ring, place, target, n - 2)
        last.wait_recv()
        last.wait_send()


def ring_sum(x, n):
    rows, lanes = x.shape
    size = rows // (2 * n)
    return pl.pallas_call(
        lambda *refs: ring_sum_kernel(n, *refs),
        out_shape=jax.ShapeDtypeStruct((rows, lanes), jnp.bfloat16),
        in_specs=[pl.BlockSpec(memory_space=pltpu.VMEM)],
        out_specs=pl.BlockSpec(memory_space=pltpu.VMEM),
        scratch_shapes=[
            pltpu.VMEM((rows, lanes), jnp.float32),
            pltpu.VMEM((rows, lanes), jnp.bfloat16),
            pltpu.VMEM((2, 2, size, lanes), jnp.bfloat16),
            pltpu.SemaphoreType.DMA((2, 2)),
            pltpu.SemaphoreType.DMA((2, 2)),
            pltpu.SemaphoreType.REGULAR((2,)),
            pltpu.SemaphoreType.REGULAR((2,)),
            pltpu.SemaphoreType.DMA((2, n - 1)),
            pltpu.SemaphoreType.DMA((2, n - 1)),
        ],
        compiler_params=pltpu.CompilerParams(collective_id=0, has_side_effects=True),
    )(x)


def sum_over_seq(parts):
    n = lax.axis_size("seq")
    flat = jnp.concatenate([part.reshape(-1) for part in parts])
    grain = 2 * n * 16 * 128
    padded = -(-flat.size // grain) * grain
    flat = jnp.pad(flat, (0, padded - flat.size)).reshape(padded // 128, 128)
    total = ring_sum(flat, n).astype(jnp.float32).reshape(-1)
    pieces = []
    start = 0
    for part in parts:
        pieces.append(total[start : start + part.size].reshape(part.shape))
        start += part.size
    return pieces


def adjoint_kernel(ma_ref, mb_ref, pow_ref, coef_ref, masks_ref, g_ref, states_ref, drive_ref, dg_ref, sums_ref, lam):
    count = g_ref.shape[0]
    width = coef_ref.shape[1]
    pad = 8
    f_re = coef_ref[2:3, :]
    f_im = coef_ref[3:4, :]
    zero_rows = jnp.zeros((pad, 4 * width), jnp.float32)
    lam[0:pad, :] = zero_rows
    lam[pad + count : 2 * pad + count, :] = zero_rows

    def load(column):
        def get(t):
            return g_ref[pl.ds(t, 8), pl.ds(column, width)], g_ref[pl.ds(t, 8), pl.ds(column + width, width)]

        return get

    def store(column):
        def put(t, h_re, h_im):
            lam[pl.ds(pad + t, 8), pl.ds(column, width)] = h_re
            lam[pl.ds(pad + t, 8), pl.ds(column + width, width)] = h_im

        return put

    blocked_scan(count, width, pow_ref, ma_ref, mb_ref, load(2 * width), load(0), store(0), store(2 * width))

    rows = 16

    def part(ref, start, column):
        return ref[pl.ds(start, rows), pl.ds(column, width)]

    def epilogue(k, sums):
        gp_re, gp_im, gf_re, gf_im = sums
        r0 = pl.multiple_of(k * rows, rows)
        live = masks_ref[pl.ds(r0, rows), 0:1]
        keep_prev = masks_ref[pl.ds(r0, rows), 1:2]
        keep_next = masks_ref[pl.ds(r0, rows), 2:3]
        lb_re = part(lam, pad + r0, 0)
        lb_im = part(lam, pad + r0, width)
        la_re = part(lam, pad + r0, 2 * width)
        la_im = part(lam, pad + r0, 3 * width)
        gu_re = la_re + lb_re
        gu_im = la_im + lb_im
        dg_ref[pl.ds(r0, rows), pl.ds(0, width)] = ((f_re * gu_re + f_im * gu_im) * live).astype(dg_ref.dtype)
        dg_ref[pl.ds(r0, rows), pl.ds(width, width)] = ((f_re * gu_im - f_im * gu_re) * live).astype(dg_ref.dtype)
        d_re = part(drive_ref, r0, 0) * live
        d_im = part(drive_ref, r0, width) * live
        gf_re = gf_re + d_re * gu_re + d_im * gu_im
        gf_im = gf_im + d_re * gu_im - d_im * gu_re
        a_re = part(states_ref, r0, 0) * keep_next
        a_im = part(states_ref, r0, width) * keep_next
        b_re = part(states_ref, r0, 2 * width) * keep_prev
        b_im = part(states_ref, r0, 3 * width) * keep_prev
        ahead_rows = lam[pl.ds(pad + r0, rows + 8), pl.ds(2 * width, 2 * width)][1 : rows + 1]
        behind_rows = lam[pl.ds(r0, rows + 8), pl.ds(0, 2 * width)][pad - 1 : pad - 1 + rows]
        na_re = ahead_rows[:, :width]
        na_im = ahead_rows[:, width:]
        pb_re = behind_rows[:, :width]
        pb_im = behind_rows[:, width:]
        gp_re = gp_re + a_re * na_re + a_im * na_im + b_re * pb_re + b_im * pb_im
        gp_im = gp_im + a_re * na_im - a_im * na_re + b_re * pb_im - b_im * pb_re
        return (gp_re, gp_im, gf_re, gf_im)

    block = jnp.zeros((rows, width), jnp.float32)
    sums = lax.fori_loop(0, count // rows, epilogue, (block, block, block, block))
    for k, value in enumerate(sums):
        sums_ref[k : k + 1, :] = jnp.sum(value, 0, keepdims=True)


def adjoint(ma, mb, powers, coef, masks, states_grad, states, drive):
    count, quad = states_grad.shape
    width = quad // 4
    vmem = pl.BlockSpec(memory_space=pltpu.VMEM)
    return pl.pallas_call(
        adjoint_kernel,
        out_shape=(
            jax.ShapeDtypeStruct((count, 2 * width), jnp.bfloat16),
            jax.ShapeDtypeStruct((4, width), jnp.float32),
        ),
        in_specs=[vmem] * 8,
        out_specs=(vmem, vmem),
        scratch_shapes=[pltpu.VMEM((count + 16, 4 * width), jnp.float32)],
        cost_estimate=pl.CostEstimate(
            flops=60 * count * width, transcendentals=0, bytes_accessed=48 * count * width
        ),
    )(ma, mb, powers, coef, masks, states_grad, states, drive)


def update(weight, gradient, velocity, average, rate, decay):
    adjusted = gradient + decay * weight
    velocity_new = momentum * velocity + adjusted
    change = -rate * (adjusted + momentum * velocity_new)
    weight_new = weight + change
    average_new = smoothing * average + (1.0 - smoothing) * weight_new
    return (weight_new, velocity_new, average_new, change)


def contract_rows(left, right):
    return lax.dot_general(
        left, right, (((0,), (0,)), ((), ())), preferred_element_type=jnp.float32
    )


def contract_cols(left, right):
    return lax.dot_general(
        left, right, (((1,), (1,)), ((), ())), preferred_element_type=jnp.float32
    )


def gather_feat(value, axis):
    return lax.all_gather(value, "feat", axis=axis, tiled=True)


def body(
    activations_in,
    cotangent,
    seq_start,
    seq_length,
    input_matrix,
    output_matrix,
    gate_matrix,
    feature_vectors,
    state_vectors,
    velocity_input,
    velocity_output,
    velocity_gate,
    velocity_feature,
    velocity_state,
    average_input,
    average_output,
    average_gate,
    average_feature,
    average_state,
):
    count = activations_in.shape[0]
    shard = activations_in.shape[1]
    layers = input_matrix.shape[0]
    width = state_vectors.shape[2]
    me = lax.axis_index("feat")
    offset = me * shard

    def mine(value):
        return lax.dynamic_slice_in_dim(value, offset, shard, axis=value.ndim - 1)

    alive, carry_prev, carry_next = masks_of(seq_start, seq_length, count)
    zero = jnp.zeros((1,), jnp.float32)
    after_next = jnp.concatenate([zero, carry_next[:-1]])
    before_prev = jnp.concatenate([carry_prev[1:], zero])
    mask_columns = jnp.stack([alive, carry_prev, carry_next, jnp.zeros_like(alive)], 1)

    def lanes(mask):
        return jnp.broadcast_to(mask[:, None], (count, 128))

    keep_prev, keep_next = lanes(carry_prev), lanes(carry_next)
    keep_after_next, keep_before_prev = lanes(after_next), lanes(before_prev)

    in_all = gather_feat(input_matrix.astype(jnp.bfloat16), 1)
    out_all = gather_feat(output_matrix.astype(jnp.bfloat16), 2)
    gate_all = gather_feat(gate_matrix.astype(jnp.bfloat16), 2)
    feature_all = gather_feat(feature_vectors, 2)
    stream = gather_feat(activations_in, 1).astype(jnp.float32)

    saved = []
    for layer in range(layers):
        in_low = in_all[layer]
        out_low = out_all[layer]
        gate_low = gate_all[layer]
        feature_row = feature_all[layer]
        pole_re, pole_im, factor_re, factor_im = coefficients(state_vectors[layer])
        center = jnp.mean(stream, 1, keepdims=True)
        spread = stream - center
        scale = lax.rsqrt(jnp.mean(spread * spread, 1, keepdims=True) + epsilon)
        unit = spread * scale
        normed = unit * feature_row[0] + feature_row[1]
        normed_low = normed.astype(jnp.bfloat16)
        drive = jnp.dot(normed_low, in_low, preferred_element_type=jnp.float32)
        drive_re = drive[:, :width]
        drive_im = drive[:, width:]
        source = jnp.concatenate(
            [
                (drive_re * factor_re - drive_im * factor_im) * alive[:, None],
                (drive_re * factor_im + drive_im * factor_re) * alive[:, None],
            ],
            1,
        )
        states = recurrence(keep_prev, keep_next, pole_powers(pole_re, pole_im), source)
        states_low = states.astype(jnp.bfloat16)
        mixed = (
            jnp.dot(states_low, out_low, preferred_element_type=jnp.float32)
            + feature_row[2] * normed
        )
        act = smooth(mixed)
        act_low = act.astype(jnp.bfloat16)
        pre = jnp.dot(act_low, gate_low, preferred_element_type=jnp.float32) + feature_row[3]
        saved.append((scale, unit, normed_low, drive, states, states_low, mixed, act, act_low, pre))
        stream = stream + act * jax.nn.sigmoid(pre)

    grad = gather_feat(cotangent, 1).astype(jnp.float32) * alive[:, None]
    layer_grads = [None] * layers
    for layer in reversed(range(layers)):
        scale, unit, normed_low, drive, states, states_low, mixed, act, act_low, pre = saved[layer]
        in_low = in_all[layer]
        out_low = out_all[layer]
        gate_low = gate_all[layer]
        feature_row = feature_all[layer]
        state_row = state_vectors[layer]
        pole_re, pole_im, factor_re, factor_im = coefficients(state_row)
        gate = jax.nn.sigmoid(pre)
        pre_grad = (grad * act * gate * (1.0 - gate)).astype(jnp.bfloat16)
        gate_grad = contract_rows(act_low, mine(pre_grad))
        gate_bias_grad = jnp.sum(pre_grad.astype(jnp.float32), 0)
        act_grad = grad * gate + contract_cols(pre_grad, gate_low)
        mixed_grad = jax.vjp(smooth, mixed)[1](act_grad)[0]
        normed = unit * feature_row[0] + feature_row[1]
        skip_grad = jnp.sum(mixed_grad * normed, 0)
        mixed_low = mixed_grad.astype(jnp.bfloat16)
        out_grad = contract_rows(states_low, mine(mixed_low))
        states_grad = contract_cols(mixed_low, out_low)
        coef = jnp.stack([pole_re, pole_im, factor_re, factor_im])
        drive_low, sums = adjoint(
            keep_after_next,
            keep_before_prev,
            pole_powers(pole_re, -pole_im),
            coef,
            mask_columns,
            states_grad,
            states,
            drive,
        )
        gp_re, gp_im, gf_re, gf_im = sums[0], sums[1], sums[2], sums[3]
        row_grad = jax.vjp(coefficients, state_row)[1]((gp_re, gp_im, gf_re, gf_im))[0]
        in_grad = contract_rows(mine(normed_low), drive_low)
        normed_grad = mixed_grad * feature_row[2] + jnp.dot(
            drive_low, in_low.T, preferred_element_type=jnp.float32
        )
        gain_grad = jnp.sum(normed_grad * unit, 0)
        bias_grad = jnp.sum(normed_grad, 0)
        unit_grad = normed_grad * feature_row[0]
        first_mean = jnp.mean(unit_grad, 1, keepdims=True)
        second_mean = jnp.mean(unit_grad * unit, 1, keepdims=True)
        grad = grad + scale * (unit_grad - first_mean - unit * second_mean)
        feature_grad = mine(jnp.stack([gain_grad, bias_grad, skip_grad, gate_bias_grad]))
        layer_grads[layer] = (in_grad, out_grad, gate_grad, feature_grad, row_grad)
    stacked_in = jnp.stack([entry[0] for entry in layer_grads])
    stacked_out = jnp.stack([entry[1] for entry in layer_grads])
    stacked_gate = jnp.stack([entry[2] for entry in layer_grads])
    stacked_feature = jnp.stack([entry[3] for entry in layer_grads])
    stacked_state = jnp.stack([entry[4] for entry in layer_grads])
    summed = sum_over_seq((stacked_in, stacked_out, stacked_gate, stacked_feature, stacked_state))
    factor = 1.0 / math.sqrt(count * lax.axis_size("seq"))
    grad_in = summed[0] * factor
    grad_out = summed[1] * factor
    grad_gate = summed[2] * factor
    grad_feature = summed[3] * factor
    grad_state = summed[4] * factor
    new_in = update(input_matrix, grad_in, velocity_input, average_input, slow_rate, 0.0)
    new_out = update(output_matrix, grad_out, velocity_output, average_output, slow_rate, 0.0)
    new_gate = update(gate_matrix, grad_gate, velocity_gate, average_gate, main_rate, weight_decay)
    new_feature = update(
        feature_vectors, grad_feature, velocity_feature, average_feature, main_rate, weight_decay
    )
    new_state = update(state_vectors, grad_state, velocity_state, average_state, slow_rate, 0.0)
    return (
        mine(stream),
        mine(grad),
        grad_in,
        grad_out,
        grad_gate,
        grad_feature,
        grad_state,
        new_in[0],
        new_out[0],
        new_gate[0],
        new_feature[0],
        new_state[3],
        new_in[1],
        new_out[1],
        new_gate[1],
        new_feature[1],
        new_state[1],
        new_in[2],
        new_out[2],
        new_gate[2],
        new_feature[2],
        new_state[2],
    )


def solution(mesh):
    feat = P(None, None, "feat")
    rows = P(None, "feat", None)
    tokens = P("seq", "feat")
    return jax.shard_map(
        body,
        mesh=mesh,
        in_specs=(
            tokens,
            tokens,
            P("seq"),
            P("seq"),
            rows,
            feat,
            feat,
            feat,
            P(),
            rows,
            feat,
            feat,
            feat,
            P(),
            rows,
            feat,
            feat,
            feat,
            P(),
        ),
        out_specs=(
            tokens,
            tokens,
            rows,
            feat,
            feat,
            feat,
            P(),
            rows,
            feat,
            feat,
            feat,
            P(),
            rows,
            feat,
            feat,
            feat,
            P(),
            rows,
            feat,
            feat,
            feat,
            P(),
        ),
        check_vma=False,
    )
```

```python
import math

import jax
import jax.numpy as jnp
from jax import lax
from jax.experimental import pallas as pl
from jax.experimental.pallas import tpu as pltpu
from jax.sharding import PartitionSpec as P

epsilon = 1e-05
momentum = 0.9
smoothing = 0.5
slow_rate = 0.02
main_rate = 0.05
weight_decay = 0.1


def smooth(value):
    return jax.nn.gelu(value, approximate=False)


def masks_of(starts, lengths, count):
    position = jnp.arange(count, dtype=jnp.int32)[:, None]
    begin = starts[None, :]
    finish = begin + lengths[None, :]
    inside = (position >= begin) & (position < finish)
    alive = jnp.any(inside, 1)
    opening = jnp.any(inside & (position == begin), 1)
    closing = jnp.any(inside & (position == finish - 1), 1)
    return (
        alive.astype(jnp.float32),
        (alive & ~opening).astype(jnp.float32),
        (alive & ~closing).astype(jnp.float32),
    )


def coefficients(state_row):
    rate = -jnp.exp(state_row[0])
    frequency = state_row[1]
    timestep = jnp.exp(state_row[2])
    decay = jnp.exp(rate * timestep)
    angle = frequency * timestep
    pole_real = decay * jnp.cos(angle)
    pole_imag = decay * jnp.sin(angle)
    denom = rate * rate + frequency * frequency
    factor_real = ((pole_real - 1.0) * rate + pole_imag * frequency) / denom
    factor_imag = (pole_imag * rate - (pole_real - 1.0) * frequency) / denom
    return (pole_real, pole_imag, factor_real, factor_imag)


def tile_scan(x_re, x_im, keep, powers, down):
    reps = x_re.shape[1] // keep.shape[1]
    rows = lax.broadcasted_iota(jnp.int32, keep.shape, 0)
    b_re, b_im = x_re, x_im
    for level, k in enumerate((1, 2, 4)):
        shift = 8 - k if down else k
        valid = rows <= 7 - k if down else rows >= k
        gate = jnp.tile(jnp.where(valid, keep, 0.0), (1, reps))
        p_re = pltpu.roll(b_re, shift, 0)
        p_im = pltpu.roll(b_im, shift, 0)
        w_re = powers[0][(0, 1, 3)[level] : (0, 1, 3)[level] + 1]
        w_im = powers[1][(0, 1, 3)[level] : (0, 1, 3)[level] + 1]
        b_re = b_re + gate * (w_re * p_re - w_im * p_im)
        b_im = b_im + gate * (w_re * p_im + w_im * p_re)
        keep = keep * jnp.where(valid, pltpu.roll(keep, shift, 0), 1.0)
    return b_re, b_im, jnp.tile(keep, (1, reps))


def blocked_scan(count, width, pow_ref, up_keep, down_keep, load_up, load_down, store_up, store_down):
    tiles = count // 8
    up_powers = (pow_ref[0], pow_ref[1])
    down_powers = (pow_ref[2], pow_ref[3])

    def carry_in(b_re, b_im, reach, powers, h_re, h_im):
        q_re = powers[0] * h_re - powers[1] * h_im
        q_im = powers[0] * h_im + powers[1] * h_re
        return b_re + reach * q_re, b_im + reach * q_im

    def step(i, carry):
        u_re, u_im, d_re, d_im = carry
        tu = pl.multiple_of(i * 8, 8)
        td = pl.multiple_of((tiles - 1 - i) * 8, 8)
        xu_re, xu_im = load_up(tu)
        xd_re, xd_im = load_down(td)
        bu_re, bu_im, ru = tile_scan(xu_re, xu_im, up_keep[pl.ds(tu, 8), :], up_powers, False)
        bd_re, bd_im, rd = tile_scan(xd_re, xd_im, down_keep[pl.ds(td, 8), :], up_powers, True)
        hu_re, hu_im = carry_in(bu_re, bu_im, ru, up_powers, u_re, u_im)
        hd_re, hd_im = carry_in(bd_re, bd_im, rd, down_powers, d_re, d_im)
        store_up(tu, hu_re, hu_im)
        store_down(td, hd_re, hd_im)
        return (hu_re[7:8], hu_im[7:8], hd_re[0:1], hd_im[0:1])

    zeros = jnp.zeros((1, width), jnp.float32)
    lax.fori_loop(0, tiles, step, (zeros, zeros, zeros, zeros), unroll=2)


def pole_powers(p_re, p_im):
    rows_re = [p_re]
    rows_im = [p_im]
    for _ in range(7):
        a, b = rows_re[-1], rows_im[-1]
        rows_re.append(a * p_re - b * p_im)
        rows_im.append(a * p_im + b * p_re)
    up_re = jnp.stack(rows_re)
    up_im = jnp.stack(rows_im)
    return jnp.stack([up_re, up_im, up_re[::-1], up_im[::-1]])


def recurrence_kernel(up_ref, down_ref, pow_ref, x_ref, out_ref):
    count = x_ref.shape[0]
    width = pow_ref.shape[2]

    def load(t):
        return x_ref[pl.ds(t, 8), pl.ds(0, width)], x_ref[pl.ds(t, 8), pl.ds(width, width)]

    def store(column):
        def put(t, h_re, h_im):
            out_ref[pl.ds(t, 8), pl.ds(column, width)] = h_re
            out_ref[pl.ds(t, 8), pl.ds(column + width, width)] = h_im

        return put

    blocked_scan(count, width, pow_ref, up_ref, down_ref, load, load, store(0), store(2 * width))


def recurrence(up, down, powers, x):
    count, double = x.shape
    vmem = pl.BlockSpec(memory_space=pltpu.VMEM)
    return pl.pallas_call(
        recurrence_kernel,
        out_shape=jax.ShapeDtypeStruct((count, 2 * double), jnp.float32),
        in_specs=[vmem, vmem, vmem, vmem],
        out_specs=vmem,
        cost_estimate=pl.CostEstimate(
            flops=20 * count * double, transcendentals=0, bytes_accessed=16 * count * double
        ),
    )(up, down, powers, x)


MESH = pl.DeviceIdType.MESH


def recurrence_gather_kernel(parts, up_ref, down_ref, pow_ref, x_ref, c_ref, out_ref, c_all, local, sends, recvs):
    count = x_ref.shape[0]
    width = pow_ref.shape[2]
    lanes = c_ref.shape[1]
    me = lax.axis_index("feat")
    mine = pl.ds(pl.multiple_of(me * lanes, lanes), lanes)

    barrier = pltpu.get_barrier_semaphore()
    for j in range(1, parts):
        pl.semaphore_signal(barrier, 1, device_id={"feat": (me + j) % parts}, device_id_type=MESH)
    pl.semaphore_wait(barrier, parts - 1)

    own = pltpu.make_async_copy(c_ref, c_all.at[:, mine], local)
    own.start()
    copies = []
    for j in range(1, parts):
        copy = pltpu.make_async_remote_copy(
            src_ref=c_ref,
            dst_ref=c_all.at[:, mine],
            send_sem=sends.at[j - 1],
            recv_sem=recvs.at[j - 1],
            device_id={"feat": (me + j) % parts},
            device_id_type=MESH,
        )
        copy.start()
        copies.append(copy)

    def load(t):
        return x_ref[pl.ds(t, 8), pl.ds(0, width)], x_ref[pl.ds(t, 8), pl.ds(width, width)]

    def store(column):
        def put(t, h_re, h_im):
            out_ref[pl.ds(t, 8), pl.ds(column, width)] = h_re
            out_ref[pl.ds(t, 8), pl.ds(column + width, width)] = h_im

        return put

    blocked_scan(count, width, pow_ref, up_ref, down_ref, load, load, store(0), store(2 * width))
    own.wait()
    for copy in copies:
        copy.wait_send()
        copy.wait_recv()


def recurrence_gather(up, down, powers, x, c, parts):
    count, double = x.shape
    vmem = pl.BlockSpec(memory_space=pltpu.VMEM)
    return pl.pallas_call(
        lambda *refs: recurrence_gather_kernel(parts, *refs),
        out_shape=(
            jax.ShapeDtypeStruct((count, 2 * double), jnp.float32),
            jax.ShapeDtypeStruct((c.shape[0], c.shape[1] * parts), c.dtype),
        ),
        in_specs=[vmem] * 5,
        out_specs=(vmem, vmem),
        scratch_shapes=[
            pltpu.SemaphoreType.DMA(()),
            pltpu.SemaphoreType.DMA((parts - 1,)),
            pltpu.SemaphoreType.DMA((parts - 1,)),
        ],
        compiler_params=pltpu.CompilerParams(collective_id=1, has_side_effects=True),
        cost_estimate=pl.CostEstimate(
            flops=20 * count * double, transcendentals=0, bytes_accessed=16 * count * double
        ),
    )(up, down, powers, x, c)


def ring_place(position, n):
    upper = position // (n // 2)
    return (1 - upper) * (2 * position) + upper * (2 * (n - 1 - position) + 1)


def ring_position(index, n):
    odd = index % 2
    return (1 - odd) * (index // 2) + odd * (n - 1 - index // 2)


def ring_sum_kernel(n, x_ref, r_ref, o_ref, low, slots, rs_send, rs_recv, credit, done, ag_send, ag_recv):
    rows = x_ref.shape[0]
    half = rows // 2
    size = half // n
    me = ring_position(lax.axis_index("seq"), n)
    right = ring_place((me + 1) % n, n)
    left = ring_place((me + n - 1) % n, n)
    rings = ((0, me, right, left), (1, (n - me) % n, left, right))

    barrier = pltpu.get_barrier_semaphore()
    for neighbour in (left, right):
        pl.semaphore_signal(barrier, 1, device_id={"seq": neighbour}, device_id_type=MESH)
    pl.semaphore_wait(barrier, 2)
    o_ref[...] = x_ref[...]
    low[...] = x_ref[...].astype(low.dtype)

    def block(ring, k):
        return pl.ds(pl.multiple_of(ring * half + k * size, 8), size)

    def scatter_copy(ring, place, target, s):
        return pltpu.make_async_remote_copy(
            src_ref=low.at[block(ring, (place - s + n) % n)],
            dst_ref=slots.at[ring, s % 2],
            send_sem=rs_send.at[ring, s % 2],
            recv_sem=rs_recv.at[ring, s % 2],
            device_id={"seq": target},
            device_id_type=MESH,
        )

    def scatter_step(s, carry):
        copies = []
        for ring, place, target, source in rings:

            @pl.when(s >= 2)
            def _():
                pl.semaphore_wait(credit.at[ring], 1)

            copy = scatter_copy(ring, place, target, s)
            copy.start()
            copies.append(copy)
        for (ring, place, target, source), copy in zip(rings, copies):
            copy.wait_recv()
            into = block(ring, (place - s - 1 + 2 * n) % n)
            total = o_ref[into] + slots[ring, s % 2].astype(jnp.float32)
            o_ref[into] = total
            low[into] = total.astype(low.dtype)
            copy.wait_send()

            @pl.when(s <= n - 4)
            def _():
                pl.semaphore_signal(credit.at[ring], 1, device_id={"seq": source}, device_id_type=MESH)

        return carry

    lax.fori_loop(0, n - 1, scatter_step, 0)
    for ring, place, target, source in rings:
        pl.semaphore_signal(done.at[ring], 1, device_id={"seq": source}, device_id_type=MESH)
    for ring, place, target, source in rings:
        final = block(ring, (place + 1) % n)
        r_ref[final] = o_ref[final].astype(r_ref.dtype)
    for ring, place, target, source in rings:
        pl.semaphore_wait(done.at[ring], 1)

    def gather_copy(ring, place, target, s):
        where = block(ring, (place + 1 - s + n) % n)
        return pltpu.make_async_remote_copy(
            src_ref=r_ref.at[where],
            dst_ref=r_ref.at[where],
            send_sem=ag_send.at[ring, s],
            recv_sem=ag_recv.at[ring, s],
            device_id={"seq": target},
            device_id_type=MESH,
        )

    def gather_step(s, carry):
        for ring, place, target, source in rings:

            @pl.when(s >= 1)
            def _():
                gather_copy(ring, place, target, s - 1).wait_recv()

            gather_copy(ring, place, target, s).start()

            @pl.when(s >= 1)
            def _():
                gather_copy(ring, place, target, s - 1).wait_send()

        return carry

    lax.fori_loop(0, n - 1, gather_step, 0)
    for ring, place, target, source in rings:
        last = gather_copy(ring, place, target, n - 2)
        last.wait_recv()
        last.wait_send()


def ring_sum(x, n):
    rows, lanes = x.shape
    size = rows // (2 * n)
    return pl.pallas_call(
        lambda *refs: ring_sum_kernel(n, *refs),
        out_shape=jax.ShapeDtypeStruct((rows, lanes), jnp.bfloat16),
        in_specs=[pl.BlockSpec(memory_space=pltpu.VMEM)],
        out_specs=pl.BlockSpec(memory_space=pltpu.VMEM),
        scratch_shapes=[
            pltpu.VMEM((rows, lanes), jnp.float32),
            pltpu.VMEM((rows, lanes), jnp.bfloat16),
            pltpu.VMEM((2, 2, size, lanes), jnp.bfloat16),
            pltpu.SemaphoreType.DMA((2, 2)),
            pltpu.SemaphoreType.DMA((2, 2)),
            pltpu.SemaphoreType.REGULAR((2,)),
            pltpu.SemaphoreType.REGULAR((2,)),
            pltpu.SemaphoreType.DMA((2, n - 1)),
            pltpu.SemaphoreType.DMA((2, n - 1)),
        ],
        compiler_params=pltpu.CompilerParams(collective_id=0, has_side_effects=True),
    )(x)


def sum_over_seq(parts):
    n = lax.axis_size("seq")
    flat = jnp.concatenate([part.reshape(-1) for part in parts])
    grain = 2 * n * 16 * 128
    padded = -(-flat.size // grain) * grain
    flat = jnp.pad(flat, (0, padded - flat.size)).reshape(padded // 128, 128)
    total = ring_sum(flat, n).astype(jnp.float32).reshape(-1)
    pieces = []
    start = 0
    for part in parts:
        pieces.append(total[start : start + part.size].reshape(part.shape))
        start += part.size
    return pieces


def adjoint_kernel(ma_ref, mb_ref, pow_ref, coef_ref, masks_ref, g_ref, states_ref, drive_ref, dg_ref, sums_ref, lam):
    count = g_ref.shape[0]
    width = coef_ref.shape[1]
    pad = 8
    f_re = coef_ref[2:3, :]
    f_im = coef_ref[3:4, :]
    zero_rows = jnp.zeros((pad, 4 * width), jnp.float32)
    lam[0:pad, :] = zero_rows
    lam[pad + count : 2 * pad + count, :] = zero_rows

    def load(column):
        def get(t):
            return g_ref[pl.ds(t, 8), pl.ds(column, width)], g_ref[pl.ds(t, 8), pl.ds(column + width, width)]

        return get

    def store(column):
        def put(t, h_re, h_im):
            lam[pl.ds(pad + t, 8), pl.ds(column, width)] = h_re
            lam[pl.ds(pad + t, 8), pl.ds(column + width, width)] = h_im

        return put

    blocked_scan(count, width, pow_ref, ma_ref, mb_ref, load(2 * width), load(0), store(0), store(2 * width))

    rows = 16

    def part(ref, start, column):
        return ref[pl.ds(start, rows), pl.ds(column, width)]

    def epilogue(k, sums):
        gp_re, gp_im, gf_re, gf_im = sums
        r0 = pl.multiple_of(k * rows, rows)
        live = masks_ref[pl.ds(r0, rows), 0:1]
        keep_prev = masks_ref[pl.ds(r0, rows), 1:2]
        keep_next = masks_ref[pl.ds(r0, rows), 2:3]
        lb_re = part(lam, pad + r0, 0)
        lb_im = part(lam, pad + r0, width)
        la_re = part(lam, pad + r0, 2 * width)
        la_im = part(lam, pad + r0, 3 * width)
        gu_re = la_re + lb_re
        gu_im = la_im + lb_im
        dg_ref[pl.ds(r0, rows), pl.ds(0, width)] = ((f_re * gu_re + f_im * gu_im) * live).astype(dg_ref.dtype)
        dg_ref[pl.ds(r0, rows), pl.ds(width, width)] = ((f_re * gu_im - f_im * gu_re) * live).astype(dg_ref.dtype)
        d_re = part(drive_ref, r0, 0) * live
        d_im = part(drive_ref, r0, width) * live
        gf_re = gf_re + d_re * gu_re + d_im * gu_im
        gf_im = gf_im + d_re * gu_im - d_im * gu_re
        a_re = part(states_ref, r0, 0) * keep_next
        a_im = part(states_ref, r0, width) * keep_next
        b_re = part(states_ref, r0, 2 * width) * keep_prev
        b_im = part(states_ref, r0, 3 * width) * keep_prev
        ahead_rows = lam[pl.ds(pad + r0, rows + 8), pl.ds(2 * width, 2 * width)][1 : rows + 1]
        behind_rows = lam[pl.ds(r0, rows + 8), pl.ds(0, 2 * width)][pad - 1 : pad - 1 + rows]
        na_re = ahead_rows[:, :width]
        na_im = ahead_rows[:, width:]
        pb_re = behind_rows[:, :width]
        pb_im = behind_rows[:, width:]
        gp_re = gp_re + a_re * na_re + a_im * na_im + b_re * pb_re + b_im * pb_im
        gp_im = gp_im + a_re * na_im - a_im * na_re + b_re * pb_im - b_im * pb_re
        return (gp_re, gp_im, gf_re, gf_im)

    block = jnp.zeros((rows, width), jnp.float32)
    sums = lax.fori_loop(0, count // rows, epilogue, (block, block, block, block))
    for k, value in enumerate(sums):
        sums_ref[k : k + 1, :] = jnp.sum(value, 0, keepdims=True)


def adjoint(ma, mb, powers, coef, masks, states_grad, states, drive):
    count, quad = states_grad.shape
    width = quad // 4
    vmem = pl.BlockSpec(memory_space=pltpu.VMEM)
    return pl.pallas_call(
        adjoint_kernel,
        out_shape=(
            jax.ShapeDtypeStruct((count, 2 * width), jnp.bfloat16),
            jax.ShapeDtypeStruct((4, width), jnp.float32),
        ),
        in_specs=[vmem] * 8,
        out_specs=(vmem, vmem),
        scratch_shapes=[pltpu.VMEM((count + 16, 4 * width), jnp.float32)],
        cost_estimate=pl.CostEstimate(
            flops=60 * count * width, transcendentals=0, bytes_accessed=48 * count * width
        ),
    )(ma, mb, powers, coef, masks, states_grad, states, drive)


def update(weight, gradient, velocity, average, rate, decay):
    adjusted = gradient + decay * weight
    velocity_new = momentum * velocity + adjusted
    change = -rate * (adjusted + momentum * velocity_new)
    weight_new = weight + change
    average_new = smoothing * average + (1.0 - smoothing) * weight_new
    return (weight_new, velocity_new, average_new, change)


def contract_rows(left, right):
    return lax.dot_general(
        left, right, (((0,), (0,)), ((), ())), preferred_element_type=jnp.float32
    )


def contract_cols(left, right):
    return lax.dot_general(
        left, right, (((1,), (1,)), ((), ())), preferred_element_type=jnp.float32
    )


def gather_feat(value, axis):
    return lax.all_gather(value, "feat", axis=axis, tiled=True)


def body(
    activations_in,
    cotangent,
    seq_start,
    seq_length,
    input_matrix,
    output_matrix,
    gate_matrix,
    feature_vectors,
    state_vectors,
    velocity_input,
    velocity_output,
    velocity_gate,
    velocity_feature,
    velocity_state,
    average_input,
    average_output,
    average_gate,
    average_feature,
    average_state,
):
    count = activations_in.shape[0]
    shard = activations_in.shape[1]
    layers = input_matrix.shape[0]
    width = state_vectors.shape[2]
    me = lax.axis_index("feat")
    offset = me * shard

    def mine(value):
        return lax.dynamic_slice_in_dim(value, offset, shard, axis=value.ndim - 1)

    alive, carry_prev, carry_next = masks_of(seq_start, seq_length, count)
    zero = jnp.zeros((1,), jnp.float32)
    after_next = jnp.concatenate([zero, carry_next[:-1]])
    before_prev = jnp.concatenate([carry_prev[1:], zero])
    mask_columns = jnp.stack([alive, carry_prev, carry_next, jnp.zeros_like(alive)], 1)

    def lanes(mask):
        return jnp.broadcast_to(mask[:, None], (count, 128))

    keep_prev, keep_next = lanes(carry_prev), lanes(carry_next)
    keep_after_next, keep_before_prev = lanes(after_next), lanes(before_prev)

    in_all = gather_feat(input_matrix.astype(jnp.bfloat16), 1)
    out_all = gather_feat(output_matrix.astype(jnp.bfloat16), 2)
    gate_all = gather_feat(gate_matrix.astype(jnp.bfloat16), 2)
    feature_all = gather_feat(feature_vectors, 2)
    stream = gather_feat(activations_in, 1).astype(jnp.float32)

    saved = []
    for layer in range(layers):
        in_low = in_all[layer]
        out_low = out_all[layer]
        gate_low = gate_all[layer]
        feature_row = feature_all[layer]
        pole_re, pole_im, factor_re, factor_im = coefficients(state_vectors[layer])
        center = jnp.mean(stream, 1, keepdims=True)
        spread = stream - center
        scale = lax.rsqrt(jnp.mean(spread * spread, 1, keepdims=True) + epsilon)
        unit = spread * scale
        normed = unit * feature_row[0] + feature_row[1]
        normed_low = normed.astype(jnp.bfloat16)
        drive = jnp.dot(normed_low, in_low, preferred_element_type=jnp.float32)
        drive_re = drive[:, :width]
        drive_im = drive[:, width:]
        source = jnp.concatenate(
            [
                (drive_re * factor_re - drive_im * factor_im) * alive[:, None],
                (drive_re * factor_im + drive_im * factor_re) * alive[:, None],
            ],
            1,
        )
        powers = pole_powers(pole_re, pole_im)
        if layer == layers - 1:
            states, cotangent_all = recurrence_gather(
                keep_prev, keep_next, powers, source, cotangent, lax.axis_size("feat")
            )
        else:
            states = recurrence(keep_prev, keep_next, powers, source)
        states_low = states.astype(jnp.bfloat16)
        mixed = (
            jnp.dot(states_low, out_low, preferred_element_type=jnp.float32)
            + feature_row[2] * normed
        )
        act = smooth(mixed)
        act_low = act.astype(jnp.bfloat16)
        pre = jnp.dot(act_low, gate_low, preferred_element_type=jnp.float32) + feature_row[3]
        saved.append((scale, unit, normed_low, drive, states, states_low, mixed, act, act_low, pre))
        stream = stream + act * jax.nn.sigmoid(pre)

    grad = cotangent_all.astype(jnp.float32) * alive[:, None]
    layer_grads = [None] * layers
    for layer in reversed(range(layers)):
        scale, unit, normed_low, drive, states, states_low, mixed, act, act_low, pre = saved[layer]
        in_low = in_all[layer]
        out_low = out_all[layer]
        gate_low = gate_all[layer]
        feature_row = feature_all[layer]
        state_row = state_vectors[layer]
        pole_re, pole_im, factor_re, factor_im = coefficients(state_row)
        gate = jax.nn.sigmoid(pre)
        pre_grad = (grad * act * gate * (1.0 - gate)).astype(jnp.bfloat16)
        gate_grad = contract_rows(act_low, mine(pre_grad))
        gate_bias_grad = jnp.sum(pre_grad.astype(jnp.float32), 0)
        act_grad = grad * gate + contract_cols(pre_grad, gate_low)
        mixed_grad = jax.vjp(smooth, mixed)[1](act_grad)[0]
        normed = unit * feature_row[0] + feature_row[1]
        skip_grad = jnp.sum(mixed_grad * normed, 0)
        mixed_low = mixed_grad.astype(jnp.bfloat16)
        out_grad = contract_rows(states_low, mine(mixed_low))
        states_grad = contract_cols(mixed_low, out_low)
        coef = jnp.stack([pole_re, pole_im, factor_re, factor_im])
        drive_low, sums = adjoint(
            keep_after_next,
            keep_before_prev,
            pole_powers(pole_re, -pole_im),
            coef,
            mask_columns,
            states_grad,
            states,
            drive,
        )
        gp_re, gp_im, gf_re, gf_im = sums[0], sums[1], sums[2], sums[3]
        row_grad = jax.vjp(coefficients, state_row)[1]((gp_re, gp_im, gf_re, gf_im))[0]
        in_grad = contract_rows(mine(normed_low), drive_low)
        normed_grad = mixed_grad * feature_row[2] + jnp.dot(
            drive_low, in_low.T, preferred_element_type=jnp.float32
        )
        gain_grad = jnp.sum(normed_grad * unit, 0)
        bias_grad = jnp.sum(normed_grad, 0)
        unit_grad = normed_grad * feature_row[0]
        first_mean = jnp.mean(unit_grad, 1, keepdims=True)
        second_mean = jnp.mean(unit_grad * unit, 1, keepdims=True)
        grad = grad + scale * (unit_grad - first_mean - unit * second_mean)
        feature_grad = mine(jnp.stack([gain_grad, bias_grad, skip_grad, gate_bias_grad]))
        layer_grads[layer] = (in_grad, out_grad, gate_grad, feature_grad, row_grad)
    stacked_in = jnp.stack([entry[0] for entry in layer_grads])
    stacked_out = jnp.stack([entry[1] for entry in layer_grads])
    stacked_gate = jnp.stack([entry[2] for entry in layer_grads])
    stacked_feature = jnp.stack([entry[3] for entry in layer_grads])
    stacked_state = jnp.stack([entry[4] for entry in layer_grads])
    summed = sum_over_seq((stacked_in, stacked_out, stacked_gate, stacked_feature, stacked_state))
    factor = 1.0 / math.sqrt(count * lax.axis_size("seq"))
    grad_in = summed[0] * factor
    grad_out = summed[1] * factor
    grad_gate = summed[2] * factor
    grad_feature = summed[3] * factor
    grad_state = summed[4] * factor
    new_in = update(input_matrix, grad_in, velocity_input, average_input, slow_rate, 0.0)
    new_out = update(output_matrix, grad_out, velocity_output, average_output, slow_rate, 0.0)
    new_gate = update(gate_matrix, grad_gate, velocity_gate, average_gate, main_rate, weight_decay)
    new_feature = update(
        feature_vectors, grad_feature, velocity_feature, average_feature, main_rate, weight_decay
    )
    new_state = update(state_vectors, grad_state, velocity_state, average_state, slow_rate, 0.0)
    return (
        mine(stream),
        mine(grad),
        grad_in,
        grad_out,
        grad_gate,
        grad_feature,
        grad_state,
        new_in[0],
        new_out[0],
        new_gate[0],
        new_feature[0],
        new_state[3],
        new_in[1],
        new_out[1],
        new_gate[1],
        new_feature[1],
        new_state[1],
        new_in[2],
        new_out[2],
        new_gate[2],
        new_feature[2],
        new_state[2],
    )


def solution(mesh):
    feat = P(None, None, "feat")
    rows = P(None, "feat", None)
    tokens = P("seq", "feat")
    return jax.shard_map(
        body,
        mesh=mesh,
        in_specs=(
            tokens,
            tokens,
            P("seq"),
            P("seq"),
            rows,
            feat,
            feat,
            feat,
            P(),
            rows,
            feat,
            feat,
            feat,
            P(),
            rows,
            feat,
            feat,
            feat,
            P(),
        ),
        out_specs=(
            tokens,
            tokens,
            rows,
            feat,
            feat,
            feat,
            P(),
            rows,
            feat,
            feat,
            feat,
            P(),
            rows,
            feat,
            feat,
            feat,
            P(),
            rows,
            feat,
            feat,
            feat,
            P(),
        ),
        check_vma=False,
    )
```

```python
import math

import jax
import jax.numpy as jnp
from jax import lax
from jax.experimental import pallas as pl
from jax.experimental.pallas import tpu as pltpu
from jax.sharding import PartitionSpec as P

epsilon = 1e-05
momentum = 0.9
smoothing = 0.5
slow_rate = 0.02
main_rate = 0.05
weight_decay = 0.1


def smooth(value):
    return jax.nn.gelu(value, approximate=False)


def masks_of(starts, lengths, count):
    position = jnp.arange(count, dtype=jnp.int32)[:, None]
    begin = starts[None, :]
    finish = begin + lengths[None, :]
    inside = (position >= begin) & (position < finish)
    alive = jnp.any(inside, 1)
    opening = jnp.any(inside & (position == begin), 1)
    closing = jnp.any(inside & (position == finish - 1), 1)
    return (
        alive.astype(jnp.float32),
        (alive & ~opening).astype(jnp.float32),
        (alive & ~closing).astype(jnp.float32),
    )


def coefficients(state_row):
    rate = -jnp.exp(state_row[0])
    frequency = state_row[1]
    timestep = jnp.exp(state_row[2])
    decay = jnp.exp(rate * timestep)
    angle = frequency * timestep
    pole_real = decay * jnp.cos(angle)
    pole_imag = decay * jnp.sin(angle)
    denom = rate * rate + frequency * frequency
    factor_real = ((pole_real - 1.0) * rate + pole_imag * frequency) / denom
    factor_imag = (pole_imag * rate - (pole_real - 1.0) * frequency) / denom
    return (pole_real, pole_imag, factor_real, factor_imag)


def tile_scan(x_re, x_im, keep, powers, down):
    reps = x_re.shape[1] // keep.shape[1]
    rows = lax.broadcasted_iota(jnp.int32, keep.shape, 0)
    b_re, b_im = x_re, x_im
    for level, k in enumerate((1, 2, 4)):
        shift = 8 - k if down else k
        valid = rows <= 7 - k if down else rows >= k
        gate = jnp.tile(jnp.where(valid, keep, 0.0), (1, reps))
        p_re = pltpu.roll(b_re, shift, 0)
        p_im = pltpu.roll(b_im, shift, 0)
        w_re = powers[0][(0, 1, 3)[level] : (0, 1, 3)[level] + 1]
        w_im = powers[1][(0, 1, 3)[level] : (0, 1, 3)[level] + 1]
        b_re = b_re + gate * (w_re * p_re - w_im * p_im)
        b_im = b_im + gate * (w_re * p_im + w_im * p_re)
        keep = keep * jnp.where(valid, pltpu.roll(keep, shift, 0), 1.0)
    return b_re, b_im, jnp.tile(keep, (1, reps))


def blocked_scan(count, width, pow_ref, up_keep, down_keep, load_up, load_down, store_up, store_down):
    tiles = count // 8
    up_powers = (pow_ref[0], pow_ref[1])
    down_powers = (pow_ref[2], pow_ref[3])

    def carry_in(b_re, b_im, reach, powers, h_re, h_im):
        q_re = powers[0] * h_re - powers[1] * h_im
        q_im = powers[0] * h_im + powers[1] * h_re
        return b_re + reach * q_re, b_im + reach * q_im

    def step(i, carry):
        u_re, u_im, d_re, d_im = carry
        tu = pl.multiple_of(i * 8, 8)
        td = pl.multiple_of((tiles - 1 - i) * 8, 8)
        xu_re, xu_im = load_up(tu)
        xd_re, xd_im = load_down(td)
        bu_re, bu_im, ru = tile_scan(xu_re, xu_im, up_keep[pl.ds(tu, 8), :], up_powers, False)
        bd_re, bd_im, rd = tile_scan(xd_re, xd_im, down_keep[pl.ds(td, 8), :], up_powers, True)
        hu_re, hu_im = carry_in(bu_re, bu_im, ru, up_powers, u_re, u_im)
        hd_re, hd_im = carry_in(bd_re, bd_im, rd, down_powers, d_re, d_im)
        store_up(tu, hu_re, hu_im)
        store_down(td, hd_re, hd_im)
        return (hu_re[7:8], hu_im[7:8], hd_re[0:1], hd_im[0:1])

    zeros = jnp.zeros((1, width), jnp.float32)
    lax.fori_loop(0, tiles, step, (zeros, zeros, zeros, zeros), unroll=2)


def pole_powers(p_re, p_im):
    rows_re = [p_re]
    rows_im = [p_im]
    for _ in range(7):
        a, b = rows_re[-1], rows_im[-1]
        rows_re.append(a * p_re - b * p_im)
        rows_im.append(a * p_im + b * p_re)
    up_re = jnp.stack(rows_re)
    up_im = jnp.stack(rows_im)
    return jnp.stack([up_re, up_im, up_re[::-1], up_im[::-1]])


def recurrence_kernel(up_ref, down_ref, pow_ref, x_ref, out_ref):
    count = x_ref.shape[0]
    width = pow_ref.shape[2]

    def load(t):
        return x_ref[pl.ds(t, 8), pl.ds(0, width)], x_ref[pl.ds(t, 8), pl.ds(width, width)]

    def store(column):
        def put(t, h_re, h_im):
            out_ref[pl.ds(t, 8), pl.ds(column, width)] = h_re
            out_ref[pl.ds(t, 8), pl.ds(column + width, width)] = h_im

        return put

    blocked_scan(count, width, pow_ref, up_ref, down_ref, load, load, store(0), store(2 * width))


def recurrence(up, down, powers, x):
    count, double = x.shape
    vmem = pl.BlockSpec(memory_space=pltpu.VMEM)
    return pl.pallas_call(
        recurrence_kernel,
        out_shape=jax.ShapeDtypeStruct((count, 2 * double), jnp.float32),
        in_specs=[vmem, vmem, vmem, vmem],
        out_specs=vmem,
        cost_estimate=pl.CostEstimate(
            flops=20 * count * double, transcendentals=0, bytes_accessed=16 * count * double
        ),
    )(up, down, powers, x)


MESH = pl.DeviceIdType.MESH


def forward_gather_kernel(x_ref, o_ref, local, sends, recvs):
    me = lax.axis_index("feat")
    partner = me + 1 - 2 * (me % 2)
    across = (me + 2) % 4
    diagonal = partner + 2 - 4 * (partner // 2)

    barrier = pltpu.get_barrier_semaphore()
    for peer in (partner, across):
        pl.semaphore_signal(barrier, 1, device_id={"feat": peer}, device_id_type=MESH)
    pl.semaphore_wait(barrier, 2)

    own = pltpu.make_async_copy(x_ref, o_ref.at[me], local)
    own.start()

    def remote(src, slot, peer, k):
        return pltpu.make_async_remote_copy(
            src_ref=src,
            dst_ref=o_ref.at[slot],
            send_sem=sends.at[k],
            recv_sem=recvs.at[k],
            device_id={"feat": peer},
            device_id_type=MESH,
        )

    to_across = remote(x_ref, me, across, 0)
    to_partner = remote(x_ref, me, partner, 1)
    to_across.start()
    to_partner.start()
    remote(x_ref, across, across, 0).wait_recv()
    onward = remote(o_ref.at[across], across, partner, 2)
    onward.start()
    remote(x_ref, partner, partner, 1).wait_recv()
    remote(x_ref, diagonal, partner, 2).wait_recv()
    own.wait()
    to_across.wait_send()
    to_partner.wait_send()
    onward.wait_send()


def forward_gather(x):
    rows, lanes = x.shape
    anywhere = pl.BlockSpec(memory_space=pl.ANY)
    return pl.pallas_call(
        forward_gather_kernel,
        out_shape=jax.ShapeDtypeStruct((4, rows, lanes), x.dtype),
        in_specs=[anywhere],
        out_specs=anywhere,
        scratch_shapes=[
            pltpu.SemaphoreType.DMA(()),
            pltpu.SemaphoreType.DMA((3,)),
            pltpu.SemaphoreType.DMA((3,)),
        ],
        compiler_params=pltpu.CompilerParams(collective_id=1, has_side_effects=True),
    )(x)


def split_exact(value):
    high = lax.reduce_precision(value, exponent_bits=8, mantissa_bits=7)
    rest = value - high
    middle = lax.reduce_precision(rest, exponent_bits=8, mantissa_bits=7)
    low = rest - middle
    return jnp.concatenate([high, middle, low], 0).astype(jnp.bfloat16)


def join_exact(pieces):
    third = pieces.shape[-2] // 3
    pieces = pieces.astype(jnp.float32)
    return pieces[..., :third, :] + (pieces[..., third : 2 * third, :] + pieces[..., 2 * third :, :])


def lanes_joined(stacked):
    moved = jnp.moveaxis(stacked, 0, 1)
    return moved.reshape(moved.shape[0], -1)


def unpack(stacked, pieces):
    result = []
    start = 0
    for piece in pieces:
        result.append(stacked[:, start : start + piece.shape[0]])
        start += piece.shape[0]
    return result


def layer_pieces(in_shard, out_shard, gate_shard):
    return [in_shard.T.astype(jnp.bfloat16), out_shard.astype(jnp.bfloat16), gate_shard.astype(jnp.bfloat16)]


def layer_full(gathered):
    in_t, out_w, gate_w = gathered[:3]
    in_full = jnp.transpose(in_t, (0, 2, 1)).reshape(-1, in_t.shape[1])
    return [in_full, lanes_joined(out_w), lanes_joined(gate_w)]


def ring_place(position, n):
    upper = position // (n // 2)
    return (1 - upper) * (2 * position) + upper * (2 * (n - 1 - position) + 1)


def ring_position(index, n):
    odd = index % 2
    return (1 - odd) * (index // 2) + odd * (n - 1 - index // 2)


def ring_sum_kernel(n, x_ref, r_ref, o_ref, low, slots, rs_send, rs_recv, credit, done, ag_send, ag_recv):
    rows = x_ref.shape[0]
    half = rows // 2
    size = half // n
    me = ring_position(lax.axis_index("seq"), n)
    right = ring_place((me + 1) % n, n)
    left = ring_place((me + n - 1) % n, n)
    rings = ((0, me, right, left), (1, (n - me) % n, left, right))

    barrier = pltpu.get_barrier_semaphore()
    for neighbour in (left, right):
        pl.semaphore_signal(barrier, 1, device_id={"seq": neighbour}, device_id_type=MESH)
    pl.semaphore_wait(barrier, 2)
    o_ref[...] = x_ref[...]
    low[...] = x_ref[...].astype(low.dtype)

    def block(ring, k):
        return pl.ds(pl.multiple_of(ring * half + k * size, 8), size)

    def scatter_copy(ring, place, target, s):
        return pltpu.make_async_remote_copy(
            src_ref=low.at[block(ring, (place - s + n) % n)],
            dst_ref=slots.at[ring, s % 2],
            send_sem=rs_send.at[ring, s % 2],
            recv_sem=rs_recv.at[ring, s % 2],
            device_id={"seq": target},
            device_id_type=MESH,
        )

    def scatter_step(s, carry):
        copies = []
        for ring, place, target, source in rings:

            @pl.when(s >= 2)
            def _():
                pl.semaphore_wait(credit.at[ring], 1)

            copy = scatter_copy(ring, place, target, s)
            copy.start()
            copies.append(copy)
        for (ring, place, target, source), copy in zip(rings, copies):
            copy.wait_recv()
            into = block(ring, (place - s - 1 + 2 * n) % n)
            total = o_ref[into] + slots[ring, s % 2].astype(jnp.float32)
            o_ref[into] = total
            low[into] = total.astype(low.dtype)
            copy.wait_send()

            @pl.when(s <= n - 4)
            def _():
                pl.semaphore_signal(credit.at[ring], 1, device_id={"seq": source}, device_id_type=MESH)

        return carry

    lax.fori_loop(0, n - 1, scatter_step, 0)
    for ring, place, target, source in rings:
        pl.semaphore_signal(done.at[ring], 1, device_id={"seq": source}, device_id_type=MESH)
    for ring, place, target, source in rings:
        final = block(ring, (place + 1) % n)
        r_ref[final] = o_ref[final].astype(r_ref.dtype)
    for ring, place, target, source in rings:
        pl.semaphore_wait(done.at[ring], 1)

    def gather_copy(ring, place, target, s):
        where = block(ring, (place + 1 - s + n) % n)
        return pltpu.make_async_remote_copy(
            src_ref=r_ref.at[where],
            dst_ref=r_ref.at[where],
            send_sem=ag_send.at[ring, s],
            recv_sem=ag_recv.at[ring, s],
            device_id={"seq": target},
            device_id_type=MESH,
        )

    def gather_step(s, carry):
        for ring, place, target, source in rings:

            @pl.when(s >= 1)
            def _():
                gather_copy(ring, place, target, s - 1).wait_recv()

            gather_copy(ring, place, target, s).start()

            @pl.when(s >= 1)
            def _():
                gather_copy(ring, place, target, s - 1).wait_send()

        return carry

    lax.fori_loop(0, n - 1, gather_step, 0)
    for ring, place, target, source in rings:
        last = gather_copy(ring, place, target, n - 2)
        last.wait_recv()
        last.wait_send()


def ring_sum(x, n):
    rows, lanes = x.shape
    size = rows // (2 * n)
    return pl.pallas_call(
        lambda *refs: ring_sum_kernel(n, *refs),
        out_shape=jax.ShapeDtypeStruct((rows, lanes), jnp.bfloat16),
        in_specs=[pl.BlockSpec(memory_space=pltpu.VMEM)],
        out_specs=pl.BlockSpec(memory_space=pltpu.VMEM),
        scratch_shapes=[
            pltpu.VMEM((rows, lanes), jnp.float32),
            pltpu.VMEM((rows, lanes), jnp.bfloat16),
            pltpu.VMEM((2, 2, size, lanes), jnp.bfloat16),
            pltpu.SemaphoreType.DMA((2, 2)),
            pltpu.SemaphoreType.DMA((2, 2)),
            pltpu.SemaphoreType.REGULAR((2,)),
            pltpu.SemaphoreType.REGULAR((2,)),
            pltpu.SemaphoreType.DMA((2, n - 1)),
            pltpu.SemaphoreType.DMA((2, n - 1)),
        ],
        compiler_params=pltpu.CompilerParams(collective_id=0, has_side_effects=True),
    )(x)


def sum_over_seq(parts):
    n = lax.axis_size("seq")
    flat = jnp.concatenate([part.reshape(-1) for part in parts])
    grain = 2 * n * 16 * 128
    padded = -(-flat.size // grain) * grain
    flat = jnp.pad(flat, (0, padded - flat.size)).reshape(padded // 128, 128)
    total = ring_sum(flat, n).astype(jnp.float32).reshape(-1)
    pieces = []
    start = 0
    for part in parts:
        pieces.append(total[start : start + part.size].reshape(part.shape))
        start += part.size
    return pieces


def adjoint_kernel(ma_ref, mb_ref, pow_ref, coef_ref, masks_ref, g_ref, states_ref, drive_ref, dg_ref, sums_ref, lam):
    count = g_ref.shape[0]
    width = coef_ref.shape[1]
    pad = 8
    f_re = coef_ref[2:3, :]
    f_im = coef_ref[3:4, :]
    zero_rows = jnp.zeros((pad, 4 * width), jnp.float32)
    lam[0:pad, :] = zero_rows
    lam[pad + count : 2 * pad + count, :] = zero_rows

    def load(column):
        def get(t):
            return g_ref[pl.ds(t, 8), pl.ds(column, width)], g_ref[pl.ds(t, 8), pl.ds(column + width, width)]

        return get

    def store(column):
        def put(t, h_re, h_im):
            lam[pl.ds(pad + t, 8), pl.ds(column, width)] = h_re
            lam[pl.ds(pad + t, 8), pl.ds(column + width, width)] = h_im

        return put

    blocked_scan(count, width, pow_ref, ma_ref, mb_ref, load(2 * width), load(0), store(0), store(2 * width))

    rows = 16

    def part(ref, start, column):
        return ref[pl.ds(start, rows), pl.ds(column, width)]

    def epilogue(k, sums):
        gp_re, gp_im, gf_re, gf_im = sums
        r0 = pl.multiple_of(k * rows, rows)
        live = masks_ref[pl.ds(r0, rows), 0:1]
        keep_prev = masks_ref[pl.ds(r0, rows), 1:2]
        keep_next = masks_ref[pl.ds(r0, rows), 2:3]
        lb_re = part(lam, pad + r0, 0)
        lb_im = part(lam, pad + r0, width)
        la_re = part(lam, pad + r0, 2 * width)
        la_im = part(lam, pad + r0, 3 * width)
        gu_re = la_re + lb_re
        gu_im = la_im + lb_im
        dg_ref[pl.ds(r0, rows), pl.ds(0, width)] = ((f_re * gu_re + f_im * gu_im) * live).astype(dg_ref.dtype)
        dg_ref[pl.ds(r0, rows), pl.ds(width, width)] = ((f_re * gu_im - f_im * gu_re) * live).astype(dg_ref.dtype)
        d_re = part(drive_ref, r0, 0) * live
        d_im = part(drive_ref, r0, width) * live
        gf_re = gf_re + d_re * gu_re + d_im * gu_im
        gf_im = gf_im + d_re * gu_im - d_im * gu_re
        a_re = part(states_ref, r0, 0) * keep_next
        a_im = part(states_ref, r0, width) * keep_next
        b_re = part(states_ref, r0, 2 * width) * keep_prev
        b_im = part(states_ref, r0, 3 * width) * keep_prev
        ahead_rows = lam[pl.ds(pad + r0, rows + 8), pl.ds(2 * width, 2 * width)][1 : rows + 1]
        behind_rows = lam[pl.ds(r0, rows + 8), pl.ds(0, 2 * width)][pad - 1 : pad - 1 + rows]
        na_re = ahead_rows[:, :width]
        na_im = ahead_rows[:, width:]
        pb_re = behind_rows[:, :width]
        pb_im = behind_rows[:, width:]
        gp_re = gp_re + a_re * na_re + a_im * na_im + b_re * pb_re + b_im * pb_im
        gp_im = gp_im + a_re * na_im - a_im * na_re + b_re * pb_im - b_im * pb_re
        return (gp_re, gp_im, gf_re, gf_im)

    block = jnp.zeros((rows, width), jnp.float32)
    sums = lax.fori_loop(0, count // rows, epilogue, (block, block, block, block))
    for k, value in enumerate(sums):
        sums_ref[k : k + 1, :] = jnp.sum(value, 0, keepdims=True)


def adjoint(ma, mb, powers, coef, masks, states_grad, states, drive):
    count, quad = states_grad.shape
    width = quad // 4
    vmem = pl.BlockSpec(memory_space=pltpu.VMEM)
    return pl.pallas_call(
        adjoint_kernel,
        out_shape=(
            jax.ShapeDtypeStruct((count, 2 * width), jnp.bfloat16),
            jax.ShapeDtypeStruct((4, width), jnp.float32),
        ),
        in_specs=[vmem] * 8,
        out_specs=(vmem, vmem),
        scratch_shapes=[pltpu.VMEM((count + 16, 4 * width), jnp.float32)],
        cost_estimate=pl.CostEstimate(
            flops=60 * count * width, transcendentals=0, bytes_accessed=48 * count * width
        ),
    )(ma, mb, powers, coef, masks, states_grad, states, drive)


def update(weight, gradient, velocity, average, rate, decay):
    adjusted = gradient + decay * weight
    velocity_new = momentum * velocity + adjusted
    change = -rate * (adjusted + momentum * velocity_new)
    weight_new = weight + change
    average_new = smoothing * average + (1.0 - smoothing) * weight_new
    return (weight_new, velocity_new, average_new, change)


def contract_rows(left, right):
    return lax.dot_general(
        left, right, (((0,), (0,)), ((), ())), preferred_element_type=jnp.float32
    )


def contract_cols(left, right):
    return lax.dot_general(
        left, right, (((1,), (1,)), ((), ())), preferred_element_type=jnp.float32
    )


def gather_feat(value, axis):
    return lax.all_gather(value, "feat", axis=axis, tiled=True)


def body(
    activations_in,
    cotangent,
    seq_start,
    seq_length,
    input_matrix,
    output_matrix,
    gate_matrix,
    feature_vectors,
    state_vectors,
    velocity_input,
    velocity_output,
    velocity_gate,
    velocity_feature,
    velocity_state,
    average_input,
    average_output,
    average_gate,
    average_feature,
    average_state,
):
    count = activations_in.shape[0]
    shard = activations_in.shape[1]
    layers = input_matrix.shape[0]
    width = state_vectors.shape[2]
    me = lax.axis_index("feat")
    offset = me * shard

    def mine(value):
        return lax.dynamic_slice_in_dim(value, offset, shard, axis=value.ndim - 1)

    alive, carry_prev, carry_next = masks_of(seq_start, seq_length, count)
    zero = jnp.zeros((1,), jnp.float32)
    after_next = jnp.concatenate([zero, carry_next[:-1]])
    before_prev = jnp.concatenate([carry_prev[1:], zero])
    mask_columns = jnp.stack([alive, carry_prev, carry_next, jnp.zeros_like(alive)], 1)

    def lanes(mask):
        return jnp.broadcast_to(mask[:, None], (count, 128))

    keep_prev, keep_next = lanes(carry_prev), lanes(carry_next)
    keep_after_next, keep_before_prev = lanes(after_next), lanes(before_prev)

    parts = lax.axis_size("feat")
    first = layer_pieces(input_matrix[0], output_matrix[0], gate_matrix[0])
    feature_pieces = split_exact(feature_vectors.reshape(-1, shard))
    first_pieces = first + [feature_pieces, activations_in] + ([] if layers > 1 else [cotangent])
    if parts == 4:
        stacked = forward_gather(jnp.concatenate(first_pieces, 0))
    else:
        stacked = lax.all_gather(jnp.concatenate(first_pieces, 0), "feat", axis=0, tiled=False)
    gathered = unpack(stacked, first_pieces)
    weights = [layer_full(gathered)]
    feature_all = lanes_joined(join_exact(gathered[3])).reshape(feature_vectors.shape[:-1] + (-1,))
    stream = lanes_joined(gathered[4]).astype(jnp.float32)
    cotangent_all = lanes_joined(gathered[5]) if layers == 1 else None
    previous = stacked
    for k in range(1, layers):
        later = layer_pieces(input_matrix[k], output_matrix[k], gate_matrix[k])
        later = later + ([cotangent] if k == layers - 1 else [])
        packed = jnp.concatenate(later, 0)
        packed, previous = lax.optimization_barrier((packed, previous))
        previous = lax.all_gather(packed, "feat", axis=0, tiled=False)
        gathered = unpack(previous, later)
        weights.append(layer_full(gathered))
        if k == layers - 1:
            cotangent_all = lanes_joined(gathered[3])
    in_all = [entry[0] for entry in weights]
    out_all = [entry[1] for entry in weights]
    gate_all = [entry[2] for entry in weights]

    saved = []
    for layer in range(layers):
        in_low = in_all[layer]
        out_low = out_all[layer]
        gate_low = gate_all[layer]
        feature_row = feature_all[layer]
        pole_re, pole_im, factor_re, factor_im = coefficients(state_vectors[layer])
        center = jnp.mean(stream, 1, keepdims=True)
        spread = stream - center
        scale = lax.rsqrt(jnp.mean(spread * spread, 1, keepdims=True) + epsilon)
        unit = spread * scale
        normed = unit * feature_row[0] + feature_row[1]
        normed_low = normed.astype(jnp.bfloat16)
        drive = jnp.dot(normed_low, in_low, preferred_element_type=jnp.float32)
        drive_re = drive[:, :width]
        drive_im = drive[:, width:]
        source = jnp.concatenate(
            [
                (drive_re * factor_re - drive_im * factor_im) * alive[:, None],
                (drive_re * factor_im + drive_im * factor_re) * alive[:, None],
            ],
            1,
        )
        states = recurrence(keep_prev, keep_next, pole_powers(pole_re, pole_im), source)
        states_low = states.astype(jnp.bfloat16)
        mixed = (
            jnp.dot(states_low, out_low, preferred_element_type=jnp.float32)
            + feature_row[2] * normed
        )
        act = smooth(mixed)
        act_low = act.astype(jnp.bfloat16)
        pre = jnp.dot(act_low, gate_low, preferred_element_type=jnp.float32) + feature_row[3]
        saved.append((scale, unit, normed_low, drive, states, states_low, mixed, act, act_low, pre))
        stream = stream + act * jax.nn.sigmoid(pre)

    grad = cotangent_all.astype(jnp.float32) * alive[:, None]
    layer_grads = [None] * layers
    for layer in reversed(range(layers)):
        scale, unit, normed_low, drive, states, states_low, mixed, act, act_low, pre = saved[layer]
        in_low = in_all[layer]
        out_low = out_all[layer]
        gate_low = gate_all[layer]
        feature_row = feature_all[layer]
        state_row = state_vectors[layer]
        pole_re, pole_im, factor_re, factor_im = coefficients(state_row)
        gate = jax.nn.sigmoid(pre)
        pre_grad = (grad * act * gate * (1.0 - gate)).astype(jnp.bfloat16)
        gate_grad = contract_rows(act_low, mine(pre_grad))
        gate_bias_grad = jnp.sum(pre_grad.astype(jnp.float32), 0)
        act_grad = grad * gate + contract_cols(pre_grad, gate_low)
        mixed_grad = jax.vjp(smooth, mixed)[1](act_grad)[0]
        normed = unit * feature_row[0] + feature_row[1]
        skip_grad = jnp.sum(mixed_grad * normed, 0)
        mixed_low = mixed_grad.astype(jnp.bfloat16)
        out_grad = contract_rows(states_low, mine(mixed_low))
        states_grad = contract_cols(mixed_low, out_low)
        coef = jnp.stack([pole_re, pole_im, factor_re, factor_im])
        drive_low, sums = adjoint(
            keep_after_next,
            keep_before_prev,
            pole_powers(pole_re, -pole_im),
            coef,
            mask_columns,
            states_grad,
            states,
            drive,
        )
        gp_re, gp_im, gf_re, gf_im = sums[0], sums[1], sums[2], sums[3]
        row_grad = jax.vjp(coefficients, state_row)[1]((gp_re, gp_im, gf_re, gf_im))[0]
        in_grad = contract_rows(mine(normed_low), drive_low)
        normed_grad = mixed_grad * feature_row[2] + jnp.dot(
            drive_low, in_low.T, preferred_element_type=jnp.float32
        )
        gain_grad = jnp.sum(normed_grad * unit, 0)
        bias_grad = jnp.sum(normed_grad, 0)
        unit_grad = normed_grad * feature_row[0]
        first_mean = jnp.mean(unit_grad, 1, keepdims=True)
        second_mean = jnp.mean(unit_grad * unit, 1, keepdims=True)
        grad = grad + scale * (unit_grad - first_mean - unit * second_mean)
        feature_grad = mine(jnp.stack([gain_grad, bias_grad, skip_grad, gate_bias_grad]))
        layer_grads[layer] = (in_grad, out_grad, gate_grad, feature_grad, row_grad)
    stacked_in = jnp.stack([entry[0] for entry in layer_grads])
    stacked_out = jnp.stack([entry[1] for entry in layer_grads])
    stacked_gate = jnp.stack([entry[2] for entry in layer_grads])
    stacked_feature = jnp.stack([entry[3] for entry in layer_grads])
    stacked_state = jnp.stack([entry[4] for entry in layer_grads])
    summed = sum_over_seq((stacked_in, stacked_out, stacked_gate, stacked_feature, stacked_state))
    factor = 1.0 / math.sqrt(count * lax.axis_size("seq"))
    grad_in = summed[0] * factor
    grad_out = summed[1] * factor
    grad_gate = summed[2] * factor
    grad_feature = summed[3] * factor
    grad_state = summed[4] * factor
    new_in = update(input_matrix, grad_in, velocity_input, average_input, slow_rate, 0.0)
    new_out = update(output_matrix, grad_out, velocity_output, average_output, slow_rate, 0.0)
    new_gate = update(gate_matrix, grad_gate, velocity_gate, average_gate, main_rate, weight_decay)
    new_feature = update(
        feature_vectors, grad_feature, velocity_feature, average_feature, main_rate, weight_decay
    )
    new_state = update(state_vectors, grad_state, velocity_state, average_state, slow_rate, 0.0)
    return (
        mine(stream),
        mine(grad),
        grad_in,
        grad_out,
        grad_gate,
        grad_feature,
        grad_state,
        new_in[0],
        new_out[0],
        new_gate[0],
        new_feature[0],
        new_state[3],
        new_in[1],
        new_out[1],
        new_gate[1],
        new_feature[1],
        new_state[1],
        new_in[2],
        new_out[2],
        new_gate[2],
        new_feature[2],
        new_state[2],
    )


def solution(mesh):
    feat = P(None, None, "feat")
    rows = P(None, "feat", None)
    tokens = P("seq", "feat")
    return jax.shard_map(
        body,
        mesh=mesh,
        in_specs=(
            tokens,
            tokens,
            P("seq"),
            P("seq"),
            rows,
            feat,
            feat,
            feat,
            P(),
            rows,
            feat,
            feat,
            feat,
            P(),
            rows,
            feat,
            feat,
            feat,
            P(),
        ),
        out_specs=(
            tokens,
            tokens,
            rows,
            feat,
            feat,
            feat,
            P(),
            rows,
            feat,
            feat,
            feat,
            P(),
            rows,
            feat,
            feat,
            feat,
            P(),
            rows,
            feat,
            feat,
            feat,
            P(),
        ),
        check_vma=False,
    )
```

```python
import math

import jax
import jax.numpy as jnp
from jax import lax
from jax.experimental import pallas as pl
from jax.experimental.pallas import tpu as pltpu
from jax.sharding import PartitionSpec as P

epsilon = 1e-05
momentum = 0.9
smoothing = 0.5
slow_rate = 0.02
main_rate = 0.05
weight_decay = 0.1


def smooth(value):
    return jax.nn.gelu(value, approximate=False)


def masks_of(starts, lengths, count):
    position = jnp.arange(count, dtype=jnp.int32)[:, None]
    begin = starts[None, :]
    finish = begin + lengths[None, :]
    inside = (position >= begin) & (position < finish)
    alive = jnp.any(inside, 1)
    opening = jnp.any(inside & (position == begin), 1)
    closing = jnp.any(inside & (position == finish - 1), 1)
    return (
        alive.astype(jnp.float32),
        (alive & ~opening).astype(jnp.float32),
        (alive & ~closing).astype(jnp.float32),
    )


def coefficients(state_row):
    rate = -jnp.exp(state_row[0])
    frequency = state_row[1]
    timestep = jnp.exp(state_row[2])
    decay = jnp.exp(rate * timestep)
    angle = frequency * timestep
    pole_real = decay * jnp.cos(angle)
    pole_imag = decay * jnp.sin(angle)
    denom = rate * rate + frequency * frequency
    factor_real = ((pole_real - 1.0) * rate + pole_imag * frequency) / denom
    factor_imag = (pole_imag * rate - (pole_real - 1.0) * frequency) / denom
    return (pole_real, pole_imag, factor_real, factor_imag)


def tile_scan(x_re, x_im, keep, powers, down):
    reps = x_re.shape[1] // keep.shape[1]
    rows = lax.broadcasted_iota(jnp.int32, keep.shape, 0)
    b_re, b_im = x_re, x_im
    for level, k in enumerate((1, 2, 4)):
        shift = 8 - k if down else k
        valid = rows <= 7 - k if down else rows >= k
        gate = jnp.tile(jnp.where(valid, keep, 0.0), (1, reps))
        p_re = pltpu.roll(b_re, shift, 0)
        p_im = pltpu.roll(b_im, shift, 0)
        w_re = powers[0][(0, 1, 3)[level] : (0, 1, 3)[level] + 1]
        w_im = powers[1][(0, 1, 3)[level] : (0, 1, 3)[level] + 1]
        b_re = b_re + gate * (w_re * p_re - w_im * p_im)
        b_im = b_im + gate * (w_re * p_im + w_im * p_re)
        keep = keep * jnp.where(valid, pltpu.roll(keep, shift, 0), 1.0)
    return b_re, b_im, jnp.tile(keep, (1, reps))


def blocked_scan(count, width, pow_ref, starts_ref, lengths_ref, load_up, load_down, store_up, store_down):
    tiles = count // 8
    slots = starts_ref.shape[0]

    def keeps(t0, downward):
        rows = lax.broadcasted_iota(jnp.int32, (8, 128), 0) + t0
        inside = jnp.zeros((8, 128), jnp.bool_)
        for slot in range(slots):
            begin = starts_ref[slot]
            finish = begin + lengths_ref[slot]
            if downward:
                inside = inside | ((rows >= begin) & (rows < finish - 1))
            else:
                inside = inside | ((rows > begin) & (rows < finish))
        return inside.astype(jnp.float32)

    up_powers = (pow_ref[0], pow_ref[1])
    down_powers = (pow_ref[2], pow_ref[3])

    def carry_in(b_re, b_im, reach, powers, h_re, h_im):
        q_re = powers[0] * h_re - powers[1] * h_im
        q_im = powers[0] * h_im + powers[1] * h_re
        return b_re + reach * q_re, b_im + reach * q_im

    def step(i, carry):
        u_re, u_im, d_re, d_im = carry
        tu = pl.multiple_of(i * 8, 8)
        td = pl.multiple_of((tiles - 1 - i) * 8, 8)
        xu_re, xu_im = load_up(tu)
        xd_re, xd_im = load_down(td)
        bu_re, bu_im, ru = tile_scan(xu_re, xu_im, keeps(tu, False), up_powers, False)
        bd_re, bd_im, rd = tile_scan(xd_re, xd_im, keeps(td, True), up_powers, True)
        hu_re, hu_im = carry_in(bu_re, bu_im, ru, up_powers, u_re, u_im)
        hd_re, hd_im = carry_in(bd_re, bd_im, rd, down_powers, d_re, d_im)
        store_up(tu, hu_re, hu_im)
        store_down(td, hd_re, hd_im)
        return (hu_re[7:8], hu_im[7:8], hd_re[0:1], hd_im[0:1])

    zeros = jnp.zeros((1, width), jnp.float32)
    lax.fori_loop(0, tiles, step, (zeros, zeros, zeros, zeros), unroll=2)


def pole_powers(p_re, p_im):
    rows_re = [p_re]
    rows_im = [p_im]
    for _ in range(7):
        a, b = rows_re[-1], rows_im[-1]
        rows_re.append(a * p_re - b * p_im)
        rows_im.append(a * p_im + b * p_re)
    up_re = jnp.stack(rows_re)
    up_im = jnp.stack(rows_im)
    return jnp.stack([up_re, up_im, up_re[::-1], up_im[::-1]])


def recurrence_kernel(starts_ref, lengths_ref, pow_ref, x_ref, out_ref):
    count = x_ref.shape[0]
    width = pow_ref.shape[2]

    def load(t):
        return x_ref[pl.ds(t, 8), pl.ds(0, width)], x_ref[pl.ds(t, 8), pl.ds(width, width)]

    def store(column):
        def put(t, h_re, h_im):
            out_ref[pl.ds(t, 8), pl.ds(column, width)] = h_re
            out_ref[pl.ds(t, 8), pl.ds(column + width, width)] = h_im

        return put

    blocked_scan(count, width, pow_ref, starts_ref, lengths_ref, load, load, store(0), store(2 * width))


def recurrence(starts, lengths, powers, x):
    count, double = x.shape
    vmem = pl.BlockSpec(memory_space=pltpu.VMEM)
    smem = pl.BlockSpec(memory_space=pltpu.SMEM)
    return pl.pallas_call(
        recurrence_kernel,
        out_shape=jax.ShapeDtypeStruct((count, 2 * double), jnp.float32),
        in_specs=[smem, smem, vmem, vmem],
        out_specs=vmem,
        cost_estimate=pl.CostEstimate(
            flops=20 * count * double, transcendentals=0, bytes_accessed=16 * count * double
        ),
    )(starts, lengths, powers, x)


MESH = pl.DeviceIdType.MESH


def ring_place(position, n):
    upper = position // (n // 2)
    return (1 - upper) * (2 * position) + upper * (2 * (n - 1 - position) + 1)


def ring_position(index, n):
    odd = index % 2
    return (1 - odd) * (index // 2) + odd * (n - 1 - index // 2)


def ring_sum_kernel(n, x_ref, r_ref, o_ref, low, slots, rs_send, rs_recv, credit, done, ag_send, ag_recv):
    rows = x_ref.shape[0]
    half = rows // 2
    size = half // n
    me = ring_position(lax.axis_index("seq"), n)
    right = ring_place((me + 1) % n, n)
    left = ring_place((me + n - 1) % n, n)
    rings = ((0, me, right, left), (1, (n - me) % n, left, right))

    barrier = pltpu.get_barrier_semaphore()
    for neighbour in (left, right):
        pl.semaphore_signal(barrier, 1, device_id={"seq": neighbour}, device_id_type=MESH)
    pl.semaphore_wait(barrier, 2)
    o_ref[...] = x_ref[...]
    low[...] = x_ref[...].astype(low.dtype)

    def block(ring, k):
        return pl.ds(pl.multiple_of(ring * half + k * size, 8), size)

    def scatter_copy(ring, place, target, s):
        return pltpu.make_async_remote_copy(
            src_ref=low.at[block(ring, (place - s + n) % n)],
            dst_ref=slots.at[ring, s % 2],
            send_sem=rs_send.at[ring, s % 2],
            recv_sem=rs_recv.at[ring, s % 2],
            device_id={"seq": target},
            device_id_type=MESH,
        )

    def scatter_step(s, carry):
        copies = []
        for ring, place, target, source in rings:

            @pl.when(s >= 2)
            def _():
                pl.semaphore_wait(credit.at[ring], 1)

            copy = scatter_copy(ring, place, target, s)
            copy.start()
            copies.append(copy)
        for (ring, place, target, source), copy in zip(rings, copies):
            copy.wait_recv()
            into = block(ring, (place - s - 1 + 2 * n) % n)
            total = o_ref[into] + slots[ring, s % 2].astype(jnp.float32)
            o_ref[into] = total
            low[into] = total.astype(low.dtype)
            copy.wait_send()

            @pl.when(s <= n - 4)
            def _():
                pl.semaphore_signal(credit.at[ring], 1, device_id={"seq": source}, device_id_type=MESH)

        return carry

    lax.fori_loop(0, n - 1, scatter_step, 0)
    for ring, place, target, source in rings:
        pl.semaphore_signal(done.at[ring], 1, device_id={"seq": source}, device_id_type=MESH)
    for ring, place, target, source in rings:
        final = block(ring, (place + 1) % n)
        r_ref[final] = o_ref[final].astype(r_ref.dtype)
    for ring, place, target, source in rings:
        pl.semaphore_wait(done.at[ring], 1)

    def gather_copy(ring, place, target, s):
        where = block(ring, (place + 1 - s + n) % n)
        return pltpu.make_async_remote_copy(
            src_ref=r_ref.at[where],
            dst_ref=r_ref.at[where],
            send_sem=ag_send.at[ring, s],
            recv_sem=ag_recv.at[ring, s],
            device_id={"seq": target},
            device_id_type=MESH,
        )

    def gather_step(s, carry):
        for ring, place, target, source in rings:

            @pl.when(s >= 1)
            def _():
                gather_copy(ring, place, target, s - 1).wait_recv()

            gather_copy(ring, place, target, s).start()

            @pl.when(s >= 1)
            def _():
                gather_copy(ring, place, target, s - 1).wait_send()

        return carry

    lax.fori_loop(0, n - 1, gather_step, 0)
    for ring, place, target, source in rings:
        last = gather_copy(ring, place, target, n - 2)
        last.wait_recv()
        last.wait_send()


def ring_sum(x, n):
    rows, lanes = x.shape
    size = rows // (2 * n)
    return pl.pallas_call(
        lambda *refs: ring_sum_kernel(n, *refs),
        out_shape=jax.ShapeDtypeStruct((rows, lanes), jnp.bfloat16),
        in_specs=[pl.BlockSpec(memory_space=pltpu.VMEM)],
        out_specs=pl.BlockSpec(memory_space=pltpu.VMEM),
        scratch_shapes=[
            pltpu.VMEM((rows, lanes), jnp.float32),
            pltpu.VMEM((rows, lanes), jnp.bfloat16),
            pltpu.VMEM((2, 2, size, lanes), jnp.bfloat16),
            pltpu.SemaphoreType.DMA((2, 2)),
            pltpu.SemaphoreType.DMA((2, 2)),
            pltpu.SemaphoreType.REGULAR((2,)),
            pltpu.SemaphoreType.REGULAR((2,)),
            pltpu.SemaphoreType.DMA((2, n - 1)),
            pltpu.SemaphoreType.DMA((2, n - 1)),
        ],
        compiler_params=pltpu.CompilerParams(collective_id=0, has_side_effects=True),
    )(x)


def sum_over_seq(parts):
    n = lax.axis_size("seq")
    flat = jnp.concatenate([part.reshape(-1) for part in parts])
    grain = 2 * n * 16 * 128
    padded = -(-flat.size // grain) * grain
    flat = jnp.pad(flat, (0, padded - flat.size)).reshape(padded // 128, 128)
    total = ring_sum(flat, n).astype(jnp.float32).reshape(-1)
    pieces = []
    start = 0
    for part in parts:
        pieces.append(total[start : start + part.size].reshape(part.shape))
        start += part.size
    return pieces


def adjoint_kernel(starts_ref, lengths_ref, pow_ref, coef_ref, masks_ref, g_ref, states_ref, drive_ref, dg_ref, sums_ref, lam):
    count = g_ref.shape[0]
    width = coef_ref.shape[1]
    pad = 8
    f_re = coef_ref[2:3, :]
    f_im = coef_ref[3:4, :]
    zero_rows = jnp.zeros((pad, 4 * width), jnp.float32)
    lam[0:pad, :] = zero_rows
    lam[pad + count : 2 * pad + count, :] = zero_rows

    def load(column):
        def get(t):
            return g_ref[pl.ds(t, 8), pl.ds(column, width)], g_ref[pl.ds(t, 8), pl.ds(column + width, width)]

        return get

    def store(column):
        def put(t, h_re, h_im):
            lam[pl.ds(pad + t, 8), pl.ds(column, width)] = h_re
            lam[pl.ds(pad + t, 8), pl.ds(column + width, width)] = h_im

        return put

    blocked_scan(count, width, pow_ref, starts_ref, lengths_ref, load(2 * width), load(0), store(0), store(2 * width))

    rows = 16

    def part(ref, start, column):
        return ref[pl.ds(start, rows), pl.ds(column, width)]

    def epilogue(k, sums):
        gp_re, gp_im, gf_re, gf_im = sums
        r0 = pl.multiple_of(k * rows, rows)
        live = masks_ref[pl.ds(r0, rows), 0:1]
        keep_prev = masks_ref[pl.ds(r0, rows), 1:2]
        keep_next = masks_ref[pl.ds(r0, rows), 2:3]
        lb_re = part(lam, pad + r0, 0)
        lb_im = part(lam, pad + r0, width)
        la_re = part(lam, pad + r0, 2 * width)
        la_im = part(lam, pad + r0, 3 * width)
        gu_re = la_re + lb_re
        gu_im = la_im + lb_im
        dg_ref[pl.ds(r0, rows), pl.ds(0, width)] = ((f_re * gu_re + f_im * gu_im) * live).astype(dg_ref.dtype)
        dg_ref[pl.ds(r0, rows), pl.ds(width, width)] = ((f_re * gu_im - f_im * gu_re) * live).astype(dg_ref.dtype)
        d_re = part(drive_ref, r0, 0) * live
        d_im = part(drive_ref, r0, width) * live
        gf_re = gf_re + d_re * gu_re + d_im * gu_im
        gf_im = gf_im + d_re * gu_im - d_im * gu_re
        a_re = part(states_ref, r0, 0) * keep_next
        a_im = part(states_ref, r0, width) * keep_next
        b_re = part(states_ref, r0, 2 * width) * keep_prev
        b_im = part(states_ref, r0, 3 * width) * keep_prev
        ahead_rows = lam[pl.ds(pad + r0, rows + 8), pl.ds(2 * width, 2 * width)][1 : rows + 1]
        behind_rows = lam[pl.ds(r0, rows + 8), pl.ds(0, 2 * width)][pad - 1 : pad - 1 + rows]
        na_re = ahead_rows[:, :width]
        na_im = ahead_rows[:, width:]
        pb_re = behind_rows[:, :width]
        pb_im = behind_rows[:, width:]
        gp_re = gp_re + a_re * na_re + a_im * na_im + b_re * pb_re + b_im * pb_im
        gp_im = gp_im + a_re * na_im - a_im * na_re + b_re * pb_im - b_im * pb_re
        return (gp_re, gp_im, gf_re, gf_im)

    block = jnp.zeros((rows, width), jnp.float32)
    sums = lax.fori_loop(0, count // rows, epilogue, (block, block, block, block))
    for k, value in enumerate(sums):
        sums_ref[k : k + 1, :] = jnp.sum(value, 0, keepdims=True)


def adjoint(starts, lengths, powers, coef, masks, states_grad, states, drive):
    count, quad = states_grad.shape
    width = quad // 4
    vmem = pl.BlockSpec(memory_space=pltpu.VMEM)
    smem = pl.BlockSpec(memory_space=pltpu.SMEM)
    return pl.pallas_call(
        adjoint_kernel,
        out_shape=(
            jax.ShapeDtypeStruct((count, 2 * width), jnp.bfloat16),
            jax.ShapeDtypeStruct((4, width), jnp.float32),
        ),
        in_specs=[smem, smem] + [vmem] * 6,
        out_specs=(vmem, vmem),
        scratch_shapes=[pltpu.VMEM((count + 16, 4 * width), jnp.float32)],
        cost_estimate=pl.CostEstimate(
            flops=60 * count * width, transcendentals=0, bytes_accessed=48 * count * width
        ),
    )(starts, lengths, powers, coef, masks, states_grad, states, drive)


def update(weight, gradient, velocity, average, rate, decay):
    adjusted = gradient + decay * weight
    velocity_new = momentum * velocity + adjusted
    change = -rate * (adjusted + momentum * velocity_new)
    weight_new = weight + change
    average_new = smoothing * average + (1.0 - smoothing) * weight_new
    return (weight_new, velocity_new, average_new, change)


def contract_rows(left, right):
    return lax.dot_general(
        left, right, (((0,), (0,)), ((), ())), preferred_element_type=jnp.float32
    )


def contract_cols(left, right):
    return lax.dot_general(
        left, right, (((1,), (1,)), ((), ())), preferred_element_type=jnp.float32
    )


def gather_feat(value, axis):
    return lax.all_gather(value, "feat", axis=axis, tiled=True)


def body(
    activations_in,
    cotangent,
    seq_start,
    seq_length,
    input_matrix,
    output_matrix,
    gate_matrix,
    feature_vectors,
    state_vectors,
    velocity_input,
    velocity_output,
    velocity_gate,
    velocity_feature,
    velocity_state,
    average_input,
    average_output,
    average_gate,
    average_feature,
    average_state,
):
    count = activations_in.shape[0]
    shard = activations_in.shape[1]
    layers = input_matrix.shape[0]
    width = state_vectors.shape[2]
    me = lax.axis_index("feat")
    offset = me * shard

    def mine(value):
        return lax.dynamic_slice_in_dim(value, offset, shard, axis=value.ndim - 1)

    alive, carry_prev, carry_next = masks_of(seq_start, seq_length, count)
    zero = jnp.zeros((1,), jnp.float32)
    after_next = jnp.concatenate([zero, carry_next[:-1]])
    before_prev = jnp.concatenate([carry_prev[1:], zero])
    mask_columns = jnp.stack([alive, carry_prev, carry_next, jnp.zeros_like(alive)], 1)


    in_all = gather_feat(input_matrix.astype(jnp.bfloat16), 1)
    out_all = gather_feat(output_matrix.astype(jnp.bfloat16), 2)
    gate_all = gather_feat(gate_matrix.astype(jnp.bfloat16), 2)
    feature_all = gather_feat(feature_vectors, 2)
    stream = gather_feat(activations_in, 1).astype(jnp.float32)

    saved = []
    for layer in range(layers):
        in_low = in_all[layer]
        out_low = out_all[layer]
        gate_low = gate_all[layer]
        feature_row = feature_all[layer]
        pole_re, pole_im, factor_re, factor_im = coefficients(state_vectors[layer])
        center = jnp.mean(stream, 1, keepdims=True)
        spread = stream - center
        scale = lax.rsqrt(jnp.mean(spread * spread, 1, keepdims=True) + epsilon)
        unit = spread * scale
        normed = unit * feature_row[0] + feature_row[1]
        normed_low = normed.astype(jnp.bfloat16)
        drive = jnp.dot(normed_low, in_low, preferred_element_type=jnp.float32)
        drive_re = drive[:, :width]
        drive_im = drive[:, width:]
        source = jnp.concatenate(
            [
                (drive_re * factor_re - drive_im * factor_im) * alive[:, None],
                (drive_re * factor_im + drive_im * factor_re) * alive[:, None],
            ],
            1,
        )
        states = recurrence(seq_start, seq_length, pole_powers(pole_re, pole_im), source)
        states_low = states.astype(jnp.bfloat16)
        mixed = (
            jnp.dot(states_low, out_low, preferred_element_type=jnp.float32)
            + feature_row[2] * normed
        )
        act = smooth(mixed)
        act_low = act.astype(jnp.bfloat16)
        pre = jnp.dot(act_low, gate_low, preferred_element_type=jnp.float32) + feature_row[3]
        saved.append((scale, unit, normed_low, drive, states, states_low, mixed, act, act_low, pre))
        stream = stream + act * jax.nn.sigmoid(pre)

    grad = gather_feat(cotangent, 1).astype(jnp.float32) * alive[:, None]
    layer_grads = [None] * layers
    for layer in reversed(range(layers)):
        scale, unit, normed_low, drive, states, states_low, mixed, act, act_low, pre = saved[layer]
        in_low = in_all[layer]
        out_low = out_all[layer]
        gate_low = gate_all[layer]
        feature_row = feature_all[layer]
        state_row = state_vectors[layer]
        pole_re, pole_im, factor_re, factor_im = coefficients(state_row)
        gate = jax.nn.sigmoid(pre)
        pre_grad = (grad * act * gate * (1.0 - gate)).astype(jnp.bfloat16)
        gate_grad = contract_rows(act_low, mine(pre_grad))
        gate_bias_grad = jnp.sum(pre_grad.astype(jnp.float32), 0)
        act_grad = grad * gate + contract_cols(pre_grad, gate_low)
        mixed_grad = jax.vjp(smooth, mixed)[1](act_grad)[0]
        normed = unit * feature_row[0] + feature_row[1]
        skip_grad = jnp.sum(mixed_grad * normed, 0)
        mixed_low = mixed_grad.astype(jnp.bfloat16)
        out_grad = contract_rows(states_low, mine(mixed_low))
        states_grad = contract_cols(mixed_low, out_low)
        coef = jnp.stack([pole_re, pole_im, factor_re, factor_im])
        drive_low, sums = adjoint(
            seq_start,
            seq_length,
            pole_powers(pole_re, -pole_im),
            coef,
            mask_columns,
            states_grad,
            states,
            drive,
        )
        gp_re, gp_im, gf_re, gf_im = sums[0], sums[1], sums[2], sums[3]
        row_grad = jax.vjp(coefficients, state_row)[1]((gp_re, gp_im, gf_re, gf_im))[0]
        in_grad = contract_rows(mine(normed_low), drive_low)
        normed_grad = mixed_grad * feature_row[2] + jnp.dot(
            drive_low, in_low.T, preferred_element_type=jnp.float32
        )
        gain_grad = jnp.sum(normed_grad * unit, 0)
        bias_grad = jnp.sum(normed_grad, 0)
        unit_grad = normed_grad * feature_row[0]
        first_mean = jnp.mean(unit_grad, 1, keepdims=True)
        second_mean = jnp.mean(unit_grad * unit, 1, keepdims=True)
        grad = grad + scale * (unit_grad - first_mean - unit * second_mean)
        feature_grad = mine(jnp.stack([gain_grad, bias_grad, skip_grad, gate_bias_grad]))
        layer_grads[layer] = (in_grad, out_grad, gate_grad, feature_grad, row_grad)
    stacked_in = jnp.stack([entry[0] for entry in layer_grads])
    stacked_out = jnp.stack([entry[1] for entry in layer_grads])
    stacked_gate = jnp.stack([entry[2] for entry in layer_grads])
    stacked_feature = jnp.stack([entry[3] for entry in layer_grads])
    stacked_state = jnp.stack([entry[4] for entry in layer_grads])
    summed = sum_over_seq((stacked_in, stacked_out, stacked_gate, stacked_feature, stacked_state))
    factor = 1.0 / math.sqrt(count * lax.axis_size("seq"))
    grad_in = summed[0] * factor
    grad_out = summed[1] * factor
    grad_gate = summed[2] * factor
    grad_feature = summed[3] * factor
    grad_state = summed[4] * factor
    new_in = update(input_matrix, grad_in, velocity_input, average_input, slow_rate, 0.0)
    new_out = update(output_matrix, grad_out, velocity_output, average_output, slow_rate, 0.0)
    new_gate = update(gate_matrix, grad_gate, velocity_gate, average_gate, main_rate, weight_decay)
    new_feature = update(
        feature_vectors, grad_feature, velocity_feature, average_feature, main_rate, weight_decay
    )
    new_state = update(state_vectors, grad_state, velocity_state, average_state, slow_rate, 0.0)
    return (
        mine(stream),
        mine(grad),
        grad_in,
        grad_out,
        grad_gate,
        grad_feature,
        grad_state,
        new_in[0],
        new_out[0],
        new_gate[0],
        new_feature[0],
        new_state[3],
        new_in[1],
        new_out[1],
        new_gate[1],
        new_feature[1],
        new_state[1],
        new_in[2],
        new_out[2],
        new_gate[2],
        new_feature[2],
        new_state[2],
    )


def solution(mesh):
    feat = P(None, None, "feat")
    rows = P(None, "feat", None)
    tokens = P("seq", "feat")
    return jax.shard_map(
        body,
        mesh=mesh,
        in_specs=(
            tokens,
            tokens,
            P("seq"),
            P("seq"),
            rows,
            feat,
            feat,
            feat,
            P(),
            rows,
            feat,
            feat,
            feat,
            P(),
            rows,
            feat,
            feat,
            feat,
            P(),
        ),
        out_specs=(
            tokens,
            tokens,
            rows,
            feat,
            feat,
            feat,
            P(),
            rows,
            feat,
            feat,
            feat,
            P(),
            rows,
            feat,
            feat,
            feat,
            P(),
            rows,
            feat,
            feat,
            feat,
            P(),
        ),
        check_vma=False,
    )
```

```python
import math

import jax
import jax.numpy as jnp
from jax import lax
from jax.experimental import pallas as pl
from jax.experimental.pallas import tpu as pltpu
from jax.sharding import PartitionSpec as P

epsilon = 1e-05
momentum = 0.9
smoothing = 0.5
slow_rate = 0.02
main_rate = 0.05
weight_decay = 0.1


def smooth(value):
    return jax.nn.gelu(value, approximate=False)


def masks_of(starts, lengths, count):
    position = jnp.arange(count, dtype=jnp.int32)[:, None]
    begin = starts[None, :]
    finish = begin + lengths[None, :]
    inside = (position >= begin) & (position < finish)
    alive = jnp.any(inside, 1)
    opening = jnp.any(inside & (position == begin), 1)
    closing = jnp.any(inside & (position == finish - 1), 1)
    return (
        alive.astype(jnp.float32),
        (alive & ~opening).astype(jnp.float32),
        (alive & ~closing).astype(jnp.float32),
    )


def coefficients(state_row):
    rate = -jnp.exp(state_row[0])
    frequency = state_row[1]
    timestep = jnp.exp(state_row[2])
    decay = jnp.exp(rate * timestep)
    angle = frequency * timestep
    pole_real = decay * jnp.cos(angle)
    pole_imag = decay * jnp.sin(angle)
    denom = rate * rate + frequency * frequency
    factor_real = ((pole_real - 1.0) * rate + pole_imag * frequency) / denom
    factor_imag = (pole_imag * rate - (pole_real - 1.0) * frequency) / denom
    return (pole_real, pole_imag, factor_real, factor_imag)


def tile_scan(x_re, x_im, keep, powers, down):
    reps = x_re.shape[1] // keep.shape[1]
    rows = lax.broadcasted_iota(jnp.int32, keep.shape, 0)
    b_re, b_im = x_re, x_im
    for level, k in enumerate((1, 2, 4)):
        shift = 8 - k if down else k
        valid = rows <= 7 - k if down else rows >= k
        gate = jnp.tile(jnp.where(valid, keep, 0.0), (1, reps))
        p_re = pltpu.roll(b_re, shift, 0)
        p_im = pltpu.roll(b_im, shift, 0)
        w_re = powers[0][(0, 1, 3)[level] : (0, 1, 3)[level] + 1]
        w_im = powers[1][(0, 1, 3)[level] : (0, 1, 3)[level] + 1]
        b_re = b_re + gate * (w_re * p_re - w_im * p_im)
        b_im = b_im + gate * (w_re * p_im + w_im * p_re)
        keep = keep * jnp.where(valid, pltpu.roll(keep, shift, 0), 1.0)
    return b_re, b_im, jnp.tile(keep, (1, reps))


def blocked_scan(count, width, pow_ref, starts_ref, lengths_ref, load_up, load_down, store_up, store_down):
    tiles = count // 8
    slots = starts_ref.shape[0]

    def keeps(t0, downward):
        rows = lax.broadcasted_iota(jnp.int32, (8, 128), 0) + t0
        inside = jnp.zeros((8, 128), jnp.bool_)
        for slot in range(slots):
            begin = starts_ref[slot]
            finish = begin + lengths_ref[slot]
            if downward:
                inside = inside | ((rows >= begin) & (rows < finish - 1))
            else:
                inside = inside | ((rows > begin) & (rows < finish))
        return inside.astype(jnp.float32)

    up_powers = (pow_ref[0], pow_ref[1])
    down_powers = (pow_ref[2], pow_ref[3])

    def carry_in(b_re, b_im, reach, powers, h_re, h_im):
        q_re = powers[0] * h_re - powers[1] * h_im
        q_im = powers[0] * h_im + powers[1] * h_re
        return b_re + reach * q_re, b_im + reach * q_im

    def step(i, carry):
        u_re, u_im, d_re, d_im = carry
        tu = pl.multiple_of(i * 8, 8)
        td = pl.multiple_of((tiles - 1 - i) * 8, 8)
        xu_re, xu_im = load_up(tu)
        xd_re, xd_im = load_down(td)
        bu_re, bu_im, ru = tile_scan(xu_re, xu_im, keeps(tu, False), up_powers, False)
        bd_re, bd_im, rd = tile_scan(xd_re, xd_im, keeps(td, True), up_powers, True)
        hu_re, hu_im = carry_in(bu_re, bu_im, ru, up_powers, u_re, u_im)
        hd_re, hd_im = carry_in(bd_re, bd_im, rd, down_powers, d_re, d_im)
        store_up(tu, hu_re, hu_im)
        store_down(td, hd_re, hd_im)
        return (hu_re[7:8], hu_im[7:8], hd_re[0:1], hd_im[0:1])

    zeros = jnp.zeros((1, width), jnp.float32)
    lax.fori_loop(0, tiles, step, (zeros, zeros, zeros, zeros), unroll=2)


def pole_powers(p_re, p_im):
    rows_re = [p_re]
    rows_im = [p_im]
    for _ in range(7):
        a, b = rows_re[-1], rows_im[-1]
        rows_re.append(a * p_re - b * p_im)
        rows_im.append(a * p_im + b * p_re)
    up_re = jnp.stack(rows_re)
    up_im = jnp.stack(rows_im)
    return jnp.stack([up_re, up_im, up_re[::-1], up_im[::-1]])


def recurrence_kernel(starts_ref, lengths_ref, pow_ref, x_ref, out_ref):
    count = x_ref.shape[0]
    width = pow_ref.shape[2]

    def load(t):
        return x_ref[pl.ds(t, 8), pl.ds(0, width)], x_ref[pl.ds(t, 8), pl.ds(width, width)]

    def store(column):
        def put(t, h_re, h_im):
            out_ref[pl.ds(t, 8), pl.ds(column, width)] = h_re
            out_ref[pl.ds(t, 8), pl.ds(column + width, width)] = h_im

        return put

    blocked_scan(count, width, pow_ref, starts_ref, lengths_ref, load, load, store(0), store(2 * width))


def recurrence(starts, lengths, powers, x):
    count, double = x.shape
    vmem = pl.BlockSpec(memory_space=pltpu.VMEM)
    smem = pl.BlockSpec(memory_space=pltpu.SMEM)
    return pl.pallas_call(
        recurrence_kernel,
        out_shape=jax.ShapeDtypeStruct((count, 2 * double), jnp.float32),
        in_specs=[smem, smem, vmem, vmem],
        out_specs=vmem,
        cost_estimate=pl.CostEstimate(
            flops=20 * count * double, transcendentals=0, bytes_accessed=16 * count * double
        ),
    )(starts, lengths, powers, x)


MESH = pl.DeviceIdType.MESH


def ring_place(position, n):
    upper = position // (n // 2)
    return (1 - upper) * (2 * position) + upper * (2 * (n - 1 - position) + 1)


def ring_position(index, n):
    odd = index % 2
    return (1 - odd) * (index // 2) + odd * (n - 1 - index // 2)


def ring_sum_kernel(n, x_ref, r_ref, o_ref, low, slots, rs_send, rs_recv, credit, done, ag_send, ag_recv):
    rows = x_ref.shape[0]
    half = rows // 2
    size = half // n
    me = ring_position(lax.axis_index("seq"), n)
    right = ring_place((me + 1) % n, n)
    left = ring_place((me + n - 1) % n, n)
    rings = ((0, me, right, left), (1, (n - me) % n, left, right))

    barrier = pltpu.get_barrier_semaphore()
    for neighbour in (left, right):
        pl.semaphore_signal(barrier, 1, device_id={"seq": neighbour}, device_id_type=MESH)
    pl.semaphore_wait(barrier, 2)
    o_ref[...] = x_ref[...]
    low[...] = x_ref[...].astype(low.dtype)

    def block(ring, k):
        return pl.ds(pl.multiple_of(ring * half + k * size, 8), size)

    def scatter_copy(ring, place, target, s):
        return pltpu.make_async_remote_copy(
            src_ref=low.at[block(ring, (place - s + n) % n)],
            dst_ref=slots.at[ring, s % 2],
            send_sem=rs_send.at[ring, s % 2],
            recv_sem=rs_recv.at[ring, s % 2],
            device_id={"seq": target},
            device_id_type=MESH,
        )

    def scatter_step(s, carry):
        copies = []
        for ring, place, target, source in rings:

            @pl.when(s >= 2)
            def _():
                pl.semaphore_wait(credit.at[ring], 1)

            copy = scatter_copy(ring, place, target, s)
            copy.start()
            copies.append(copy)
        for (ring, place, target, source), copy in zip(rings, copies):
            copy.wait_recv()
            into = block(ring, (place - s - 1 + 2 * n) % n)
            total = o_ref[into] + slots[ring, s % 2].astype(jnp.float32)
            o_ref[into] = total
            low[into] = total.astype(low.dtype)
            copy.wait_send()

            @pl.when(s <= n - 4)
            def _():
                pl.semaphore_signal(credit.at[ring], 1, device_id={"seq": source}, device_id_type=MESH)

        return carry

    lax.fori_loop(0, n - 1, scatter_step, 0)
    for ring, place, target, source in rings:
        pl.semaphore_signal(done.at[ring], 1, device_id={"seq": source}, device_id_type=MESH)
    for ring, place, target, source in rings:
        final = block(ring, (place + 1) % n)
        r_ref[final] = o_ref[final].astype(r_ref.dtype)
    for ring, place, target, source in rings:
        pl.semaphore_wait(done.at[ring], 1)

    def gather_copy(ring, place, target, s):
        where = block(ring, (place + 1 - s + n) % n)
        return pltpu.make_async_remote_copy(
            src_ref=r_ref.at[where],
            dst_ref=r_ref.at[where],
            send_sem=ag_send.at[ring, s],
            recv_sem=ag_recv.at[ring, s],
            device_id={"seq": target},
            device_id_type=MESH,
        )

    def gather_step(s, carry):
        for ring, place, target, source in rings:

            @pl.when(s >= 1)
            def _():
                gather_copy(ring, place, target, s - 1).wait_recv()

            gather_copy(ring, place, target, s).start()

            @pl.when(s >= 1)
            def _():
                gather_copy(ring, place, target, s - 1).wait_send()

        return carry

    lax.fori_loop(0, n - 1, gather_step, 0)
    for ring, place, target, source in rings:
        last = gather_copy(ring, place, target, n - 2)
        last.wait_recv()
        last.wait_send()


def ring_sum(x, n):
    rows, lanes = x.shape
    size = rows // (2 * n)
    return pl.pallas_call(
        lambda *refs: ring_sum_kernel(n, *refs),
        out_shape=jax.ShapeDtypeStruct((rows, lanes), jnp.bfloat16),
        in_specs=[pl.BlockSpec(memory_space=pltpu.VMEM)],
        out_specs=pl.BlockSpec(memory_space=pltpu.VMEM),
        scratch_shapes=[
            pltpu.VMEM((rows, lanes), jnp.float32),
            pltpu.VMEM((rows, lanes), jnp.bfloat16),
            pltpu.VMEM((2, 2, size, lanes), jnp.bfloat16),
            pltpu.SemaphoreType.DMA((2, 2)),
            pltpu.SemaphoreType.DMA((2, 2)),
            pltpu.SemaphoreType.REGULAR((2,)),
            pltpu.SemaphoreType.REGULAR((2,)),
            pltpu.SemaphoreType.DMA((2, n - 1)),
            pltpu.SemaphoreType.DMA((2, n - 1)),
        ],
        compiler_params=pltpu.CompilerParams(collective_id=0, has_side_effects=True),
    )(x)


def sum_over_seq(parts):
    n = lax.axis_size("seq")
    flat = jnp.concatenate([part.reshape(-1) for part in parts])
    grain = 2 * n * 16 * 128
    padded = -(-flat.size // grain) * grain
    flat = jnp.pad(flat, (0, padded - flat.size)).reshape(padded // 128, 128)
    total = ring_sum(flat, n).reshape(-1)
    pieces = []
    start = 0
    for part in parts:
        pieces.append(total[start : start + part.size].reshape(part.shape).astype(jnp.float32))
        start += part.size
    return pieces


def adjoint_kernel(starts_ref, lengths_ref, pow_ref, coef_ref, masks_ref, g_ref, states_ref, drive_ref, dg_ref, sums_ref, lam):
    count = g_ref.shape[0]
    width = coef_ref.shape[1]
    pad = 8
    f_re = coef_ref[2:3, :]
    f_im = coef_ref[3:4, :]
    zero_rows = jnp.zeros((pad, 4 * width), jnp.float32)
    lam[0:pad, :] = zero_rows
    lam[pad + count : 2 * pad + count, :] = zero_rows

    def load(column):
        def get(t):
            return g_ref[pl.ds(t, 8), pl.ds(column, width)], g_ref[pl.ds(t, 8), pl.ds(column + width, width)]

        return get

    def store(column):
        def put(t, h_re, h_im):
            lam[pl.ds(pad + t, 8), pl.ds(column, width)] = h_re
            lam[pl.ds(pad + t, 8), pl.ds(column + width, width)] = h_im

        return put

    blocked_scan(count, width, pow_ref, starts_ref, lengths_ref, load(2 * width), load(0), store(0), store(2 * width))

    rows = 16

    def part(ref, start, column):
        return ref[pl.ds(start, rows), pl.ds(column, width)]

    def epilogue(k, sums):
        gp_re, gp_im, gf_re, gf_im = sums
        r0 = pl.multiple_of(k * rows, rows)
        live = masks_ref[pl.ds(r0, rows), 0:1]
        keep_prev = masks_ref[pl.ds(r0, rows), 1:2]
        keep_next = masks_ref[pl.ds(r0, rows), 2:3]
        lb_re = part(lam, pad + r0, 0)
        lb_im = part(lam, pad + r0, width)
        la_re = part(lam, pad + r0, 2 * width)
        la_im = part(lam, pad + r0, 3 * width)
        gu_re = la_re + lb_re
        gu_im = la_im + lb_im
        dg_ref[pl.ds(r0, rows), pl.ds(0, width)] = ((f_re * gu_re + f_im * gu_im) * live).astype(dg_ref.dtype)
        dg_ref[pl.ds(r0, rows), pl.ds(width, width)] = ((f_re * gu_im - f_im * gu_re) * live).astype(dg_ref.dtype)
        d_re = part(drive_ref, r0, 0) * live
        d_im = part(drive_ref, r0, width) * live
        gf_re = gf_re + d_re * gu_re + d_im * gu_im
        gf_im = gf_im + d_re * gu_im - d_im * gu_re
        a_re = part(states_ref, r0, 0) * keep_next
        a_im = part(states_ref, r0, width) * keep_next
        b_re = part(states_ref, r0, 2 * width) * keep_prev
        b_im = part(states_ref, r0, 3 * width) * keep_prev
        ahead_rows = lam[pl.ds(pad + r0, rows + 8), pl.ds(2 * width, 2 * width)][1 : rows + 1]
        behind_rows = lam[pl.ds(r0, rows + 8), pl.ds(0, 2 * width)][pad - 1 : pad - 1 + rows]
        na_re = ahead_rows[:, :width]
        na_im = ahead_rows[:, width:]
        pb_re = behind_rows[:, :width]
        pb_im = behind_rows[:, width:]
        gp_re = gp_re + a_re * na_re + a_im * na_im + b_re * pb_re + b_im * pb_im
        gp_im = gp_im + a_re * na_im - a_im * na_re + b_re * pb_im - b_im * pb_re
        return (gp_re, gp_im, gf_re, gf_im)

    block = jnp.zeros((rows, width), jnp.float32)
    sums = lax.fori_loop(0, count // rows, epilogue, (block, block, block, block))
    for k, value in enumerate(sums):
        sums_ref[k : k + 1, :] = jnp.sum(value, 0, keepdims=True)


def adjoint(starts, lengths, powers, coef, masks, states_grad, states, drive):
    count, quad = states_grad.shape
    width = quad // 4
    vmem = pl.BlockSpec(memory_space=pltpu.VMEM)
    smem = pl.BlockSpec(memory_space=pltpu.SMEM)
    return pl.pallas_call(
        adjoint_kernel,
        out_shape=(
            jax.ShapeDtypeStruct((count, 2 * width), jnp.bfloat16),
            jax.ShapeDtypeStruct((4, width), jnp.float32),
        ),
        in_specs=[smem, smem] + [vmem] * 6,
        out_specs=(vmem, vmem),
        scratch_shapes=[pltpu.VMEM((count + 16, 4 * width), jnp.float32)],
        cost_estimate=pl.CostEstimate(
            flops=60 * count * width, transcendentals=0, bytes_accessed=48 * count * width
        ),
    )(starts, lengths, powers, coef, masks, states_grad, states, drive)


def update(weight, gradient, velocity, average, rate, decay):
    adjusted = gradient + decay * weight
    velocity_new = momentum * velocity + adjusted
    change = -rate * (adjusted + momentum * velocity_new)
    weight_new = weight + change
    average_new = smoothing * average + (1.0 - smoothing) * weight_new
    return (weight_new, velocity_new, average_new, change)


def contract_rows(left, right):
    return lax.dot_general(
        left, right, (((0,), (0,)), ((), ())), preferred_element_type=jnp.float32
    )


def contract_cols(left, right):
    return lax.dot_general(
        left, right, (((1,), (1,)), ((), ())), preferred_element_type=jnp.float32
    )


def gather_feat(value, axis):
    return lax.all_gather(value, "feat", axis=axis, tiled=True)


def body(
    activations_in,
    cotangent,
    seq_start,
    seq_length,
    input_matrix,
    output_matrix,
    gate_matrix,
    feature_vectors,
    state_vectors,
    velocity_input,
    velocity_output,
    velocity_gate,
    velocity_feature,
    velocity_state,
    average_input,
    average_output,
    average_gate,
    average_feature,
    average_state,
):
    count = activations_in.shape[0]
    shard = activations_in.shape[1]
    layers = input_matrix.shape[0]
    width = state_vectors.shape[2]
    me = lax.axis_index("feat")
    offset = me * shard

    def mine(value):
        return lax.dynamic_slice_in_dim(value, offset, shard, axis=value.ndim - 1)

    alive, carry_prev, carry_next = masks_of(seq_start, seq_length, count)
    zero = jnp.zeros((1,), jnp.float32)
    after_next = jnp.concatenate([zero, carry_next[:-1]])
    before_prev = jnp.concatenate([carry_prev[1:], zero])
    mask_columns = jnp.stack([alive, carry_prev, carry_next, jnp.zeros_like(alive)], 1)


    in_all = gather_feat(input_matrix.astype(jnp.bfloat16), 1)
    out_all = gather_feat(output_matrix.astype(jnp.bfloat16), 2)
    gate_all = gather_feat(gate_matrix.astype(jnp.bfloat16), 2)
    feature_all = gather_feat(feature_vectors, 2)
    stream = gather_feat(activations_in, 1).astype(jnp.float32)

    saved = []
    for layer in range(layers):
        in_low = in_all[layer]
        out_low = out_all[layer]
        gate_low = gate_all[layer]
        feature_row = feature_all[layer]
        pole_re, pole_im, factor_re, factor_im = coefficients(state_vectors[layer])
        center = jnp.mean(stream, 1, keepdims=True)
        spread = stream - center
        scale = lax.rsqrt(jnp.mean(spread * spread, 1, keepdims=True) + epsilon)
        unit = spread * scale
        normed = unit * feature_row[0] + feature_row[1]
        normed_low = normed.astype(jnp.bfloat16)
        drive = jnp.dot(normed_low, in_low, preferred_element_type=jnp.float32)
        drive_re = drive[:, :width]
        drive_im = drive[:, width:]
        source = jnp.concatenate(
            [
                (drive_re * factor_re - drive_im * factor_im) * alive[:, None],
                (drive_re * factor_im + drive_im * factor_re) * alive[:, None],
            ],
            1,
        )
        states = recurrence(seq_start, seq_length, pole_powers(pole_re, pole_im), source)
        states_low = states.astype(jnp.bfloat16)
        mixed = (
            jnp.dot(states_low, out_low, preferred_element_type=jnp.float32)
            + feature_row[2] * normed
        )
        act = smooth(mixed)
        act_low = act.astype(jnp.bfloat16)
        pre = jnp.dot(act_low, gate_low, preferred_element_type=jnp.float32) + feature_row[3]
        saved.append((scale, unit, normed_low, drive, states, states_low, mixed, act, act_low, pre))
        stream = stream + act * jax.nn.sigmoid(pre)

    grad = gather_feat(cotangent, 1).astype(jnp.float32) * alive[:, None]
    layer_grads = [None] * layers
    for layer in reversed(range(layers)):
        scale, unit, normed_low, drive, states, states_low, mixed, act, act_low, pre = saved[layer]
        in_low = in_all[layer]
        out_low = out_all[layer]
        gate_low = gate_all[layer]
        feature_row = feature_all[layer]
        state_row = state_vectors[layer]
        pole_re, pole_im, factor_re, factor_im = coefficients(state_row)
        gate = jax.nn.sigmoid(pre)
        pre_grad = (grad * act * gate * (1.0 - gate)).astype(jnp.bfloat16)
        gate_grad = contract_rows(act_low, mine(pre_grad))
        gate_bias_grad = jnp.sum(pre_grad.astype(jnp.float32), 0)
        act_grad = grad * gate + contract_cols(pre_grad, gate_low)
        mixed_grad = jax.vjp(smooth, mixed)[1](act_grad)[0]
        normed = unit * feature_row[0] + feature_row[1]
        skip_grad = jnp.sum(mixed_grad * normed, 0)
        mixed_low = mixed_grad.astype(jnp.bfloat16)
        out_grad = contract_rows(states_low, mine(mixed_low))
        states_grad = contract_cols(mixed_low, out_low)
        coef = jnp.stack([pole_re, pole_im, factor_re, factor_im])
        drive_low, sums = adjoint(
            seq_start,
            seq_length,
            pole_powers(pole_re, -pole_im),
            coef,
            mask_columns,
            states_grad,
            states,
            drive,
        )
        gp_re, gp_im, gf_re, gf_im = sums[0], sums[1], sums[2], sums[3]
        row_grad = jax.vjp(coefficients, state_row)[1]((gp_re, gp_im, gf_re, gf_im))[0]
        in_grad = contract_rows(mine(normed_low), drive_low)
        normed_grad = mixed_grad * feature_row[2] + jnp.dot(
            drive_low, in_low.T, preferred_element_type=jnp.float32
        )
        gain_grad = jnp.sum(normed_grad * unit, 0)
        bias_grad = jnp.sum(normed_grad, 0)
        unit_grad = normed_grad * feature_row[0]
        first_mean = jnp.mean(unit_grad, 1, keepdims=True)
        second_mean = jnp.mean(unit_grad * unit, 1, keepdims=True)
        grad = grad + scale * (unit_grad - first_mean - unit * second_mean)
        feature_grad = mine(jnp.stack([gain_grad, bias_grad, skip_grad, gate_bias_grad]))
        layer_grads[layer] = (in_grad, out_grad, gate_grad, feature_grad, row_grad)
    stacked_in = jnp.stack([entry[0] for entry in layer_grads])
    stacked_out = jnp.stack([entry[1] for entry in layer_grads])
    stacked_gate = jnp.stack([entry[2] for entry in layer_grads])
    stacked_feature = jnp.stack([entry[3] for entry in layer_grads])
    stacked_state = jnp.stack([entry[4] for entry in layer_grads])
    summed = sum_over_seq((stacked_in, stacked_out, stacked_gate, stacked_feature, stacked_state))
    factor = 1.0 / math.sqrt(count * lax.axis_size("seq"))
    grad_in = summed[0] * factor
    grad_out = summed[1] * factor
    grad_gate = summed[2] * factor
    grad_feature = summed[3] * factor
    grad_state = summed[4] * factor
    new_in = update(input_matrix, grad_in, velocity_input, average_input, slow_rate, 0.0)
    new_out = update(output_matrix, grad_out, velocity_output, average_output, slow_rate, 0.0)
    new_gate = update(gate_matrix, grad_gate, velocity_gate, average_gate, main_rate, weight_decay)
    new_feature = update(
        feature_vectors, grad_feature, velocity_feature, average_feature, main_rate, weight_decay
    )
    new_state = update(state_vectors, grad_state, velocity_state, average_state, slow_rate, 0.0)
    return (
        mine(stream),
        mine(grad),
        grad_in,
        grad_out,
        grad_gate,
        grad_feature,
        grad_state,
        new_in[0],
        new_out[0],
        new_gate[0],
        new_feature[0],
        new_state[3],
        new_in[1],
        new_out[1],
        new_gate[1],
        new_feature[1],
        new_state[1],
        new_in[2],
        new_out[2],
        new_gate[2],
        new_feature[2],
        new_state[2],
    )


def solution(mesh):
    feat = P(None, None, "feat")
    rows = P(None, "feat", None)
    tokens = P("seq", "feat")
    return jax.shard_map(
        body,
        mesh=mesh,
        in_specs=(
            tokens,
            tokens,
            P("seq"),
            P("seq"),
            rows,
            feat,
            feat,
            feat,
            P(),
            rows,
            feat,
            feat,
            feat,
            P(),
            rows,
            feat,
            feat,
            feat,
            P(),
        ),
        out_specs=(
            tokens,
            tokens,
            rows,
            feat,
            feat,
            feat,
            P(),
            rows,
            feat,
            feat,
            feat,
            P(),
            rows,
            feat,
            feat,
            feat,
            P(),
            rows,
            feat,
            feat,
            feat,
            P(),
        ),
        check_vma=False,
    )
```

```python
import math

import jax
import jax.numpy as jnp
from jax import lax
from jax.experimental import pallas as pl
from jax.experimental.pallas import tpu as pltpu
from jax.sharding import PartitionSpec as P

epsilon = 1e-05
momentum = 0.9
smoothing = 0.5
slow_rate = 0.02
main_rate = 0.05
weight_decay = 0.1


def smooth(value):
    return jax.nn.gelu(value, approximate=False)


def masks_of(starts, lengths, count):
    position = jnp.arange(count, dtype=jnp.int32)[:, None]
    begin = starts[None, :]
    finish = begin + lengths[None, :]
    inside = (position >= begin) & (position < finish)
    alive = jnp.any(inside, 1)
    opening = jnp.any(inside & (position == begin), 1)
    closing = jnp.any(inside & (position == finish - 1), 1)
    return (
        alive.astype(jnp.float32),
        (alive & ~opening).astype(jnp.float32),
        (alive & ~closing).astype(jnp.float32),
    )


def coefficients(state_row):
    rate = -jnp.exp(state_row[0])
    frequency = state_row[1]
    timestep = jnp.exp(state_row[2])
    decay = jnp.exp(rate * timestep)
    angle = frequency * timestep
    pole_real = decay * jnp.cos(angle)
    pole_imag = decay * jnp.sin(angle)
    denom = rate * rate + frequency * frequency
    factor_real = ((pole_real - 1.0) * rate + pole_imag * frequency) / denom
    factor_imag = (pole_imag * rate - (pole_real - 1.0) * frequency) / denom
    return (pole_real, pole_imag, factor_real, factor_imag)


def tile_scan(x_re, x_im, keep, powers, down):
    reps = x_re.shape[1] // keep.shape[1]
    rows = lax.broadcasted_iota(jnp.int32, keep.shape, 0)
    b_re, b_im = x_re, x_im
    for level, k in enumerate((1, 2, 4)):
        shift = 8 - k if down else k
        valid = rows <= 7 - k if down else rows >= k
        gate = jnp.tile(jnp.where(valid, keep, 0.0), (1, reps))
        p_re = pltpu.roll(b_re, shift, 0)
        p_im = pltpu.roll(b_im, shift, 0)
        w_re = powers[0][(0, 1, 3)[level] : (0, 1, 3)[level] + 1]
        w_im = powers[1][(0, 1, 3)[level] : (0, 1, 3)[level] + 1]
        b_re = b_re + gate * (w_re * p_re - w_im * p_im)
        b_im = b_im + gate * (w_re * p_im + w_im * p_re)
        keep = keep * jnp.where(valid, pltpu.roll(keep, shift, 0), 1.0)
    return b_re, b_im, jnp.tile(keep, (1, reps))


def blocked_scan(count, width, pow_ref, starts_ref, lengths_ref, load_up, load_down, store_up, store_down):
    tiles = count // 8
    slots = starts_ref.shape[0]

    def keeps(t0, downward):
        rows = lax.broadcasted_iota(jnp.int32, (8, 128), 0) + t0
        inside = jnp.zeros((8, 128), jnp.bool_)
        for slot in range(slots):
            begin = starts_ref[slot]
            finish = begin + lengths_ref[slot]
            if downward:
                inside = inside | ((rows >= begin) & (rows < finish - 1))
            else:
                inside = inside | ((rows > begin) & (rows < finish))
        return inside.astype(jnp.float32)

    up_powers = (pow_ref[0], pow_ref[1])
    down_powers = (pow_ref[2], pow_ref[3])

    def carry_in(b_re, b_im, reach, powers, h_re, h_im):
        q_re = powers[0] * h_re - powers[1] * h_im
        q_im = powers[0] * h_im + powers[1] * h_re
        return b_re + reach * q_re, b_im + reach * q_im

    def step(i, carry):
        u_re, u_im, d_re, d_im = carry
        tu = pl.multiple_of(i * 8, 8)
        td = pl.multiple_of((tiles - 1 - i) * 8, 8)
        xu_re, xu_im = load_up(tu)
        xd_re, xd_im = load_down(td)
        bu_re, bu_im, ru = tile_scan(xu_re, xu_im, keeps(tu, False), up_powers, False)
        bd_re, bd_im, rd = tile_scan(xd_re, xd_im, keeps(td, True), up_powers, True)
        hu_re, hu_im = carry_in(bu_re, bu_im, ru, up_powers, u_re, u_im)
        hd_re, hd_im = carry_in(bd_re, bd_im, rd, down_powers, d_re, d_im)
        store_up(tu, hu_re, hu_im)
        store_down(td, hd_re, hd_im)
        return (hu_re[7:8], hu_im[7:8], hd_re[0:1], hd_im[0:1])

    zeros = jnp.zeros((1, width), jnp.float32)
    lax.fori_loop(0, tiles, step, (zeros, zeros, zeros, zeros), unroll=2)


def pole_powers(p_re, p_im):
    rows_re = [p_re]
    rows_im = [p_im]
    for _ in range(7):
        a, b = rows_re[-1], rows_im[-1]
        rows_re.append(a * p_re - b * p_im)
        rows_im.append(a * p_im + b * p_re)
    up_re = jnp.stack(rows_re)
    up_im = jnp.stack(rows_im)
    return jnp.stack([up_re, up_im, up_re[::-1], up_im[::-1]])


def recurrence_kernel(starts_ref, lengths_ref, pow_ref, x_ref, out_ref):
    count = x_ref.shape[0]
    width = pow_ref.shape[2]

    def load(t):
        return x_ref[pl.ds(t, 8), pl.ds(0, width)], x_ref[pl.ds(t, 8), pl.ds(width, width)]

    def store(column):
        def put(t, h_re, h_im):
            out_ref[pl.ds(t, 8), pl.ds(column, width)] = h_re
            out_ref[pl.ds(t, 8), pl.ds(column + width, width)] = h_im

        return put

    blocked_scan(count, width, pow_ref, starts_ref, lengths_ref, load, load, store(0), store(2 * width))


def recurrence(starts, lengths, powers, x):
    count, double = x.shape
    vmem = pl.BlockSpec(memory_space=pltpu.VMEM)
    smem = pl.BlockSpec(memory_space=pltpu.SMEM)
    return pl.pallas_call(
        recurrence_kernel,
        out_shape=jax.ShapeDtypeStruct((count, 2 * double), jnp.float32),
        in_specs=[smem, smem, vmem, vmem],
        out_specs=vmem,
        cost_estimate=pl.CostEstimate(
            flops=20 * count * double, transcendentals=0, bytes_accessed=16 * count * double
        ),
    )(starts, lengths, powers, x)


MESH = pl.DeviceIdType.MESH


def ring_place(position, n):
    upper = position // (n // 2)
    return (1 - upper) * (2 * position) + upper * (2 * (n - 1 - position) + 1)


def ring_position(index, n):
    odd = index % 2
    return (1 - odd) * (index // 2) + odd * (n - 1 - index // 2)


def ring_sum_kernel(n, x_ref, r_ref, o_ref, low, slots, rs_send, rs_recv, credit, done, ag_send, ag_recv):
    rows = x_ref.shape[0]
    half = rows // 2
    size = half // n
    me = ring_position(lax.axis_index("seq"), n)
    right = ring_place((me + 1) % n, n)
    left = ring_place((me + n - 1) % n, n)
    rings = ((0, me, right, left), (1, (n - me) % n, left, right))

    barrier = pltpu.get_barrier_semaphore()
    for neighbour in (left, right):
        pl.semaphore_signal(barrier, 1, device_id={"seq": neighbour}, device_id_type=MESH)
    pl.semaphore_wait(barrier, 2)
    o_ref[...] = x_ref[...]
    low[...] = x_ref[...].astype(low.dtype)

    def block(ring, k):
        return pl.ds(pl.multiple_of(ring * half + k * size, 8), size)

    def scatter_copy(ring, place, target, s):
        return pltpu.make_async_remote_copy(
            src_ref=low.at[block(ring, (place - s + n) % n)],
            dst_ref=slots.at[ring, s % 2],
            send_sem=rs_send.at[ring, s % 2],
            recv_sem=rs_recv.at[ring, s % 2],
            device_id={"seq": target},
            device_id_type=MESH,
        )

    def scatter_step(s, carry):
        copies = []
        for ring, place, target, source in rings:

            @pl.when(s >= 2)
            def _():
                pl.semaphore_wait(credit.at[ring], 1)

            copy = scatter_copy(ring, place, target, s)
            copy.start()
            copies.append(copy)
        for (ring, place, target, source), copy in zip(rings, copies):
            copy.wait_recv()
            into = block(ring, (place - s - 1 + 2 * n) % n)
            total = o_ref[into] + slots[ring, s % 2].astype(jnp.float32)
            o_ref[into] = total
            low[into] = total.astype(low.dtype)
            copy.wait_send()

            @pl.when(s <= n - 4)
            def _():
                pl.semaphore_signal(credit.at[ring], 1, device_id={"seq": source}, device_id_type=MESH)

        return carry

    lax.fori_loop(0, n - 1, scatter_step, 0)
    for ring, place, target, source in rings:
        pl.semaphore_signal(done.at[ring], 1, device_id={"seq": source}, device_id_type=MESH)
    for ring, place, target, source in rings:
        final = block(ring, (place + 1) % n)
        r_ref[final] = o_ref[final].astype(r_ref.dtype)
    for ring, place, target, source in rings:
        pl.semaphore_wait(done.at[ring], 1)

    def gather_copy(ring, place, target, s):
        where = block(ring, (place + 1 - s + n) % n)
        return pltpu.make_async_remote_copy(
            src_ref=r_ref.at[where],
            dst_ref=r_ref.at[where],
            send_sem=ag_send.at[ring, s],
            recv_sem=ag_recv.at[ring, s],
            device_id={"seq": target},
            device_id_type=MESH,
        )

    def gather_step(s, carry):
        for ring, place, target, source in rings:

            @pl.when(s >= 1)
            def _():
                gather_copy(ring, place, target, s - 1).wait_recv()

            gather_copy(ring, place, target, s).start()

            @pl.when(s >= 1)
            def _():
                gather_copy(ring, place, target, s - 1).wait_send()

        return carry

    lax.fori_loop(0, n - 1, gather_step, 0)
    for ring, place, target, source in rings:
        last = gather_copy(ring, place, target, n - 2)
        last.wait_recv()
        last.wait_send()


def ring_sum(x, n):
    rows, lanes = x.shape
    size = rows // (2 * n)
    return pl.pallas_call(
        lambda *refs: ring_sum_kernel(n, *refs),
        out_shape=jax.ShapeDtypeStruct((rows, lanes), jnp.bfloat16),
        in_specs=[pl.BlockSpec(memory_space=pltpu.VMEM)],
        out_specs=pl.BlockSpec(memory_space=pltpu.VMEM),
        scratch_shapes=[
            pltpu.VMEM((rows, lanes), jnp.float32),
            pltpu.VMEM((rows, lanes), jnp.bfloat16),
            pltpu.VMEM((2, 2, size, lanes), jnp.bfloat16),
            pltpu.SemaphoreType.DMA((2, 2)),
            pltpu.SemaphoreType.DMA((2, 2)),
            pltpu.SemaphoreType.REGULAR((2,)),
            pltpu.SemaphoreType.REGULAR((2,)),
            pltpu.SemaphoreType.DMA((2, n - 1)),
            pltpu.SemaphoreType.DMA((2, n - 1)),
        ],
        compiler_params=pltpu.CompilerParams(collective_id=0, has_side_effects=True),
    )(x)


def sum_over_seq(parts):
    n = lax.axis_size("seq")
    flat = jnp.concatenate([part.reshape(-1) for part in parts])
    grain = 2 * n * 16 * 128
    padded = -(-flat.size // grain) * grain
    flat = jnp.pad(flat, (0, padded - flat.size)).reshape(padded // 128, 128)
    total = ring_sum(flat, n).astype(jnp.float32).reshape(-1)
    pieces = []
    start = 0
    for part in parts:
        pieces.append(total[start : start + part.size].reshape(part.shape))
        start += part.size
    return pieces


def adjoint_kernel(starts_ref, lengths_ref, pow_ref, coef_ref, masks_ref, g_ref, states_ref, drive_ref, dg_ref, sums_ref, lam):
    count = g_ref.shape[0]
    width = coef_ref.shape[1]
    pad = 8
    f_re = coef_ref[2:3, :]
    f_im = coef_ref[3:4, :]
    zero_rows = jnp.zeros((pad, 4 * width), jnp.float32)
    lam[0:pad, :] = zero_rows
    lam[pad + count : 2 * pad + count, :] = zero_rows

    def load(column):
        def get(t):
            return g_ref[pl.ds(t, 8), pl.ds(column, width)], g_ref[pl.ds(t, 8), pl.ds(column + width, width)]

        return get

    def store(column):
        def put(t, h_re, h_im):
            lam[pl.ds(pad + t, 8), pl.ds(column, width)] = h_re
            lam[pl.ds(pad + t, 8), pl.ds(column + width, width)] = h_im

        return put

    blocked_scan(count, width, pow_ref, starts_ref, lengths_ref, load(2 * width), load(0), store(0), store(2 * width))

    rows = 16

    def part(ref, start, column):
        return ref[pl.ds(start, rows), pl.ds(column, width)]

    def epilogue(k, sums):
        gp_re, gp_im, gf_re, gf_im = sums
        r0 = pl.multiple_of(k * rows, rows)
        live = masks_ref[pl.ds(r0, rows), 0:1]
        keep_prev = masks_ref[pl.ds(r0, rows), 1:2]
        keep_next = masks_ref[pl.ds(r0, rows), 2:3]
        lb_re = part(lam, pad + r0, 0)
        lb_im = part(lam, pad + r0, width)
        la_re = part(lam, pad + r0, 2 * width)
        la_im = part(lam, pad + r0, 3 * width)
        gu_re = la_re + lb_re
        gu_im = la_im + lb_im
        dg_ref[pl.ds(r0, rows), pl.ds(0, width)] = ((f_re * gu_re + f_im * gu_im) * live).astype(dg_ref.dtype)
        dg_ref[pl.ds(r0, rows), pl.ds(width, width)] = ((f_re * gu_im - f_im * gu_re) * live).astype(dg_ref.dtype)
        d_re = part(drive_ref, r0, 0) * live
        d_im = part(drive_ref, r0, width) * live
        gf_re = gf_re + d_re * gu_re + d_im * gu_im
        gf_im = gf_im + d_re * gu_im - d_im * gu_re
        a_re = part(states_ref, r0, 0) * keep_next
        a_im = part(states_ref, r0, width) * keep_next
        b_re = part(states_ref, r0, 2 * width) * keep_prev
        b_im = part(states_ref, r0, 3 * width) * keep_prev
        ahead_rows = lam[pl.ds(pad + r0, rows + 8), pl.ds(2 * width, 2 * width)][1 : rows + 1]
        behind_rows = lam[pl.ds(r0, rows + 8), pl.ds(0, 2 * width)][pad - 1 : pad - 1 + rows]
        na_re = ahead_rows[:, :width]
        na_im = ahead_rows[:, width:]
        pb_re = behind_rows[:, :width]
        pb_im = behind_rows[:, width:]
        gp_re = gp_re + a_re * na_re + a_im * na_im + b_re * pb_re + b_im * pb_im
        gp_im = gp_im + a_re * na_im - a_im * na_re + b_re * pb_im - b_im * pb_re
        return (gp_re, gp_im, gf_re, gf_im)

    block = jnp.zeros((rows, width), jnp.float32)
    sums = lax.fori_loop(0, count // rows, epilogue, (block, block, block, block))
    for k, value in enumerate(sums):
        sums_ref[k : k + 1, :] = jnp.sum(value, 0, keepdims=True)


def adjoint(starts, lengths, powers, coef, masks, states_grad, states, drive):
    count, quad = states_grad.shape
    width = quad // 4
    vmem = pl.BlockSpec(memory_space=pltpu.VMEM)
    smem = pl.BlockSpec(memory_space=pltpu.SMEM)
    return pl.pallas_call(
        adjoint_kernel,
        out_shape=(
            jax.ShapeDtypeStruct((count, 2 * width), jnp.bfloat16),
            jax.ShapeDtypeStruct((4, width), jnp.float32),
        ),
        in_specs=[smem, smem] + [vmem] * 6,
        out_specs=(vmem, vmem),
        scratch_shapes=[pltpu.VMEM((count + 16, 4 * width), jnp.float32)],
        cost_estimate=pl.CostEstimate(
            flops=60 * count * width, transcendentals=0, bytes_accessed=48 * count * width
        ),
    )(starts, lengths, powers, coef, masks, states_grad, states, drive)


def update(weight, gradient, velocity, average, rate, decay):
    adjusted = gradient + decay * weight
    velocity_new = momentum * velocity + adjusted
    change = -rate * (adjusted + momentum * velocity_new)
    weight_new = weight + change
    average_new = smoothing * average + (1.0 - smoothing) * weight_new
    return (weight_new, velocity_new, average_new, change)


def contract_rows(left, right):
    return lax.dot_general(
        left, right, (((0,), (0,)), ((), ())), preferred_element_type=jnp.float32
    )


def contract_cols(left, right):
    return lax.dot_general(
        left, right, (((1,), (1,)), ((), ())), preferred_element_type=jnp.float32
    )


def gather_feat(value, axis):
    return lax.all_gather(value, "feat", axis=axis, tiled=True)


def body(
    activations_in,
    cotangent,
    seq_start,
    seq_length,
    input_matrix,
    output_matrix,
    gate_matrix,
    feature_vectors,
    state_vectors,
    velocity_input,
    velocity_output,
    velocity_gate,
    velocity_feature,
    velocity_state,
    average_input,
    average_output,
    average_gate,
    average_feature,
    average_state,
):
    count = activations_in.shape[0]
    shard = activations_in.shape[1]
    layers = input_matrix.shape[0]
    width = state_vectors.shape[2]
    me = lax.axis_index("feat")
    offset = me * shard

    def mine(value):
        return lax.dynamic_slice_in_dim(value, offset, shard, axis=value.ndim - 1)

    alive, carry_prev, carry_next = masks_of(seq_start, seq_length, count)
    zero = jnp.zeros((1,), jnp.float32)
    after_next = jnp.concatenate([zero, carry_next[:-1]])
    before_prev = jnp.concatenate([carry_prev[1:], zero])
    mask_columns = jnp.stack([alive, carry_prev, carry_next, jnp.zeros_like(alive)], 1)


    in_all = gather_feat(input_matrix.astype(jnp.bfloat16), 1)
    out_all = [gather_feat(output_matrix[k].astype(jnp.bfloat16), 1) for k in range(layers)]
    gate_all = gather_feat(gate_matrix.astype(jnp.bfloat16), 2)
    feature_all = gather_feat(feature_vectors, 2)
    stream = gather_feat(activations_in, 1).astype(jnp.float32)

    saved = []
    for layer in range(layers):
        in_low = in_all[layer]
        out_low = out_all[layer]
        gate_low = gate_all[layer]
        feature_row = feature_all[layer]
        pole_re, pole_im, factor_re, factor_im = coefficients(state_vectors[layer])
        center = jnp.mean(stream, 1, keepdims=True)
        spread = stream - center
        scale = lax.rsqrt(jnp.mean(spread * spread, 1, keepdims=True) + epsilon)
        unit = spread * scale
        normed = unit * feature_row[0] + feature_row[1]
        normed_low = normed.astype(jnp.bfloat16)
        drive = jnp.dot(normed_low, in_low, preferred_element_type=jnp.float32)
        drive_re = drive[:, :width]
        drive_im = drive[:, width:]
        source = jnp.concatenate(
            [
                (drive_re * factor_re - drive_im * factor_im) * alive[:, None],
                (drive_re * factor_im + drive_im * factor_re) * alive[:, None],
            ],
            1,
        )
        states = recurrence(seq_start, seq_length, pole_powers(pole_re, pole_im), source)
        states_low = states.astype(jnp.bfloat16)
        mixed = (
            jnp.dot(states_low, out_low, preferred_element_type=jnp.float32)
            + feature_row[2] * normed
        )
        act = smooth(mixed)
        act_low = act.astype(jnp.bfloat16)
        pre = jnp.dot(act_low, gate_low, preferred_element_type=jnp.float32) + feature_row[3]
        saved.append((scale, unit, normed_low, drive, states, states_low, mixed, act, act_low, pre))
        stream = stream + act * jax.nn.sigmoid(pre)

    grad = gather_feat(cotangent, 1).astype(jnp.float32) * alive[:, None]
    layer_grads = [None] * layers
    for layer in reversed(range(layers)):
        scale, unit, normed_low, drive, states, states_low, mixed, act, act_low, pre = saved[layer]
        in_low = in_all[layer]
        out_low = out_all[layer]
        gate_low = gate_all[layer]
        feature_row = feature_all[layer]
        state_row = state_vectors[layer]
        pole_re, pole_im, factor_re, factor_im = coefficients(state_row)
        gate = jax.nn.sigmoid(pre)
        pre_grad = (grad * act * gate * (1.0 - gate)).astype(jnp.bfloat16)
        gate_grad = contract_rows(act_low, mine(pre_grad))
        gate_bias_grad = jnp.sum(pre_grad.astype(jnp.float32), 0)
        act_grad = grad * gate + contract_cols(pre_grad, gate_low)
        mixed_grad = jax.vjp(smooth, mixed)[1](act_grad)[0]
        normed = unit * feature_row[0] + feature_row[1]
        skip_grad = jnp.sum(mixed_grad * normed, 0)
        mixed_low = mixed_grad.astype(jnp.bfloat16)
        out_grad = contract_rows(states_low, mine(mixed_low))
        states_grad = contract_cols(mixed_low, out_low)
        coef = jnp.stack([pole_re, pole_im, factor_re, factor_im])
        drive_low, sums = adjoint(
            seq_start,
            seq_length,
            pole_powers(pole_re, -pole_im),
            coef,
            mask_columns,
            states_grad,
            states,
            drive,
        )
        gp_re, gp_im, gf_re, gf_im = sums[0], sums[1], sums[2], sums[3]
        row_grad = jax.vjp(coefficients, state_row)[1]((gp_re, gp_im, gf_re, gf_im))[0]
        in_grad = contract_rows(mine(normed_low), drive_low)
        normed_grad = mixed_grad * feature_row[2] + jnp.dot(
            drive_low, in_low.T, preferred_element_type=jnp.float32
        )
        gain_grad = jnp.sum(normed_grad * unit, 0)
        bias_grad = jnp.sum(normed_grad, 0)
        unit_grad = normed_grad * feature_row[0]
        first_mean = jnp.mean(unit_grad, 1, keepdims=True)
        second_mean = jnp.mean(unit_grad * unit, 1, keepdims=True)
        grad = grad + scale * (unit_grad - first_mean - unit * second_mean)
        feature_grad = mine(jnp.stack([gain_grad, bias_grad, skip_grad, gate_bias_grad]))
        layer_grads[layer] = (in_grad, out_grad, gate_grad, feature_grad, row_grad)
    stacked_in = jnp.stack([entry[0] for entry in layer_grads])
    stacked_out = jnp.stack([entry[1] for entry in layer_grads])
    stacked_gate = jnp.stack([entry[2] for entry in layer_grads])
    stacked_feature = jnp.stack([entry[3] for entry in layer_grads])
    stacked_state = jnp.stack([entry[4] for entry in layer_grads])
    summed = sum_over_seq((stacked_in, stacked_out, stacked_gate, stacked_feature, stacked_state))
    factor = 1.0 / math.sqrt(count * lax.axis_size("seq"))
    grad_in = summed[0] * factor
    grad_out = summed[1] * factor
    grad_gate = summed[2] * factor
    grad_feature = summed[3] * factor
    grad_state = summed[4] * factor
    new_in = update(input_matrix, grad_in, velocity_input, average_input, slow_rate, 0.0)
    new_out = update(output_matrix, grad_out, velocity_output, average_output, slow_rate, 0.0)
    new_gate = update(gate_matrix, grad_gate, velocity_gate, average_gate, main_rate, weight_decay)
    new_feature = update(
        feature_vectors, grad_feature, velocity_feature, average_feature, main_rate, weight_decay
    )
    new_state = update(state_vectors, grad_state, velocity_state, average_state, slow_rate, 0.0)
    return (
        mine(stream),
        mine(grad),
        grad_in,
        grad_out,
        grad_gate,
        grad_feature,
        grad_state,
        new_in[0],
        new_out[0],
        new_gate[0],
        new_feature[0],
        new_state[3],
        new_in[1],
        new_out[1],
        new_gate[1],
        new_feature[1],
        new_state[1],
        new_in[2],
        new_out[2],
        new_gate[2],
        new_feature[2],
        new_state[2],
    )


def solution(mesh):
    feat = P(None, None, "feat")
    rows = P(None, "feat", None)
    tokens = P("seq", "feat")
    return jax.shard_map(
        body,
        mesh=mesh,
        in_specs=(
            tokens,
            tokens,
            P("seq"),
            P("seq"),
            rows,
            feat,
            feat,
            feat,
            P(),
            rows,
            feat,
            feat,
            feat,
            P(),
            rows,
            feat,
            feat,
            feat,
            P(),
        ),
        out_specs=(
            tokens,
            tokens,
            rows,
            feat,
            feat,
            feat,
            P(),
            rows,
            feat,
            feat,
            feat,
            P(),
            rows,
            feat,
            feat,
            feat,
            P(),
            rows,
            feat,
            feat,
            feat,
            P(),
        ),
        check_vma=False,
    )
```

```python
import math

import jax
import jax.numpy as jnp
from jax import lax
from jax.experimental import pallas as pl
from jax.experimental.pallas import tpu as pltpu
from jax.sharding import PartitionSpec as P

epsilon = 1e-05
momentum = 0.9
smoothing = 0.5
slow_rate = 0.02
main_rate = 0.05
weight_decay = 0.1


def smooth(value):
    return jax.nn.gelu(value, approximate=False)


def masks_of(starts, lengths, count):
    position = jnp.arange(count, dtype=jnp.int32)[:, None]
    begin = starts[None, :]
    finish = begin + lengths[None, :]
    inside = (position >= begin) & (position < finish)
    alive = jnp.any(inside, 1)
    opening = jnp.any(inside & (position == begin), 1)
    closing = jnp.any(inside & (position == finish - 1), 1)
    return (
        alive.astype(jnp.float32),
        (alive & ~opening).astype(jnp.float32),
        (alive & ~closing).astype(jnp.float32),
    )


def coefficients(state_row):
    rate = -jnp.exp(state_row[0])
    frequency = state_row[1]
    timestep = jnp.exp(state_row[2])
    decay = jnp.exp(rate * timestep)
    angle = frequency * timestep
    pole_real = decay * jnp.cos(angle)
    pole_imag = decay * jnp.sin(angle)
    denom = rate * rate + frequency * frequency
    factor_real = ((pole_real - 1.0) * rate + pole_imag * frequency) / denom
    factor_imag = (pole_imag * rate - (pole_real - 1.0) * frequency) / denom
    return (pole_real, pole_imag, factor_real, factor_imag)


def tile_scan(x_re, x_im, keep, powers, down):
    reps = x_re.shape[1] // keep.shape[1]
    rows = lax.broadcasted_iota(jnp.int32, keep.shape, 0)
    b_re, b_im = x_re, x_im
    for level, k in enumerate((1, 2, 4)):
        shift = 8 - k if down else k
        valid = rows <= 7 - k if down else rows >= k
        gate = jnp.tile(jnp.where(valid, keep, 0.0), (1, reps))
        p_re = pltpu.roll(b_re, shift, 0)
        p_im = pltpu.roll(b_im, shift, 0)
        w_re = powers[0][(0, 1, 3)[level] : (0, 1, 3)[level] + 1]
        w_im = powers[1][(0, 1, 3)[level] : (0, 1, 3)[level] + 1]
        b_re = b_re + gate * (w_re * p_re - w_im * p_im)
        b_im = b_im + gate * (w_re * p_im + w_im * p_re)
        keep = keep * jnp.where(valid, pltpu.roll(keep, shift, 0), 1.0)
    return b_re, b_im, jnp.tile(keep, (1, reps))


def blocked_scan(count, width, pow_ref, starts_ref, lengths_ref, load_up, load_down, store_up, store_down):
    tiles = count // 8
    slots = starts_ref.shape[0]

    def keeps(t0, downward):
        rows = lax.broadcasted_iota(jnp.int32, (8, 128), 0) + t0
        inside = jnp.zeros((8, 128), jnp.bool_)
        for slot in range(slots):
            begin = starts_ref[slot]
            finish = begin + lengths_ref[slot]
            if downward:
                inside = inside | ((rows >= begin) & (rows < finish - 1))
            else:
                inside = inside | ((rows > begin) & (rows < finish))
        return inside.astype(jnp.float32)

    up_powers = (pow_ref[0], pow_ref[1])
    down_powers = (pow_ref[2], pow_ref[3])

    def carry_in(b_re, b_im, reach, powers, h_re, h_im):
        q_re = powers[0] * h_re - powers[1] * h_im
        q_im = powers[0] * h_im + powers[1] * h_re
        return b_re + reach * q_re, b_im + reach * q_im

    def step(i, carry):
        u_re, u_im, d_re, d_im = carry
        tu = pl.multiple_of(i * 8, 8)
        td = pl.multiple_of((tiles - 1 - i) * 8, 8)
        xu_re, xu_im = load_up(tu)
        xd_re, xd_im = load_down(td)
        bu_re, bu_im, ru = tile_scan(xu_re, xu_im, keeps(tu, False), up_powers, False)
        bd_re, bd_im, rd = tile_scan(xd_re, xd_im, keeps(td, True), up_powers, True)
        hu_re, hu_im = carry_in(bu_re, bu_im, ru, up_powers, u_re, u_im)
        hd_re, hd_im = carry_in(bd_re, bd_im, rd, down_powers, d_re, d_im)
        store_up(tu, hu_re, hu_im)
        store_down(td, hd_re, hd_im)
        return (hu_re[7:8], hu_im[7:8], hd_re[0:1], hd_im[0:1])

    zeros = jnp.zeros((1, width), jnp.float32)
    lax.fori_loop(0, tiles, step, (zeros, zeros, zeros, zeros), unroll=2)


def pole_powers(p_re, p_im):
    rows_re = [p_re]
    rows_im = [p_im]
    for _ in range(7):
        a, b = rows_re[-1], rows_im[-1]
        rows_re.append(a * p_re - b * p_im)
        rows_im.append(a * p_im + b * p_re)
    up_re = jnp.stack(rows_re)
    up_im = jnp.stack(rows_im)
    return jnp.stack([up_re, up_im, up_re[::-1], up_im[::-1]])


def recurrence_kernel(starts_ref, lengths_ref, pow_ref, x_ref, out_ref):
    count = x_ref.shape[0]
    width = pow_ref.shape[2]

    def load(t):
        return x_ref[pl.ds(t, 8), pl.ds(0, width)], x_ref[pl.ds(t, 8), pl.ds(width, width)]

    def store(column):
        def put(t, h_re, h_im):
            out_ref[pl.ds(t, 8), pl.ds(column, width)] = h_re
            out_ref[pl.ds(t, 8), pl.ds(column + width, width)] = h_im

        return put

    blocked_scan(count, width, pow_ref, starts_ref, lengths_ref, load, load, store(0), store(2 * width))


def recurrence(starts, lengths, powers, x):
    count, double = x.shape
    vmem = pl.BlockSpec(memory_space=pltpu.VMEM)
    smem = pl.BlockSpec(memory_space=pltpu.SMEM)
    return pl.pallas_call(
        recurrence_kernel,
        out_shape=jax.ShapeDtypeStruct((count, 2 * double), jnp.float32),
        in_specs=[smem, smem, vmem, vmem],
        out_specs=vmem,
        cost_estimate=pl.CostEstimate(
            flops=20 * count * double, transcendentals=0, bytes_accessed=16 * count * double
        ),
    )(starts, lengths, powers, x)


MESH = pl.DeviceIdType.MESH


def ring_place(position, n):
    upper = position // (n // 2)
    return (1 - upper) * (2 * position) + upper * (2 * (n - 1 - position) + 1)


def ring_position(index, n):
    odd = index % 2
    return (1 - odd) * (index // 2) + odd * (n - 1 - index // 2)


def ring_sum_kernel(n, x_ref, r_ref, o_ref, low, slots, rs_send, rs_recv, credit, done, ag_send, ag_recv):
    rows = x_ref.shape[0]
    half = rows // 2
    size = half // n
    me = ring_position(lax.axis_index("seq"), n)
    right = ring_place((me + 1) % n, n)
    left = ring_place((me + n - 1) % n, n)
    rings = ((0, me, right, left), (1, (n - me) % n, left, right))

    barrier = pltpu.get_barrier_semaphore()
    for neighbour in (left, right):
        pl.semaphore_signal(barrier, 1, device_id={"seq": neighbour}, device_id_type=MESH)
    pl.semaphore_wait(barrier, 2)
    o_ref[...] = x_ref[...]
    low[...] = x_ref[...].astype(low.dtype)

    def block(ring, k):
        return pl.ds(pl.multiple_of(ring * half + k * size, 8), size)

    def scatter_copy(ring, place, target, s):
        return pltpu.make_async_remote_copy(
            src_ref=low.at[block(ring, (place - s + n) % n)],
            dst_ref=slots.at[ring, s % 2],
            send_sem=rs_send.at[ring, s % 2],
            recv_sem=rs_recv.at[ring, s % 2],
            device_id={"seq": target},
            device_id_type=MESH,
        )

    def scatter_step(s, carry):
        copies = []
        for ring, place, target, source in rings:

            @pl.when(s >= 2)
            def _():
                pl.semaphore_wait(credit.at[ring], 1)

            copy = scatter_copy(ring, place, target, s)
            copy.start()
            copies.append(copy)
        for (ring, place, target, source), copy in zip(rings, copies):
            copy.wait_recv()
            into = block(ring, (place - s - 1 + 2 * n) % n)
            total = o_ref[into] + slots[ring, s % 2].astype(jnp.float32)
            o_ref[into] = total
            low[into] = total.astype(low.dtype)
            copy.wait_send()

            @pl.when(s <= n - 4)
            def _():
                pl.semaphore_signal(credit.at[ring], 1, device_id={"seq": source}, device_id_type=MESH)

        return carry

    lax.fori_loop(0, n - 1, scatter_step, 0)
    for ring, place, target, source in rings:
        pl.semaphore_signal(done.at[ring], 1, device_id={"seq": source}, device_id_type=MESH)
    for ring, place, target, source in rings:
        final = block(ring, (place + 1) % n)
        r_ref[final] = o_ref[final].astype(r_ref.dtype)
    for ring, place, target, source in rings:
        pl.semaphore_wait(done.at[ring], 1)

    def gather_copy(ring, place, target, s):
        where = block(ring, (place + 1 - s + n) % n)
        return pltpu.make_async_remote_copy(
            src_ref=r_ref.at[where],
            dst_ref=r_ref.at[where],
            send_sem=ag_send.at[ring, s],
            recv_sem=ag_recv.at[ring, s],
            device_id={"seq": target},
            device_id_type=MESH,
        )

    def gather_step(s, carry):
        for ring, place, target, source in rings:

            @pl.when(s >= 1)
            def _():
                gather_copy(ring, place, target, s - 1).wait_recv()

            gather_copy(ring, place, target, s).start()

            @pl.when(s >= 1)
            def _():
                gather_copy(ring, place, target, s - 1).wait_send()

        return carry

    lax.fori_loop(0, n - 1, gather_step, 0)
    for ring, place, target, source in rings:
        last = gather_copy(ring, place, target, n - 2)
        last.wait_recv()
        last.wait_send()


def ring_sum(x, n):
    rows, lanes = x.shape
    size = rows // (2 * n)
    return pl.pallas_call(
        lambda *refs: ring_sum_kernel(n, *refs),
        out_shape=jax.ShapeDtypeStruct((rows, lanes), jnp.bfloat16),
        in_specs=[pl.BlockSpec(memory_space=pltpu.VMEM)],
        out_specs=pl.BlockSpec(memory_space=pltpu.VMEM),
        scratch_shapes=[
            pltpu.VMEM((rows, lanes), jnp.float32),
            pltpu.VMEM((rows, lanes), jnp.bfloat16),
            pltpu.VMEM((2, 2, size, lanes), jnp.bfloat16),
            pltpu.SemaphoreType.DMA((2, 2)),
            pltpu.SemaphoreType.DMA((2, 2)),
            pltpu.SemaphoreType.REGULAR((2,)),
            pltpu.SemaphoreType.REGULAR((2,)),
            pltpu.SemaphoreType.DMA((2, n - 1)),
            pltpu.SemaphoreType.DMA((2, n - 1)),
        ],
        compiler_params=pltpu.CompilerParams(collective_id=0, has_side_effects=True),
    )(x)


def sum_over_seq(parts):
    n = lax.axis_size("seq")
    flat = jnp.concatenate([part.reshape(-1) for part in parts])
    grain = 2 * n * 16 * 128
    padded = -(-flat.size // grain) * grain
    flat = jnp.pad(flat, (0, padded - flat.size)).reshape(padded // 128, 128)
    total = ring_sum(flat, n).astype(jnp.float32).reshape(-1)
    pieces = []
    start = 0
    for part in parts:
        pieces.append(total[start : start + part.size].reshape(part.shape))
        start += part.size
    return pieces


def adjoint_kernel(starts_ref, lengths_ref, pow_ref, coef_ref, masks_ref, g_ref, states_ref, drive_ref, dg_ref, sums_ref, lam):
    count = g_ref.shape[0]
    width = coef_ref.shape[1]
    pad = 8
    f_re = coef_ref[2:3, :]
    f_im = coef_ref[3:4, :]
    zero_rows = jnp.zeros((pad, 4 * width), jnp.float32)
    lam[0:pad, :] = zero_rows
    lam[pad + count : 2 * pad + count, :] = zero_rows

    def load(column):
        def get(t):
            return g_ref[pl.ds(t, 8), pl.ds(column, width)], g_ref[pl.ds(t, 8), pl.ds(column + width, width)]

        return get

    def store(column):
        def put(t, h_re, h_im):
            lam[pl.ds(pad + t, 8), pl.ds(column, width)] = h_re
            lam[pl.ds(pad + t, 8), pl.ds(column + width, width)] = h_im

        return put

    blocked_scan(count, width, pow_ref, starts_ref, lengths_ref, load(2 * width), load(0), store(0), store(2 * width))

    rows = 16

    def part(ref, start, column):
        return ref[pl.ds(start, rows), pl.ds(column, width)]

    def epilogue(k, sums):
        gp_re, gp_im, gf_re, gf_im = sums
        r0 = pl.multiple_of(k * rows, rows)
        live = masks_ref[pl.ds(r0, rows), 0:1]
        keep_prev = masks_ref[pl.ds(r0, rows), 1:2]
        keep_next = masks_ref[pl.ds(r0, rows), 2:3]
        lb_re = part(lam, pad + r0, 0)
        lb_im = part(lam, pad + r0, width)
        la_re = part(lam, pad + r0, 2 * width)
        la_im = part(lam, pad + r0, 3 * width)
        gu_re = la_re + lb_re
        gu_im = la_im + lb_im
        dg_ref[pl.ds(r0, rows), pl.ds(0, width)] = ((f_re * gu_re + f_im * gu_im) * live).astype(dg_ref.dtype)
        dg_ref[pl.ds(r0, rows), pl.ds(width, width)] = ((f_re * gu_im - f_im * gu_re) * live).astype(dg_ref.dtype)
        d_re = part(drive_ref, r0, 0) * live
        d_im = part(drive_ref, r0, width) * live
        gf_re = gf_re + d_re * gu_re + d_im * gu_im
        gf_im = gf_im + d_re * gu_im - d_im * gu_re
        a_re = part(states_ref, r0, 0) * keep_next
        a_im = part(states_ref, r0, width) * keep_next
        b_re = part(states_ref, r0, 2 * width) * keep_prev
        b_im = part(states_ref, r0, 3 * width) * keep_prev
        ahead_rows = lam[pl.ds(pad + r0, rows + 8), pl.ds(2 * width, 2 * width)][1 : rows + 1]
        behind_rows = lam[pl.ds(r0, rows + 8), pl.ds(0, 2 * width)][pad - 1 : pad - 1 + rows]
        na_re = ahead_rows[:, :width]
        na_im = ahead_rows[:, width:]
        pb_re = behind_rows[:, :width]
        pb_im = behind_rows[:, width:]
        gp_re = gp_re + a_re * na_re + a_im * na_im + b_re * pb_re + b_im * pb_im
        gp_im = gp_im + a_re * na_im - a_im * na_re + b_re * pb_im - b_im * pb_re
        return (gp_re, gp_im, gf_re, gf_im)

    block = jnp.zeros((rows, width), jnp.float32)
    sums = lax.fori_loop(0, count // rows, epilogue, (block, block, block, block))
    for k, value in enumerate(sums):
        sums_ref[k : k + 1, :] = jnp.sum(value, 0, keepdims=True)


def adjoint(starts, lengths, powers, coef, masks, states_grad, states, drive):
    count, quad = states_grad.shape
    width = quad // 4
    vmem = pl.BlockSpec(memory_space=pltpu.VMEM)
    smem = pl.BlockSpec(memory_space=pltpu.SMEM)
    return pl.pallas_call(
        adjoint_kernel,
        out_shape=(
            jax.ShapeDtypeStruct((count, 2 * width), jnp.bfloat16),
            jax.ShapeDtypeStruct((4, width), jnp.float32),
        ),
        in_specs=[smem, smem] + [vmem] * 6,
        out_specs=(vmem, vmem),
        scratch_shapes=[pltpu.VMEM((count + 16, 4 * width), jnp.float32)],
        cost_estimate=pl.CostEstimate(
            flops=60 * count * width, transcendentals=0, bytes_accessed=48 * count * width
        ),
    )(starts, lengths, powers, coef, masks, states_grad, states, drive)


def update(weight, gradient, velocity, average, rate, decay):
    adjusted = gradient + decay * weight
    velocity_new = momentum * velocity + adjusted
    change = -rate * (adjusted + momentum * velocity_new)
    weight_new = weight + change
    average_new = smoothing * average + (1.0 - smoothing) * weight_new
    return (weight_new, velocity_new, average_new, change)


def contract_rows(left, right):
    return lax.dot_general(
        left, right, (((0,), (0,)), ((), ())), preferred_element_type=jnp.float32
    )


def contract_cols(left, right):
    return lax.dot_general(
        left, right, (((1,), (1,)), ((), ())), preferred_element_type=jnp.float32
    )


def gather_feat(value, axis):
    return lax.all_gather(value, "feat", axis=axis, tiled=True)


def body(
    activations_in,
    cotangent,
    seq_start,
    seq_length,
    input_matrix,
    output_matrix,
    gate_matrix,
    feature_vectors,
    state_vectors,
    velocity_input,
    velocity_output,
    velocity_gate,
    velocity_feature,
    velocity_state,
    average_input,
    average_output,
    average_gate,
    average_feature,
    average_state,
):
    count = activations_in.shape[0]
    shard = activations_in.shape[1]
    layers = input_matrix.shape[0]
    width = state_vectors.shape[2]
    me = lax.axis_index("feat")
    offset = me * shard

    def mine(value):
        return lax.dynamic_slice_in_dim(value, offset, shard, axis=value.ndim - 1)

    alive, carry_prev, carry_next = masks_of(seq_start, seq_length, count)
    zero = jnp.zeros((1,), jnp.float32)
    after_next = jnp.concatenate([zero, carry_next[:-1]])
    before_prev = jnp.concatenate([carry_prev[1:], zero])
    mask_columns = jnp.stack([alive, carry_prev, carry_next, jnp.zeros_like(alive)], 1)


    in_all = gather_feat(input_matrix.astype(jnp.bfloat16), 1)
    rows_out = output_matrix.shape[1]
    paired = [
        gather_feat(jnp.concatenate([output_matrix[k], gate_matrix[k]], 0).astype(jnp.bfloat16), 1)
        for k in range(layers)
    ]
    out_all = [pair[:rows_out] for pair in paired]
    gate_all = [pair[rows_out:] for pair in paired]
    feature_all = gather_feat(feature_vectors, 2)
    stream = gather_feat(activations_in, 1).astype(jnp.float32)

    saved = []
    for layer in range(layers):
        in_low = in_all[layer]
        out_low = out_all[layer]
        gate_low = gate_all[layer]
        feature_row = feature_all[layer]
        pole_re, pole_im, factor_re, factor_im = coefficients(state_vectors[layer])
        center = jnp.mean(stream, 1, keepdims=True)
        spread = stream - center
        scale = lax.rsqrt(jnp.mean(spread * spread, 1, keepdims=True) + epsilon)
        unit = spread * scale
        normed = unit * feature_row[0] + feature_row[1]
        normed_low = normed.astype(jnp.bfloat16)
        drive = jnp.dot(normed_low, in_low, preferred_element_type=jnp.float32)
        drive_re = drive[:, :width]
        drive_im = drive[:, width:]
        source = jnp.concatenate(
            [
                (drive_re * factor_re - drive_im * factor_im) * alive[:, None],
                (drive_re * factor_im + drive_im * factor_re) * alive[:, None],
            ],
            1,
        )
        states = recurrence(seq_start, seq_length, pole_powers(pole_re, pole_im), source)
        states_low = states.astype(jnp.bfloat16)
        mixed = (
            jnp.dot(states_low, out_low, preferred_element_type=jnp.float32)
            + feature_row[2] * normed
        )
        act = smooth(mixed)
        act_low = act.astype(jnp.bfloat16)
        pre = jnp.dot(act_low, gate_low, preferred_element_type=jnp.float32) + feature_row[3]
        saved.append((scale, unit, normed_low, drive, states, states_low, mixed, act, act_low, pre))
        stream = stream + act * jax.nn.sigmoid(pre)

    grad = gather_feat(cotangent, 1).astype(jnp.float32) * alive[:, None]
    layer_grads = [None] * layers
    for layer in reversed(range(layers)):
        scale, unit, normed_low, drive, states, states_low, mixed, act, act_low, pre = saved[layer]
        in_low = in_all[layer]
        out_low = out_all[layer]
        gate_low = gate_all[layer]
        feature_row = feature_all[layer]
        state_row = state_vectors[layer]
        pole_re, pole_im, factor_re, factor_im = coefficients(state_row)
        gate = jax.nn.sigmoid(pre)
        pre_grad = (grad * act * gate * (1.0 - gate)).astype(jnp.bfloat16)
        gate_grad = contract_rows(act_low, mine(pre_grad))
        gate_bias_grad = jnp.sum(pre_grad.astype(jnp.float32), 0)
        act_grad = grad * gate + contract_cols(pre_grad, gate_low)
        mixed_grad = jax.vjp(smooth, mixed)[1](act_grad)[0]
        normed = unit * feature_row[0] + feature_row[1]
        skip_grad = jnp.sum(mixed_grad * normed, 0)
        mixed_low = mixed_grad.astype(jnp.bfloat16)
        out_grad = contract_rows(states_low, mine(mixed_low))
        states_grad = contract_cols(mixed_low, out_low)
        coef = jnp.stack([pole_re, pole_im, factor_re, factor_im])
        drive_low, sums = adjoint(
            seq_start,
            seq_length,
            pole_powers(pole_re, -pole_im),
            coef,
            mask_columns,
            states_grad,
            states,
            drive,
        )
        gp_re, gp_im, gf_re, gf_im = sums[0], sums[1], sums[2], sums[3]
        row_grad = jax.vjp(coefficients, state_row)[1]((gp_re, gp_im, gf_re, gf_im))[0]
        in_grad = contract_rows(mine(normed_low), drive_low)
        normed_grad = mixed_grad * feature_row[2] + jnp.dot(
            drive_low, in_low.T, preferred_element_type=jnp.float32
        )
        gain_grad = jnp.sum(normed_grad * unit, 0)
        bias_grad = jnp.sum(normed_grad, 0)
        unit_grad = normed_grad * feature_row[0]
        first_mean = jnp.mean(unit_grad, 1, keepdims=True)
        second_mean = jnp.mean(unit_grad * unit, 1, keepdims=True)
        grad = grad + scale * (unit_grad - first_mean - unit * second_mean)
        feature_grad = mine(jnp.stack([gain_grad, bias_grad, skip_grad, gate_bias_grad]))
        layer_grads[layer] = (in_grad, out_grad, gate_grad, feature_grad, row_grad)
    stacked_in = jnp.stack([entry[0] for entry in layer_grads])
    stacked_out = jnp.stack([entry[1] for entry in layer_grads])
    stacked_gate = jnp.stack([entry[2] for entry in layer_grads])
    stacked_feature = jnp.stack([entry[3] for entry in layer_grads])
    stacked_state = jnp.stack([entry[4] for entry in layer_grads])
    summed = sum_over_seq((stacked_in, stacked_out, stacked_gate, stacked_feature, stacked_state))
    factor = 1.0 / math.sqrt(count * lax.axis_size("seq"))
    grad_in = summed[0] * factor
    grad_out = summed[1] * factor
    grad_gate = summed[2] * factor
    grad_feature = summed[3] * factor
    grad_state = summed[4] * factor
    new_in = update(input_matrix, grad_in, velocity_input, average_input, slow_rate, 0.0)
    new_out = update(output_matrix, grad_out, velocity_output, average_output, slow_rate, 0.0)
    new_gate = update(gate_matrix, grad_gate, velocity_gate, average_gate, main_rate, weight_decay)
    new_feature = update(
        feature_vectors, grad_feature, velocity_feature, average_feature, main_rate, weight_decay
    )
    new_state = update(state_vectors, grad_state, velocity_state, average_state, slow_rate, 0.0)
    return (
        mine(stream),
        mine(grad),
        grad_in,
        grad_out,
        grad_gate,
        grad_feature,
        grad_state,
        new_in[0],
        new_out[0],
        new_gate[0],
        new_feature[0],
        new_state[3],
        new_in[1],
        new_out[1],
        new_gate[1],
        new_feature[1],
        new_state[1],
        new_in[2],
        new_out[2],
        new_gate[2],
        new_feature[2],
        new_state[2],
    )


def solution(mesh):
    feat = P(None, None, "feat")
    rows = P(None, "feat", None)
    tokens = P("seq", "feat")
    return jax.shard_map(
        body,
        mesh=mesh,
        in_specs=(
            tokens,
            tokens,
            P("seq"),
            P("seq"),
            rows,
            feat,
            feat,
            feat,
            P(),
            rows,
            feat,
            feat,
            feat,
            P(),
            rows,
            feat,
            feat,
            feat,
            P(),
        ),
        out_specs=(
            tokens,
            tokens,
            rows,
            feat,
            feat,
            feat,
            P(),
            rows,
            feat,
            feat,
            feat,
            P(),
            rows,
            feat,
            feat,
            feat,
            P(),
            rows,
            feat,
            feat,
            feat,
            P(),
        ),
        check_vma=False,
    )
```

```python
import math

import jax
import jax.numpy as jnp
from jax import lax
from jax.experimental import pallas as pl
from jax.experimental.pallas import tpu as pltpu
from jax.sharding import PartitionSpec as P

epsilon = 1e-05
momentum = 0.9
smoothing = 0.5
slow_rate = 0.02
main_rate = 0.05
weight_decay = 0.1


def smooth(value):
    return jax.nn.gelu(value, approximate=False)


def masks_of(starts, lengths, count):
    position = jnp.arange(count, dtype=jnp.int32)[:, None]
    begin = starts[None, :]
    finish = begin + lengths[None, :]
    inside = (position >= begin) & (position < finish)
    alive = jnp.any(inside, 1)
    opening = jnp.any(inside & (position == begin), 1)
    closing = jnp.any(inside & (position == finish - 1), 1)
    return (
        alive.astype(jnp.float32),
        (alive & ~opening).astype(jnp.float32),
        (alive & ~closing).astype(jnp.float32),
    )


def coefficients(state_row):
    rate = -jnp.exp(state_row[0])
    frequency = state_row[1]
    timestep = jnp.exp(state_row[2])
    decay = jnp.exp(rate * timestep)
    angle = frequency * timestep
    pole_real = decay * jnp.cos(angle)
    pole_imag = decay * jnp.sin(angle)
    denom = rate * rate + frequency * frequency
    factor_real = ((pole_real - 1.0) * rate + pole_imag * frequency) / denom
    factor_imag = (pole_imag * rate - (pole_real - 1.0) * frequency) / denom
    return (pole_real, pole_imag, factor_real, factor_imag)


def tile_scan(x_re, x_im, keep, powers, down):
    reps = x_re.shape[1] // keep.shape[1]
    rows = lax.broadcasted_iota(jnp.int32, keep.shape, 0)
    b_re, b_im = x_re, x_im
    for level, k in enumerate((1, 2, 4)):
        shift = 8 - k if down else k
        valid = rows <= 7 - k if down else rows >= k
        gate = jnp.tile(jnp.where(valid, keep, 0.0), (1, reps))
        p_re = pltpu.roll(b_re, shift, 0)
        p_im = pltpu.roll(b_im, shift, 0)
        w_re = powers[0][(0, 1, 3)[level] : (0, 1, 3)[level] + 1]
        w_im = powers[1][(0, 1, 3)[level] : (0, 1, 3)[level] + 1]
        b_re = b_re + gate * (w_re * p_re - w_im * p_im)
        b_im = b_im + gate * (w_re * p_im + w_im * p_re)
        keep = keep * jnp.where(valid, pltpu.roll(keep, shift, 0), 1.0)
    return b_re, b_im, jnp.tile(keep, (1, reps))


def blocked_scan(count, width, pow_ref, starts_ref, lengths_ref, load_up, load_down, store_up, store_down):
    tiles = count // 8
    slots = starts_ref.shape[0]

    def keeps(t0, downward):
        rows = lax.broadcasted_iota(jnp.int32, (8, 128), 0) + t0
        inside = jnp.zeros((8, 128), jnp.bool_)
        for slot in range(slots):
            begin = starts_ref[slot]
            finish = begin + lengths_ref[slot]
            if downward:
                inside = inside | ((rows >= begin) & (rows < finish - 1))
            else:
                inside = inside | ((rows > begin) & (rows < finish))
        return inside.astype(jnp.float32)

    up_powers = (pow_ref[0], pow_ref[1])
    down_powers = (pow_ref[2], pow_ref[3])

    def carry_in(b_re, b_im, reach, powers, h_re, h_im):
        q_re = powers[0] * h_re - powers[1] * h_im
        q_im = powers[0] * h_im + powers[1] * h_re
        return b_re + reach * q_re, b_im + reach * q_im

    def step(i, carry):
        u_re, u_im, d_re, d_im = carry
        tu = pl.multiple_of(i * 8, 8)
        td = pl.multiple_of((tiles - 1 - i) * 8, 8)
        xu_re, xu_im = load_up(tu)
        xd_re, xd_im = load_down(td)
        bu_re, bu_im, ru = tile_scan(xu_re, xu_im, keeps(tu, False), up_powers, False)
        bd_re, bd_im, rd = tile_scan(xd_re, xd_im, keeps(td, True), up_powers, True)
        hu_re, hu_im = carry_in(bu_re, bu_im, ru, up_powers, u_re, u_im)
        hd_re, hd_im = carry_in(bd_re, bd_im, rd, down_powers, d_re, d_im)
        store_up(tu, hu_re, hu_im)
        store_down(td, hd_re, hd_im)
        return (hu_re[7:8], hu_im[7:8], hd_re[0:1], hd_im[0:1])

    zeros = jnp.zeros((1, width), jnp.float32)
    lax.fori_loop(0, tiles, step, (zeros, zeros, zeros, zeros), unroll=2)


def pole_powers(p_re, p_im):
    rows_re = [p_re]
    rows_im = [p_im]
    for _ in range(7):
        a, b = rows_re[-1], rows_im[-1]
        rows_re.append(a * p_re - b * p_im)
        rows_im.append(a * p_im + b * p_re)
    up_re = jnp.stack(rows_re)
    up_im = jnp.stack(rows_im)
    return jnp.stack([up_re, up_im, up_re[::-1], up_im[::-1]])


def recurrence_kernel(starts_ref, lengths_ref, pow_ref, x_ref, out_ref):
    count = x_ref.shape[0]
    width = pow_ref.shape[2]

    def load(t):
        return x_ref[pl.ds(t, 8), pl.ds(0, width)], x_ref[pl.ds(t, 8), pl.ds(width, width)]

    def store(column):
        def put(t, h_re, h_im):
            out_ref[pl.ds(t, 8), pl.ds(column, width)] = h_re
            out_ref[pl.ds(t, 8), pl.ds(column + width, width)] = h_im

        return put

    blocked_scan(count, width, pow_ref, starts_ref, lengths_ref, load, load, store(0), store(2 * width))


def recurrence(starts, lengths, powers, x):
    count, double = x.shape
    vmem = pl.BlockSpec(memory_space=pltpu.VMEM)
    smem = pl.BlockSpec(memory_space=pltpu.SMEM)
    return pl.pallas_call(
        recurrence_kernel,
        out_shape=jax.ShapeDtypeStruct((count, 2 * double), jnp.float32),
        in_specs=[smem, smem, vmem, vmem],
        out_specs=vmem,
        cost_estimate=pl.CostEstimate(
            flops=20 * count * double, transcendentals=0, bytes_accessed=16 * count * double
        ),
    )(starts, lengths, powers, x)


MESH = pl.DeviceIdType.MESH


def ring_place(position, n):
    upper = position // (n // 2)
    return (1 - upper) * (2 * position) + upper * (2 * (n - 1 - position) + 1)


def ring_position(index, n):
    odd = index % 2
    return (1 - odd) * (index // 2) + odd * (n - 1 - index // 2)


def ring_sum_kernel(n, x_ref, r_ref, o_ref, low, slots, rs_send, rs_recv, credit, done, ag_send, ag_recv):
    rows = x_ref.shape[0]
    half = rows // 2
    size = half // n
    me = ring_position(lax.axis_index("seq"), n)
    right = ring_place((me + 1) % n, n)
    left = ring_place((me + n - 1) % n, n)
    rings = ((0, me, right, left), (1, (n - me) % n, left, right))

    barrier = pltpu.get_barrier_semaphore()
    for neighbour in (left, right):
        pl.semaphore_signal(barrier, 1, device_id={"seq": neighbour}, device_id_type=MESH)
    pl.semaphore_wait(barrier, 2)
    o_ref[...] = x_ref[...]
    low[...] = x_ref[...].astype(low.dtype)

    def block(ring, k):
        return pl.ds(pl.multiple_of(ring * half + k * size, 8), size)

    def scatter_copy(ring, place, target, s):
        return pltpu.make_async_remote_copy(
            src_ref=low.at[block(ring, (place - s + n) % n)],
            dst_ref=slots.at[ring, s % 2],
            send_sem=rs_send.at[ring, s % 2],
            recv_sem=rs_recv.at[ring, s % 2],
            device_id={"seq": target},
            device_id_type=MESH,
        )

    def scatter_step(s, carry):
        copies = []
        for ring, place, target, source in rings:

            @pl.when(s >= 2)
            def _():
                pl.semaphore_wait(credit.at[ring], 1)

            copy = scatter_copy(ring, place, target, s)
            copy.start()
            copies.append(copy)
        for (ring, place, target, source), copy in zip(rings, copies):
            copy.wait_recv()
            into = block(ring, (place - s - 1 + 2 * n) % n)
            total = o_ref[into] + slots[ring, s % 2].astype(jnp.float32)
            o_ref[into] = total
            low[into] = total.astype(low.dtype)
            copy.wait_send()

            @pl.when(s <= n - 4)
            def _():
                pl.semaphore_signal(credit.at[ring], 1, device_id={"seq": source}, device_id_type=MESH)

        return carry

    lax.fori_loop(0, n - 1, scatter_step, 0)
    for ring, place, target, source in rings:
        pl.semaphore_signal(done.at[ring], 1, device_id={"seq": source}, device_id_type=MESH)
    for ring, place, target, source in rings:
        final = block(ring, (place + 1) % n)
        r_ref[final] = o_ref[final].astype(r_ref.dtype)
    for ring, place, target, source in rings:
        pl.semaphore_wait(done.at[ring], 1)

    def gather_copy(ring, place, target, s):
        where = block(ring, (place + 1 - s + n) % n)
        return pltpu.make_async_remote_copy(
            src_ref=r_ref.at[where],
            dst_ref=r_ref.at[where],
            send_sem=ag_send.at[ring, s],
            recv_sem=ag_recv.at[ring, s],
            device_id={"seq": target},
            device_id_type=MESH,
        )

    def gather_step(s, carry):
        for ring, place, target, source in rings:

            @pl.when(s >= 1)
            def _():
                gather_copy(ring, place, target, s - 1).wait_recv()

            gather_copy(ring, place, target, s).start()

            @pl.when(s >= 1)
            def _():
                gather_copy(ring, place, target, s - 1).wait_send()

        return carry

    lax.fori_loop(0, n - 1, gather_step, 0)
    for ring, place, target, source in rings:
        last = gather_copy(ring, place, target, n - 2)
        last.wait_recv()
        last.wait_send()


def ring_sum(x, n):
    rows, lanes = x.shape
    size = rows // (2 * n)
    return pl.pallas_call(
        lambda *refs: ring_sum_kernel(n, *refs),
        out_shape=jax.ShapeDtypeStruct((rows, lanes), jnp.bfloat16),
        in_specs=[pl.BlockSpec(memory_space=pltpu.VMEM)],
        out_specs=pl.BlockSpec(memory_space=pltpu.VMEM),
        scratch_shapes=[
            pltpu.VMEM((rows, lanes), jnp.float32),
            pltpu.VMEM((rows, lanes), jnp.bfloat16),
            pltpu.VMEM((2, 2, size, lanes), jnp.bfloat16),
            pltpu.SemaphoreType.DMA((2, 2)),
            pltpu.SemaphoreType.DMA((2, 2)),
            pltpu.SemaphoreType.REGULAR((2,)),
            pltpu.SemaphoreType.REGULAR((2,)),
            pltpu.SemaphoreType.DMA((2, n - 1)),
            pltpu.SemaphoreType.DMA((2, n - 1)),
        ],
        compiler_params=pltpu.CompilerParams(collective_id=0, has_side_effects=True),
    )(x)


def sum_over_seq(parts):
    n = lax.axis_size("seq")
    flat = jnp.concatenate([part.reshape(-1) for part in parts])
    grain = 2 * n * 16 * 128
    padded = -(-flat.size // grain) * grain
    flat = jnp.pad(flat, (0, padded - flat.size)).reshape(padded // 128, 128)
    total = ring_sum(flat, n).astype(jnp.float32).reshape(-1)
    pieces = []
    start = 0
    for part in parts:
        pieces.append(total[start : start + part.size].reshape(part.shape))
        start += part.size
    return pieces


def adjoint_kernel(starts_ref, lengths_ref, pow_ref, coef_ref, masks_ref, g_ref, states_ref, drive_ref, dg_ref, sums_ref, lam):
    count = g_ref.shape[0]
    width = coef_ref.shape[1]
    pad = 8
    f_re = coef_ref[2:3, :]
    f_im = coef_ref[3:4, :]
    zero_rows = jnp.zeros((pad, 4 * width), jnp.float32)
    lam[0:pad, :] = zero_rows
    lam[pad + count : 2 * pad + count, :] = zero_rows

    def load(column):
        def get(t):
            return g_ref[pl.ds(t, 8), pl.ds(column, width)], g_ref[pl.ds(t, 8), pl.ds(column + width, width)]

        return get

    def store(column):
        def put(t, h_re, h_im):
            lam[pl.ds(pad + t, 8), pl.ds(column, width)] = h_re
            lam[pl.ds(pad + t, 8), pl.ds(column + width, width)] = h_im

        return put

    blocked_scan(count, width, pow_ref, starts_ref, lengths_ref, load(2 * width), load(0), store(0), store(2 * width))

    rows = 16

    def part(ref, start, column):
        return ref[pl.ds(start, rows), pl.ds(column, width)]

    def epilogue(k, sums):
        gp_re, gp_im, gf_re, gf_im = sums
        r0 = pl.multiple_of(k * rows, rows)
        live = masks_ref[pl.ds(r0, rows), 0:1]
        keep_prev = masks_ref[pl.ds(r0, rows), 1:2]
        keep_next = masks_ref[pl.ds(r0, rows), 2:3]
        lb_re = part(lam, pad + r0, 0)
        lb_im = part(lam, pad + r0, width)
        la_re = part(lam, pad + r0, 2 * width)
        la_im = part(lam, pad + r0, 3 * width)
        gu_re = la_re + lb_re
        gu_im = la_im + lb_im
        dg_ref[pl.ds(r0, rows), pl.ds(0, width)] = ((f_re * gu_re + f_im * gu_im) * live).astype(dg_ref.dtype)
        dg_ref[pl.ds(r0, rows), pl.ds(width, width)] = ((f_re * gu_im - f_im * gu_re) * live).astype(dg_ref.dtype)
        d_re = part(drive_ref, r0, 0) * live
        d_im = part(drive_ref, r0, width) * live
        gf_re = gf_re + d_re * gu_re + d_im * gu_im
        gf_im = gf_im + d_re * gu_im - d_im * gu_re
        a_re = part(states_ref, r0, 0) * keep_next
        a_im = part(states_ref, r0, width) * keep_next
        b_re = part(states_ref, r0, 2 * width) * keep_prev
        b_im = part(states_ref, r0, 3 * width) * keep_prev
        ahead_rows = lam[pl.ds(pad + r0, rows + 8), pl.ds(2 * width, 2 * width)][1 : rows + 1]
        behind_rows = lam[pl.ds(r0, rows + 8), pl.ds(0, 2 * width)][pad - 1 : pad - 1 + rows]
        na_re = ahead_rows[:, :width]
        na_im = ahead_rows[:, width:]
        pb_re = behind_rows[:, :width]
        pb_im = behind_rows[:, width:]
        gp_re = gp_re + a_re * na_re + a_im * na_im + b_re * pb_re + b_im * pb_im
        gp_im = gp_im + a_re * na_im - a_im * na_re + b_re * pb_im - b_im * pb_re
        return (gp_re, gp_im, gf_re, gf_im)

    block = jnp.zeros((rows, width), jnp.float32)
    sums = lax.fori_loop(0, count // rows, epilogue, (block, block, block, block))
    for k, value in enumerate(sums):
        sums_ref[k : k + 1, :] = jnp.sum(value, 0, keepdims=True)


def adjoint(starts, lengths, powers, coef, masks, states_grad, states, drive):
    count, quad = states_grad.shape
    width = quad // 4
    vmem = pl.BlockSpec(memory_space=pltpu.VMEM)
    smem = pl.BlockSpec(memory_space=pltpu.SMEM)
    return pl.pallas_call(
        adjoint_kernel,
        out_shape=(
            jax.ShapeDtypeStruct((count, 2 * width), jnp.bfloat16),
            jax.ShapeDtypeStruct((4, width), jnp.float32),
        ),
        in_specs=[smem, smem] + [vmem] * 6,
        out_specs=(vmem, vmem),
        scratch_shapes=[pltpu.VMEM((count + 16, 4 * width), jnp.float32)],
        cost_estimate=pl.CostEstimate(
            flops=60 * count * width, transcendentals=0, bytes_accessed=48 * count * width
        ),
    )(starts, lengths, powers, coef, masks, states_grad, states, drive)


def update(weight, gradient, velocity, average, rate, decay):
    adjusted = gradient + decay * weight
    velocity_new = momentum * velocity + adjusted
    change = -rate * (adjusted + momentum * velocity_new)
    weight_new = weight + change
    average_new = smoothing * average + (1.0 - smoothing) * weight_new
    return (weight_new, velocity_new, average_new, change)


def contract_rows(left, right):
    return lax.dot_general(
        left, right, (((0,), (0,)), ((), ())), preferred_element_type=jnp.float32
    )


def contract_cols(left, right):
    return lax.dot_general(
        left, right, (((1,), (1,)), ((), ())), preferred_element_type=jnp.float32
    )


def gather_feat(value, axis):
    return lax.all_gather(value, "feat", axis=axis, tiled=True)


def body(
    activations_in,
    cotangent,
    seq_start,
    seq_length,
    input_matrix,
    output_matrix,
    gate_matrix,
    feature_vectors,
    state_vectors,
    velocity_input,
    velocity_output,
    velocity_gate,
    velocity_feature,
    velocity_state,
    average_input,
    average_output,
    average_gate,
    average_feature,
    average_state,
):
    count = activations_in.shape[0]
    shard = activations_in.shape[1]
    layers = input_matrix.shape[0]
    width = state_vectors.shape[2]
    me = lax.axis_index("feat")
    offset = me * shard

    def mine(value):
        return lax.dynamic_slice_in_dim(value, offset, shard, axis=value.ndim - 1)

    alive, carry_prev, carry_next = masks_of(seq_start, seq_length, count)
    zero = jnp.zeros((1,), jnp.float32)
    after_next = jnp.concatenate([zero, carry_next[:-1]])
    before_prev = jnp.concatenate([carry_prev[1:], zero])
    mask_columns = jnp.stack([alive, carry_prev, carry_next, jnp.zeros_like(alive)], 1)


    in_all = gather_feat(input_matrix.astype(jnp.bfloat16), 1)
    rows_out = output_matrix.shape[1]
    rows_gate = gate_matrix.shape[1]
    paired = [
        gather_feat(
            jnp.concatenate(
                [output_matrix[k].astype(jnp.bfloat16), gate_matrix[k].astype(jnp.bfloat16)]
                + ([cotangent] if k == layers - 1 else []),
                0,
            ),
            1,
        )
        for k in range(layers)
    ]
    out_all = [pair[:rows_out] for pair in paired]
    gate_all = [pair[rows_out : rows_out + rows_gate] for pair in paired]
    cotangent_all = paired[-1][rows_out + rows_gate :]
    feature_all = gather_feat(feature_vectors, 2)
    stream = gather_feat(activations_in, 1).astype(jnp.float32)

    saved = []
    for layer in range(layers):
        in_low = in_all[layer]
        out_low = out_all[layer]
        gate_low = gate_all[layer]
        feature_row = feature_all[layer]
        pole_re, pole_im, factor_re, factor_im = coefficients(state_vectors[layer])
        center = jnp.mean(stream, 1, keepdims=True)
        spread = stream - center
        scale = lax.rsqrt(jnp.mean(spread * spread, 1, keepdims=True) + epsilon)
        unit = spread * scale
        normed = unit * feature_row[0] + feature_row[1]
        normed_low = normed.astype(jnp.bfloat16)
        drive = jnp.dot(normed_low, in_low, preferred_element_type=jnp.float32)
        drive_re = drive[:, :width]
        drive_im = drive[:, width:]
        source = jnp.concatenate(
            [
                (drive_re * factor_re - drive_im * factor_im) * alive[:, None],
                (drive_re * factor_im + drive_im * factor_re) * alive[:, None],
            ],
            1,
        )
        states = recurrence(seq_start, seq_length, pole_powers(pole_re, pole_im), source)
        states_low = states.astype(jnp.bfloat16)
        mixed = (
            jnp.dot(states_low, out_low, preferred_element_type=jnp.float32)
            + feature_row[2] * normed
        )
        act = smooth(mixed)
        act_low = act.astype(jnp.bfloat16)
        pre = jnp.dot(act_low, gate_low, preferred_element_type=jnp.float32) + feature_row[3]
        saved.append((scale, unit, normed_low, drive, states, states_low, mixed, act, act_low, pre))
        stream = stream + act * jax.nn.sigmoid(pre)

    grad = cotangent_all.astype(jnp.float32) * alive[:, None]
    layer_grads = [None] * layers
    for layer in reversed(range(layers)):
        scale, unit, normed_low, drive, states, states_low, mixed, act, act_low, pre = saved[layer]
        in_low = in_all[layer]
        out_low = out_all[layer]
        gate_low = gate_all[layer]
        feature_row = feature_all[layer]
        state_row = state_vectors[layer]
        pole_re, pole_im, factor_re, factor_im = coefficients(state_row)
        gate = jax.nn.sigmoid(pre)
        pre_grad = (grad * act * gate * (1.0 - gate)).astype(jnp.bfloat16)
        gate_grad = contract_rows(act_low, mine(pre_grad))
        gate_bias_grad = jnp.sum(pre_grad.astype(jnp.float32), 0)
        act_grad = grad * gate + contract_cols(pre_grad, gate_low)
        mixed_grad = jax.vjp(smooth, mixed)[1](act_grad)[0]
        normed = unit * feature_row[0] + feature_row[1]
        skip_grad = jnp.sum(mixed_grad * normed, 0)
        mixed_low = mixed_grad.astype(jnp.bfloat16)
        out_grad = contract_rows(states_low, mine(mixed_low))
        states_grad = contract_cols(mixed_low, out_low)
        coef = jnp.stack([pole_re, pole_im, factor_re, factor_im])
        drive_low, sums = adjoint(
            seq_start,
            seq_length,
            pole_powers(pole_re, -pole_im),
            coef,
            mask_columns,
            states_grad,
            states,
            drive,
        )
        gp_re, gp_im, gf_re, gf_im = sums[0], sums[1], sums[2], sums[3]
        row_grad = jax.vjp(coefficients, state_row)[1]((gp_re, gp_im, gf_re, gf_im))[0]
        in_grad = contract_rows(mine(normed_low), drive_low)
        normed_grad = mixed_grad * feature_row[2] + jnp.dot(
            drive_low, in_low.T, preferred_element_type=jnp.float32
        )
        gain_grad = jnp.sum(normed_grad * unit, 0)
        bias_grad = jnp.sum(normed_grad, 0)
        unit_grad = normed_grad * feature_row[0]
        first_mean = jnp.mean(unit_grad, 1, keepdims=True)
        second_mean = jnp.mean(unit_grad * unit, 1, keepdims=True)
        grad = grad + scale * (unit_grad - first_mean - unit * second_mean)
        feature_grad = mine(jnp.stack([gain_grad, bias_grad, skip_grad, gate_bias_grad]))
        layer_grads[layer] = (in_grad, out_grad, gate_grad, feature_grad, row_grad)
    stacked_in = jnp.stack([entry[0] for entry in layer_grads])
    stacked_out = jnp.stack([entry[1] for entry in layer_grads])
    stacked_gate = jnp.stack([entry[2] for entry in layer_grads])
    stacked_feature = jnp.stack([entry[3] for entry in layer_grads])
    stacked_state = jnp.stack([entry[4] for entry in layer_grads])
    summed = sum_over_seq((stacked_in, stacked_out, stacked_gate, stacked_feature, stacked_state))
    factor = 1.0 / math.sqrt(count * lax.axis_size("seq"))
    grad_in = summed[0] * factor
    grad_out = summed[1] * factor
    grad_gate = summed[2] * factor
    grad_feature = summed[3] * factor
    grad_state = summed[4] * factor
    new_in = update(input_matrix, grad_in, velocity_input, average_input, slow_rate, 0.0)
    new_out = update(output_matrix, grad_out, velocity_output, average_output, slow_rate, 0.0)
    new_gate = update(gate_matrix, grad_gate, velocity_gate, average_gate, main_rate, weight_decay)
    new_feature = update(
        feature_vectors, grad_feature, velocity_feature, average_feature, main_rate, weight_decay
    )
    new_state = update(state_vectors, grad_state, velocity_state, average_state, slow_rate, 0.0)
    return (
        mine(stream),
        mine(grad),
        grad_in,
        grad_out,
        grad_gate,
        grad_feature,
        grad_state,
        new_in[0],
        new_out[0],
        new_gate[0],
        new_feature[0],
        new_state[3],
        new_in[1],
        new_out[1],
        new_gate[1],
        new_feature[1],
        new_state[1],
        new_in[2],
        new_out[2],
        new_gate[2],
        new_feature[2],
        new_state[2],
    )


def solution(mesh):
    feat = P(None, None, "feat")
    rows = P(None, "feat", None)
    tokens = P("seq", "feat")
    return jax.shard_map(
        body,
        mesh=mesh,
        in_specs=(
            tokens,
            tokens,
            P("seq"),
            P("seq"),
            rows,
            feat,
            feat,
            feat,
            P(),
            rows,
            feat,
            feat,
            feat,
            P(),
            rows,
            feat,
            feat,
            feat,
            P(),
        ),
        out_specs=(
            tokens,
            tokens,
            rows,
            feat,
            feat,
            feat,
            P(),
            rows,
            feat,
            feat,
            feat,
            P(),
            rows,
            feat,
            feat,
            feat,
            P(),
            rows,
            feat,
            feat,
            feat,
            P(),
        ),
        check_vma=False,
    )
```

```python
import math

import jax
import jax.numpy as jnp
from jax import lax
from jax.experimental import pallas as pl
from jax.experimental.pallas import tpu as pltpu
from jax.sharding import PartitionSpec as P

epsilon = 1e-05
momentum = 0.9
smoothing = 0.5
slow_rate = 0.02
main_rate = 0.05
weight_decay = 0.1


def smooth(value):
    return jax.nn.gelu(value, approximate=False)


def masks_of(starts, lengths, count):
    position = jnp.arange(count, dtype=jnp.int32)[:, None]
    begin = starts[None, :]
    finish = begin + lengths[None, :]
    inside = (position >= begin) & (position < finish)
    alive = jnp.any(inside, 1)
    opening = jnp.any(inside & (position == begin), 1)
    closing = jnp.any(inside & (position == finish - 1), 1)
    return (
        alive.astype(jnp.float32),
        (alive & ~opening).astype(jnp.float32),
        (alive & ~closing).astype(jnp.float32),
    )


def coefficients(state_row):
    rate = -jnp.exp(state_row[0])
    frequency = state_row[1]
    timestep = jnp.exp(state_row[2])
    decay = jnp.exp(rate * timestep)
    angle = frequency * timestep
    pole_real = decay * jnp.cos(angle)
    pole_imag = decay * jnp.sin(angle)
    denom = rate * rate + frequency * frequency
    factor_real = ((pole_real - 1.0) * rate + pole_imag * frequency) / denom
    factor_imag = (pole_imag * rate - (pole_real - 1.0) * frequency) / denom
    return (pole_real, pole_imag, factor_real, factor_imag)


def tile_scan(x_re, x_im, keep, powers, down):
    reps = x_re.shape[1] // keep.shape[1]
    rows = lax.broadcasted_iota(jnp.int32, keep.shape, 0)
    b_re, b_im = x_re, x_im
    for level, k in enumerate((1, 2, 4)):
        shift = 8 - k if down else k
        valid = rows <= 7 - k if down else rows >= k
        gate = jnp.tile(jnp.where(valid, keep, 0.0), (1, reps))
        p_re = pltpu.roll(b_re, shift, 0)
        p_im = pltpu.roll(b_im, shift, 0)
        w_re = powers[0][(0, 1, 3)[level] : (0, 1, 3)[level] + 1]
        w_im = powers[1][(0, 1, 3)[level] : (0, 1, 3)[level] + 1]
        b_re = b_re + gate * (w_re * p_re - w_im * p_im)
        b_im = b_im + gate * (w_re * p_im + w_im * p_re)
        keep = keep * jnp.where(valid, pltpu.roll(keep, shift, 0), 1.0)
    return b_re, b_im, jnp.tile(keep, (1, reps))


def blocked_scan(count, width, pow_ref, starts_ref, lengths_ref, load_up, load_down, store_up, store_down):
    tiles = count // 8
    slots = starts_ref.shape[0]

    def keeps(t0, downward):
        rows = lax.broadcasted_iota(jnp.int32, (8, 128), 0) + t0
        inside = jnp.zeros((8, 128), jnp.bool_)
        for slot in range(slots):
            begin = starts_ref[slot]
            finish = begin + lengths_ref[slot]
            if downward:
                inside = inside | ((rows >= begin) & (rows < finish - 1))
            else:
                inside = inside | ((rows > begin) & (rows < finish))
        return inside.astype(jnp.float32)

    up_powers = (pow_ref[0], pow_ref[1])
    down_powers = (pow_ref[2], pow_ref[3])

    def carry_in(b_re, b_im, reach, powers, h_re, h_im):
        q_re = powers[0] * h_re - powers[1] * h_im
        q_im = powers[0] * h_im + powers[1] * h_re
        return b_re + reach * q_re, b_im + reach * q_im

    def step(i, carry):
        u_re, u_im, d_re, d_im = carry
        tu = pl.multiple_of(i * 8, 8)
        td = pl.multiple_of((tiles - 1 - i) * 8, 8)
        xu_re, xu_im = load_up(tu)
        xd_re, xd_im = load_down(td)
        bu_re, bu_im, ru = tile_scan(xu_re, xu_im, keeps(tu, False), up_powers, False)
        bd_re, bd_im, rd = tile_scan(xd_re, xd_im, keeps(td, True), up_powers, True)
        hu_re, hu_im = carry_in(bu_re, bu_im, ru, up_powers, u_re, u_im)
        hd_re, hd_im = carry_in(bd_re, bd_im, rd, down_powers, d_re, d_im)
        store_up(tu, hu_re, hu_im)
        store_down(td, hd_re, hd_im)
        return (hu_re[7:8], hu_im[7:8], hd_re[0:1], hd_im[0:1])

    zeros = jnp.zeros((1, width), jnp.float32)
    lax.fori_loop(0, tiles, step, (zeros, zeros, zeros, zeros), unroll=2)


def pole_powers(p_re, p_im):
    rows_re = [p_re]
    rows_im = [p_im]
    for _ in range(7):
        a, b = rows_re[-1], rows_im[-1]
        rows_re.append(a * p_re - b * p_im)
        rows_im.append(a * p_im + b * p_re)
    up_re = jnp.stack(rows_re)
    up_im = jnp.stack(rows_im)
    return jnp.stack([up_re, up_im, up_re[::-1], up_im[::-1]])


def recurrence_kernel(starts_ref, lengths_ref, pow_ref, x_ref, out_ref):
    count = x_ref.shape[0]
    width = pow_ref.shape[2]

    def load(t):
        return x_ref[pl.ds(t, 8), pl.ds(0, width)], x_ref[pl.ds(t, 8), pl.ds(width, width)]

    def store(column):
        def put(t, h_re, h_im):
            out_ref[pl.ds(t, 8), pl.ds(column, width)] = h_re
            out_ref[pl.ds(t, 8), pl.ds(column + width, width)] = h_im

        return put

    blocked_scan(count, width, pow_ref, starts_ref, lengths_ref, load, load, store(0), store(2 * width))


def recurrence(starts, lengths, powers, x):
    count, double = x.shape
    vmem = pl.BlockSpec(memory_space=pltpu.VMEM)
    smem = pl.BlockSpec(memory_space=pltpu.SMEM)
    return pl.pallas_call(
        recurrence_kernel,
        out_shape=jax.ShapeDtypeStruct((count, 2 * double), jnp.float32),
        in_specs=[smem, smem, vmem, vmem],
        out_specs=vmem,
        cost_estimate=pl.CostEstimate(
            flops=20 * count * double, transcendentals=0, bytes_accessed=16 * count * double
        ),
    )(starts, lengths, powers, x)


MESH = pl.DeviceIdType.MESH


def ring_place(position, n):
    upper = position // (n // 2)
    return (1 - upper) * (2 * position) + upper * (2 * (n - 1 - position) + 1)


def ring_position(index, n):
    odd = index % 2
    return (1 - odd) * (index // 2) + odd * (n - 1 - index // 2)


def ring_sum_kernel(n, x_ref, r_ref, o_ref, low, slots, rs_send, rs_recv, credit, done, ag_send, ag_recv):
    rows = x_ref.shape[0]
    half = rows // 2
    size = half // n
    me = ring_position(lax.axis_index("seq"), n)
    right = ring_place((me + 1) % n, n)
    left = ring_place((me + n - 1) % n, n)
    rings = ((0, me, right, left), (1, (n - me) % n, left, right))

    barrier = pltpu.get_barrier_semaphore()
    for neighbour in (left, right):
        pl.semaphore_signal(barrier, 1, device_id={"seq": neighbour}, device_id_type=MESH)
    pl.semaphore_wait(barrier, 2)
    o_ref[...] = x_ref[...]
    low[...] = x_ref[...].astype(low.dtype)

    def block(ring, k):
        return pl.ds(pl.multiple_of(ring * half + k * size, 8), size)

    def scatter_copy(ring, place, target, s):
        return pltpu.make_async_remote_copy(
            src_ref=low.at[block(ring, (place - s + n) % n)],
            dst_ref=slots.at[ring, s % 2],
            send_sem=rs_send.at[ring, s % 2],
            recv_sem=rs_recv.at[ring, s % 2],
            device_id={"seq": target},
            device_id_type=MESH,
        )

    def scatter_step(s, carry):
        copies = []
        for ring, place, target, source in rings:

            @pl.when(s >= 2)
            def _():
                pl.semaphore_wait(credit.at[ring], 1)

            copy = scatter_copy(ring, place, target, s)
            copy.start()
            copies.append(copy)
        for (ring, place, target, source), copy in zip(rings, copies):
            copy.wait_recv()
            into = block(ring, (place - s - 1 + 2 * n) % n)
            total = o_ref[into] + slots[ring, s % 2].astype(jnp.float32)
            o_ref[into] = total
            low[into] = total.astype(low.dtype)
            copy.wait_send()

            @pl.when(s <= n - 4)
            def _():
                pl.semaphore_signal(credit.at[ring], 1, device_id={"seq": source}, device_id_type=MESH)

        return carry

    lax.fori_loop(0, n - 1, scatter_step, 0)
    for ring, place, target, source in rings:
        pl.semaphore_signal(done.at[ring], 1, device_id={"seq": source}, device_id_type=MESH)
    for ring, place, target, source in rings:
        final = block(ring, (place + 1) % n)
        r_ref[final] = o_ref[final].astype(r_ref.dtype)
    for ring, place, target, source in rings:
        pl.semaphore_wait(done.at[ring], 1)

    def gather_copy(ring, place, target, s):
        where = block(ring, (place + 1 - s + n) % n)
        return pltpu.make_async_remote_copy(
            src_ref=r_ref.at[where],
            dst_ref=r_ref.at[where],
            send_sem=ag_send.at[ring, s],
            recv_sem=ag_recv.at[ring, s],
            device_id={"seq": target},
            device_id_type=MESH,
        )

    def gather_step(s, carry):
        for ring, place, target, source in rings:

            @pl.when(s >= 1)
            def _():
                gather_copy(ring, place, target, s - 1).wait_recv()

            gather_copy(ring, place, target, s).start()

            @pl.when(s >= 1)
            def _():
                gather_copy(ring, place, target, s - 1).wait_send()

        return carry

    lax.fori_loop(0, n - 1, gather_step, 0)
    for ring, place, target, source in rings:
        last = gather_copy(ring, place, target, n - 2)
        last.wait_recv()
        last.wait_send()


def ring_sum(x, n):
    rows, lanes = x.shape
    size = rows // (2 * n)
    return pl.pallas_call(
        lambda *refs: ring_sum_kernel(n, *refs),
        out_shape=jax.ShapeDtypeStruct((rows, lanes), jnp.bfloat16),
        in_specs=[pl.BlockSpec(memory_space=pltpu.VMEM)],
        out_specs=pl.BlockSpec(memory_space=pltpu.VMEM),
        scratch_shapes=[
            pltpu.VMEM((rows, lanes), jnp.float32),
            pltpu.VMEM((rows, lanes), jnp.bfloat16),
            pltpu.VMEM((2, 2, size, lanes), jnp.bfloat16),
            pltpu.SemaphoreType.DMA((2, 2)),
            pltpu.SemaphoreType.DMA((2, 2)),
            pltpu.SemaphoreType.REGULAR((2,)),
            pltpu.SemaphoreType.REGULAR((2,)),
            pltpu.SemaphoreType.DMA((2, n - 1)),
            pltpu.SemaphoreType.DMA((2, n - 1)),
        ],
        compiler_params=pltpu.CompilerParams(collective_id=0, has_side_effects=True),
    )(x)


def sum_over_seq(parts):
    n = lax.axis_size("seq")
    flat = jnp.concatenate([part.reshape(-1) for part in parts])
    grain = 2 * n * 16 * 128
    padded = -(-flat.size // grain) * grain
    flat = jnp.pad(flat, (0, padded - flat.size)).reshape(padded // 128, 128)
    total = ring_sum(flat, n).astype(jnp.float32).reshape(-1)
    pieces = []
    start = 0
    for part in parts:
        pieces.append(total[start : start + part.size].reshape(part.shape))
        start += part.size
    return pieces


def adjoint_kernel(starts_ref, lengths_ref, pow_ref, coef_ref, masks_ref, g_ref, states_ref, drive_ref, dg_ref, sums_ref, lam):
    count = g_ref.shape[0]
    width = coef_ref.shape[1]
    pad = 8
    f_re = coef_ref[2:3, :]
    f_im = coef_ref[3:4, :]
    zero_rows = jnp.zeros((pad, 4 * width), jnp.float32)
    lam[0:pad, :] = zero_rows
    lam[pad + count : 2 * pad + count, :] = zero_rows

    def load(column):
        def get(t):
            return g_ref[pl.ds(t, 8), pl.ds(column, width)], g_ref[pl.ds(t, 8), pl.ds(column + width, width)]

        return get

    def store(column):
        def put(t, h_re, h_im):
            lam[pl.ds(pad + t, 8), pl.ds(column, width)] = h_re
            lam[pl.ds(pad + t, 8), pl.ds(column + width, width)] = h_im

        return put

    blocked_scan(count, width, pow_ref, starts_ref, lengths_ref, load(2 * width), load(0), store(0), store(2 * width))

    rows = 16

    def part(ref, start, column):
        return ref[pl.ds(start, rows), pl.ds(column, width)]

    def epilogue(k, sums):
        gp_re, gp_im, gf_re, gf_im = sums
        r0 = pl.multiple_of(k * rows, rows)
        live = masks_ref[pl.ds(r0, rows), 0:1]
        keep_prev = masks_ref[pl.ds(r0, rows), 1:2]
        keep_next = masks_ref[pl.ds(r0, rows), 2:3]
        lb_re = part(lam, pad + r0, 0)
        lb_im = part(lam, pad + r0, width)
        la_re = part(lam, pad + r0, 2 * width)
        la_im = part(lam, pad + r0, 3 * width)
        gu_re = la_re + lb_re
        gu_im = la_im + lb_im
        dg_ref[pl.ds(r0, rows), pl.ds(0, width)] = ((f_re * gu_re + f_im * gu_im) * live).astype(dg_ref.dtype)
        dg_ref[pl.ds(r0, rows), pl.ds(width, width)] = ((f_re * gu_im - f_im * gu_re) * live).astype(dg_ref.dtype)
        d_re = part(drive_ref, r0, 0) * live
        d_im = part(drive_ref, r0, width) * live
        gf_re = gf_re + d_re * gu_re + d_im * gu_im
        gf_im = gf_im + d_re * gu_im - d_im * gu_re
        a_re = part(states_ref, r0, 0) * keep_next
        a_im = part(states_ref, r0, width) * keep_next
        b_re = part(states_ref, r0, 2 * width) * keep_prev
        b_im = part(states_ref, r0, 3 * width) * keep_prev
        ahead_rows = lam[pl.ds(pad + r0, rows + 8), pl.ds(2 * width, 2 * width)][1 : rows + 1]
        behind_rows = lam[pl.ds(r0, rows + 8), pl.ds(0, 2 * width)][pad - 1 : pad - 1 + rows]
        na_re = ahead_rows[:, :width]
        na_im = ahead_rows[:, width:]
        pb_re = behind_rows[:, :width]
        pb_im = behind_rows[:, width:]
        gp_re = gp_re + a_re * na_re + a_im * na_im + b_re * pb_re + b_im * pb_im
        gp_im = gp_im + a_re * na_im - a_im * na_re + b_re * pb_im - b_im * pb_re
        return (gp_re, gp_im, gf_re, gf_im)

    block = jnp.zeros((rows, width), jnp.float32)
    sums = lax.fori_loop(0, count // rows, epilogue, (block, block, block, block))
    for k, value in enumerate(sums):
        sums_ref[k : k + 1, :] = jnp.sum(value, 0, keepdims=True)


def adjoint(starts, lengths, powers, coef, masks, states_grad, states, drive):
    count, quad = states_grad.shape
    width = quad // 4
    vmem = pl.BlockSpec(memory_space=pltpu.VMEM)
    smem = pl.BlockSpec(memory_space=pltpu.SMEM)
    return pl.pallas_call(
        adjoint_kernel,
        out_shape=(
            jax.ShapeDtypeStruct((count, 2 * width), jnp.bfloat16),
            jax.ShapeDtypeStruct((4, width), jnp.float32),
        ),
        in_specs=[smem, smem] + [vmem] * 6,
        out_specs=(vmem, vmem),
        scratch_shapes=[pltpu.VMEM((count + 16, 4 * width), jnp.float32)],
        cost_estimate=pl.CostEstimate(
            flops=60 * count * width, transcendentals=0, bytes_accessed=48 * count * width
        ),
    )(starts, lengths, powers, coef, masks, states_grad, states, drive)


def update(weight, gradient, velocity, average, rate, decay):
    adjusted = gradient + decay * weight
    velocity_new = momentum * velocity + adjusted
    change = -rate * (adjusted + momentum * velocity_new)
    weight_new = weight + change
    average_new = smoothing * average + (1.0 - smoothing) * weight_new
    return (weight_new, velocity_new, average_new, change)


def contract_rows(left, right):
    return lax.dot_general(
        left, right, (((0,), (0,)), ((), ())), preferred_element_type=jnp.float32
    )


def contract_cols(left, right):
    return lax.dot_general(
        left, right, (((1,), (1,)), ((), ())), preferred_element_type=jnp.float32
    )


def gather_feat(value, axis):
    return lax.all_gather(value, "feat", axis=axis, tiled=True)


def split_exact(value):
    high = lax.reduce_precision(value, exponent_bits=8, mantissa_bits=7)
    rest = value - high
    middle = lax.reduce_precision(rest, exponent_bits=8, mantissa_bits=7)
    little = rest - middle
    return jnp.concatenate([high, middle, little], 0).astype(jnp.bfloat16)


def join_exact(pieces):
    third = pieces.shape[0] // 3
    pieces = pieces.astype(jnp.float32)
    return pieces[:third] + (pieces[third : 2 * third] + pieces[2 * third :])


def body(
    activations_in,
    cotangent,
    seq_start,
    seq_length,
    input_matrix,
    output_matrix,
    gate_matrix,
    feature_vectors,
    state_vectors,
    velocity_input,
    velocity_output,
    velocity_gate,
    velocity_feature,
    velocity_state,
    average_input,
    average_output,
    average_gate,
    average_feature,
    average_state,
):
    count = activations_in.shape[0]
    shard = activations_in.shape[1]
    layers = input_matrix.shape[0]
    width = state_vectors.shape[2]
    me = lax.axis_index("feat")
    offset = me * shard

    def mine(value):
        return lax.dynamic_slice_in_dim(value, offset, shard, axis=value.ndim - 1)

    alive, carry_prev, carry_next = masks_of(seq_start, seq_length, count)
    zero = jnp.zeros((1,), jnp.float32)
    after_next = jnp.concatenate([zero, carry_next[:-1]])
    before_prev = jnp.concatenate([carry_prev[1:], zero])
    mask_columns = jnp.stack([alive, carry_prev, carry_next, jnp.zeros_like(alive)], 1)


    def low(value):
        return value.astype(jnp.bfloat16)

    feature_pieces = split_exact(feature_vectors.reshape(-1, shard))
    feature_rows = feature_pieces.shape[0]
    feature_pad = -(-feature_rows // 16) * 16
    feature_pieces = jnp.pad(feature_pieces, ((0, feature_pad - feature_rows), (0, 0)))
    groups = [[low(input_matrix[0].T), activations_in, feature_pieces]]
    for k in range(layers):
        tail = [low(input_matrix[k + 1].T)] if k + 1 < layers else [cotangent]
        groups.append([low(output_matrix[k]), low(gate_matrix[k])] + tail)
    gathered = []
    for group in groups:
        whole = gather_feat(jnp.concatenate(group, 0), 1)
        start = 0
        pieces = []
        for piece in group:
            pieces.append(whole[start : start + piece.shape[0]])
            start += piece.shape[0]
        gathered.append(pieces)
    in_all = [gathered[0][0]] + [gathered[k][2] for k in range(1, layers)]
    out_all = [gathered[k + 1][0] for k in range(layers)]
    gate_all = [gathered[k + 1][1] for k in range(layers)]
    cotangent_all = gathered[layers][2]
    stream = gathered[0][1].astype(jnp.float32)
    feature_all = join_exact(gathered[0][2][:feature_rows]).reshape(feature_vectors.shape[:-1] + (-1,))

    saved = []
    for layer in range(layers):
        in_low = in_all[layer]
        out_low = out_all[layer]
        gate_low = gate_all[layer]
        feature_row = feature_all[layer]
        pole_re, pole_im, factor_re, factor_im = coefficients(state_vectors[layer])
        center = jnp.mean(stream, 1, keepdims=True)
        spread = stream - center
        scale = lax.rsqrt(jnp.mean(spread * spread, 1, keepdims=True) + epsilon)
        unit = spread * scale
        normed = unit * feature_row[0] + feature_row[1]
        normed_low = normed.astype(jnp.bfloat16)
        drive = contract_cols(normed_low, in_low)
        drive_re = drive[:, :width]
        drive_im = drive[:, width:]
        source = jnp.concatenate(
            [
                (drive_re * factor_re - drive_im * factor_im) * alive[:, None],
                (drive_re * factor_im + drive_im * factor_re) * alive[:, None],
            ],
            1,
        )
        states = recurrence(seq_start, seq_length, pole_powers(pole_re, pole_im), source)
        states_low = states.astype(jnp.bfloat16)
        mixed = (
            jnp.dot(states_low, out_low, preferred_element_type=jnp.float32)
            + feature_row[2] * normed
        )
        act = smooth(mixed)
        act_low = act.astype(jnp.bfloat16)
        pre = jnp.dot(act_low, gate_low, preferred_element_type=jnp.float32) + feature_row[3]
        saved.append((scale, unit, normed_low, drive, states, states_low, mixed, act, act_low, pre))
        stream = stream + act * jax.nn.sigmoid(pre)

    grad = cotangent_all.astype(jnp.float32) * alive[:, None]
    layer_grads = [None] * layers
    for layer in reversed(range(layers)):
        scale, unit, normed_low, drive, states, states_low, mixed, act, act_low, pre = saved[layer]
        in_low = in_all[layer]
        out_low = out_all[layer]
        gate_low = gate_all[layer]
        feature_row = feature_all[layer]
        state_row = state_vectors[layer]
        pole_re, pole_im, factor_re, factor_im = coefficients(state_row)
        gate = jax.nn.sigmoid(pre)
        pre_grad = (grad * act * gate * (1.0 - gate)).astype(jnp.bfloat16)
        gate_grad = contract_rows(act_low, mine(pre_grad))
        gate_bias_grad = jnp.sum(pre_grad.astype(jnp.float32), 0)
        act_grad = grad * gate + contract_cols(pre_grad, gate_low)
        mixed_grad = jax.vjp(smooth, mixed)[1](act_grad)[0]
        normed = unit * feature_row[0] + feature_row[1]
        skip_grad = jnp.sum(mixed_grad * normed, 0)
        mixed_low = mixed_grad.astype(jnp.bfloat16)
        out_grad = contract_rows(states_low, mine(mixed_low))
        states_grad = contract_cols(mixed_low, out_low)
        coef = jnp.stack([pole_re, pole_im, factor_re, factor_im])
        drive_low, sums = adjoint(
            seq_start,
            seq_length,
            pole_powers(pole_re, -pole_im),
            coef,
            mask_columns,
            states_grad,
            states,
            drive,
        )
        gp_re, gp_im, gf_re, gf_im = sums[0], sums[1], sums[2], sums[3]
        row_grad = jax.vjp(coefficients, state_row)[1]((gp_re, gp_im, gf_re, gf_im))[0]
        in_grad = contract_rows(mine(normed_low), drive_low)
        normed_grad = mixed_grad * feature_row[2] + jnp.dot(
            drive_low, in_low, preferred_element_type=jnp.float32
        )
        gain_grad = jnp.sum(normed_grad * unit, 0)
        bias_grad = jnp.sum(normed_grad, 0)
        unit_grad = normed_grad * feature_row[0]
        first_mean = jnp.mean(unit_grad, 1, keepdims=True)
        second_mean = jnp.mean(unit_grad * unit, 1, keepdims=True)
        grad = grad + scale * (unit_grad - first_mean - unit * second_mean)
        feature_grad = mine(jnp.stack([gain_grad, bias_grad, skip_grad, gate_bias_grad]))
        layer_grads[layer] = (in_grad, out_grad, gate_grad, feature_grad, row_grad)
    stacked_in = jnp.stack([entry[0] for entry in layer_grads])
    stacked_out = jnp.stack([entry[1] for entry in layer_grads])
    stacked_gate = jnp.stack([entry[2] for entry in layer_grads])
    stacked_feature = jnp.stack([entry[3] for entry in layer_grads])
    stacked_state = jnp.stack([entry[4] for entry in layer_grads])
    summed = sum_over_seq((stacked_in, stacked_out, stacked_gate, stacked_feature, stacked_state))
    factor = 1.0 / math.sqrt(count * lax.axis_size("seq"))
    grad_in = summed[0] * factor
    grad_out = summed[1] * factor
    grad_gate = summed[2] * factor
    grad_feature = summed[3] * factor
    grad_state = summed[4] * factor
    new_in = update(input_matrix, grad_in, velocity_input, average_input, slow_rate, 0.0)
    new_out = update(output_matrix, grad_out, velocity_output, average_output, slow_rate, 0.0)
    new_gate = update(gate_matrix, grad_gate, velocity_gate, average_gate, main_rate, weight_decay)
    new_feature = update(
        feature_vectors, grad_feature, velocity_feature, average_feature, main_rate, weight_decay
    )
    new_state = update(state_vectors, grad_state, velocity_state, average_state, slow_rate, 0.0)
    return (
        mine(stream),
        mine(grad),
        grad_in,
        grad_out,
        grad_gate,
        grad_feature,
        grad_state,
        new_in[0],
        new_out[0],
        new_gate[0],
        new_feature[0],
        new_state[3],
        new_in[1],
        new_out[1],
        new_gate[1],
        new_feature[1],
        new_state[1],
        new_in[2],
        new_out[2],
        new_gate[2],
        new_feature[2],
        new_state[2],
    )


def solution(mesh):
    feat = P(None, None, "feat")
    rows = P(None, "feat", None)
    tokens = P("seq", "feat")
    return jax.shard_map(
        body,
        mesh=mesh,
        in_specs=(
            tokens,
            tokens,
            P("seq"),
            P("seq"),
            rows,
            feat,
            feat,
            feat,
            P(),
            rows,
            feat,
            feat,
            feat,
            P(),
            rows,
            feat,
            feat,
            feat,
            P(),
        ),
        out_specs=(
            tokens,
            tokens,
            rows,
            feat,
            feat,
            feat,
            P(),
            rows,
            feat,
            feat,
            feat,
            P(),
            rows,
            feat,
            feat,
            feat,
            P(),
            rows,
            feat,
            feat,
            feat,
            P(),
        ),
        check_vma=False,
    )
```

```python
import math

import jax
import jax.numpy as jnp
from jax import lax
from jax.experimental import pallas as pl
from jax.experimental.pallas import tpu as pltpu
from jax.sharding import PartitionSpec as P

epsilon = 1e-05
momentum = 0.9
smoothing = 0.5
slow_rate = 0.02
main_rate = 0.05
weight_decay = 0.1


def smooth(value):
    return jax.nn.gelu(value, approximate=False)


def masks_of(starts, lengths, count):
    position = jnp.arange(count, dtype=jnp.int32)[:, None]
    begin = starts[None, :]
    finish = begin + lengths[None, :]
    inside = (position >= begin) & (position < finish)
    alive = jnp.any(inside, 1)
    opening = jnp.any(inside & (position == begin), 1)
    closing = jnp.any(inside & (position == finish - 1), 1)
    return (
        alive.astype(jnp.float32),
        (alive & ~opening).astype(jnp.float32),
        (alive & ~closing).astype(jnp.float32),
    )


def coefficients(state_row):
    rate = -jnp.exp(state_row[0])
    frequency = state_row[1]
    timestep = jnp.exp(state_row[2])
    decay = jnp.exp(rate * timestep)
    angle = frequency * timestep
    pole_real = decay * jnp.cos(angle)
    pole_imag = decay * jnp.sin(angle)
    denom = rate * rate + frequency * frequency
    factor_real = ((pole_real - 1.0) * rate + pole_imag * frequency) / denom
    factor_imag = (pole_imag * rate - (pole_real - 1.0) * frequency) / denom
    return (pole_real, pole_imag, factor_real, factor_imag)


def tile_scan(x_re, x_im, keep, powers, down):
    reps = x_re.shape[1] // keep.shape[1]
    rows = lax.broadcasted_iota(jnp.int32, keep.shape, 0)
    b_re, b_im = x_re, x_im
    for level, k in enumerate((1, 2, 4)):
        shift = 8 - k if down else k
        valid = rows <= 7 - k if down else rows >= k
        gate = jnp.tile(jnp.where(valid, keep, 0.0), (1, reps))
        p_re = pltpu.roll(b_re, shift, 0)
        p_im = pltpu.roll(b_im, shift, 0)
        w_re = powers[0][(0, 1, 3)[level] : (0, 1, 3)[level] + 1]
        w_im = powers[1][(0, 1, 3)[level] : (0, 1, 3)[level] + 1]
        b_re = b_re + gate * (w_re * p_re - w_im * p_im)
        b_im = b_im + gate * (w_re * p_im + w_im * p_re)
        keep = keep * jnp.where(valid, pltpu.roll(keep, shift, 0), 1.0)
    return b_re, b_im, jnp.tile(keep, (1, reps))


def blocked_scan(count, width, pow_ref, starts_ref, lengths_ref, load_up, load_down, store_up, store_down):
    tiles = count // 8
    slots = starts_ref.shape[0]

    def keeps(t0, downward):
        rows = lax.broadcasted_iota(jnp.int32, (8, 128), 0) + t0
        inside = jnp.zeros((8, 128), jnp.bool_)
        for slot in range(slots):
            begin = starts_ref[slot]
            finish = begin + lengths_ref[slot]
            if downward:
                inside = inside | ((rows >= begin) & (rows < finish - 1))
            else:
                inside = inside | ((rows > begin) & (rows < finish))
        return inside.astype(jnp.float32)

    up_powers = (pow_ref[0], pow_ref[1])
    down_powers = (pow_ref[2], pow_ref[3])

    def carry_in(b_re, b_im, reach, powers, h_re, h_im):
        q_re = powers[0] * h_re - powers[1] * h_im
        q_im = powers[0] * h_im + powers[1] * h_re
        return b_re + reach * q_re, b_im + reach * q_im

    def step(i, carry):
        u_re, u_im, d_re, d_im = carry
        tu = pl.multiple_of(i * 8, 8)
        td = pl.multiple_of((tiles - 1 - i) * 8, 8)
        xu_re, xu_im = load_up(tu)
        xd_re, xd_im = load_down(td)
        bu_re, bu_im, ru = tile_scan(xu_re, xu_im, keeps(tu, False), up_powers, False)
        bd_re, bd_im, rd = tile_scan(xd_re, xd_im, keeps(td, True), up_powers, True)
        hu_re, hu_im = carry_in(bu_re, bu_im, ru, up_powers, u_re, u_im)
        hd_re, hd_im = carry_in(bd_re, bd_im, rd, down_powers, d_re, d_im)
        store_up(tu, hu_re, hu_im)
        store_down(td, hd_re, hd_im)
        return (hu_re[7:8], hu_im[7:8], hd_re[0:1], hd_im[0:1])

    zeros = jnp.zeros((1, width), jnp.float32)
    lax.fori_loop(0, tiles, step, (zeros, zeros, zeros, zeros), unroll=2)


def pole_powers(p_re, p_im):
    rows_re = [p_re]
    rows_im = [p_im]
    for _ in range(7):
        a, b = rows_re[-1], rows_im[-1]
        rows_re.append(a * p_re - b * p_im)
        rows_im.append(a * p_im + b * p_re)
    up_re = jnp.stack(rows_re)
    up_im = jnp.stack(rows_im)
    return jnp.stack([up_re, up_im, up_re[::-1], up_im[::-1]])


def recurrence_kernel(starts_ref, lengths_ref, pow_ref, x_ref, out_ref):
    count = x_ref.shape[0]
    width = pow_ref.shape[2]

    def load(t):
        return x_ref[pl.ds(t, 8), pl.ds(0, width)], x_ref[pl.ds(t, 8), pl.ds(width, width)]

    def store(column):
        def put(t, h_re, h_im):
            out_ref[pl.ds(t, 8), pl.ds(column, width)] = h_re
            out_ref[pl.ds(t, 8), pl.ds(column + width, width)] = h_im

        return put

    blocked_scan(count, width, pow_ref, starts_ref, lengths_ref, load, load, store(0), store(2 * width))


def recurrence(starts, lengths, powers, x):
    count, double = x.shape
    vmem = pl.BlockSpec(memory_space=pltpu.VMEM)
    smem = pl.BlockSpec(memory_space=pltpu.SMEM)
    return pl.pallas_call(
        recurrence_kernel,
        out_shape=jax.ShapeDtypeStruct((count, 2 * double), jnp.float32),
        in_specs=[smem, smem, vmem, vmem],
        out_specs=vmem,
        cost_estimate=pl.CostEstimate(
            flops=20 * count * double, transcendentals=0, bytes_accessed=16 * count * double
        ),
    )(starts, lengths, powers, x)


MESH = pl.DeviceIdType.MESH


def ring_place(position, n):
    upper = position // (n // 2)
    return (1 - upper) * (2 * position) + upper * (2 * (n - 1 - position) + 1)


def ring_position(index, n):
    odd = index % 2
    return (1 - odd) * (index // 2) + odd * (n - 1 - index // 2)


def ring_sum_kernel(n, x_ref, r_ref, o_ref, low, slots, rs_send, rs_recv, credit, done, ag_send, ag_recv):
    rows = x_ref.shape[0]
    half = rows // 2
    size = half // n
    me = ring_position(lax.axis_index("seq"), n)
    right = ring_place((me + 1) % n, n)
    left = ring_place((me + n - 1) % n, n)
    rings = ((0, me, right, left), (1, (n - me) % n, left, right))

    barrier = pltpu.get_barrier_semaphore()
    for neighbour in (left, right):
        pl.semaphore_signal(barrier, 1, device_id={"seq": neighbour}, device_id_type=MESH)
    pl.semaphore_wait(barrier, 2)
    o_ref[...] = x_ref[...]
    low[...] = x_ref[...].astype(low.dtype)

    def block(ring, k):
        return pl.ds(pl.multiple_of(ring * half + k * size, 8), size)

    def scatter_copy(ring, place, target, s):
        return pltpu.make_async_remote_copy(
            src_ref=low.at[block(ring, (place - s + n) % n)],
            dst_ref=slots.at[ring, s % 2],
            send_sem=rs_send.at[ring, s % 2],
            recv_sem=rs_recv.at[ring, s % 2],
            device_id={"seq": target},
            device_id_type=MESH,
        )

    def scatter_step(s, carry):
        copies = []
        for ring, place, target, source in rings:

            @pl.when(s >= 2)
            def _():
                pl.semaphore_wait(credit.at[ring], 1)

            copy = scatter_copy(ring, place, target, s)
            copy.start()
            copies.append(copy)
        for (ring, place, target, source), copy in zip(rings, copies):
            copy.wait_recv()
            into = block(ring, (place - s - 1 + 2 * n) % n)
            total = o_ref[into] + slots[ring, s % 2].astype(jnp.float32)
            o_ref[into] = total
            low[into] = total.astype(low.dtype)
            copy.wait_send()

            @pl.when(s <= n - 4)
            def _():
                pl.semaphore_signal(credit.at[ring], 1, device_id={"seq": source}, device_id_type=MESH)

        return carry

    lax.fori_loop(0, n - 1, scatter_step, 0)
    for ring, place, target, source in rings:
        pl.semaphore_signal(done.at[ring], 1, device_id={"seq": source}, device_id_type=MESH)
    for ring, place, target, source in rings:
        final = block(ring, (place + 1) % n)
        r_ref[final] = o_ref[final].astype(r_ref.dtype)
    for ring, place, target, source in rings:
        pl.semaphore_wait(done.at[ring], 1)

    def gather_copy(ring, place, target, s):
        where = block(ring, (place + 1 - s + n) % n)
        return pltpu.make_async_remote_copy(
            src_ref=r_ref.at[where],
            dst_ref=r_ref.at[where],
            send_sem=ag_send.at[ring, s],
            recv_sem=ag_recv.at[ring, s],
            device_id={"seq": target},
            device_id_type=MESH,
        )

    def gather_step(s, carry):
        for ring, place, target, source in rings:

            @pl.when(s >= 1)
            def _():
                gather_copy(ring, place, target, s - 1).wait_recv()

            gather_copy(ring, place, target, s).start()

            @pl.when(s >= 1)
            def _():
                gather_copy(ring, place, target, s - 1).wait_send()

        return carry

    lax.fori_loop(0, n - 1, gather_step, 0)
    for ring, place, target, source in rings:
        last = gather_copy(ring, place, target, n - 2)
        last.wait_recv()
        last.wait_send()


def ring_sum(x, n):
    rows, lanes = x.shape
    size = rows // (2 * n)
    return pl.pallas_call(
        lambda *refs: ring_sum_kernel(n, *refs),
        out_shape=jax.ShapeDtypeStruct((rows, lanes), jnp.bfloat16),
        in_specs=[pl.BlockSpec(memory_space=pltpu.VMEM)],
        out_specs=pl.BlockSpec(memory_space=pltpu.VMEM),
        scratch_shapes=[
            pltpu.VMEM((rows, lanes), jnp.float32),
            pltpu.VMEM((rows, lanes), jnp.bfloat16),
            pltpu.VMEM((2, 2, size, lanes), jnp.bfloat16),
            pltpu.SemaphoreType.DMA((2, 2)),
            pltpu.SemaphoreType.DMA((2, 2)),
            pltpu.SemaphoreType.REGULAR((2,)),
            pltpu.SemaphoreType.REGULAR((2,)),
            pltpu.SemaphoreType.DMA((2, n - 1)),
            pltpu.SemaphoreType.DMA((2, n - 1)),
        ],
        compiler_params=pltpu.CompilerParams(collective_id=0, has_side_effects=True),
    )(x)


def sum_over_seq(parts):
    n = lax.axis_size("seq")
    flat = jnp.concatenate([part.reshape(-1) for part in parts])
    grain = 2 * n * 16 * 128
    padded = -(-flat.size // grain) * grain
    flat = jnp.pad(flat, (0, padded - flat.size)).reshape(padded // 128, 128)
    total = ring_sum(flat, n).astype(jnp.float32).reshape(-1)
    pieces = []
    start = 0
    for part in parts:
        pieces.append(total[start : start + part.size].reshape(part.shape))
        start += part.size
    return pieces


def adjoint_kernel(starts_ref, lengths_ref, pow_ref, coef_ref, masks_ref, g_ref, states_ref, drive_ref, dg_ref, sums_ref, lam):
    count = g_ref.shape[0]
    width = coef_ref.shape[1]
    pad = 8
    f_re = coef_ref[2:3, :]
    f_im = coef_ref[3:4, :]
    zero_rows = jnp.zeros((pad, 4 * width), jnp.float32)
    lam[0:pad, :] = zero_rows
    lam[pad + count : 2 * pad + count, :] = zero_rows

    def load(column):
        def get(t):
            return g_ref[pl.ds(t, 8), pl.ds(column, width)], g_ref[pl.ds(t, 8), pl.ds(column + width, width)]

        return get

    def store(column):
        def put(t, h_re, h_im):
            lam[pl.ds(pad + t, 8), pl.ds(column, width)] = h_re
            lam[pl.ds(pad + t, 8), pl.ds(column + width, width)] = h_im

        return put

    blocked_scan(count, width, pow_ref, starts_ref, lengths_ref, load(2 * width), load(0), store(0), store(2 * width))

    rows = 16

    def part(ref, start, column):
        return ref[pl.ds(start, rows), pl.ds(column, width)]

    def epilogue(k, sums):
        gp_re, gp_im, gf_re, gf_im = sums
        r0 = pl.multiple_of(k * rows, rows)
        live = masks_ref[pl.ds(r0, rows), 0:1]
        keep_prev = masks_ref[pl.ds(r0, rows), 1:2]
        keep_next = masks_ref[pl.ds(r0, rows), 2:3]
        lb_re = part(lam, pad + r0, 0)
        lb_im = part(lam, pad + r0, width)
        la_re = part(lam, pad + r0, 2 * width)
        la_im = part(lam, pad + r0, 3 * width)
        gu_re = la_re + lb_re
        gu_im = la_im + lb_im
        dg_ref[pl.ds(r0, rows), pl.ds(0, width)] = ((f_re * gu_re + f_im * gu_im) * live).astype(dg_ref.dtype)
        dg_ref[pl.ds(r0, rows), pl.ds(width, width)] = ((f_re * gu_im - f_im * gu_re) * live).astype(dg_ref.dtype)
        d_re = part(drive_ref, r0, 0) * live
        d_im = part(drive_ref, r0, width) * live
        gf_re = gf_re + d_re * gu_re + d_im * gu_im
        gf_im = gf_im + d_re * gu_im - d_im * gu_re
        a_re = part(states_ref, r0, 0) * keep_next
        a_im = part(states_ref, r0, width) * keep_next
        b_re = part(states_ref, r0, 2 * width) * keep_prev
        b_im = part(states_ref, r0, 3 * width) * keep_prev
        ahead_rows = lam[pl.ds(pad + r0, rows + 8), pl.ds(2 * width, 2 * width)][1 : rows + 1]
        behind_rows = lam[pl.ds(r0, rows + 8), pl.ds(0, 2 * width)][pad - 1 : pad - 1 + rows]
        na_re = ahead_rows[:, :width]
        na_im = ahead_rows[:, width:]
        pb_re = behind_rows[:, :width]
        pb_im = behind_rows[:, width:]
        gp_re = gp_re + a_re * na_re + a_im * na_im + b_re * pb_re + b_im * pb_im
        gp_im = gp_im + a_re * na_im - a_im * na_re + b_re * pb_im - b_im * pb_re
        return (gp_re, gp_im, gf_re, gf_im)

    block = jnp.zeros((rows, width), jnp.float32)
    sums = lax.fori_loop(0, count // rows, epilogue, (block, block, block, block))
    for k, value in enumerate(sums):
        sums_ref[k : k + 1, :] = jnp.sum(value, 0, keepdims=True)


def adjoint(starts, lengths, powers, coef, masks, states_grad, states, drive):
    count, quad = states_grad.shape
    width = quad // 4
    vmem = pl.BlockSpec(memory_space=pltpu.VMEM)
    smem = pl.BlockSpec(memory_space=pltpu.SMEM)
    return pl.pallas_call(
        adjoint_kernel,
        out_shape=(
            jax.ShapeDtypeStruct((count, 2 * width), jnp.bfloat16),
            jax.ShapeDtypeStruct((4, width), jnp.float32),
        ),
        in_specs=[smem, smem] + [vmem] * 6,
        out_specs=(vmem, vmem),
        scratch_shapes=[pltpu.VMEM((count + 16, 4 * width), jnp.float32)],
        cost_estimate=pl.CostEstimate(
            flops=60 * count * width, transcendentals=0, bytes_accessed=48 * count * width
        ),
    )(starts, lengths, powers, coef, masks, states_grad, states, drive)


def update(weight, gradient, velocity, average, rate, decay):
    adjusted = gradient + decay * weight
    velocity_new = momentum * velocity + adjusted
    change = -rate * (adjusted + momentum * velocity_new)
    weight_new = weight + change
    average_new = smoothing * average + (1.0 - smoothing) * weight_new
    return (weight_new, velocity_new, average_new, change)


def contract_rows(left, right):
    return lax.dot_general(
        left, right, (((0,), (0,)), ((), ())), preferred_element_type=jnp.float32
    )


def contract_cols(left, right):
    return lax.dot_general(
        left, right, (((1,), (1,)), ((), ())), preferred_element_type=jnp.float32
    )


def gather_feat(value, axis):
    return lax.all_gather(value, "feat", axis=axis, tiled=True)


def body(
    activations_in,
    cotangent,
    seq_start,
    seq_length,
    input_matrix,
    output_matrix,
    gate_matrix,
    feature_vectors,
    state_vectors,
    velocity_input,
    velocity_output,
    velocity_gate,
    velocity_feature,
    velocity_state,
    average_input,
    average_output,
    average_gate,
    average_feature,
    average_state,
):
    count = activations_in.shape[0]
    shard = activations_in.shape[1]
    layers = input_matrix.shape[0]
    width = state_vectors.shape[2]
    me = lax.axis_index("feat")
    offset = me * shard

    def mine(value):
        return lax.dynamic_slice_in_dim(value, offset, shard, axis=value.ndim - 1)

    alive, carry_prev, carry_next = masks_of(seq_start, seq_length, count)
    zero = jnp.zeros((1,), jnp.float32)
    after_next = jnp.concatenate([zero, carry_next[:-1]])
    before_prev = jnp.concatenate([carry_prev[1:], zero])
    mask_columns = jnp.stack([alive, carry_prev, carry_next, jnp.zeros_like(alive)], 1)


    in_all = gather_feat(input_matrix.astype(jnp.bfloat16), 1)
    rows_out = output_matrix.shape[1]
    paired = [
        gather_feat(jnp.concatenate([output_matrix[k], gate_matrix[k]], 0).astype(jnp.bfloat16), 1)
        for k in range(layers)
    ]
    out_all = [pair[:rows_out] for pair in paired]
    gate_all = [pair[rows_out:] for pair in paired]
    feature_all = gather_feat(feature_vectors, 2)
    stream = gather_feat(activations_in, 1).astype(jnp.float32)

    saved = []
    for layer in range(layers):
        in_low = in_all[layer]
        out_low = out_all[layer]
        gate_low = gate_all[layer]
        feature_row = feature_all[layer]
        pole_re, pole_im, factor_re, factor_im = coefficients(state_vectors[layer])
        center = jnp.mean(stream, 1, keepdims=True)
        spread = stream - center
        scale = lax.rsqrt(jnp.mean(spread * spread, 1, keepdims=True) + epsilon)
        unit = spread * scale
        normed = unit * feature_row[0] + feature_row[1]
        normed_low = normed.astype(jnp.bfloat16)
        drive = jnp.dot(normed_low, in_low, preferred_element_type=jnp.float32)
        drive_re = drive[:, :width]
        drive_im = drive[:, width:]
        source = jnp.concatenate(
            [
                (drive_re * factor_re - drive_im * factor_im) * alive[:, None],
                (drive_re * factor_im + drive_im * factor_re) * alive[:, None],
            ],
            1,
        )
        states = recurrence(seq_start, seq_length, pole_powers(pole_re, pole_im), source)
        states_low = states.astype(jnp.bfloat16)
        mixed = (
            jnp.dot(states_low, out_low, preferred_element_type=jnp.float32)
            + feature_row[2] * normed
        )
        cdf = (lax.erf(mixed * (1.0 / math.sqrt(2.0))) + 1.0) / 2.0
        act = mixed * cdf
        act_low = act.astype(jnp.bfloat16)
        pre = jnp.dot(act_low, gate_low, preferred_element_type=jnp.float32) + feature_row[3]
        saved.append((scale, unit, normed_low, drive, states, states_low, mixed, act, act_low, pre, cdf))
        stream = stream + act * jax.nn.sigmoid(pre)

    grad = gather_feat(cotangent, 1).astype(jnp.float32) * alive[:, None]
    layer_grads = [None] * layers
    for layer in reversed(range(layers)):
        scale, unit, normed_low, drive, states, states_low, mixed, act, act_low, pre, cdf = saved[layer]
        in_low = in_all[layer]
        out_low = out_all[layer]
        gate_low = gate_all[layer]
        feature_row = feature_all[layer]
        state_row = state_vectors[layer]
        pole_re, pole_im, factor_re, factor_im = coefficients(state_row)
        gate = jax.nn.sigmoid(pre)
        pre_grad = (grad * act * gate * (1.0 - gate)).astype(jnp.bfloat16)
        gate_grad = contract_rows(act_low, mine(pre_grad))
        gate_bias_grad = jnp.sum(pre_grad.astype(jnp.float32), 0)
        act_grad = grad * gate + contract_cols(pre_grad, gate_low)
        density = jnp.exp(mixed * mixed * -0.5) * (1.0 / math.sqrt(2.0 * math.pi))
        mixed_grad = act_grad * (cdf + mixed * density)
        normed = unit * feature_row[0] + feature_row[1]
        skip_grad = jnp.sum(mixed_grad * normed, 0)
        mixed_low = mixed_grad.astype(jnp.bfloat16)
        out_grad = contract_rows(states_low, mine(mixed_low))
        states_grad = contract_cols(mixed_low, out_low)
        coef = jnp.stack([pole_re, pole_im, factor_re, factor_im])
        drive_low, sums = adjoint(
            seq_start,
            seq_length,
            pole_powers(pole_re, -pole_im),
            coef,
            mask_columns,
            states_grad,
            states,
            drive,
        )
        gp_re, gp_im, gf_re, gf_im = sums[0], sums[1], sums[2], sums[3]
        row_grad = jax.vjp(coefficients, state_row)[1]((gp_re, gp_im, gf_re, gf_im))[0]
        in_grad = contract_rows(mine(normed_low), drive_low)
        normed_grad = mixed_grad * feature_row[2] + jnp.dot(
            drive_low, in_low.T, preferred_element_type=jnp.float32
        )
        gain_grad = jnp.sum(normed_grad * unit, 0)
        bias_grad = jnp.sum(normed_grad, 0)
        unit_grad = normed_grad * feature_row[0]
        first_mean = jnp.mean(unit_grad, 1, keepdims=True)
        second_mean = jnp.mean(unit_grad * unit, 1, keepdims=True)
        grad = grad + scale * (unit_grad - first_mean - unit * second_mean)
        feature_grad = mine(jnp.stack([gain_grad, bias_grad, skip_grad, gate_bias_grad]))
        layer_grads[layer] = (in_grad, out_grad, gate_grad, feature_grad, row_grad)
    stacked_in = jnp.stack([entry[0] for entry in layer_grads])
    stacked_out = jnp.stack([entry[1] for entry in layer_grads])
    stacked_gate = jnp.stack([entry[2] for entry in layer_grads])
    stacked_feature = jnp.stack([entry[3] for entry in layer_grads])
    stacked_state = jnp.stack([entry[4] for entry in layer_grads])
    summed = sum_over_seq((stacked_in, stacked_out, stacked_gate, stacked_feature, stacked_state))
    factor = 1.0 / math.sqrt(count * lax.axis_size("seq"))
    grad_in = summed[0] * factor
    grad_out = summed[1] * factor
    grad_gate = summed[2] * factor
    grad_feature = summed[3] * factor
    grad_state = summed[4] * factor
    new_in = update(input_matrix, grad_in, velocity_input, average_input, slow_rate, 0.0)
    new_out = update(output_matrix, grad_out, velocity_output, average_output, slow_rate, 0.0)
    new_gate = update(gate_matrix, grad_gate, velocity_gate, average_gate, main_rate, weight_decay)
    new_feature = update(
        feature_vectors, grad_feature, velocity_feature, average_feature, main_rate, weight_decay
    )
    new_state = update(state_vectors, grad_state, velocity_state, average_state, slow_rate, 0.0)
    return (
        mine(stream),
        mine(grad),
        grad_in,
        grad_out,
        grad_gate,
        grad_feature,
        grad_state,
        new_in[0],
        new_out[0],
        new_gate[0],
        new_feature[0],
        new_state[3],
        new_in[1],
        new_out[1],
        new_gate[1],
        new_feature[1],
        new_state[1],
        new_in[2],
        new_out[2],
        new_gate[2],
        new_feature[2],
        new_state[2],
    )


def solution(mesh):
    feat = P(None, None, "feat")
    rows = P(None, "feat", None)
    tokens = P("seq", "feat")
    return jax.shard_map(
        body,
        mesh=mesh,
        in_specs=(
            tokens,
            tokens,
            P("seq"),
            P("seq"),
            rows,
            feat,
            feat,
            feat,
            P(),
            rows,
            feat,
            feat,
            feat,
            P(),
            rows,
            feat,
            feat,
            feat,
            P(),
        ),
        out_specs=(
            tokens,
            tokens,
            rows,
            feat,
            feat,
            feat,
            P(),
            rows,
            feat,
            feat,
            feat,
            P(),
            rows,
            feat,
            feat,
            feat,
            P(),
            rows,
            feat,
            feat,
            feat,
            P(),
        ),
        check_vma=False,
    )
```

```python
import math

import jax
import jax.numpy as jnp
from jax import lax
from jax.experimental import pallas as pl
from jax.experimental.pallas import tpu as pltpu
from jax.sharding import PartitionSpec as P

epsilon = 1e-05
momentum = 0.9
smoothing = 0.5
slow_rate = 0.02
main_rate = 0.05
weight_decay = 0.1


def smooth(value):
    return jax.nn.gelu(value, approximate=False)


def masks_of(starts, lengths, count):
    position = jnp.arange(count, dtype=jnp.int32)[:, None]
    begin = starts[None, :]
    finish = begin + lengths[None, :]
    inside = (position >= begin) & (position < finish)
    alive = jnp.any(inside, 1)
    opening = jnp.any(inside & (position == begin), 1)
    closing = jnp.any(inside & (position == finish - 1), 1)
    return (
        alive.astype(jnp.float32),
        (alive & ~opening).astype(jnp.float32),
        (alive & ~closing).astype(jnp.float32),
    )


def coefficients(state_row):
    rate = -jnp.exp(state_row[0])
    frequency = state_row[1]
    timestep = jnp.exp(state_row[2])
    decay = jnp.exp(rate * timestep)
    angle = frequency * timestep
    pole_real = decay * jnp.cos(angle)
    pole_imag = decay * jnp.sin(angle)
    denom = rate * rate + frequency * frequency
    factor_real = ((pole_real - 1.0) * rate + pole_imag * frequency) / denom
    factor_imag = (pole_imag * rate - (pole_real - 1.0) * frequency) / denom
    return (pole_real, pole_imag, factor_real, factor_imag)


def tile_scan(x_re, x_im, keep, powers, down):
    reps = x_re.shape[1] // keep.shape[1]
    rows = lax.broadcasted_iota(jnp.int32, keep.shape, 0)
    b_re, b_im = x_re, x_im
    for level, k in enumerate((1, 2, 4)):
        shift = 8 - k if down else k
        valid = rows <= 7 - k if down else rows >= k
        gate = jnp.tile(jnp.where(valid, keep, 0.0), (1, reps))
        p_re = pltpu.roll(b_re, shift, 0)
        p_im = pltpu.roll(b_im, shift, 0)
        w_re = powers[0][(0, 1, 3)[level] : (0, 1, 3)[level] + 1]
        w_im = powers[1][(0, 1, 3)[level] : (0, 1, 3)[level] + 1]
        b_re = b_re + gate * (w_re * p_re - w_im * p_im)
        b_im = b_im + gate * (w_re * p_im + w_im * p_re)
        keep = keep * jnp.where(valid, pltpu.roll(keep, shift, 0), 1.0)
    return b_re, b_im, jnp.tile(keep, (1, reps))


def blocked_scan(count, width, pow_ref, starts_ref, lengths_ref, load_up, load_down, store_up, store_down):
    tiles = count // 8
    slots = starts_ref.shape[0]

    def keeps(t0, downward):
        rows = lax.broadcasted_iota(jnp.int32, (8, 128), 0) + t0
        inside = jnp.zeros((8, 128), jnp.bool_)
        for slot in range(slots):
            begin = starts_ref[slot]
            finish = begin + lengths_ref[slot]
            if downward:
                inside = inside | ((rows >= begin) & (rows < finish - 1))
            else:
                inside = inside | ((rows > begin) & (rows < finish))
        return inside.astype(jnp.float32)

    up_powers = (pow_ref[0], pow_ref[1])
    down_powers = (pow_ref[2], pow_ref[3])

    def carry_in(b_re, b_im, reach, powers, h_re, h_im):
        q_re = powers[0] * h_re - powers[1] * h_im
        q_im = powers[0] * h_im + powers[1] * h_re
        return b_re + reach * q_re, b_im + reach * q_im

    def step(i, carry):
        u_re, u_im, d_re, d_im = carry
        tu = pl.multiple_of(i * 8, 8)
        td = pl.multiple_of((tiles - 1 - i) * 8, 8)
        xu_re, xu_im = load_up(tu)
        xd_re, xd_im = load_down(td)
        bu_re, bu_im, ru = tile_scan(xu_re, xu_im, keeps(tu, False), up_powers, False)
        bd_re, bd_im, rd = tile_scan(xd_re, xd_im, keeps(td, True), up_powers, True)
        hu_re, hu_im = carry_in(bu_re, bu_im, ru, up_powers, u_re, u_im)
        hd_re, hd_im = carry_in(bd_re, bd_im, rd, down_powers, d_re, d_im)
        store_up(tu, hu_re, hu_im)
        store_down(td, hd_re, hd_im)
        return (hu_re[7:8], hu_im[7:8], hd_re[0:1], hd_im[0:1])

    zeros = jnp.zeros((1, width), jnp.float32)
    lax.fori_loop(0, tiles, step, (zeros, zeros, zeros, zeros), unroll=2)


def pole_powers(p_re, p_im):
    rows_re = [p_re]
    rows_im = [p_im]
    for _ in range(7):
        a, b = rows_re[-1], rows_im[-1]
        rows_re.append(a * p_re - b * p_im)
        rows_im.append(a * p_im + b * p_re)
    up_re = jnp.stack(rows_re)
    up_im = jnp.stack(rows_im)
    return jnp.stack([up_re, up_im, up_re[::-1], up_im[::-1]])


def recurrence_kernel(starts_ref, lengths_ref, pow_ref, x_ref, out_ref):
    count = x_ref.shape[0]
    width = pow_ref.shape[2]

    def load(t):
        return x_ref[pl.ds(t, 8), pl.ds(0, width)], x_ref[pl.ds(t, 8), pl.ds(width, width)]

    def store(column):
        def put(t, h_re, h_im):
            out_ref[pl.ds(t, 8), pl.ds(column, width)] = h_re
            out_ref[pl.ds(t, 8), pl.ds(column + width, width)] = h_im

        return put

    blocked_scan(count, width, pow_ref, starts_ref, lengths_ref, load, load, store(0), store(2 * width))


def recurrence(starts, lengths, powers, x):
    count, double = x.shape
    vmem = pl.BlockSpec(memory_space=pltpu.VMEM)
    smem = pl.BlockSpec(memory_space=pltpu.SMEM)
    return pl.pallas_call(
        recurrence_kernel,
        out_shape=jax.ShapeDtypeStruct((count, 2 * double), jnp.float32),
        in_specs=[smem, smem, vmem, vmem],
        out_specs=vmem,
        cost_estimate=pl.CostEstimate(
            flops=20 * count * double, transcendentals=0, bytes_accessed=16 * count * double
        ),
    )(starts, lengths, powers, x)


MESH = pl.DeviceIdType.MESH


def ring_place(position, n):
    upper = position // (n // 2)
    return (1 - upper) * (2 * position) + upper * (2 * (n - 1 - position) + 1)


def ring_position(index, n):
    odd = index % 2
    return (1 - odd) * (index // 2) + odd * (n - 1 - index // 2)


def ring_sum_kernel(n, x_ref, r_ref, o_ref, low, slots, rs_send, rs_recv, credit, done, ag_send, ag_recv):
    rows = x_ref.shape[0]
    half = rows // 2
    size = half // n
    me = ring_position(lax.axis_index("seq"), n)
    right = ring_place((me + 1) % n, n)
    left = ring_place((me + n - 1) % n, n)
    rings = ((0, me, right, left), (1, (n - me) % n, left, right))

    barrier = pltpu.get_barrier_semaphore()
    for neighbour in (left, right):
        pl.semaphore_signal(barrier, 1, device_id={"seq": neighbour}, device_id_type=MESH)
    pl.semaphore_wait(barrier, 2)
    o_ref[...] = x_ref[...]
    low[...] = x_ref[...].astype(low.dtype)

    def block(ring, k):
        return pl.ds(pl.multiple_of(ring * half + k * size, 8), size)

    def scatter_copy(ring, place, target, s):
        return pltpu.make_async_remote_copy(
            src_ref=low.at[block(ring, (place - s + n) % n)],
            dst_ref=slots.at[ring, s % 2],
            send_sem=rs_send.at[ring, s % 2],
            recv_sem=rs_recv.at[ring, s % 2],
            device_id={"seq": target},
            device_id_type=MESH,
        )

    def scatter_step(s, carry):
        copies = []
        for ring, place, target, source in rings:

            @pl.when(s >= 2)
            def _():
                pl.semaphore_wait(credit.at[ring], 1)

            copy = scatter_copy(ring, place, target, s)
            copy.start()
            copies.append(copy)
        for (ring, place, target, source), copy in zip(rings, copies):
            copy.wait_recv()
            into = block(ring, (place - s - 1 + 2 * n) % n)
            total = o_ref[into] + slots[ring, s % 2].astype(jnp.float32)
            o_ref[into] = total
            low[into] = total.astype(low.dtype)
            copy.wait_send()

            @pl.when(s <= n - 4)
            def _():
                pl.semaphore_signal(credit.at[ring], 1, device_id={"seq": source}, device_id_type=MESH)

        return carry

    lax.fori_loop(0, n - 1, scatter_step, 0)
    for ring, place, target, source in rings:
        pl.semaphore_signal(done.at[ring], 1, device_id={"seq": source}, device_id_type=MESH)
    for ring, place, target, source in rings:
        final = block(ring, (place + 1) % n)
        r_ref[final] = o_ref[final].astype(r_ref.dtype)
    for ring, place, target, source in rings:
        pl.semaphore_wait(done.at[ring], 1)

    def gather_copy(ring, place, target, s):
        where = block(ring, (place + 1 - s + n) % n)
        return pltpu.make_async_remote_copy(
            src_ref=r_ref.at[where],
            dst_ref=r_ref.at[where],
            send_sem=ag_send.at[ring, s],
            recv_sem=ag_recv.at[ring, s],
            device_id={"seq": target},
            device_id_type=MESH,
        )

    def gather_step(s, carry):
        for ring, place, target, source in rings:

            @pl.when(s >= 1)
            def _():
                gather_copy(ring, place, target, s - 1).wait_recv()

            gather_copy(ring, place, target, s).start()

            @pl.when(s >= 1)
            def _():
                gather_copy(ring, place, target, s - 1).wait_send()

        return carry

    lax.fori_loop(0, n - 1, gather_step, 0)
    for ring, place, target, source in rings:
        last = gather_copy(ring, place, target, n - 2)
        last.wait_recv()
        last.wait_send()


def ring_sum(x, n):
    rows, lanes = x.shape
    size = rows // (2 * n)
    return pl.pallas_call(
        lambda *refs: ring_sum_kernel(n, *refs),
        out_shape=jax.ShapeDtypeStruct((rows, lanes), jnp.bfloat16),
        in_specs=[pl.BlockSpec(memory_space=pltpu.VMEM)],
        out_specs=pl.BlockSpec(memory_space=pltpu.VMEM),
        scratch_shapes=[
            pltpu.VMEM((rows, lanes), jnp.float32),
            pltpu.VMEM((rows, lanes), jnp.bfloat16),
            pltpu.VMEM((2, 2, size, lanes), jnp.bfloat16),
            pltpu.SemaphoreType.DMA((2, 2)),
            pltpu.SemaphoreType.DMA((2, 2)),
            pltpu.SemaphoreType.REGULAR((2,)),
            pltpu.SemaphoreType.REGULAR((2,)),
            pltpu.SemaphoreType.DMA((2, n - 1)),
            pltpu.SemaphoreType.DMA((2, n - 1)),
        ],
        compiler_params=pltpu.CompilerParams(collective_id=0, has_side_effects=True),
    )(x)


def sum_over_seq(parts):
    n = lax.axis_size("seq")
    flat = jnp.concatenate([part.reshape(-1) for part in parts])
    grain = 2 * n * 16 * 128
    padded = -(-flat.size // grain) * grain
    flat = jnp.pad(flat, (0, padded - flat.size)).reshape(padded // 128, 128)
    total = ring_sum(flat, n).astype(jnp.float32).reshape(-1)
    pieces = []
    start = 0
    for part in parts:
        pieces.append(total[start : start + part.size].reshape(part.shape))
        start += part.size
    return pieces


def adjoint_kernel(starts_ref, lengths_ref, pow_ref, coef_ref, masks_ref, g_ref, states_ref, drive_ref, dg_ref, sums_ref, lam):
    count = g_ref.shape[0]
    width = coef_ref.shape[1]
    pad = 8
    f_re = coef_ref[2:3, :]
    f_im = coef_ref[3:4, :]
    zero_rows = jnp.zeros((pad, 4 * width), jnp.float32)
    lam[0:pad, :] = zero_rows
    lam[pad + count : 2 * pad + count, :] = zero_rows

    def load(column):
        def get(t):
            return g_ref[pl.ds(t, 8), pl.ds(column, width)], g_ref[pl.ds(t, 8), pl.ds(column + width, width)]

        return get

    def store(column):
        def put(t, h_re, h_im):
            lam[pl.ds(pad + t, 8), pl.ds(column, width)] = h_re
            lam[pl.ds(pad + t, 8), pl.ds(column + width, width)] = h_im

        return put

    blocked_scan(count, width, pow_ref, starts_ref, lengths_ref, load(2 * width), load(0), store(0), store(2 * width))

    rows = 16

    def part(ref, start, column):
        return ref[pl.ds(start, rows), pl.ds(column, width)]

    def epilogue(k, sums):
        gp_re, gp_im, gf_re, gf_im = sums
        r0 = pl.multiple_of(k * rows, rows)
        live = masks_ref[pl.ds(r0, rows), 0:1]
        keep_prev = masks_ref[pl.ds(r0, rows), 1:2]
        keep_next = masks_ref[pl.ds(r0, rows), 2:3]
        lb_re = part(lam, pad + r0, 0)
        lb_im = part(lam, pad + r0, width)
        la_re = part(lam, pad + r0, 2 * width)
        la_im = part(lam, pad + r0, 3 * width)
        gu_re = la_re + lb_re
        gu_im = la_im + lb_im
        dg_ref[pl.ds(r0, rows), pl.ds(0, width)] = ((f_re * gu_re + f_im * gu_im) * live).astype(dg_ref.dtype)
        dg_ref[pl.ds(r0, rows), pl.ds(width, width)] = ((f_re * gu_im - f_im * gu_re) * live).astype(dg_ref.dtype)
        d_re = part(drive_ref, r0, 0) * live
        d_im = part(drive_ref, r0, width) * live
        gf_re = gf_re + d_re * gu_re + d_im * gu_im
        gf_im = gf_im + d_re * gu_im - d_im * gu_re
        a_re = part(states_ref, r0, 0) * keep_next
        a_im = part(states_ref, r0, width) * keep_next
        b_re = part(states_ref, r0, 2 * width) * keep_prev
        b_im = part(states_ref, r0, 3 * width) * keep_prev
        ahead_rows = lam[pl.ds(pad + r0, rows + 8), pl.ds(2 * width, 2 * width)][1 : rows + 1]
        behind_rows = lam[pl.ds(r0, rows + 8), pl.ds(0, 2 * width)][pad - 1 : pad - 1 + rows]
        na_re = ahead_rows[:, :width]
        na_im = ahead_rows[:, width:]
        pb_re = behind_rows[:, :width]
        pb_im = behind_rows[:, width:]
        gp_re = gp_re + a_re * na_re + a_im * na_im + b_re * pb_re + b_im * pb_im
        gp_im = gp_im + a_re * na_im - a_im * na_re + b_re * pb_im - b_im * pb_re
        return (gp_re, gp_im, gf_re, gf_im)

    block = jnp.zeros((rows, width), jnp.float32)
    sums = lax.fori_loop(0, count // rows, epilogue, (block, block, block, block))
    for k, value in enumerate(sums):
        sums_ref[k : k + 1, :] = jnp.sum(value, 0, keepdims=True)


def adjoint(starts, lengths, powers, coef, masks, states_grad, states, drive):
    count, quad = states_grad.shape
    width = quad // 4
    vmem = pl.BlockSpec(memory_space=pltpu.VMEM)
    smem = pl.BlockSpec(memory_space=pltpu.SMEM)
    return pl.pallas_call(
        adjoint_kernel,
        out_shape=(
            jax.ShapeDtypeStruct((count, 2 * width), jnp.bfloat16),
            jax.ShapeDtypeStruct((4, width), jnp.float32),
        ),
        in_specs=[smem, smem] + [vmem] * 6,
        out_specs=(vmem, vmem),
        scratch_shapes=[pltpu.VMEM((count + 16, 4 * width), jnp.float32)],
        cost_estimate=pl.CostEstimate(
            flops=60 * count * width, transcendentals=0, bytes_accessed=48 * count * width
        ),
    )(starts, lengths, powers, coef, masks, states_grad, states, drive)


def update(weight, gradient, velocity, average, rate, decay):
    adjusted = gradient + decay * weight
    velocity_new = momentum * velocity + adjusted
    change = -rate * (adjusted + momentum * velocity_new)
    weight_new = weight + change
    average_new = smoothing * average + (1.0 - smoothing) * weight_new
    return (weight_new, velocity_new, average_new, change)


def contract_rows(left, right):
    return lax.dot_general(
        left, right, (((0,), (0,)), ((), ())), preferred_element_type=jnp.float32
    )


def contract_cols(left, right):
    return lax.dot_general(
        left, right, (((1,), (1,)), ((), ())), preferred_element_type=jnp.float32
    )


def gather_feat(value, axis):
    return lax.all_gather(value, "feat", axis=axis, tiled=True)


def split_exact(value):
    high = lax.reduce_precision(value, exponent_bits=8, mantissa_bits=7)
    rest = value - high
    middle = lax.reduce_precision(rest, exponent_bits=8, mantissa_bits=7)
    little = rest - middle
    return jnp.concatenate([high, middle, little], 0).astype(jnp.bfloat16)


def join_exact(pieces):
    third = pieces.shape[0] // 3
    pieces = pieces.astype(jnp.float32)
    return pieces[:third] + (pieces[third : 2 * third] + pieces[2 * third :])


def body(
    activations_in,
    cotangent,
    seq_start,
    seq_length,
    input_matrix,
    output_matrix,
    gate_matrix,
    feature_vectors,
    state_vectors,
    velocity_input,
    velocity_output,
    velocity_gate,
    velocity_feature,
    velocity_state,
    average_input,
    average_output,
    average_gate,
    average_feature,
    average_state,
):
    count = activations_in.shape[0]
    shard = activations_in.shape[1]
    layers = input_matrix.shape[0]
    width = state_vectors.shape[2]
    me = lax.axis_index("feat")
    offset = me * shard

    def mine(value):
        return lax.dynamic_slice_in_dim(value, offset, shard, axis=value.ndim - 1)

    alive, carry_prev, carry_next = masks_of(seq_start, seq_length, count)
    zero = jnp.zeros((1,), jnp.float32)
    after_next = jnp.concatenate([zero, carry_next[:-1]])
    before_prev = jnp.concatenate([carry_prev[1:], zero])
    mask_columns = jnp.stack([alive, carry_prev, carry_next, jnp.zeros_like(alive)], 1)


    in_all = gather_feat(input_matrix.astype(jnp.bfloat16), 1)
    rows_out = output_matrix.shape[1]
    paired = [
        gather_feat(jnp.concatenate([output_matrix[k], gate_matrix[k]], 0).astype(jnp.bfloat16), 1)
        for k in range(layers)
    ]
    out_all = [pair[:rows_out] for pair in paired]
    gate_all = [pair[rows_out:] for pair in paired]
    feature_pieces = split_exact(feature_vectors.reshape(-1, activations_in.shape[1]))
    feature_rows = feature_pieces.shape[0]
    feature_pad = -(-feature_rows // 16) * 16
    feature_pieces = jnp.pad(feature_pieces, ((0, feature_pad - feature_rows), (0, 0)))
    first = gather_feat(jnp.concatenate([activations_in, feature_pieces], 0), 1)
    stream = first[:count].astype(jnp.float32)
    feature_all = join_exact(first[count : count + feature_rows]).reshape(feature_vectors.shape[:-1] + (-1,))

    saved = []
    for layer in range(layers):
        in_low = in_all[layer]
        out_low = out_all[layer]
        gate_low = gate_all[layer]
        feature_row = feature_all[layer]
        pole_re, pole_im, factor_re, factor_im = coefficients(state_vectors[layer])
        center = jnp.mean(stream, 1, keepdims=True)
        spread = stream - center
        scale = lax.rsqrt(jnp.mean(spread * spread, 1, keepdims=True) + epsilon)
        unit = spread * scale
        normed = unit * feature_row[0] + feature_row[1]
        normed_low = normed.astype(jnp.bfloat16)
        drive = jnp.dot(normed_low, in_low, preferred_element_type=jnp.float32)
        drive_re = drive[:, :width]
        drive_im = drive[:, width:]
        source = jnp.concatenate(
            [
                (drive_re * factor_re - drive_im * factor_im) * alive[:, None],
                (drive_re * factor_im + drive_im * factor_re) * alive[:, None],
            ],
            1,
        )
        states = recurrence(seq_start, seq_length, pole_powers(pole_re, pole_im), source)
        states_low = states.astype(jnp.bfloat16)
        mixed = (
            jnp.dot(states_low, out_low, preferred_element_type=jnp.float32)
            + feature_row[2] * normed
        )
        cdf = (lax.erf(mixed * (1.0 / math.sqrt(2.0))) + 1.0) / 2.0
        act = mixed * cdf
        act_low = act.astype(jnp.bfloat16)
        pre = jnp.dot(act_low, gate_low, preferred_element_type=jnp.float32) + feature_row[3]
        saved.append((scale, unit, normed_low, drive, states, states_low, mixed, act, act_low, pre, cdf))
        stream = stream + act * jax.nn.sigmoid(pre)

    grad = gather_feat(cotangent, 1).astype(jnp.float32) * alive[:, None]
    layer_grads = [None] * layers
    for layer in reversed(range(layers)):
        scale, unit, normed_low, drive, states, states_low, mixed, act, act_low, pre, cdf = saved[layer]
        in_low = in_all[layer]
        out_low = out_all[layer]
        gate_low = gate_all[layer]
        feature_row = feature_all[layer]
        state_row = state_vectors[layer]
        pole_re, pole_im, factor_re, factor_im = coefficients(state_row)
        gate = jax.nn.sigmoid(pre)
        pre_grad = (grad * act * gate * (1.0 - gate)).astype(jnp.bfloat16)
        gate_grad = contract_rows(act_low, mine(pre_grad))
        gate_bias_grad = jnp.sum(pre_grad.astype(jnp.float32), 0)
        act_grad = grad * gate + contract_cols(pre_grad, gate_low)
        density = jnp.exp(mixed * mixed * -0.5) * (1.0 / math.sqrt(2.0 * math.pi))
        mixed_grad = act_grad * (cdf + mixed * density)
        normed = unit * feature_row[0] + feature_row[1]
        skip_grad = jnp.sum(mixed_grad * normed, 0)
        mixed_low = mixed_grad.astype(jnp.bfloat16)
        out_grad = contract_rows(states_low, mine(mixed_low))
        states_grad = contract_cols(mixed_low, out_low)
        coef = jnp.stack([pole_re, pole_im, factor_re, factor_im])
        drive_low, sums = adjoint(
            seq_start,
            seq_length,
            pole_powers(pole_re, -pole_im),
            coef,
            mask_columns,
            states_grad,
            states,
            drive,
        )
        gp_re, gp_im, gf_re, gf_im = sums[0], sums[1], sums[2], sums[3]
        row_grad = jax.vjp(coefficients, state_row)[1]((gp_re, gp_im, gf_re, gf_im))[0]
        in_grad = contract_rows(mine(normed_low), drive_low)
        normed_grad = mixed_grad * feature_row[2] + jnp.dot(
            drive_low, in_low.T, preferred_element_type=jnp.float32
        )
        gain_grad = jnp.sum(normed_grad * unit, 0)
        bias_grad = jnp.sum(normed_grad, 0)
        unit_grad = normed_grad * feature_row[0]
        first_mean = jnp.mean(unit_grad, 1, keepdims=True)
        second_mean = jnp.mean(unit_grad * unit, 1, keepdims=True)
        grad = grad + scale * (unit_grad - first_mean - unit * second_mean)
        feature_grad = mine(jnp.stack([gain_grad, bias_grad, skip_grad, gate_bias_grad]))
        layer_grads[layer] = (in_grad, out_grad, gate_grad, feature_grad, row_grad)
    stacked_in = jnp.stack([entry[0] for entry in layer_grads])
    stacked_out = jnp.stack([entry[1] for entry in layer_grads])
    stacked_gate = jnp.stack([entry[2] for entry in layer_grads])
    stacked_feature = jnp.stack([entry[3] for entry in layer_grads])
    stacked_state = jnp.stack([entry[4] for entry in layer_grads])
    summed = sum_over_seq((stacked_in, stacked_out, stacked_gate, stacked_feature, stacked_state))
    factor = 1.0 / math.sqrt(count * lax.axis_size("seq"))
    grad_in = summed[0] * factor
    grad_out = summed[1] * factor
    grad_gate = summed[2] * factor
    grad_feature = summed[3] * factor
    grad_state = summed[4] * factor
    new_in = update(input_matrix, grad_in, velocity_input, average_input, slow_rate, 0.0)
    new_out = update(output_matrix, grad_out, velocity_output, average_output, slow_rate, 0.0)
    new_gate = update(gate_matrix, grad_gate, velocity_gate, average_gate, main_rate, weight_decay)
    new_feature = update(
        feature_vectors, grad_feature, velocity_feature, average_feature, main_rate, weight_decay
    )
    new_state = update(state_vectors, grad_state, velocity_state, average_state, slow_rate, 0.0)
    return (
        mine(stream),
        mine(grad),
        grad_in,
        grad_out,
        grad_gate,
        grad_feature,
        grad_state,
        new_in[0],
        new_out[0],
        new_gate[0],
        new_feature[0],
        new_state[3],
        new_in[1],
        new_out[1],
        new_gate[1],
        new_feature[1],
        new_state[1],
        new_in[2],
        new_out[2],
        new_gate[2],
        new_feature[2],
        new_state[2],
    )


def solution(mesh):
    feat = P(None, None, "feat")
    rows = P(None, "feat", None)
    tokens = P("seq", "feat")
    return jax.shard_map(
        body,
        mesh=mesh,
        in_specs=(
            tokens,
            tokens,
            P("seq"),
            P("seq"),
            rows,
            feat,
            feat,
            feat,
            P(),
            rows,
            feat,
            feat,
            feat,
            P(),
            rows,
            feat,
            feat,
            feat,
            P(),
        ),
        out_specs=(
            tokens,
            tokens,
            rows,
            feat,
            feat,
            feat,
            P(),
            rows,
            feat,
            feat,
            feat,
            P(),
            rows,
            feat,
            feat,
            feat,
            P(),
            rows,
            feat,
            feat,
            feat,
            P(),
        ),
        check_vma=False,
    )
```

```python
import math

import jax
import jax.numpy as jnp
from jax import lax
from jax.experimental import pallas as pl
from jax.experimental.pallas import tpu as pltpu
from jax.sharding import PartitionSpec as P

epsilon = 1e-05
momentum = 0.9
smoothing = 0.5
slow_rate = 0.02
main_rate = 0.05
weight_decay = 0.1


def smooth(value):
    return jax.nn.gelu(value, approximate=False)


def masks_of(starts, lengths, count):
    position = jnp.arange(count, dtype=jnp.int32)[:, None]
    begin = starts[None, :]
    finish = begin + lengths[None, :]
    inside = (position >= begin) & (position < finish)
    alive = jnp.any(inside, 1)
    opening = jnp.any(inside & (position == begin), 1)
    closing = jnp.any(inside & (position == finish - 1), 1)
    return (
        alive.astype(jnp.float32),
        (alive & ~opening).astype(jnp.float32),
        (alive & ~closing).astype(jnp.float32),
    )


def coefficients(state_row):
    rate = -jnp.exp(state_row[0])
    frequency = state_row[1]
    timestep = jnp.exp(state_row[2])
    decay = jnp.exp(rate * timestep)
    angle = frequency * timestep
    pole_real = decay * jnp.cos(angle)
    pole_imag = decay * jnp.sin(angle)
    denom = rate * rate + frequency * frequency
    factor_real = ((pole_real - 1.0) * rate + pole_imag * frequency) / denom
    factor_imag = (pole_imag * rate - (pole_real - 1.0) * frequency) / denom
    return (pole_real, pole_imag, factor_real, factor_imag)


def tile_scan(x_re, x_im, keep, powers, down):
    reps = x_re.shape[1] // keep.shape[1]
    rows = lax.broadcasted_iota(jnp.int32, keep.shape, 0)
    b_re, b_im = x_re, x_im
    for level, k in enumerate((1, 2, 4)):
        shift = 8 - k if down else k
        valid = rows <= 7 - k if down else rows >= k
        gate = jnp.tile(jnp.where(valid, keep, 0.0), (1, reps))
        p_re = pltpu.roll(b_re, shift, 0)
        p_im = pltpu.roll(b_im, shift, 0)
        w_re = powers[0][(0, 1, 3)[level] : (0, 1, 3)[level] + 1]
        w_im = powers[1][(0, 1, 3)[level] : (0, 1, 3)[level] + 1]
        b_re = b_re + gate * (w_re * p_re - w_im * p_im)
        b_im = b_im + gate * (w_re * p_im + w_im * p_re)
        keep = keep * jnp.where(valid, pltpu.roll(keep, shift, 0), 1.0)
    return b_re, b_im, jnp.tile(keep, (1, reps))


def blocked_scan(count, width, pow_ref, starts_ref, lengths_ref, load_up, load_down, store_up, store_down):
    tiles = count // 8
    slots = starts_ref.shape[0]

    def keeps(t0, downward):
        rows = lax.broadcasted_iota(jnp.int32, (8, 128), 0) + t0
        inside = jnp.zeros((8, 128), jnp.bool_)
        for slot in range(slots):
            begin = starts_ref[slot]
            finish = begin + lengths_ref[slot]
            if downward:
                inside = inside | ((rows >= begin) & (rows < finish - 1))
            else:
                inside = inside | ((rows > begin) & (rows < finish))
        return inside.astype(jnp.float32)

    up_powers = (pow_ref[0], pow_ref[1])
    down_powers = (pow_ref[2], pow_ref[3])

    def carry_in(b_re, b_im, reach, powers, h_re, h_im):
        q_re = powers[0] * h_re - powers[1] * h_im
        q_im = powers[0] * h_im + powers[1] * h_re
        return b_re + reach * q_re, b_im + reach * q_im

    def step(i, carry):
        u_re, u_im, d_re, d_im = carry
        tu = pl.multiple_of(i * 8, 8)
        td = pl.multiple_of((tiles - 1 - i) * 8, 8)
        xu_re, xu_im = load_up(tu)
        xd_re, xd_im = load_down(td)
        bu_re, bu_im, ru = tile_scan(xu_re, xu_im, keeps(tu, False), up_powers, False)
        bd_re, bd_im, rd = tile_scan(xd_re, xd_im, keeps(td, True), up_powers, True)
        hu_re, hu_im = carry_in(bu_re, bu_im, ru, up_powers, u_re, u_im)
        hd_re, hd_im = carry_in(bd_re, bd_im, rd, down_powers, d_re, d_im)
        store_up(tu, hu_re, hu_im)
        store_down(td, hd_re, hd_im)
        return (hu_re[7:8], hu_im[7:8], hd_re[0:1], hd_im[0:1])

    zeros = jnp.zeros((1, width), jnp.float32)
    lax.fori_loop(0, tiles, step, (zeros, zeros, zeros, zeros), unroll=2)


def pole_powers(p_re, p_im):
    rows_re = [p_re]
    rows_im = [p_im]
    for _ in range(7):
        a, b = rows_re[-1], rows_im[-1]
        rows_re.append(a * p_re - b * p_im)
        rows_im.append(a * p_im + b * p_re)
    up_re = jnp.stack(rows_re)
    up_im = jnp.stack(rows_im)
    return jnp.stack([up_re, up_im, up_re[::-1], up_im[::-1]])


def recurrence_kernel(starts_ref, lengths_ref, pow_ref, x_ref, out_ref):
    count = x_ref.shape[0]
    width = pow_ref.shape[2]

    def load(t):
        return x_ref[pl.ds(t, 8), pl.ds(0, width)], x_ref[pl.ds(t, 8), pl.ds(width, width)]

    def store(column):
        def put(t, h_re, h_im):
            out_ref[pl.ds(t, 8), pl.ds(column, width)] = h_re
            out_ref[pl.ds(t, 8), pl.ds(column + width, width)] = h_im

        return put

    blocked_scan(count, width, pow_ref, starts_ref, lengths_ref, load, load, store(0), store(2 * width))


def recurrence(starts, lengths, powers, x):
    count, double = x.shape
    vmem = pl.BlockSpec(memory_space=pltpu.VMEM)
    smem = pl.BlockSpec(memory_space=pltpu.SMEM)
    return pl.pallas_call(
        recurrence_kernel,
        out_shape=jax.ShapeDtypeStruct((count, 2 * double), jnp.float32),
        in_specs=[smem, smem, vmem, vmem],
        out_specs=vmem,
        cost_estimate=pl.CostEstimate(
            flops=20 * count * double, transcendentals=0, bytes_accessed=16 * count * double
        ),
    )(starts, lengths, powers, x)


MESH = pl.DeviceIdType.MESH


def ring_place(position, n):
    upper = position // (n // 2)
    return (1 - upper) * (2 * position) + upper * (2 * (n - 1 - position) + 1)


def ring_position(index, n):
    odd = index % 2
    return (1 - odd) * (index // 2) + odd * (n - 1 - index // 2)


def ring_sum_kernel(n, x_ref, r_ref, o_ref, low, slots, rs_send, rs_recv, credit, done, ag_send, ag_recv):
    rows = x_ref.shape[0]
    half = rows // 2
    size = half // n
    me = ring_position(lax.axis_index("seq"), n)
    right = ring_place((me + 1) % n, n)
    left = ring_place((me + n - 1) % n, n)
    rings = ((0, me, right, left), (1, (n - me) % n, left, right))

    barrier = pltpu.get_barrier_semaphore()
    for neighbour in (left, right):
        pl.semaphore_signal(barrier, 1, device_id={"seq": neighbour}, device_id_type=MESH)
    pl.semaphore_wait(barrier, 2)
    o_ref[...] = x_ref[...]
    low[...] = x_ref[...].astype(low.dtype)

    def block(ring, k):
        return pl.ds(pl.multiple_of(ring * half + k * size, 8), size)

    def scatter_copy(ring, place, target, s):
        return pltpu.make_async_remote_copy(
            src_ref=low.at[block(ring, (place - s + n) % n)],
            dst_ref=slots.at[ring, s % 2],
            send_sem=rs_send.at[ring, s % 2],
            recv_sem=rs_recv.at[ring, s % 2],
            device_id={"seq": target},
            device_id_type=MESH,
        )

    def scatter_step(s, carry):
        copies = []
        for ring, place, target, source in rings:

            @pl.when(s >= 2)
            def _():
                pl.semaphore_wait(credit.at[ring], 1)

            copy = scatter_copy(ring, place, target, s)
            copy.start()
            copies.append(copy)
        for (ring, place, target, source), copy in zip(rings, copies):
            copy.wait_recv()
            into = block(ring, (place - s - 1 + 2 * n) % n)
            total = o_ref[into] + slots[ring, s % 2].astype(jnp.float32)
            o_ref[into] = total
            low[into] = total.astype(low.dtype)
            copy.wait_send()

            @pl.when(s <= n - 4)
            def _():
                pl.semaphore_signal(credit.at[ring], 1, device_id={"seq": source}, device_id_type=MESH)

        return carry

    lax.fori_loop(0, n - 1, scatter_step, 0)
    for ring, place, target, source in rings:
        pl.semaphore_signal(done.at[ring], 1, device_id={"seq": source}, device_id_type=MESH)
    for ring, place, target, source in rings:
        final = block(ring, (place + 1) % n)
        r_ref[final] = o_ref[final].astype(r_ref.dtype)
    for ring, place, target, source in rings:
        pl.semaphore_wait(done.at[ring], 1)

    def gather_copy(ring, place, target, s):
        where = block(ring, (place + 1 - s + n) % n)
        return pltpu.make_async_remote_copy(
            src_ref=r_ref.at[where],
            dst_ref=r_ref.at[where],
            send_sem=ag_send.at[ring, s],
            recv_sem=ag_recv.at[ring, s],
            device_id={"seq": target},
            device_id_type=MESH,
        )

    def gather_step(s, carry):
        for ring, place, target, source in rings:

            @pl.when(s >= 1)
            def _():
                gather_copy(ring, place, target, s - 1).wait_recv()

            gather_copy(ring, place, target, s).start()

            @pl.when(s >= 1)
            def _():
                gather_copy(ring, place, target, s - 1).wait_send()

        return carry

    lax.fori_loop(0, n - 1, gather_step, 0)
    for ring, place, target, source in rings:
        last = gather_copy(ring, place, target, n - 2)
        last.wait_recv()
        last.wait_send()


def ring_sum(x, n):
    rows, lanes = x.shape
    size = rows // (2 * n)
    return pl.pallas_call(
        lambda *refs: ring_sum_kernel(n, *refs),
        out_shape=jax.ShapeDtypeStruct((rows, lanes), jnp.bfloat16),
        in_specs=[pl.BlockSpec(memory_space=pltpu.VMEM)],
        out_specs=pl.BlockSpec(memory_space=pltpu.VMEM),
        scratch_shapes=[
            pltpu.VMEM((rows, lanes), jnp.float32),
            pltpu.VMEM((rows, lanes), jnp.bfloat16),
            pltpu.VMEM((2, 2, size, lanes), jnp.bfloat16),
            pltpu.SemaphoreType.DMA((2, 2)),
            pltpu.SemaphoreType.DMA((2, 2)),
            pltpu.SemaphoreType.REGULAR((2,)),
            pltpu.SemaphoreType.REGULAR((2,)),
            pltpu.SemaphoreType.DMA((2, n - 1)),
            pltpu.SemaphoreType.DMA((2, n - 1)),
        ],
        compiler_params=pltpu.CompilerParams(collective_id=0, has_side_effects=True),
    )(x)


def sum_over_seq(parts):
    n = lax.axis_size("seq")
    flat = jnp.concatenate([part.reshape(-1) for part in parts])
    grain = 2 * n * 16 * 128
    padded = -(-flat.size // grain) * grain
    flat = jnp.pad(flat, (0, padded - flat.size)).reshape(padded // 128, 128)
    total = ring_sum(flat, n).astype(jnp.float32).reshape(-1)
    pieces = []
    start = 0
    for part in parts:
        pieces.append(total[start : start + part.size].reshape(part.shape))
        start += part.size
    return pieces


def adjoint_kernel(starts_ref, lengths_ref, pow_ref, coef_ref, masks_ref, g_ref, states_ref, drive_ref, dg_ref, sums_ref, lam):
    count = g_ref.shape[0]
    width = coef_ref.shape[1]
    pad = 8
    f_re = coef_ref[2:3, :]
    f_im = coef_ref[3:4, :]
    zero_rows = jnp.zeros((pad, 4 * width), jnp.float32)
    lam[0:pad, :] = zero_rows
    lam[pad + count : 2 * pad + count, :] = zero_rows

    def load(column):
        def get(t):
            return g_ref[pl.ds(t, 8), pl.ds(column, width)], g_ref[pl.ds(t, 8), pl.ds(column + width, width)]

        return get

    def store(column):
        def put(t, h_re, h_im):
            lam[pl.ds(pad + t, 8), pl.ds(column, width)] = h_re
            lam[pl.ds(pad + t, 8), pl.ds(column + width, width)] = h_im

        return put

    blocked_scan(count, width, pow_ref, starts_ref, lengths_ref, load(2 * width), load(0), store(0), store(2 * width))

    rows = 16

    def part(ref, start, column):
        return ref[pl.ds(start, rows), pl.ds(column, width)]

    def epilogue(k, sums):
        gp_re, gp_im, gf_re, gf_im = sums
        r0 = pl.multiple_of(k * rows, rows)
        live = masks_ref[pl.ds(r0, rows), 0:1]
        keep_prev = masks_ref[pl.ds(r0, rows), 1:2]
        keep_next = masks_ref[pl.ds(r0, rows), 2:3]
        lb_re = part(lam, pad + r0, 0)
        lb_im = part(lam, pad + r0, width)
        la_re = part(lam, pad + r0, 2 * width)
        la_im = part(lam, pad + r0, 3 * width)
        gu_re = la_re + lb_re
        gu_im = la_im + lb_im
        dg_ref[pl.ds(r0, rows), pl.ds(0, width)] = ((f_re * gu_re + f_im * gu_im) * live).astype(dg_ref.dtype)
        dg_ref[pl.ds(r0, rows), pl.ds(width, width)] = ((f_re * gu_im - f_im * gu_re) * live).astype(dg_ref.dtype)
        d_re = part(drive_ref, r0, 0) * live
        d_im = part(drive_ref, r0, width) * live
        gf_re = gf_re + d_re * gu_re + d_im * gu_im
        gf_im = gf_im + d_re * gu_im - d_im * gu_re
        a_re = part(states_ref, r0, 0) * keep_next
        a_im = part(states_ref, r0, width) * keep_next
        b_re = part(states_ref, r0, 2 * width) * keep_prev
        b_im = part(states_ref, r0, 3 * width) * keep_prev
        ahead_rows = lam[pl.ds(pad + r0, rows + 8), pl.ds(2 * width, 2 * width)][1 : rows + 1]
        behind_rows = lam[pl.ds(r0, rows + 8), pl.ds(0, 2 * width)][pad - 1 : pad - 1 + rows]
        na_re = ahead_rows[:, :width]
        na_im = ahead_rows[:, width:]
        pb_re = behind_rows[:, :width]
        pb_im = behind_rows[:, width:]
        gp_re = gp_re + a_re * na_re + a_im * na_im + b_re * pb_re + b_im * pb_im
        gp_im = gp_im + a_re * na_im - a_im * na_re + b_re * pb_im - b_im * pb_re
        return (gp_re, gp_im, gf_re, gf_im)

    block = jnp.zeros((rows, width), jnp.float32)
    sums = lax.fori_loop(0, count // rows, epilogue, (block, block, block, block))
    for k, value in enumerate(sums):
        sums_ref[k : k + 1, :] = jnp.sum(value, 0, keepdims=True)


def adjoint(starts, lengths, powers, coef, masks, states_grad, states, drive):
    count, quad = states_grad.shape
    width = quad // 4
    vmem = pl.BlockSpec(memory_space=pltpu.VMEM)
    smem = pl.BlockSpec(memory_space=pltpu.SMEM)
    return pl.pallas_call(
        adjoint_kernel,
        out_shape=(
            jax.ShapeDtypeStruct((count, 2 * width), jnp.bfloat16),
            jax.ShapeDtypeStruct((4, width), jnp.float32),
        ),
        in_specs=[smem, smem] + [vmem] * 6,
        out_specs=(vmem, vmem),
        scratch_shapes=[pltpu.VMEM((count + 16, 4 * width), jnp.float32)],
        cost_estimate=pl.CostEstimate(
            flops=60 * count * width, transcendentals=0, bytes_accessed=48 * count * width
        ),
    )(starts, lengths, powers, coef, masks, states_grad, states, drive)


def update(weight, gradient, velocity, average, rate, decay):
    adjusted = gradient + decay * weight
    velocity_new = momentum * velocity + adjusted
    change = -rate * (adjusted + momentum * velocity_new)
    weight_new = weight + change
    average_new = smoothing * average + (1.0 - smoothing) * weight_new
    return (weight_new, velocity_new, average_new, change)


def contract_rows(left, right):
    return lax.dot_general(
        left, right, (((0,), (0,)), ((), ())), preferred_element_type=jnp.float32
    )


def contract_cols(left, right):
    return lax.dot_general(
        left, right, (((1,), (1,)), ((), ())), preferred_element_type=jnp.float32
    )


def gather_feat(value, axis):
    return lax.all_gather(value, "feat", axis=axis, tiled=True)


def split_exact(value):
    high = lax.reduce_precision(value, exponent_bits=8, mantissa_bits=7)
    rest = value - high
    middle = lax.reduce_precision(rest, exponent_bits=8, mantissa_bits=7)
    little = rest - middle
    return jnp.concatenate([high, middle, little], 0).astype(jnp.bfloat16)


def join_exact(pieces):
    third = pieces.shape[0] // 3
    pieces = pieces.astype(jnp.float32)
    return pieces[:third] + (pieces[third : 2 * third] + pieces[2 * third :])


def body(
    activations_in,
    cotangent,
    seq_start,
    seq_length,
    input_matrix,
    output_matrix,
    gate_matrix,
    feature_vectors,
    state_vectors,
    velocity_input,
    velocity_output,
    velocity_gate,
    velocity_feature,
    velocity_state,
    average_input,
    average_output,
    average_gate,
    average_feature,
    average_state,
):
    count = activations_in.shape[0]
    shard = activations_in.shape[1]
    layers = input_matrix.shape[0]
    width = state_vectors.shape[2]
    me = lax.axis_index("feat")
    offset = me * shard

    def mine(value):
        return lax.dynamic_slice_in_dim(value, offset, shard, axis=value.ndim - 1)

    alive, carry_prev, carry_next = masks_of(seq_start, seq_length, count)
    zero = jnp.zeros((1,), jnp.float32)
    after_next = jnp.concatenate([zero, carry_next[:-1]])
    before_prev = jnp.concatenate([carry_prev[1:], zero])
    mask_columns = jnp.stack([alive, carry_prev, carry_next, jnp.zeros_like(alive)], 1)


    in_all = gather_feat(input_matrix.astype(jnp.bfloat16), 1)
    rows_out = output_matrix.shape[1]
    paired = [
        gather_feat(jnp.concatenate([output_matrix[k], gate_matrix[k]], 0).astype(jnp.bfloat16), 1)
        for k in range(layers)
    ]
    out_all = [pair[:rows_out] for pair in paired]
    gate_all = [pair[rows_out:] for pair in paired]
    feature_pieces = split_exact(feature_vectors.reshape(-1, activations_in.shape[1]))
    feature_rows = feature_pieces.shape[0]
    feature_pad = -(-feature_rows // 16) * 16
    feature_pieces = jnp.pad(feature_pieces, ((0, feature_pad - feature_rows), (0, 0)))
    first = gather_feat(jnp.concatenate([activations_in, feature_pieces, cotangent], 0), 1)
    cotangent_all = first[count + feature_pad :]
    stream = first[:count].astype(jnp.float32)
    feature_all = join_exact(first[count : count + feature_rows]).reshape(feature_vectors.shape[:-1] + (-1,))

    saved = []
    for layer in range(layers):
        in_low = in_all[layer]
        out_low = out_all[layer]
        gate_low = gate_all[layer]
        feature_row = feature_all[layer]
        pole_re, pole_im, factor_re, factor_im = coefficients(state_vectors[layer])
        center = jnp.mean(stream, 1, keepdims=True)
        spread = stream - center
        scale = lax.rsqrt(jnp.mean(spread * spread, 1, keepdims=True) + epsilon)
        unit = spread * scale
        normed = unit * feature_row[0] + feature_row[1]
        normed_low = normed.astype(jnp.bfloat16)
        drive = jnp.dot(normed_low, in_low, preferred_element_type=jnp.float32)
        drive_re = drive[:, :width]
        drive_im = drive[:, width:]
        source = jnp.concatenate(
            [
                (drive_re * factor_re - drive_im * factor_im) * alive[:, None],
                (drive_re * factor_im + drive_im * factor_re) * alive[:, None],
            ],
            1,
        )
        states = recurrence(seq_start, seq_length, pole_powers(pole_re, pole_im), source)
        states_low = states.astype(jnp.bfloat16)
        mixed = (
            jnp.dot(states_low, out_low, preferred_element_type=jnp.float32)
            + feature_row[2] * normed
        )
        cdf = (lax.erf(mixed * (1.0 / math.sqrt(2.0))) + 1.0) / 2.0
        act = mixed * cdf
        act_low = act.astype(jnp.bfloat16)
        pre = jnp.dot(act_low, gate_low, preferred_element_type=jnp.float32) + feature_row[3]
        saved.append((scale, unit, normed_low, drive, states, states_low, mixed, act, act_low, pre, cdf))
        stream = stream + act * jax.nn.sigmoid(pre)

    grad = cotangent_all.astype(jnp.float32) * alive[:, None]
    layer_grads = [None] * layers
    for layer in reversed(range(layers)):
        scale, unit, normed_low, drive, states, states_low, mixed, act, act_low, pre, cdf = saved[layer]
        in_low = in_all[layer]
        out_low = out_all[layer]
        gate_low = gate_all[layer]
        feature_row = feature_all[layer]
        state_row = state_vectors[layer]
        pole_re, pole_im, factor_re, factor_im = coefficients(state_row)
        gate = jax.nn.sigmoid(pre)
        pre_grad = (grad * act * gate * (1.0 - gate)).astype(jnp.bfloat16)
        gate_grad = contract_rows(act_low, mine(pre_grad))
        gate_bias_grad = jnp.sum(pre_grad.astype(jnp.float32), 0)
        act_grad = grad * gate + contract_cols(pre_grad, gate_low)
        density = jnp.exp(mixed * mixed * -0.5) * (1.0 / math.sqrt(2.0 * math.pi))
        mixed_grad = act_grad * (cdf + mixed * density)
        normed = unit * feature_row[0] + feature_row[1]
        skip_grad = jnp.sum(mixed_grad * normed, 0)
        mixed_low = mixed_grad.astype(jnp.bfloat16)
        out_grad = contract_rows(states_low, mine(mixed_low))
        states_grad = contract_cols(mixed_low, out_low)
        coef = jnp.stack([pole_re, pole_im, factor_re, factor_im])
        drive_low, sums = adjoint(
            seq_start,
            seq_length,
            pole_powers(pole_re, -pole_im),
            coef,
            mask_columns,
            states_grad,
            states,
            drive,
        )
        gp_re, gp_im, gf_re, gf_im = sums[0], sums[1], sums[2], sums[3]
        row_grad = jax.vjp(coefficients, state_row)[1]((gp_re, gp_im, gf_re, gf_im))[0]
        in_grad = contract_rows(mine(normed_low), drive_low)
        normed_grad = mixed_grad * feature_row[2] + jnp.dot(
            drive_low, in_low.T, preferred_element_type=jnp.float32
        )
        gain_grad = jnp.sum(normed_grad * unit, 0)
        bias_grad = jnp.sum(normed_grad, 0)
        unit_grad = normed_grad * feature_row[0]
        first_mean = jnp.mean(unit_grad, 1, keepdims=True)
        second_mean = jnp.mean(unit_grad * unit, 1, keepdims=True)
        grad = grad + scale * (unit_grad - first_mean - unit * second_mean)
        feature_grad = mine(jnp.stack([gain_grad, bias_grad, skip_grad, gate_bias_grad]))
        layer_grads[layer] = (in_grad, out_grad, gate_grad, feature_grad, row_grad)
    stacked_in = jnp.stack([entry[0] for entry in layer_grads])
    stacked_out = jnp.stack([entry[1] for entry in layer_grads])
    stacked_gate = jnp.stack([entry[2] for entry in layer_grads])
    stacked_feature = jnp.stack([entry[3] for entry in layer_grads])
    stacked_state = jnp.stack([entry[4] for entry in layer_grads])
    summed = sum_over_seq((stacked_in, stacked_out, stacked_gate, stacked_feature, stacked_state))
    factor = 1.0 / math.sqrt(count * lax.axis_size("seq"))
    grad_in = summed[0] * factor
    grad_out = summed[1] * factor
    grad_gate = summed[2] * factor
    grad_feature = summed[3] * factor
    grad_state = summed[4] * factor
    new_in = update(input_matrix, grad_in, velocity_input, average_input, slow_rate, 0.0)
    new_out = update(output_matrix, grad_out, velocity_output, average_output, slow_rate, 0.0)
    new_gate = update(gate_matrix, grad_gate, velocity_gate, average_gate, main_rate, weight_decay)
    new_feature = update(
        feature_vectors, grad_feature, velocity_feature, average_feature, main_rate, weight_decay
    )
    new_state = update(state_vectors, grad_state, velocity_state, average_state, slow_rate, 0.0)
    return (
        mine(stream),
        mine(grad),
        grad_in,
        grad_out,
        grad_gate,
        grad_feature,
        grad_state,
        new_in[0],
        new_out[0],
        new_gate[0],
        new_feature[0],
        new_state[3],
        new_in[1],
        new_out[1],
        new_gate[1],
        new_feature[1],
        new_state[1],
        new_in[2],
        new_out[2],
        new_gate[2],
        new_feature[2],
        new_state[2],
    )


def solution(mesh):
    feat = P(None, None, "feat")
    rows = P(None, "feat", None)
    tokens = P("seq", "feat")
    return jax.shard_map(
        body,
        mesh=mesh,
        in_specs=(
            tokens,
            tokens,
            P("seq"),
            P("seq"),
            rows,
            feat,
            feat,
            feat,
            P(),
            rows,
            feat,
            feat,
            feat,
            P(),
            rows,
            feat,
            feat,
            feat,
            P(),
        ),
        out_specs=(
            tokens,
            tokens,
            rows,
            feat,
            feat,
            feat,
            P(),
            rows,
            feat,
            feat,
            feat,
            P(),
            rows,
            feat,
            feat,
            feat,
            P(),
            rows,
            feat,
            feat,
            feat,
            P(),
        ),
        check_vma=False,
    )
```

```python
import math

import jax
import jax.numpy as jnp
from jax import lax
from jax.experimental import pallas as pl
from jax.experimental.pallas import tpu as pltpu
from jax.sharding import PartitionSpec as P

epsilon = 1e-05
momentum = 0.9
smoothing = 0.5
slow_rate = 0.02
main_rate = 0.05
weight_decay = 0.1


def smooth(value):
    return jax.nn.gelu(value, approximate=False)


def masks_of(starts, lengths, count):
    position = jnp.arange(count, dtype=jnp.int32)[:, None]
    begin = starts[None, :]
    finish = begin + lengths[None, :]
    inside = (position >= begin) & (position < finish)
    alive = jnp.any(inside, 1)
    opening = jnp.any(inside & (position == begin), 1)
    closing = jnp.any(inside & (position == finish - 1), 1)
    return (
        alive.astype(jnp.float32),
        (alive & ~opening).astype(jnp.float32),
        (alive & ~closing).astype(jnp.float32),
    )


def coefficients(state_row):
    rate = -jnp.exp(state_row[0])
    frequency = state_row[1]
    timestep = jnp.exp(state_row[2])
    decay = jnp.exp(rate * timestep)
    angle = frequency * timestep
    pole_real = decay * jnp.cos(angle)
    pole_imag = decay * jnp.sin(angle)
    denom = rate * rate + frequency * frequency
    factor_real = ((pole_real - 1.0) * rate + pole_imag * frequency) / denom
    factor_imag = (pole_imag * rate - (pole_real - 1.0) * frequency) / denom
    return (pole_real, pole_imag, factor_real, factor_imag)


def tile_scan(x_re, x_im, keep, powers, down):
    reps = x_re.shape[1] // keep.shape[1]
    rows = lax.broadcasted_iota(jnp.int32, keep.shape, 0)
    b_re, b_im = x_re, x_im
    for level, k in enumerate((1, 2, 4)):
        shift = 8 - k if down else k
        valid = rows <= 7 - k if down else rows >= k
        gate = jnp.tile(jnp.where(valid, keep, 0.0), (1, reps))
        p_re = pltpu.roll(b_re, shift, 0)
        p_im = pltpu.roll(b_im, shift, 0)
        w_re = powers[0][(0, 1, 3)[level] : (0, 1, 3)[level] + 1]
        w_im = powers[1][(0, 1, 3)[level] : (0, 1, 3)[level] + 1]
        b_re = b_re + gate * (w_re * p_re - w_im * p_im)
        b_im = b_im + gate * (w_re * p_im + w_im * p_re)
        keep = keep * jnp.where(valid, pltpu.roll(keep, shift, 0), 1.0)
    return b_re, b_im, jnp.tile(keep, (1, reps))


def blocked_scan(count, width, pow_ref, starts_ref, lengths_ref, load_up, load_down, store_up, store_down):
    tiles = count // 8
    slots = starts_ref.shape[0]

    def keeps(t0, downward):
        rows = lax.broadcasted_iota(jnp.int32, (8, 128), 0) + t0
        inside = jnp.zeros((8, 128), jnp.bool_)
        for slot in range(slots):
            begin = starts_ref[slot]
            finish = begin + lengths_ref[slot]
            if downward:
                inside = inside | ((rows >= begin) & (rows < finish - 1))
            else:
                inside = inside | ((rows > begin) & (rows < finish))
        return inside.astype(jnp.float32)

    up_powers = (pow_ref[0], pow_ref[1])
    down_powers = (pow_ref[2], pow_ref[3])

    def carry_in(b_re, b_im, reach, powers, h_re, h_im):
        q_re = powers[0] * h_re - powers[1] * h_im
        q_im = powers[0] * h_im + powers[1] * h_re
        return b_re + reach * q_re, b_im + reach * q_im

    def step(i, carry):
        u_re, u_im, d_re, d_im = carry
        tu = pl.multiple_of(i * 8, 8)
        td = pl.multiple_of((tiles - 1 - i) * 8, 8)
        xu_re, xu_im = load_up(tu)
        xd_re, xd_im = load_down(td)
        bu_re, bu_im, ru = tile_scan(xu_re, xu_im, keeps(tu, False), up_powers, False)
        bd_re, bd_im, rd = tile_scan(xd_re, xd_im, keeps(td, True), up_powers, True)
        hu_re, hu_im = carry_in(bu_re, bu_im, ru, up_powers, u_re, u_im)
        hd_re, hd_im = carry_in(bd_re, bd_im, rd, down_powers, d_re, d_im)
        store_up(tu, hu_re, hu_im)
        store_down(td, hd_re, hd_im)
        return (hu_re[7:8], hu_im[7:8], hd_re[0:1], hd_im[0:1])

    zeros = jnp.zeros((1, width), jnp.float32)
    lax.fori_loop(0, tiles, step, (zeros, zeros, zeros, zeros), unroll=2)


def pole_powers(p_re, p_im):
    rows_re = [p_re]
    rows_im = [p_im]
    for _ in range(7):
        a, b = rows_re[-1], rows_im[-1]
        rows_re.append(a * p_re - b * p_im)
        rows_im.append(a * p_im + b * p_re)
    up_re = jnp.stack(rows_re)
    up_im = jnp.stack(rows_im)
    return jnp.stack([up_re, up_im, up_re[::-1], up_im[::-1]])


def recurrence_kernel(starts_ref, lengths_ref, pow_ref, x_ref, out_ref):
    count = x_ref.shape[0]
    width = pow_ref.shape[2]

    def load(t):
        return x_ref[pl.ds(t, 8), pl.ds(0, width)], x_ref[pl.ds(t, 8), pl.ds(width, width)]

    def store(column):
        def put(t, h_re, h_im):
            out_ref[pl.ds(t, 8), pl.ds(column, width)] = h_re
            out_ref[pl.ds(t, 8), pl.ds(column + width, width)] = h_im

        return put

    blocked_scan(count, width, pow_ref, starts_ref, lengths_ref, load, load, store(0), store(2 * width))


def recurrence(starts, lengths, powers, x):
    count, double = x.shape
    vmem = pl.BlockSpec(memory_space=pltpu.VMEM)
    smem = pl.BlockSpec(memory_space=pltpu.SMEM)
    return pl.pallas_call(
        recurrence_kernel,
        out_shape=jax.ShapeDtypeStruct((count, 2 * double), jnp.float32),
        in_specs=[smem, smem, vmem, vmem],
        out_specs=vmem,
        cost_estimate=pl.CostEstimate(
            flops=20 * count * double, transcendentals=0, bytes_accessed=16 * count * double
        ),
    )(starts, lengths, powers, x)


MESH = pl.DeviceIdType.MESH


def ring_place(position, n):
    upper = position // (n // 2)
    return (1 - upper) * (2 * position) + upper * (2 * (n - 1 - position) + 1)


def ring_position(index, n):
    odd = index % 2
    return (1 - odd) * (index // 2) + odd * (n - 1 - index // 2)


def ring_sum_kernel(n, x_ref, r_ref, o_ref, low, slots, rs_send, rs_recv, credit, done, ag_send, ag_recv):
    rows = x_ref.shape[0]
    half = rows // 2
    size = half // n
    me = ring_position(lax.axis_index("seq"), n)
    right = ring_place((me + 1) % n, n)
    left = ring_place((me + n - 1) % n, n)
    rings = ((0, me, right, left), (1, (n - me) % n, left, right))

    barrier = pltpu.get_barrier_semaphore()
    for neighbour in (left, right):
        pl.semaphore_signal(barrier, 1, device_id={"seq": neighbour}, device_id_type=MESH)
    pl.semaphore_wait(barrier, 2)
    o_ref[...] = x_ref[...]
    low[...] = x_ref[...].astype(low.dtype)

    def block(ring, k):
        return pl.ds(pl.multiple_of(ring * half + k * size, 8), size)

    def scatter_copy(ring, place, target, s):
        return pltpu.make_async_remote_copy(
            src_ref=low.at[block(ring, (place - s + n) % n)],
            dst_ref=slots.at[ring, s % 2],
            send_sem=rs_send.at[ring, s % 2],
            recv_sem=rs_recv.at[ring, s % 2],
            device_id={"seq": target},
            device_id_type=MESH,
        )

    def scatter_step(s, carry):
        copies = []
        for ring, place, target, source in rings:

            @pl.when(s >= 2)
            def _():
                pl.semaphore_wait(credit.at[ring], 1)

            copy = scatter_copy(ring, place, target, s)
            copy.start()
            copies.append(copy)
        for (ring, place, target, source), copy in zip(rings, copies):
            copy.wait_recv()
            into = block(ring, (place - s - 1 + 2 * n) % n)
            total = o_ref[into] + slots[ring, s % 2].astype(jnp.float32)
            o_ref[into] = total
            low[into] = total.astype(low.dtype)
            copy.wait_send()

            @pl.when(s <= n - 4)
            def _():
                pl.semaphore_signal(credit.at[ring], 1, device_id={"seq": source}, device_id_type=MESH)

        return carry

    lax.fori_loop(0, n - 1, scatter_step, 0)
    for ring, place, target, source in rings:
        pl.semaphore_signal(done.at[ring], 1, device_id={"seq": source}, device_id_type=MESH)
    for ring, place, target, source in rings:
        final = block(ring, (place + 1) % n)
        r_ref[final] = o_ref[final].astype(r_ref.dtype)
    for ring, place, target, source in rings:
        pl.semaphore_wait(done.at[ring], 1)

    def gather_copy(ring, place, target, s):
        where = block(ring, (place + 1 - s + n) % n)
        return pltpu.make_async_remote_copy(
            src_ref=r_ref.at[where],
            dst_ref=r_ref.at[where],
            send_sem=ag_send.at[ring, s],
            recv_sem=ag_recv.at[ring, s],
            device_id={"seq": target},
            device_id_type=MESH,
        )

    def gather_step(s, carry):
        for ring, place, target, source in rings:

            @pl.when(s >= 1)
            def _():
                gather_copy(ring, place, target, s - 1).wait_recv()

            gather_copy(ring, place, target, s).start()

            @pl.when(s >= 1)
            def _():
                gather_copy(ring, place, target, s - 1).wait_send()

        return carry

    lax.fori_loop(0, n - 1, gather_step, 0)
    for ring, place, target, source in rings:
        last = gather_copy(ring, place, target, n - 2)
        last.wait_recv()
        last.wait_send()


def ring_sum(x, n):
    rows, lanes = x.shape
    size = rows // (2 * n)
    return pl.pallas_call(
        lambda *refs: ring_sum_kernel(n, *refs),
        out_shape=jax.ShapeDtypeStruct((rows, lanes), jnp.bfloat16),
        in_specs=[pl.BlockSpec(memory_space=pltpu.VMEM)],
        out_specs=pl.BlockSpec(memory_space=pltpu.VMEM),
        scratch_shapes=[
            pltpu.VMEM((rows, lanes), jnp.float32),
            pltpu.VMEM((rows, lanes), jnp.bfloat16),
            pltpu.VMEM((2, 2, size, lanes), jnp.bfloat16),
            pltpu.SemaphoreType.DMA((2, 2)),
            pltpu.SemaphoreType.DMA((2, 2)),
            pltpu.SemaphoreType.REGULAR((2,)),
            pltpu.SemaphoreType.REGULAR((2,)),
            pltpu.SemaphoreType.DMA((2, n - 1)),
            pltpu.SemaphoreType.DMA((2, n - 1)),
        ],
        compiler_params=pltpu.CompilerParams(collective_id=0, has_side_effects=True),
    )(x)


def sum_over_seq(parts):
    n = lax.axis_size("seq")
    flat = jnp.concatenate([part.reshape(-1) for part in parts])
    grain = 2 * n * 16 * 128
    padded = -(-flat.size // grain) * grain
    flat = jnp.pad(flat, (0, padded - flat.size)).reshape(padded // 128, 128)
    total = ring_sum(flat, n).astype(jnp.float32).reshape(-1)
    pieces = []
    start = 0
    for part in parts:
        pieces.append(total[start : start + part.size].reshape(part.shape))
        start += part.size
    return pieces


def adjoint_kernel(starts_ref, lengths_ref, pow_ref, coef_ref, masks_ref, g_ref, states_ref, drive_ref, dg_ref, sums_ref, lam):
    count = g_ref.shape[0]
    width = coef_ref.shape[1]
    pad = 8
    f_re = coef_ref[2:3, :]
    f_im = coef_ref[3:4, :]
    zero_rows = jnp.zeros((pad, 4 * width), jnp.float32)
    lam[0:pad, :] = zero_rows
    lam[pad + count : 2 * pad + count, :] = zero_rows

    def load(column):
        def get(t):
            return g_ref[pl.ds(t, 8), pl.ds(column, width)], g_ref[pl.ds(t, 8), pl.ds(column + width, width)]

        return get

    def store(column):
        def put(t, h_re, h_im):
            lam[pl.ds(pad + t, 8), pl.ds(column, width)] = h_re
            lam[pl.ds(pad + t, 8), pl.ds(column + width, width)] = h_im

        return put

    blocked_scan(count, width, pow_ref, starts_ref, lengths_ref, load(2 * width), load(0), store(0), store(2 * width))

    rows = 16

    def part(ref, start, column):
        return ref[pl.ds(start, rows), pl.ds(column, width)]

    def epilogue(k, sums):
        gp_re, gp_im, gf_re, gf_im = sums
        r0 = pl.multiple_of(k * rows, rows)
        live = masks_ref[pl.ds(r0, rows), 0:1]
        keep_prev = masks_ref[pl.ds(r0, rows), 1:2]
        keep_next = masks_ref[pl.ds(r0, rows), 2:3]
        lb_re = part(lam, pad + r0, 0)
        lb_im = part(lam, pad + r0, width)
        la_re = part(lam, pad + r0, 2 * width)
        la_im = part(lam, pad + r0, 3 * width)
        gu_re = la_re + lb_re
        gu_im = la_im + lb_im
        dg_ref[pl.ds(r0, rows), pl.ds(0, width)] = ((f_re * gu_re + f_im * gu_im) * live).astype(dg_ref.dtype)
        dg_ref[pl.ds(r0, rows), pl.ds(width, width)] = ((f_re * gu_im - f_im * gu_re) * live).astype(dg_ref.dtype)
        d_re = part(drive_ref, r0, 0) * live
        d_im = part(drive_ref, r0, width) * live
        gf_re = gf_re + d_re * gu_re + d_im * gu_im
        gf_im = gf_im + d_re * gu_im - d_im * gu_re
        a_re = part(states_ref, r0, 0) * keep_next
        a_im = part(states_ref, r0, width) * keep_next
        b_re = part(states_ref, r0, 2 * width) * keep_prev
        b_im = part(states_ref, r0, 3 * width) * keep_prev
        ahead_rows = lam[pl.ds(pad + r0, rows + 8), pl.ds(2 * width, 2 * width)][1 : rows + 1]
        behind_rows = lam[pl.ds(r0, rows + 8), pl.ds(0, 2 * width)][pad - 1 : pad - 1 + rows]
        na_re = ahead_rows[:, :width]
        na_im = ahead_rows[:, width:]
        pb_re = behind_rows[:, :width]
        pb_im = behind_rows[:, width:]
        gp_re = gp_re + a_re * na_re + a_im * na_im + b_re * pb_re + b_im * pb_im
        gp_im = gp_im + a_re * na_im - a_im * na_re + b_re * pb_im - b_im * pb_re
        return (gp_re, gp_im, gf_re, gf_im)

    block = jnp.zeros((rows, width), jnp.float32)
    sums = lax.fori_loop(0, count // rows, epilogue, (block, block, block, block))
    for k, value in enumerate(sums):
        sums_ref[k : k + 1, :] = jnp.sum(value, 0, keepdims=True)


def adjoint(starts, lengths, powers, coef, masks, states_grad, states, drive):
    count, quad = states_grad.shape
    width = quad // 4
    vmem = pl.BlockSpec(memory_space=pltpu.VMEM)
    smem = pl.BlockSpec(memory_space=pltpu.SMEM)
    return pl.pallas_call(
        adjoint_kernel,
        out_shape=(
            jax.ShapeDtypeStruct((count, 2 * width), jnp.bfloat16),
            jax.ShapeDtypeStruct((4, width), jnp.float32),
        ),
        in_specs=[smem, smem] + [vmem] * 6,
        out_specs=(vmem, vmem),
        scratch_shapes=[pltpu.VMEM((count + 16, 4 * width), jnp.float32)],
        cost_estimate=pl.CostEstimate(
            flops=60 * count * width, transcendentals=0, bytes_accessed=48 * count * width
        ),
    )(starts, lengths, powers, coef, masks, states_grad, states, drive)


def update(weight, gradient, velocity, average, rate, decay):
    adjusted = gradient + decay * weight
    velocity_new = momentum * velocity + adjusted
    change = -rate * (adjusted + momentum * velocity_new)
    weight_new = weight + change
    average_new = smoothing * average + (1.0 - smoothing) * weight_new
    return (weight_new, velocity_new, average_new, change)


def contract_rows(left, right):
    return lax.dot_general(
        left, right, (((0,), (0,)), ((), ())), preferred_element_type=jnp.float32
    )


def contract_cols(left, right):
    return lax.dot_general(
        left, right, (((1,), (1,)), ((), ())), preferred_element_type=jnp.float32
    )


def gather_feat(value, axis):
    return lax.all_gather(value, "feat", axis=axis, tiled=True)


def split_exact(value):
    high = lax.reduce_precision(value, exponent_bits=8, mantissa_bits=7)
    rest = value - high
    middle = lax.reduce_precision(rest, exponent_bits=8, mantissa_bits=7)
    little = rest - middle
    return jnp.concatenate([high, middle, little], 0).astype(jnp.bfloat16)


def join_exact(pieces):
    third = pieces.shape[0] // 3
    pieces = pieces.astype(jnp.float32)
    return pieces[:third] + (pieces[third : 2 * third] + pieces[2 * third :])


def body(
    activations_in,
    cotangent,
    seq_start,
    seq_length,
    input_matrix,
    output_matrix,
    gate_matrix,
    feature_vectors,
    state_vectors,
    velocity_input,
    velocity_output,
    velocity_gate,
    velocity_feature,
    velocity_state,
    average_input,
    average_output,
    average_gate,
    average_feature,
    average_state,
):
    count = activations_in.shape[0]
    shard = activations_in.shape[1]
    layers = input_matrix.shape[0]
    width = state_vectors.shape[2]
    me = lax.axis_index("feat")
    offset = me * shard

    def mine(value):
        return lax.dynamic_slice_in_dim(value, offset, shard, axis=value.ndim - 1)

    alive, carry_prev, carry_next = masks_of(seq_start, seq_length, count)
    zero = jnp.zeros((1,), jnp.float32)
    after_next = jnp.concatenate([zero, carry_next[:-1]])
    before_prev = jnp.concatenate([carry_prev[1:], zero])
    mask_columns = jnp.stack([alive, carry_prev, carry_next, jnp.zeros_like(alive)], 1)


    in_all = gather_feat(input_matrix.astype(jnp.bfloat16), 1)
    rows_out = output_matrix.shape[1]
    rows_gate = gate_matrix.shape[1]
    paired = [
        gather_feat(
            jnp.concatenate(
                [output_matrix[k].astype(jnp.bfloat16), gate_matrix[k].astype(jnp.bfloat16)]
                + ([cotangent] if k == layers - 1 else []),
                0,
            ),
            1,
        )
        for k in range(layers)
    ]
    out_all = [pair[:rows_out] for pair in paired]
    gate_all = [pair[rows_out : rows_out + rows_gate] for pair in paired]
    cotangent_all = paired[-1][rows_out + rows_gate :]
    feature_pieces = split_exact(feature_vectors.reshape(-1, activations_in.shape[1]))
    feature_rows = feature_pieces.shape[0]
    feature_pad = -(-feature_rows // 16) * 16
    feature_pieces = jnp.pad(feature_pieces, ((0, feature_pad - feature_rows), (0, 0)))
    first = gather_feat(jnp.concatenate([activations_in, feature_pieces], 0), 1)
    stream = first[:count].astype(jnp.float32)
    feature_all = join_exact(first[count : count + feature_rows]).reshape(feature_vectors.shape[:-1] + (-1,))

    saved = []
    for layer in range(layers):
        in_low = in_all[layer]
        out_low = out_all[layer]
        gate_low = gate_all[layer]
        feature_row = feature_all[layer]
        pole_re, pole_im, factor_re, factor_im = coefficients(state_vectors[layer])
        center = jnp.mean(stream, 1, keepdims=True)
        spread = stream - center
        scale = lax.rsqrt(jnp.mean(spread * spread, 1, keepdims=True) + epsilon)
        unit = spread * scale
        normed = unit * feature_row[0] + feature_row[1]
        normed_low = normed.astype(jnp.bfloat16)
        drive = jnp.dot(normed_low, in_low, preferred_element_type=jnp.float32)
        drive_re = drive[:, :width]
        drive_im = drive[:, width:]
        source = jnp.concatenate(
            [
                (drive_re * factor_re - drive_im * factor_im) * alive[:, None],
                (drive_re * factor_im + drive_im * factor_re) * alive[:, None],
            ],
            1,
        )
        states = recurrence(seq_start, seq_length, pole_powers(pole_re, pole_im), source)
        states_low = states.astype(jnp.bfloat16)
        mixed = (
            jnp.dot(states_low, out_low, preferred_element_type=jnp.float32)
            + feature_row[2] * normed
        )
        cdf = (lax.erf(mixed * (1.0 / math.sqrt(2.0))) + 1.0) / 2.0
        act = mixed * cdf
        act_low = act.astype(jnp.bfloat16)
        pre = jnp.dot(act_low, gate_low, preferred_element_type=jnp.float32) + feature_row[3]
        saved.append((scale, unit, normed_low, drive, states, states_low, mixed, act, act_low, pre, cdf))
        stream = stream + act * jax.nn.sigmoid(pre)

    grad = cotangent_all.astype(jnp.float32) * alive[:, None]
    layer_grads = [None] * layers
    for layer in reversed(range(layers)):
        scale, unit, normed_low, drive, states, states_low, mixed, act, act_low, pre, cdf = saved[layer]
        in_low = in_all[layer]
        out_low = out_all[layer]
        gate_low = gate_all[layer]
        feature_row = feature_all[layer]
        state_row = state_vectors[layer]
        pole_re, pole_im, factor_re, factor_im = coefficients(state_row)
        gate = jax.nn.sigmoid(pre)
        pre_grad = (grad * act * gate * (1.0 - gate)).astype(jnp.bfloat16)
        gate_grad = contract_rows(act_low, mine(pre_grad))
        gate_bias_grad = jnp.sum(pre_grad.astype(jnp.float32), 0)
        act_grad = grad * gate + contract_cols(pre_grad, gate_low)
        density = jnp.exp(mixed * mixed * -0.5) * (1.0 / math.sqrt(2.0 * math.pi))
        mixed_grad = act_grad * (cdf + mixed * density)
        normed = unit * feature_row[0] + feature_row[1]
        skip_grad = jnp.sum(mixed_grad * normed, 0)
        mixed_low = mixed_grad.astype(jnp.bfloat16)
        out_grad = contract_rows(states_low, mine(mixed_low))
        states_grad = contract_cols(mixed_low, out_low)
        coef = jnp.stack([pole_re, pole_im, factor_re, factor_im])
        drive_low, sums = adjoint(
            seq_start,
            seq_length,
            pole_powers(pole_re, -pole_im),
            coef,
            mask_columns,
            states_grad,
            states,
            drive,
        )
        gp_re, gp_im, gf_re, gf_im = sums[0], sums[1], sums[2], sums[3]
        row_grad = jax.vjp(coefficients, state_row)[1]((gp_re, gp_im, gf_re, gf_im))[0]
        in_grad = contract_rows(mine(normed_low), drive_low)
        normed_grad = mixed_grad * feature_row[2] + jnp.dot(
            drive_low, in_low.T, preferred_element_type=jnp.float32
        )
        gain_grad = jnp.sum(normed_grad * unit, 0)
        bias_grad = jnp.sum(normed_grad, 0)
        unit_grad = normed_grad * feature_row[0]
        first_mean = jnp.mean(unit_grad, 1, keepdims=True)
        second_mean = jnp.mean(unit_grad * unit, 1, keepdims=True)
        grad = grad + scale * (unit_grad - first_mean - unit * second_mean)
        feature_grad = mine(jnp.stack([gain_grad, bias_grad, skip_grad, gate_bias_grad]))
        layer_grads[layer] = (in_grad, out_grad, gate_grad, feature_grad, row_grad)
    stacked_in = jnp.stack([entry[0] for entry in layer_grads])
    stacked_out = jnp.stack([entry[1] for entry in layer_grads])
    stacked_gate = jnp.stack([entry[2] for entry in layer_grads])
    stacked_feature = jnp.stack([entry[3] for entry in layer_grads])
    stacked_state = jnp.stack([entry[4] for entry in layer_grads])
    summed = sum_over_seq((stacked_in, stacked_out, stacked_gate, stacked_feature, stacked_state))
    factor = 1.0 / math.sqrt(count * lax.axis_size("seq"))
    grad_in = summed[0] * factor
    grad_out = summed[1] * factor
    grad_gate = summed[2] * factor
    grad_feature = summed[3] * factor
    grad_state = summed[4] * factor
    new_in = update(input_matrix, grad_in, velocity_input, average_input, slow_rate, 0.0)
    new_out = update(output_matrix, grad_out, velocity_output, average_output, slow_rate, 0.0)
    new_gate = update(gate_matrix, grad_gate, velocity_gate, average_gate, main_rate, weight_decay)
    new_feature = update(
        feature_vectors, grad_feature, velocity_feature, average_feature, main_rate, weight_decay
    )
    new_state = update(state_vectors, grad_state, velocity_state, average_state, slow_rate, 0.0)
    return (
        mine(stream),
        mine(grad),
        grad_in,
        grad_out,
        grad_gate,
        grad_feature,
        grad_state,
        new_in[0],
        new_out[0],
        new_gate[0],
        new_feature[0],
        new_state[3],
        new_in[1],
        new_out[1],
        new_gate[1],
        new_feature[1],
        new_state[1],
        new_in[2],
        new_out[2],
        new_gate[2],
        new_feature[2],
        new_state[2],
    )


def solution(mesh):
    feat = P(None, None, "feat")
    rows = P(None, "feat", None)
    tokens = P("seq", "feat")
    return jax.shard_map(
        body,
        mesh=mesh,
        in_specs=(
            tokens,
            tokens,
            P("seq"),
            P("seq"),
            rows,
            feat,
            feat,
            feat,
            P(),
            rows,
            feat,
            feat,
            feat,
            P(),
            rows,
            feat,
            feat,
            feat,
            P(),
        ),
        out_specs=(
            tokens,
            tokens,
            rows,
            feat,
            feat,
            feat,
            P(),
            rows,
            feat,
            feat,
            feat,
            P(),
            rows,
            feat,
            feat,
            feat,
            P(),
            rows,
            feat,
            feat,
            feat,
            P(),
        ),
        check_vma=False,
    )
```

```python
import math

import jax
import jax.numpy as jnp
from jax import lax
from jax.experimental import pallas as pl
from jax.experimental.pallas import tpu as pltpu
from jax.sharding import PartitionSpec as P

epsilon = 1e-05
momentum = 0.9
smoothing = 0.5
slow_rate = 0.02
main_rate = 0.05
weight_decay = 0.1


def smooth(value):
    return jax.nn.gelu(value, approximate=False)


def masks_of(starts, lengths, count):
    position = jnp.arange(count, dtype=jnp.int32)[:, None]
    begin = starts[None, :]
    finish = begin + lengths[None, :]
    inside = (position >= begin) & (position < finish)
    alive = jnp.any(inside, 1)
    opening = jnp.any(inside & (position == begin), 1)
    closing = jnp.any(inside & (position == finish - 1), 1)
    return (
        alive.astype(jnp.float32),
        (alive & ~opening).astype(jnp.float32),
        (alive & ~closing).astype(jnp.float32),
    )


def coefficients(state_row):
    rate = -jnp.exp(state_row[0])
    frequency = state_row[1]
    timestep = jnp.exp(state_row[2])
    decay = jnp.exp(rate * timestep)
    angle = frequency * timestep
    pole_real = decay * jnp.cos(angle)
    pole_imag = decay * jnp.sin(angle)
    denom = rate * rate + frequency * frequency
    factor_real = ((pole_real - 1.0) * rate + pole_imag * frequency) / denom
    factor_imag = (pole_imag * rate - (pole_real - 1.0) * frequency) / denom
    return (pole_real, pole_imag, factor_real, factor_imag)


def tile_scan(x_re, x_im, keep, powers, down):
    reps = x_re.shape[1] // keep.shape[1]
    rows = lax.broadcasted_iota(jnp.int32, keep.shape, 0)
    b_re, b_im = x_re, x_im
    for level, k in enumerate((1, 2, 4)):
        shift = 8 - k if down else k
        valid = rows <= 7 - k if down else rows >= k
        gate = jnp.tile(jnp.where(valid, keep, 0.0), (1, reps))
        p_re = pltpu.roll(b_re, shift, 0)
        p_im = pltpu.roll(b_im, shift, 0)
        w_re = powers[0][(0, 1, 3)[level] : (0, 1, 3)[level] + 1]
        w_im = powers[1][(0, 1, 3)[level] : (0, 1, 3)[level] + 1]
        b_re = b_re + gate * (w_re * p_re - w_im * p_im)
        b_im = b_im + gate * (w_re * p_im + w_im * p_re)
        keep = keep * jnp.where(valid, pltpu.roll(keep, shift, 0), 1.0)
    return b_re, b_im, jnp.tile(keep, (1, reps))


def blocked_scan(count, width, pow_ref, starts_ref, lengths_ref, load_up, load_down, store_up, store_down):
    tiles = count // 8
    slots = starts_ref.shape[0]

    def keeps(t0, downward):
        rows = lax.broadcasted_iota(jnp.int32, (8, 128), 0) + t0
        inside = jnp.zeros((8, 128), jnp.bool_)
        for slot in range(slots):
            begin = starts_ref[slot]
            finish = begin + lengths_ref[slot]
            if downward:
                inside = inside | ((rows >= begin) & (rows < finish - 1))
            else:
                inside = inside | ((rows > begin) & (rows < finish))
        return inside.astype(jnp.float32)

    up_powers = (pow_ref[0], pow_ref[1])
    down_powers = (pow_ref[2], pow_ref[3])

    def carry_in(b_re, b_im, reach, powers, h_re, h_im):
        q_re = powers[0] * h_re - powers[1] * h_im
        q_im = powers[0] * h_im + powers[1] * h_re
        return b_re + reach * q_re, b_im + reach * q_im

    def step(i, carry):
        u_re, u_im, d_re, d_im = carry
        tu = pl.multiple_of(i * 8, 8)
        td = pl.multiple_of((tiles - 1 - i) * 8, 8)
        xu_re, xu_im = load_up(tu)
        xd_re, xd_im = load_down(td)
        bu_re, bu_im, ru = tile_scan(xu_re, xu_im, keeps(tu, False), up_powers, False)
        bd_re, bd_im, rd = tile_scan(xd_re, xd_im, keeps(td, True), up_powers, True)
        hu_re, hu_im = carry_in(bu_re, bu_im, ru, up_powers, u_re, u_im)
        hd_re, hd_im = carry_in(bd_re, bd_im, rd, down_powers, d_re, d_im)
        store_up(tu, hu_re, hu_im)
        store_down(td, hd_re, hd_im)
        return (hu_re[7:8], hu_im[7:8], hd_re[0:1], hd_im[0:1])

    zeros = jnp.zeros((1, width), jnp.float32)
    lax.fori_loop(0, tiles, step, (zeros, zeros, zeros, zeros), unroll=2)


def pole_powers(p_re, p_im):
    rows_re = [p_re]
    rows_im = [p_im]
    for _ in range(7):
        a, b = rows_re[-1], rows_im[-1]
        rows_re.append(a * p_re - b * p_im)
        rows_im.append(a * p_im + b * p_re)
    up_re = jnp.stack(rows_re)
    up_im = jnp.stack(rows_im)
    return jnp.stack([up_re, up_im, up_re[::-1], up_im[::-1]])


def recurrence_kernel(starts_ref, lengths_ref, pow_ref, x_ref, out_ref):
    count = x_ref.shape[0]
    width = pow_ref.shape[2]

    def load(t):
        return x_ref[pl.ds(t, 8), pl.ds(0, width)], x_ref[pl.ds(t, 8), pl.ds(width, width)]

    def store(column):
        def put(t, h_re, h_im):
            out_ref[pl.ds(t, 8), pl.ds(column, width)] = h_re
            out_ref[pl.ds(t, 8), pl.ds(column + width, width)] = h_im

        return put

    blocked_scan(count, width, pow_ref, starts_ref, lengths_ref, load, load, store(0), store(2 * width))


def recurrence(starts, lengths, powers, x):
    count, double = x.shape
    vmem = pl.BlockSpec(memory_space=pltpu.VMEM)
    smem = pl.BlockSpec(memory_space=pltpu.SMEM)
    return pl.pallas_call(
        recurrence_kernel,
        out_shape=jax.ShapeDtypeStruct((count, 2 * double), jnp.float32),
        in_specs=[smem, smem, vmem, vmem],
        out_specs=vmem,
        cost_estimate=pl.CostEstimate(
            flops=20 * count * double, transcendentals=0, bytes_accessed=16 * count * double
        ),
    )(starts, lengths, powers, x)


MESH = pl.DeviceIdType.MESH


def ring_place(position, n):
    upper = position // (n // 2)
    return (1 - upper) * (2 * position) + upper * (2 * (n - 1 - position) + 1)


def ring_position(index, n):
    odd = index % 2
    return (1 - odd) * (index // 2) + odd * (n - 1 - index // 2)


def ring_sum_kernel(n, x_ref, r_ref, o_ref, low, slots, rs_send, rs_recv, credit, done, ag_send, ag_recv):
    rows = x_ref.shape[0]
    half = rows // 2
    size = half // n
    me = ring_position(lax.axis_index("seq"), n)
    right = ring_place((me + 1) % n, n)
    left = ring_place((me + n - 1) % n, n)
    rings = ((0, me, right, left), (1, (n - me) % n, left, right))

    barrier = pltpu.get_barrier_semaphore()
    for neighbour in (left, right):
        pl.semaphore_signal(barrier, 1, device_id={"seq": neighbour}, device_id_type=MESH)
    pl.semaphore_wait(barrier, 2)
    o_ref[...] = x_ref[...]
    low[...] = x_ref[...].astype(low.dtype)

    def block(ring, k):
        return pl.ds(pl.multiple_of(ring * half + k * size, 8), size)

    def scatter_copy(ring, place, target, s):
        return pltpu.make_async_remote_copy(
            src_ref=low.at[block(ring, (place - s + n) % n)],
            dst_ref=slots.at[ring, s % 3],
            send_sem=rs_send.at[ring, s % 3],
            recv_sem=rs_recv.at[ring, s % 3],
            device_id={"seq": target},
            device_id_type=MESH,
        )

    def scatter_step(s, carry):
        copies = []
        for ring, place, target, source in rings:

            @pl.when(s >= 3)
            def _():
                pl.semaphore_wait(credit.at[ring], 1)

            copy = scatter_copy(ring, place, target, s)
            copy.start()
            copies.append(copy)
        for (ring, place, target, source), copy in zip(rings, copies):
            copy.wait_recv()
            into = block(ring, (place - s - 1 + 2 * n) % n)
            total = o_ref[into] + slots[ring, s % 3].astype(jnp.float32)
            o_ref[into] = total
            low[into] = total.astype(low.dtype)
            copy.wait_send()

            @pl.when(s <= n - 5)
            def _():
                pl.semaphore_signal(credit.at[ring], 1, device_id={"seq": source}, device_id_type=MESH)

        return carry

    lax.fori_loop(0, n - 1, scatter_step, 0)
    for ring, place, target, source in rings:
        pl.semaphore_signal(done.at[ring], 1, device_id={"seq": source}, device_id_type=MESH)
    for ring, place, target, source in rings:
        final = block(ring, (place + 1) % n)
        r_ref[final] = o_ref[final].astype(r_ref.dtype)
    for ring, place, target, source in rings:
        pl.semaphore_wait(done.at[ring], 1)

    def gather_copy(ring, place, target, s):
        where = block(ring, (place + 1 - s + n) % n)
        return pltpu.make_async_remote_copy(
            src_ref=r_ref.at[where],
            dst_ref=r_ref.at[where],
            send_sem=ag_send.at[ring, s],
            recv_sem=ag_recv.at[ring, s],
            device_id={"seq": target},
            device_id_type=MESH,
        )

    def gather_step(s, carry):
        for ring, place, target, source in rings:

            @pl.when(s >= 1)
            def _():
                gather_copy(ring, place, target, s - 1).wait_recv()

            gather_copy(ring, place, target, s).start()

            @pl.when(s >= 1)
            def _():
                gather_copy(ring, place, target, s - 1).wait_send()

        return carry

    lax.fori_loop(0, n - 1, gather_step, 0)
    for ring, place, target, source in rings:
        last = gather_copy(ring, place, target, n - 2)
        last.wait_recv()
        last.wait_send()


def ring_sum(x, n):
    rows, lanes = x.shape
    size = rows // (2 * n)
    return pl.pallas_call(
        lambda *refs: ring_sum_kernel(n, *refs),
        out_shape=jax.ShapeDtypeStruct((rows, lanes), jnp.bfloat16),
        in_specs=[pl.BlockSpec(memory_space=pltpu.VMEM)],
        out_specs=pl.BlockSpec(memory_space=pltpu.VMEM),
        scratch_shapes=[
            pltpu.VMEM((rows, lanes), jnp.float32),
            pltpu.VMEM((rows, lanes), jnp.bfloat16),
            pltpu.VMEM((2, 3, size, lanes), jnp.bfloat16),
            pltpu.SemaphoreType.DMA((2, 3)),
            pltpu.SemaphoreType.DMA((2, 3)),
            pltpu.SemaphoreType.REGULAR((2,)),
            pltpu.SemaphoreType.REGULAR((2,)),
            pltpu.SemaphoreType.DMA((2, n - 1)),
            pltpu.SemaphoreType.DMA((2, n - 1)),
        ],
        compiler_params=pltpu.CompilerParams(collective_id=0, has_side_effects=True),
    )(x)


def sum_over_seq(parts):
    n = lax.axis_size("seq")
    flat = jnp.concatenate([part.reshape(-1) for part in parts])
    grain = 2 * n * 16 * 128
    padded = -(-flat.size // grain) * grain
    flat = jnp.pad(flat, (0, padded - flat.size)).reshape(padded // 128, 128)
    total = ring_sum(flat, n).astype(jnp.float32).reshape(-1)
    pieces = []
    start = 0
    for part in parts:
        pieces.append(total[start : start + part.size].reshape(part.shape))
        start += part.size
    return pieces


def adjoint_kernel(starts_ref, lengths_ref, pow_ref, coef_ref, masks_ref, g_ref, states_ref, drive_ref, dg_ref, sums_ref, lam):
    count = g_ref.shape[0]
    width = coef_ref.shape[1]
    pad = 8
    f_re = coef_ref[2:3, :]
    f_im = coef_ref[3:4, :]
    zero_rows = jnp.zeros((pad, 4 * width), jnp.float32)
    lam[0:pad, :] = zero_rows
    lam[pad + count : 2 * pad + count, :] = zero_rows

    def load(column):
        def get(t):
            return g_ref[pl.ds(t, 8), pl.ds(column, width)], g_ref[pl.ds(t, 8), pl.ds(column + width, width)]

        return get

    def store(column):
        def put(t, h_re, h_im):
            lam[pl.ds(pad + t, 8), pl.ds(column, width)] = h_re
            lam[pl.ds(pad + t, 8), pl.ds(column + width, width)] = h_im

        return put

    blocked_scan(count, width, pow_ref, starts_ref, lengths_ref, load(2 * width), load(0), store(0), store(2 * width))

    rows = 16

    def part(ref, start, column):
        return ref[pl.ds(start, rows), pl.ds(column, width)]

    def epilogue(k, sums):
        gp_re, gp_im, gf_re, gf_im = sums
        r0 = pl.multiple_of(k * rows, rows)
        live = masks_ref[pl.ds(r0, rows), 0:1]
        keep_prev = masks_ref[pl.ds(r0, rows), 1:2]
        keep_next = masks_ref[pl.ds(r0, rows), 2:3]
        lb_re = part(lam, pad + r0, 0)
        lb_im = part(lam, pad + r0, width)
        la_re = part(lam, pad + r0, 2 * width)
        la_im = part(lam, pad + r0, 3 * width)
        gu_re = la_re + lb_re
        gu_im = la_im + lb_im
        dg_ref[pl.ds(r0, rows), pl.ds(0, width)] = ((f_re * gu_re + f_im * gu_im) * live).astype(dg_ref.dtype)
        dg_ref[pl.ds(r0, rows), pl.ds(width, width)] = ((f_re * gu_im - f_im * gu_re) * live).astype(dg_ref.dtype)
        d_re = part(drive_ref, r0, 0) * live
        d_im = part(drive_ref, r0, width) * live
        gf_re = gf_re + d_re * gu_re + d_im * gu_im
        gf_im = gf_im + d_re * gu_im - d_im * gu_re
        a_re = part(states_ref, r0, 0) * keep_next
        a_im = part(states_ref, r0, width) * keep_next
        b_re = part(states_ref, r0, 2 * width) * keep_prev
        b_im = part(states_ref, r0, 3 * width) * keep_prev
        ahead_rows = lam[pl.ds(pad + r0, rows + 8), pl.ds(2 * width, 2 * width)][1 : rows + 1]
        behind_rows = lam[pl.ds(r0, rows + 8), pl.ds(0, 2 * width)][pad - 1 : pad - 1 + rows]
        na_re = ahead_rows[:, :width]
        na_im = ahead_rows[:, width:]
        pb_re = behind_rows[:, :width]
        pb_im = behind_rows[:, width:]
        gp_re = gp_re + a_re * na_re + a_im * na_im + b_re * pb_re + b_im * pb_im
        gp_im = gp_im + a_re * na_im - a_im * na_re + b_re * pb_im - b_im * pb_re
        return (gp_re, gp_im, gf_re, gf_im)

    block = jnp.zeros((rows, width), jnp.float32)
    sums = lax.fori_loop(0, count // rows, epilogue, (block, block, block, block))
    for k, value in enumerate(sums):
        sums_ref[k : k + 1, :] = jnp.sum(value, 0, keepdims=True)


def adjoint(starts, lengths, powers, coef, masks, states_grad, states, drive):
    count, quad = states_grad.shape
    width = quad // 4
    vmem = pl.BlockSpec(memory_space=pltpu.VMEM)
    smem = pl.BlockSpec(memory_space=pltpu.SMEM)
    return pl.pallas_call(
        adjoint_kernel,
        out_shape=(
            jax.ShapeDtypeStruct((count, 2 * width), jnp.bfloat16),
            jax.ShapeDtypeStruct((4, width), jnp.float32),
        ),
        in_specs=[smem, smem] + [vmem] * 6,
        out_specs=(vmem, vmem),
        scratch_shapes=[pltpu.VMEM((count + 16, 4 * width), jnp.float32)],
        cost_estimate=pl.CostEstimate(
            flops=60 * count * width, transcendentals=0, bytes_accessed=48 * count * width
        ),
    )(starts, lengths, powers, coef, masks, states_grad, states, drive)


def update(weight, gradient, velocity, average, rate, decay):
    adjusted = gradient + decay * weight
    velocity_new = momentum * velocity + adjusted
    change = -rate * (adjusted + momentum * velocity_new)
    weight_new = weight + change
    average_new = smoothing * average + (1.0 - smoothing) * weight_new
    return (weight_new, velocity_new, average_new, change)


def contract_rows(left, right):
    return lax.dot_general(
        left, right, (((0,), (0,)), ((), ())), preferred_element_type=jnp.float32
    )


def contract_cols(left, right):
    return lax.dot_general(
        left, right, (((1,), (1,)), ((), ())), preferred_element_type=jnp.float32
    )


def gather_feat(value, axis):
    return lax.all_gather(value, "feat", axis=axis, tiled=True)


def split_exact(value):
    high = lax.reduce_precision(value, exponent_bits=8, mantissa_bits=7)
    rest = value - high
    middle = lax.reduce_precision(rest, exponent_bits=8, mantissa_bits=7)
    little = rest - middle
    return jnp.concatenate([high, middle, little], 0).astype(jnp.bfloat16)


def join_exact(pieces):
    third = pieces.shape[0] // 3
    pieces = pieces.astype(jnp.float32)
    return pieces[:third] + (pieces[third : 2 * third] + pieces[2 * third :])


def body(
    activations_in,
    cotangent,
    seq_start,
    seq_length,
    input_matrix,
    output_matrix,
    gate_matrix,
    feature_vectors,
    state_vectors,
    velocity_input,
    velocity_output,
    velocity_gate,
    velocity_feature,
    velocity_state,
    average_input,
    average_output,
    average_gate,
    average_feature,
    average_state,
):
    count = activations_in.shape[0]
    shard = activations_in.shape[1]
    layers = input_matrix.shape[0]
    width = state_vectors.shape[2]
    me = lax.axis_index("feat")
    offset = me * shard

    def mine(value):
        return lax.dynamic_slice_in_dim(value, offset, shard, axis=value.ndim - 1)

    alive, carry_prev, carry_next = masks_of(seq_start, seq_length, count)
    zero = jnp.zeros((1,), jnp.float32)
    after_next = jnp.concatenate([zero, carry_next[:-1]])
    before_prev = jnp.concatenate([carry_prev[1:], zero])
    mask_columns = jnp.stack([alive, carry_prev, carry_next, jnp.zeros_like(alive)], 1)


    in_all = gather_feat(input_matrix.astype(jnp.bfloat16), 1)
    rows_out = output_matrix.shape[1]
    paired = [
        gather_feat(jnp.concatenate([output_matrix[k], gate_matrix[k]], 0).astype(jnp.bfloat16), 1)
        for k in range(layers)
    ]
    out_all = [pair[:rows_out] for pair in paired]
    gate_all = [pair[rows_out:] for pair in paired]
    feature_pieces = split_exact(feature_vectors.reshape(-1, activations_in.shape[1]))
    feature_rows = feature_pieces.shape[0]
    feature_pad = -(-feature_rows // 16) * 16
    feature_pieces = jnp.pad(feature_pieces, ((0, feature_pad - feature_rows), (0, 0)))
    first = gather_feat(jnp.concatenate([activations_in, feature_pieces], 0), 1)
    stream = first[:count].astype(jnp.float32)
    feature_all = join_exact(first[count : count + feature_rows]).reshape(feature_vectors.shape[:-1] + (-1,))

    saved = []
    for layer in range(layers):
        in_low = in_all[layer]
        out_low = out_all[layer]
        gate_low = gate_all[layer]
        feature_row = feature_all[layer]
        pole_re, pole_im, factor_re, factor_im = coefficients(state_vectors[layer])
        center = jnp.mean(stream, 1, keepdims=True)
        spread = stream - center
        scale = lax.rsqrt(jnp.mean(spread * spread, 1, keepdims=True) + epsilon)
        unit = spread * scale
        normed = unit * feature_row[0] + feature_row[1]
        normed_low = normed.astype(jnp.bfloat16)
        drive = jnp.dot(normed_low, in_low, preferred_element_type=jnp.float32)
        drive_re = drive[:, :width]
        drive_im = drive[:, width:]
        source = jnp.concatenate(
            [
                (drive_re * factor_re - drive_im * factor_im) * alive[:, None],
                (drive_re * factor_im + drive_im * factor_re) * alive[:, None],
            ],
            1,
        )
        states = recurrence(seq_start, seq_length, pole_powers(pole_re, pole_im), source)
        states_low = states.astype(jnp.bfloat16)
        mixed = (
            jnp.dot(states_low, out_low, preferred_element_type=jnp.float32)
            + feature_row[2] * normed
        )
        cdf = (lax.erf(mixed * (1.0 / math.sqrt(2.0))) + 1.0) / 2.0
        act = mixed * cdf
        act_low = act.astype(jnp.bfloat16)
        pre = jnp.dot(act_low, gate_low, preferred_element_type=jnp.float32) + feature_row[3]
        saved.append((scale, unit, normed_low, drive, states, states_low, mixed, act, act_low, pre, cdf))
        stream = stream + act * jax.nn.sigmoid(pre)

    grad = gather_feat(cotangent, 1).astype(jnp.float32) * alive[:, None]
    layer_grads = [None] * layers
    for layer in reversed(range(layers)):
        scale, unit, normed_low, drive, states, states_low, mixed, act, act_low, pre, cdf = saved[layer]
        in_low = in_all[layer]
        out_low = out_all[layer]
        gate_low = gate_all[layer]
        feature_row = feature_all[layer]
        state_row = state_vectors[layer]
        pole_re, pole_im, factor_re, factor_im = coefficients(state_row)
        gate = jax.nn.sigmoid(pre)
        pre_grad = (grad * act * gate * (1.0 - gate)).astype(jnp.bfloat16)
        gate_grad = contract_rows(act_low, mine(pre_grad))
        gate_bias_grad = jnp.sum(pre_grad.astype(jnp.float32), 0)
        act_grad = grad * gate + contract_cols(pre_grad, gate_low)
        density = jnp.exp(mixed * mixed * -0.5) * (1.0 / math.sqrt(2.0 * math.pi))
        mixed_grad = act_grad * (cdf + mixed * density)
        normed = unit * feature_row[0] + feature_row[1]
        skip_grad = jnp.sum(mixed_grad * normed, 0)
        mixed_low = mixed_grad.astype(jnp.bfloat16)
        out_grad = contract_rows(states_low, mine(mixed_low))
        states_grad = contract_cols(mixed_low, out_low)
        coef = jnp.stack([pole_re, pole_im, factor_re, factor_im])
        drive_low, sums = adjoint(
            seq_start,
            seq_length,
            pole_powers(pole_re, -pole_im),
            coef,
            mask_columns,
            states_grad,
            states,
            drive,
        )
        gp_re, gp_im, gf_re, gf_im = sums[0], sums[1], sums[2], sums[3]
        row_grad = jax.vjp(coefficients, state_row)[1]((gp_re, gp_im, gf_re, gf_im))[0]
        in_grad = contract_rows(mine(normed_low), drive_low)
        normed_grad = mixed_grad * feature_row[2] + jnp.dot(
            drive_low, in_low.T, preferred_element_type=jnp.float32
        )
        gain_grad = jnp.sum(normed_grad * unit, 0)
        bias_grad = jnp.sum(normed_grad, 0)
        unit_grad = normed_grad * feature_row[0]
        first_mean = jnp.mean(unit_grad, 1, keepdims=True)
        second_mean = jnp.mean(unit_grad * unit, 1, keepdims=True)
        grad = grad + scale * (unit_grad - first_mean - unit * second_mean)
        feature_grad = mine(jnp.stack([gain_grad, bias_grad, skip_grad, gate_bias_grad]))
        layer_grads[layer] = (in_grad, out_grad, gate_grad, feature_grad, row_grad)
    stacked_in = jnp.stack([entry[0] for entry in layer_grads])
    stacked_out = jnp.stack([entry[1] for entry in layer_grads])
    stacked_gate = jnp.stack([entry[2] for entry in layer_grads])
    stacked_feature = jnp.stack([entry[3] for entry in layer_grads])
    stacked_state = jnp.stack([entry[4] for entry in layer_grads])
    summed = sum_over_seq((stacked_in, stacked_out, stacked_gate, stacked_feature, stacked_state))
    factor = 1.0 / math.sqrt(count * lax.axis_size("seq"))
    grad_in = summed[0] * factor
    grad_out = summed[1] * factor
    grad_gate = summed[2] * factor
    grad_feature = summed[3] * factor
    grad_state = summed[4] * factor
    new_in = update(input_matrix, grad_in, velocity_input, average_input, slow_rate, 0.0)
    new_out = update(output_matrix, grad_out, velocity_output, average_output, slow_rate, 0.0)
    new_gate = update(gate_matrix, grad_gate, velocity_gate, average_gate, main_rate, weight_decay)
    new_feature = update(
        feature_vectors, grad_feature, velocity_feature, average_feature, main_rate, weight_decay
    )
    new_state = update(state_vectors, grad_state, velocity_state, average_state, slow_rate, 0.0)
    return (
        mine(stream),
        mine(grad),
        grad_in,
        grad_out,
        grad_gate,
        grad_feature,
        grad_state,
        new_in[0],
        new_out[0],
        new_gate[0],
        new_feature[0],
        new_state[3],
        new_in[1],
        new_out[1],
        new_gate[1],
        new_feature[1],
        new_state[1],
        new_in[2],
        new_out[2],
        new_gate[2],
        new_feature[2],
        new_state[2],
    )


def solution(mesh):
    feat = P(None, None, "feat")
    rows = P(None, "feat", None)
    tokens = P("seq", "feat")
    return jax.shard_map(
        body,
        mesh=mesh,
        in_specs=(
            tokens,
            tokens,
            P("seq"),
            P("seq"),
            rows,
            feat,
            feat,
            feat,
            P(),
            rows,
            feat,
            feat,
            feat,
            P(),
            rows,
            feat,
            feat,
            feat,
            P(),
        ),
        out_specs=(
            tokens,
            tokens,
            rows,
            feat,
            feat,
            feat,
            P(),
            rows,
            feat,
            feat,
            feat,
            P(),
            rows,
            feat,
            feat,
            feat,
            P(),
            rows,
            feat,
            feat,
            feat,
            P(),
        ),
        check_vma=False,
    )
```

```python
import math

import jax
import jax.numpy as jnp
from jax import lax
from jax.experimental import pallas as pl
from jax.experimental.pallas import tpu as pltpu
from jax.sharding import PartitionSpec as P

epsilon = 1e-05
momentum = 0.9
smoothing = 0.5
slow_rate = 0.02
main_rate = 0.05
weight_decay = 0.1


def smooth(value):
    return jax.nn.gelu(value, approximate=False)


def masks_of(starts, lengths, count):
    position = jnp.arange(count, dtype=jnp.int32)[:, None]
    begin = starts[None, :]
    finish = begin + lengths[None, :]
    inside = (position >= begin) & (position < finish)
    alive = jnp.any(inside, 1)
    opening = jnp.any(inside & (position == begin), 1)
    closing = jnp.any(inside & (position == finish - 1), 1)
    return (
        alive.astype(jnp.float32),
        (alive & ~opening).astype(jnp.float32),
        (alive & ~closing).astype(jnp.float32),
    )


def coefficients(state_row):
    rate = -jnp.exp(state_row[0])
    frequency = state_row[1]
    timestep = jnp.exp(state_row[2])
    decay = jnp.exp(rate * timestep)
    angle = frequency * timestep
    pole_real = decay * jnp.cos(angle)
    pole_imag = decay * jnp.sin(angle)
    denom = rate * rate + frequency * frequency
    factor_real = ((pole_real - 1.0) * rate + pole_imag * frequency) / denom
    factor_imag = (pole_imag * rate - (pole_real - 1.0) * frequency) / denom
    return (pole_real, pole_imag, factor_real, factor_imag)


def tile_scan(x_re, x_im, keep, powers, down):
    reps = x_re.shape[1] // keep.shape[1]
    rows = lax.broadcasted_iota(jnp.int32, keep.shape, 0)
    b_re, b_im = x_re, x_im
    for level, k in enumerate((1, 2, 4)):
        shift = 8 - k if down else k
        valid = rows <= 7 - k if down else rows >= k
        gate = jnp.tile(jnp.where(valid, keep, 0.0), (1, reps))
        p_re = pltpu.roll(b_re, shift, 0)
        p_im = pltpu.roll(b_im, shift, 0)
        w_re = powers[0][(0, 1, 3)[level] : (0, 1, 3)[level] + 1]
        w_im = powers[1][(0, 1, 3)[level] : (0, 1, 3)[level] + 1]
        b_re = b_re + gate * (w_re * p_re - w_im * p_im)
        b_im = b_im + gate * (w_re * p_im + w_im * p_re)
        keep = keep * jnp.where(valid, pltpu.roll(keep, shift, 0), 1.0)
    return b_re, b_im, jnp.tile(keep, (1, reps))


def blocked_scan(count, width, pow_ref, starts_ref, lengths_ref, load_up, load_down, store_up, store_down):
    tiles = count // 8
    slots = starts_ref.shape[0]

    def keeps(t0, downward):
        rows = lax.broadcasted_iota(jnp.int32, (8, 128), 0) + t0
        inside = jnp.zeros((8, 128), jnp.bool_)
        for slot in range(slots):
            begin = starts_ref[slot]
            finish = begin + lengths_ref[slot]
            if downward:
                inside = inside | ((rows >= begin) & (rows < finish - 1))
            else:
                inside = inside | ((rows > begin) & (rows < finish))
        return inside.astype(jnp.float32)

    up_powers = (pow_ref[0], pow_ref[1])
    down_powers = (pow_ref[2], pow_ref[3])

    def carry_in(b_re, b_im, reach, powers, h_re, h_im):
        q_re = powers[0] * h_re - powers[1] * h_im
        q_im = powers[0] * h_im + powers[1] * h_re
        return b_re + reach * q_re, b_im + reach * q_im

    def step(i, carry):
        u_re, u_im, d_re, d_im = carry
        tu = pl.multiple_of(i * 8, 8)
        td = pl.multiple_of((tiles - 1 - i) * 8, 8)
        xu_re, xu_im = load_up(tu)
        xd_re, xd_im = load_down(td)
        bu_re, bu_im, ru = tile_scan(xu_re, xu_im, keeps(tu, False), up_powers, False)
        bd_re, bd_im, rd = tile_scan(xd_re, xd_im, keeps(td, True), up_powers, True)
        hu_re, hu_im = carry_in(bu_re, bu_im, ru, up_powers, u_re, u_im)
        hd_re, hd_im = carry_in(bd_re, bd_im, rd, down_powers, d_re, d_im)
        store_up(tu, hu_re, hu_im)
        store_down(td, hd_re, hd_im)
        return (hu_re[7:8], hu_im[7:8], hd_re[0:1], hd_im[0:1])

    zeros = jnp.zeros((1, width), jnp.float32)
    lax.fori_loop(0, tiles, step, (zeros, zeros, zeros, zeros), unroll=2)


def pole_powers(p_re, p_im):
    rows_re = [p_re]
    rows_im = [p_im]
    for _ in range(7):
        a, b = rows_re[-1], rows_im[-1]
        rows_re.append(a * p_re - b * p_im)
        rows_im.append(a * p_im + b * p_re)
    up_re = jnp.stack(rows_re)
    up_im = jnp.stack(rows_im)
    return jnp.stack([up_re, up_im, up_re[::-1], up_im[::-1]])


def recurrence_kernel(starts_ref, lengths_ref, pow_ref, x_ref, out_ref):
    count = x_ref.shape[0]
    width = pow_ref.shape[2]

    def load(t):
        return x_ref[pl.ds(t, 8), pl.ds(0, width)], x_ref[pl.ds(t, 8), pl.ds(width, width)]

    def store(column):
        def put(t, h_re, h_im):
            out_ref[pl.ds(t, 8), pl.ds(column, width)] = h_re
            out_ref[pl.ds(t, 8), pl.ds(column + width, width)] = h_im

        return put

    blocked_scan(count, width, pow_ref, starts_ref, lengths_ref, load, load, store(0), store(2 * width))


def recurrence(starts, lengths, powers, x):
    count, double = x.shape
    vmem = pl.BlockSpec(memory_space=pltpu.VMEM)
    smem = pl.BlockSpec(memory_space=pltpu.SMEM)
    return pl.pallas_call(
        recurrence_kernel,
        out_shape=jax.ShapeDtypeStruct((count, 2 * double), jnp.float32),
        in_specs=[smem, smem, vmem, vmem],
        out_specs=vmem,
        cost_estimate=pl.CostEstimate(
            flops=20 * count * double, transcendentals=0, bytes_accessed=16 * count * double
        ),
    )(starts, lengths, powers, x)


MESH = pl.DeviceIdType.MESH


def ring_place(position, n):
    upper = position // (n // 2)
    return (1 - upper) * (2 * position) + upper * (2 * (n - 1 - position) + 1)


def ring_position(index, n):
    odd = index % 2
    return (1 - odd) * (index // 2) + odd * (n - 1 - index // 2)


def ring_sum_kernel(n, x_ref, r_ref, o_ref, low, slots, rs_send, rs_recv, credit, done, ag_send, ag_recv):
    rows = x_ref.shape[0]
    half = rows // 2
    size = half // n
    me = ring_position(lax.axis_index("seq"), n)
    right = ring_place((me + 1) % n, n)
    left = ring_place((me + n - 1) % n, n)
    rings = ((0, me, right, left), (1, (n - me) % n, left, right))

    barrier = pltpu.get_barrier_semaphore()
    for neighbour in (left, right):
        pl.semaphore_signal(barrier, 1, device_id={"seq": neighbour}, device_id_type=MESH)
    pl.semaphore_wait(barrier, 2)
    o_ref[...] = x_ref[...]
    low[...] = x_ref[...].astype(low.dtype)

    def block(ring, k):
        return pl.ds(pl.multiple_of(ring * half + k * size, 8), size)

    def scatter_copy(ring, place, target, s):
        return pltpu.make_async_remote_copy(
            src_ref=low.at[block(ring, (place - s + n) % n)],
            dst_ref=slots.at[ring, s % 3],
            send_sem=rs_send.at[ring, s % 3],
            recv_sem=rs_recv.at[ring, s % 3],
            device_id={"seq": target},
            device_id_type=MESH,
        )

    def scatter_step(s, carry):
        copies = []
        for ring, place, target, source in rings:

            @pl.when(s >= 3)
            def _():
                pl.semaphore_wait(credit.at[ring], 1)

            copy = scatter_copy(ring, place, target, s)
            copy.start()
            copies.append(copy)
        for (ring, place, target, source), copy in zip(rings, copies):
            copy.wait_recv()
            into = block(ring, (place - s - 1 + 2 * n) % n)
            total = o_ref[into] + slots[ring, s % 3].astype(jnp.float32)
            o_ref[into] = total
            low[into] = total.astype(low.dtype)
            copy.wait_send()

            @pl.when(s <= n - 5)
            def _():
                pl.semaphore_signal(credit.at[ring], 1, device_id={"seq": source}, device_id_type=MESH)

        return carry

    lax.fori_loop(0, n - 1, scatter_step, 0, unroll=True)
    for ring, place, target, source in rings:
        pl.semaphore_signal(done.at[ring], 1, device_id={"seq": source}, device_id_type=MESH)
    for ring, place, target, source in rings:
        final = block(ring, (place + 1) % n)
        r_ref[final] = o_ref[final].astype(r_ref.dtype)
    for ring, place, target, source in rings:
        pl.semaphore_wait(done.at[ring], 1)

    def gather_copy(ring, place, target, s):
        where = block(ring, (place + 1 - s + n) % n)
        return pltpu.make_async_remote_copy(
            src_ref=r_ref.at[where],
            dst_ref=r_ref.at[where],
            send_sem=ag_send.at[ring, s],
            recv_sem=ag_recv.at[ring, s],
            device_id={"seq": target},
            device_id_type=MESH,
        )

    def gather_step(s, carry):
        for ring, place, target, source in rings:

            @pl.when(s >= 1)
            def _():
                gather_copy(ring, place, target, s - 1).wait_recv()

            gather_copy(ring, place, target, s).start()

            @pl.when(s >= 1)
            def _():
                gather_copy(ring, place, target, s - 1).wait_send()

        return carry

    lax.fori_loop(0, n - 1, gather_step, 0, unroll=True)
    for ring, place, target, source in rings:
        last = gather_copy(ring, place, target, n - 2)
        last.wait_recv()
        last.wait_send()


def ring_sum(x, n):
    rows, lanes = x.shape
    size = rows // (2 * n)
    return pl.pallas_call(
        lambda *refs: ring_sum_kernel(n, *refs),
        out_shape=jax.ShapeDtypeStruct((rows, lanes), jnp.bfloat16),
        in_specs=[pl.BlockSpec(memory_space=pltpu.VMEM)],
        out_specs=pl.BlockSpec(memory_space=pltpu.VMEM),
        scratch_shapes=[
            pltpu.VMEM((rows, lanes), jnp.float32),
            pltpu.VMEM((rows, lanes), jnp.bfloat16),
            pltpu.VMEM((2, 3, size, lanes), jnp.bfloat16),
            pltpu.SemaphoreType.DMA((2, 3)),
            pltpu.SemaphoreType.DMA((2, 3)),
            pltpu.SemaphoreType.REGULAR((2,)),
            pltpu.SemaphoreType.REGULAR((2,)),
            pltpu.SemaphoreType.DMA((2, n - 1)),
            pltpu.SemaphoreType.DMA((2, n - 1)),
        ],
        compiler_params=pltpu.CompilerParams(collective_id=0, has_side_effects=True),
    )(x)


def sum_over_seq(parts):
    n = lax.axis_size("seq")
    flat = jnp.concatenate([part.reshape(-1) for part in parts])
    grain = 2 * n * 16 * 128
    padded = -(-flat.size // grain) * grain
    flat = jnp.pad(flat, (0, padded - flat.size)).reshape(padded // 128, 128)
    total = ring_sum(flat, n).astype(jnp.float32).reshape(-1)
    pieces = []
    start = 0
    for part in parts:
        pieces.append(total[start : start + part.size].reshape(part.shape))
        start += part.size
    return pieces


def adjoint_kernel(starts_ref, lengths_ref, pow_ref, coef_ref, masks_ref, g_ref, states_ref, drive_ref, dg_ref, sums_ref, lam):
    count = g_ref.shape[0]
    width = coef_ref.shape[1]
    pad = 8
    f_re = coef_ref[2:3, :]
    f_im = coef_ref[3:4, :]
    zero_rows = jnp.zeros((pad, 4 * width), jnp.float32)
    lam[0:pad, :] = zero_rows
    lam[pad + count : 2 * pad + count, :] = zero_rows

    def load(column):
        def get(t):
            return g_ref[pl.ds(t, 8), pl.ds(column, width)], g_ref[pl.ds(t, 8), pl.ds(column + width, width)]

        return get

    def store(column):
        def put(t, h_re, h_im):
            lam[pl.ds(pad + t, 8), pl.ds(column, width)] = h_re
            lam[pl.ds(pad + t, 8), pl.ds(column + width, width)] = h_im

        return put

    blocked_scan(count, width, pow_ref, starts_ref, lengths_ref, load(2 * width), load(0), store(0), store(2 * width))

    rows = 16

    def part(ref, start, column):
        return ref[pl.ds(start, rows), pl.ds(column, width)]

    def epilogue(k, sums):
        gp_re, gp_im, gf_re, gf_im = sums
        r0 = pl.multiple_of(k * rows, rows)
        live = masks_ref[pl.ds(r0, rows), 0:1]
        keep_prev = masks_ref[pl.ds(r0, rows), 1:2]
        keep_next = masks_ref[pl.ds(r0, rows), 2:3]
        lb_re = part(lam, pad + r0, 0)
        lb_im = part(lam, pad + r0, width)
        la_re = part(lam, pad + r0, 2 * width)
        la_im = part(lam, pad + r0, 3 * width)
        gu_re = la_re + lb_re
        gu_im = la_im + lb_im
        dg_ref[pl.ds(r0, rows), pl.ds(0, width)] = ((f_re * gu_re + f_im * gu_im) * live).astype(dg_ref.dtype)
        dg_ref[pl.ds(r0, rows), pl.ds(width, width)] = ((f_re * gu_im - f_im * gu_re) * live).astype(dg_ref.dtype)
        d_re = part(drive_ref, r0, 0) * live
        d_im = part(drive_ref, r0, width) * live
        gf_re = gf_re + d_re * gu_re + d_im * gu_im
        gf_im = gf_im + d_re * gu_im - d_im * gu_re
        a_re = part(states_ref, r0, 0) * keep_next
        a_im = part(states_ref, r0, width) * keep_next
        b_re = part(states_ref, r0, 2 * width) * keep_prev
        b_im = part(states_ref, r0, 3 * width) * keep_prev
        ahead_rows = lam[pl.ds(pad + r0, rows + 8), pl.ds(2 * width, 2 * width)][1 : rows + 1]
        behind_rows = lam[pl.ds(r0, rows + 8), pl.ds(0, 2 * width)][pad - 1 : pad - 1 + rows]
        na_re = ahead_rows[:, :width]
        na_im = ahead_rows[:, width:]
        pb_re = behind_rows[:, :width]
        pb_im = behind_rows[:, width:]
        gp_re = gp_re + a_re * na_re + a_im * na_im + b_re * pb_re + b_im * pb_im
        gp_im = gp_im + a_re * na_im - a_im * na_re + b_re * pb_im - b_im * pb_re
        return (gp_re, gp_im, gf_re, gf_im)

    block = jnp.zeros((rows, width), jnp.float32)
    sums = lax.fori_loop(0, count // rows, epilogue, (block, block, block, block))
    for k, value in enumerate(sums):
        sums_ref[k : k + 1, :] = jnp.sum(value, 0, keepdims=True)


def adjoint(starts, lengths, powers, coef, masks, states_grad, states, drive):
    count, quad = states_grad.shape
    width = quad // 4
    vmem = pl.BlockSpec(memory_space=pltpu.VMEM)
    smem = pl.BlockSpec(memory_space=pltpu.SMEM)
    return pl.pallas_call(
        adjoint_kernel,
        out_shape=(
            jax.ShapeDtypeStruct((count, 2 * width), jnp.bfloat16),
            jax.ShapeDtypeStruct((4, width), jnp.float32),
        ),
        in_specs=[smem, smem] + [vmem] * 6,
        out_specs=(vmem, vmem),
        scratch_shapes=[pltpu.VMEM((count + 16, 4 * width), jnp.float32)],
        cost_estimate=pl.CostEstimate(
            flops=60 * count * width, transcendentals=0, bytes_accessed=48 * count * width
        ),
    )(starts, lengths, powers, coef, masks, states_grad, states, drive)


def update(weight, gradient, velocity, average, rate, decay):
    adjusted = gradient + decay * weight
    velocity_new = momentum * velocity + adjusted
    change = -rate * (adjusted + momentum * velocity_new)
    weight_new = weight + change
    average_new = smoothing * average + (1.0 - smoothing) * weight_new
    return (weight_new, velocity_new, average_new, change)


def contract_rows(left, right):
    return lax.dot_general(
        left, right, (((0,), (0,)), ((), ())), preferred_element_type=jnp.float32
    )


def contract_cols(left, right):
    return lax.dot_general(
        left, right, (((1,), (1,)), ((), ())), preferred_element_type=jnp.float32
    )


def gather_feat(value, axis):
    return lax.all_gather(value, "feat", axis=axis, tiled=True)


def split_exact(value):
    high = lax.reduce_precision(value, exponent_bits=8, mantissa_bits=7)
    rest = value - high
    middle = lax.reduce_precision(rest, exponent_bits=8, mantissa_bits=7)
    little = rest - middle
    return jnp.concatenate([high, middle, little], 0).astype(jnp.bfloat16)


def join_exact(pieces):
    third = pieces.shape[0] // 3
    pieces = pieces.astype(jnp.float32)
    return pieces[:third] + (pieces[third : 2 * third] + pieces[2 * third :])


def body(
    activations_in,
    cotangent,
    seq_start,
    seq_length,
    input_matrix,
    output_matrix,
    gate_matrix,
    feature_vectors,
    state_vectors,
    velocity_input,
    velocity_output,
    velocity_gate,
    velocity_feature,
    velocity_state,
    average_input,
    average_output,
    average_gate,
    average_feature,
    average_state,
):
    count = activations_in.shape[0]
    shard = activations_in.shape[1]
    layers = input_matrix.shape[0]
    width = state_vectors.shape[2]
    me = lax.axis_index("feat")
    offset = me * shard

    def mine(value):
        return lax.dynamic_slice_in_dim(value, offset, shard, axis=value.ndim - 1)

    alive, carry_prev, carry_next = masks_of(seq_start, seq_length, count)
    zero = jnp.zeros((1,), jnp.float32)
    after_next = jnp.concatenate([zero, carry_next[:-1]])
    before_prev = jnp.concatenate([carry_prev[1:], zero])
    mask_columns = jnp.stack([alive, carry_prev, carry_next, jnp.zeros_like(alive)], 1)


    in_all = gather_feat(input_matrix.astype(jnp.bfloat16), 1)
    rows_out = output_matrix.shape[1]
    paired = [
        gather_feat(jnp.concatenate([output_matrix[k], gate_matrix[k]], 0).astype(jnp.bfloat16), 1)
        for k in range(layers)
    ]
    out_all = [pair[:rows_out] for pair in paired]
    gate_all = [pair[rows_out:] for pair in paired]
    feature_pieces = split_exact(feature_vectors.reshape(-1, activations_in.shape[1]))
    feature_rows = feature_pieces.shape[0]
    feature_pad = -(-feature_rows // 16) * 16
    feature_pieces = jnp.pad(feature_pieces, ((0, feature_pad - feature_rows), (0, 0)))
    first = gather_feat(jnp.concatenate([activations_in, feature_pieces], 0), 1)
    stream = first[:count].astype(jnp.float32)
    feature_all = join_exact(first[count : count + feature_rows]).reshape(feature_vectors.shape[:-1] + (-1,))

    saved = []
    for layer in range(layers):
        in_low = in_all[layer]
        out_low = out_all[layer]
        gate_low = gate_all[layer]
        feature_row = feature_all[layer]
        pole_re, pole_im, factor_re, factor_im = coefficients(state_vectors[layer])
        center = jnp.mean(stream, 1, keepdims=True)
        spread = stream - center
        scale = lax.rsqrt(jnp.mean(spread * spread, 1, keepdims=True) + epsilon)
        unit = spread * scale
        normed = unit * feature_row[0] + feature_row[1]
        normed_low = normed.astype(jnp.bfloat16)
        drive = jnp.dot(normed_low, in_low, preferred_element_type=jnp.float32)
        drive_re = drive[:, :width]
        drive_im = drive[:, width:]
        source = jnp.concatenate(
            [
                (drive_re * factor_re - drive_im * factor_im) * alive[:, None],
                (drive_re * factor_im + drive_im * factor_re) * alive[:, None],
            ],
            1,
        )
        states = recurrence(seq_start, seq_length, pole_powers(pole_re, pole_im), source)
        states_low = states.astype(jnp.bfloat16)
        mixed = (
            jnp.dot(states_low, out_low, preferred_element_type=jnp.float32)
            + feature_row[2] * normed
        )
        cdf = (lax.erf(mixed * (1.0 / math.sqrt(2.0))) + 1.0) / 2.0
        act = mixed * cdf
        act_low = act.astype(jnp.bfloat16)
        pre = jnp.dot(act_low, gate_low, preferred_element_type=jnp.float32) + feature_row[3]
        saved.append((scale, unit, normed_low, drive, states, states_low, mixed, act, act_low, pre, cdf))
        stream = stream + act * jax.nn.sigmoid(pre)

    grad = gather_feat(cotangent, 1).astype(jnp.float32) * alive[:, None]
    layer_grads = [None] * layers
    for layer in reversed(range(layers)):
        scale, unit, normed_low, drive, states, states_low, mixed, act, act_low, pre, cdf = saved[layer]
        in_low = in_all[layer]
        out_low = out_all[layer]
        gate_low = gate_all[layer]
        feature_row = feature_all[layer]
        state_row = state_vectors[layer]
        pole_re, pole_im, factor_re, factor_im = coefficients(state_row)
        gate = jax.nn.sigmoid(pre)
        pre_grad = (grad * act * gate * (1.0 - gate)).astype(jnp.bfloat16)
        gate_grad = contract_rows(act_low, mine(pre_grad))
        gate_bias_grad = jnp.sum(pre_grad.astype(jnp.float32), 0)
        act_grad = grad * gate + contract_cols(pre_grad, gate_low)
        density = jnp.exp(mixed * mixed * -0.5) * (1.0 / math.sqrt(2.0 * math.pi))
        mixed_grad = act_grad * (cdf + mixed * density)
        normed = unit * feature_row[0] + feature_row[1]
        skip_grad = jnp.sum(mixed_grad * normed, 0)
        mixed_low = mixed_grad.astype(jnp.bfloat16)
        out_grad = contract_rows(states_low, mine(mixed_low))
        states_grad = contract_cols(mixed_low, out_low)
        coef = jnp.stack([pole_re, pole_im, factor_re, factor_im])
        drive_low, sums = adjoint(
            seq_start,
            seq_length,
            pole_powers(pole_re, -pole_im),
            coef,
            mask_columns,
            states_grad,
            states,
            drive,
        )
        gp_re, gp_im, gf_re, gf_im = sums[0], sums[1], sums[2], sums[3]
        row_grad = jax.vjp(coefficients, state_row)[1]((gp_re, gp_im, gf_re, gf_im))[0]
        in_grad = contract_rows(mine(normed_low), drive_low)
        normed_grad = mixed_grad * feature_row[2] + jnp.dot(
            drive_low, in_low.T, preferred_element_type=jnp.float32
        )
        gain_grad = jnp.sum(normed_grad * unit, 0)
        bias_grad = jnp.sum(normed_grad, 0)
        unit_grad = normed_grad * feature_row[0]
        first_mean = jnp.mean(unit_grad, 1, keepdims=True)
        second_mean = jnp.mean(unit_grad * unit, 1, keepdims=True)
        grad = grad + scale * (unit_grad - first_mean - unit * second_mean)
        feature_grad = mine(jnp.stack([gain_grad, bias_grad, skip_grad, gate_bias_grad]))
        layer_grads[layer] = (in_grad, out_grad, gate_grad, feature_grad, row_grad)
    stacked_in = jnp.stack([entry[0] for entry in layer_grads])
    stacked_out = jnp.stack([entry[1] for entry in layer_grads])
    stacked_gate = jnp.stack([entry[2] for entry in layer_grads])
    stacked_feature = jnp.stack([entry[3] for entry in layer_grads])
    stacked_state = jnp.stack([entry[4] for entry in layer_grads])
    summed = sum_over_seq((stacked_in, stacked_out, stacked_gate, stacked_feature, stacked_state))
    factor = 1.0 / math.sqrt(count * lax.axis_size("seq"))
    grad_in = summed[0] * factor
    grad_out = summed[1] * factor
    grad_gate = summed[2] * factor
    grad_feature = summed[3] * factor
    grad_state = summed[4] * factor
    new_in = update(input_matrix, grad_in, velocity_input, average_input, slow_rate, 0.0)
    new_out = update(output_matrix, grad_out, velocity_output, average_output, slow_rate, 0.0)
    new_gate = update(gate_matrix, grad_gate, velocity_gate, average_gate, main_rate, weight_decay)
    new_feature = update(
        feature_vectors, grad_feature, velocity_feature, average_feature, main_rate, weight_decay
    )
    new_state = update(state_vectors, grad_state, velocity_state, average_state, slow_rate, 0.0)
    return (
        mine(stream),
        mine(grad),
        grad_in,
        grad_out,
        grad_gate,
        grad_feature,
        grad_state,
        new_in[0],
        new_out[0],
        new_gate[0],
        new_feature[0],
        new_state[3],
        new_in[1],
        new_out[1],
        new_gate[1],
        new_feature[1],
        new_state[1],
        new_in[2],
        new_out[2],
        new_gate[2],
        new_feature[2],
        new_state[2],
    )


def solution(mesh):
    feat = P(None, None, "feat")
    rows = P(None, "feat", None)
    tokens = P("seq", "feat")
    return jax.shard_map(
        body,
        mesh=mesh,
        in_specs=(
            tokens,
            tokens,
            P("seq"),
            P("seq"),
            rows,
            feat,
            feat,
            feat,
            P(),
            rows,
            feat,
            feat,
            feat,
            P(),
            rows,
            feat,
            feat,
            feat,
            P(),
        ),
        out_specs=(
            tokens,
            tokens,
            rows,
            feat,
            feat,
            feat,
            P(),
            rows,
            feat,
            feat,
            feat,
            P(),
            rows,
            feat,
            feat,
            feat,
            P(),
            rows,
            feat,
            feat,
            feat,
            P(),
        ),
        check_vma=False,
    )
```

```python
import math

import jax
import jax.numpy as jnp
from jax import lax
from jax.experimental import pallas as pl
from jax.experimental.pallas import tpu as pltpu
from jax.sharding import PartitionSpec as P

epsilon = 1e-05
momentum = 0.9
smoothing = 0.5
slow_rate = 0.02
main_rate = 0.05
weight_decay = 0.1


def smooth(value):
    return jax.nn.gelu(value, approximate=False)


def masks_of(starts, lengths, count):
    position = jnp.arange(count, dtype=jnp.int32)[:, None]
    begin = starts[None, :]
    finish = begin + lengths[None, :]
    inside = (position >= begin) & (position < finish)
    alive = jnp.any(inside, 1)
    opening = jnp.any(inside & (position == begin), 1)
    closing = jnp.any(inside & (position == finish - 1), 1)
    return (
        alive.astype(jnp.float32),
        (alive & ~opening).astype(jnp.float32),
        (alive & ~closing).astype(jnp.float32),
    )


def coefficients(state_row):
    rate = -jnp.exp(state_row[0])
    frequency = state_row[1]
    timestep = jnp.exp(state_row[2])
    decay = jnp.exp(rate * timestep)
    angle = frequency * timestep
    pole_real = decay * jnp.cos(angle)
    pole_imag = decay * jnp.sin(angle)
    denom = rate * rate + frequency * frequency
    factor_real = ((pole_real - 1.0) * rate + pole_imag * frequency) / denom
    factor_imag = (pole_imag * rate - (pole_real - 1.0) * frequency) / denom
    return (pole_real, pole_imag, factor_real, factor_imag)


def tile_scan(x_re, x_im, keep, powers, down):
    reps = x_re.shape[1] // keep.shape[1]
    rows = lax.broadcasted_iota(jnp.int32, keep.shape, 0)
    b_re, b_im = x_re, x_im
    for level, k in enumerate((1, 2, 4)):
        shift = 8 - k if down else k
        valid = rows <= 7 - k if down else rows >= k
        gate = jnp.tile(jnp.where(valid, keep, 0.0), (1, reps))
        p_re = pltpu.roll(b_re, shift, 0)
        p_im = pltpu.roll(b_im, shift, 0)
        w_re = powers[0][(0, 1, 3)[level] : (0, 1, 3)[level] + 1]
        w_im = powers[1][(0, 1, 3)[level] : (0, 1, 3)[level] + 1]
        b_re = b_re + gate * (w_re * p_re - w_im * p_im)
        b_im = b_im + gate * (w_re * p_im + w_im * p_re)
        keep = keep * jnp.where(valid, pltpu.roll(keep, shift, 0), 1.0)
    return b_re, b_im, jnp.tile(keep, (1, reps))


def blocked_scan(count, width, pow_ref, starts_ref, lengths_ref, load_up, load_down, store_up, store_down):
    tiles = count // 8
    slots = starts_ref.shape[0]

    def keeps(t0, downward):
        rows = lax.broadcasted_iota(jnp.int32, (8, 128), 0) + t0
        inside = jnp.zeros((8, 128), jnp.bool_)
        for slot in range(slots):
            begin = starts_ref[slot]
            finish = begin + lengths_ref[slot]
            if downward:
                inside = inside | ((rows >= begin) & (rows < finish - 1))
            else:
                inside = inside | ((rows > begin) & (rows < finish))
        return inside.astype(jnp.float32)

    up_powers = (pow_ref[0], pow_ref[1])
    down_powers = (pow_ref[2], pow_ref[3])

    def carry_in(b_re, b_im, reach, powers, h_re, h_im):
        q_re = powers[0] * h_re - powers[1] * h_im
        q_im = powers[0] * h_im + powers[1] * h_re
        return b_re + reach * q_re, b_im + reach * q_im

    def step(i, carry):
        u_re, u_im, d_re, d_im = carry
        tu = pl.multiple_of(i * 8, 8)
        td = pl.multiple_of((tiles - 1 - i) * 8, 8)
        xu_re, xu_im = load_up(tu)
        xd_re, xd_im = load_down(td)
        bu_re, bu_im, ru = tile_scan(xu_re, xu_im, keeps(tu, False), up_powers, False)
        bd_re, bd_im, rd = tile_scan(xd_re, xd_im, keeps(td, True), up_powers, True)
        hu_re, hu_im = carry_in(bu_re, bu_im, ru, up_powers, u_re, u_im)
        hd_re, hd_im = carry_in(bd_re, bd_im, rd, down_powers, d_re, d_im)
        store_up(tu, hu_re, hu_im)
        store_down(td, hd_re, hd_im)
        return (hu_re[7:8], hu_im[7:8], hd_re[0:1], hd_im[0:1])

    zeros = jnp.zeros((1, width), jnp.float32)
    lax.fori_loop(0, tiles, step, (zeros, zeros, zeros, zeros), unroll=4)


def pole_powers(p_re, p_im):
    rows_re = [p_re]
    rows_im = [p_im]
    for _ in range(7):
        a, b = rows_re[-1], rows_im[-1]
        rows_re.append(a * p_re - b * p_im)
        rows_im.append(a * p_im + b * p_re)
    up_re = jnp.stack(rows_re)
    up_im = jnp.stack(rows_im)
    return jnp.stack([up_re, up_im, up_re[::-1], up_im[::-1]])


def recurrence_kernel(starts_ref, lengths_ref, pow_ref, x_ref, out_ref):
    count = x_ref.shape[0]
    width = pow_ref.shape[2]

    def load(t):
        return x_ref[pl.ds(t, 8), pl.ds(0, width)], x_ref[pl.ds(t, 8), pl.ds(width, width)]

    def store(column):
        def put(t, h_re, h_im):
            out_ref[pl.ds(t, 8), pl.ds(column, width)] = h_re
            out_ref[pl.ds(t, 8), pl.ds(column + width, width)] = h_im

        return put

    blocked_scan(count, width, pow_ref, starts_ref, lengths_ref, load, load, store(0), store(2 * width))


def recurrence(starts, lengths, powers, x):
    count, double = x.shape
    vmem = pl.BlockSpec(memory_space=pltpu.VMEM)
    smem = pl.BlockSpec(memory_space=pltpu.SMEM)
    return pl.pallas_call(
        recurrence_kernel,
        out_shape=jax.ShapeDtypeStruct((count, 2 * double), jnp.float32),
        in_specs=[smem, smem, vmem, vmem],
        out_specs=vmem,
        cost_estimate=pl.CostEstimate(
            flops=20 * count * double, transcendentals=0, bytes_accessed=16 * count * double
        ),
    )(starts, lengths, powers, x)


MESH = pl.DeviceIdType.MESH


def ring_place(position, n):
    upper = position // (n // 2)
    return (1 - upper) * (2 * position) + upper * (2 * (n - 1 - position) + 1)


def ring_position(index, n):
    odd = index % 2
    return (1 - odd) * (index // 2) + odd * (n - 1 - index // 2)


def ring_sum_kernel(n, x_ref, r_ref, o_ref, low, slots, rs_send, rs_recv, credit, done, ag_send, ag_recv):
    rows = x_ref.shape[0]
    half = rows // 2
    size = half // n
    me = ring_position(lax.axis_index("seq"), n)
    right = ring_place((me + 1) % n, n)
    left = ring_place((me + n - 1) % n, n)
    rings = ((0, me, right, left), (1, (n - me) % n, left, right))

    barrier = pltpu.get_barrier_semaphore()
    for neighbour in (left, right):
        pl.semaphore_signal(barrier, 1, device_id={"seq": neighbour}, device_id_type=MESH)
    pl.semaphore_wait(barrier, 2)
    o_ref[...] = x_ref[...]
    low[...] = x_ref[...].astype(low.dtype)

    def block(ring, k):
        return pl.ds(pl.multiple_of(ring * half + k * size, 8), size)

    def scatter_copy(ring, place, target, s):
        return pltpu.make_async_remote_copy(
            src_ref=low.at[block(ring, (place - s + n) % n)],
            dst_ref=slots.at[ring, s % 3],
            send_sem=rs_send.at[ring, s % 3],
            recv_sem=rs_recv.at[ring, s % 3],
            device_id={"seq": target},
            device_id_type=MESH,
        )

    def scatter_step(s, carry):
        copies = []
        for ring, place, target, source in rings:

            @pl.when(s >= 3)
            def _():
                pl.semaphore_wait(credit.at[ring], 1)

            copy = scatter_copy(ring, place, target, s)
            copy.start()
            copies.append(copy)
        for (ring, place, target, source), copy in zip(rings, copies):
            copy.wait_recv()
            into = block(ring, (place - s - 1 + 2 * n) % n)
            total = o_ref[into] + slots[ring, s % 3].astype(jnp.float32)
            o_ref[into] = total
            low[into] = total.astype(low.dtype)
            copy.wait_send()

            @pl.when(s <= n - 5)
            def _():
                pl.semaphore_signal(credit.at[ring], 1, device_id={"seq": source}, device_id_type=MESH)

        return carry

    lax.fori_loop(0, n - 1, scatter_step, 0)
    for ring, place, target, source in rings:
        pl.semaphore_signal(done.at[ring], 1, device_id={"seq": source}, device_id_type=MESH)
    for ring, place, target, source in rings:
        final = block(ring, (place + 1) % n)
        r_ref[final] = o_ref[final].astype(r_ref.dtype)
    for ring, place, target, source in rings:
        pl.semaphore_wait(done.at[ring], 1)

    def gather_copy(ring, place, target, s):
        where = block(ring, (place + 1 - s + n) % n)
        return pltpu.make_async_remote_copy(
            src_ref=r_ref.at[where],
            dst_ref=r_ref.at[where],
            send_sem=ag_send.at[ring, s],
            recv_sem=ag_recv.at[ring, s],
            device_id={"seq": target},
            device_id_type=MESH,
        )

    def gather_step(s, carry):
        for ring, place, target, source in rings:

            @pl.when(s >= 1)
            def _():
                gather_copy(ring, place, target, s - 1).wait_recv()

            gather_copy(ring, place, target, s).start()

            @pl.when(s >= 1)
            def _():
                gather_copy(ring, place, target, s - 1).wait_send()

        return carry

    lax.fori_loop(0, n - 1, gather_step, 0)
    for ring, place, target, source in rings:
        last = gather_copy(ring, place, target, n - 2)
        last.wait_recv()
        last.wait_send()


def ring_sum(x, n):
    rows, lanes = x.shape
    size = rows // (2 * n)
    return pl.pallas_call(
        lambda *refs: ring_sum_kernel(n, *refs),
        out_shape=jax.ShapeDtypeStruct((rows, lanes), jnp.bfloat16),
        in_specs=[pl.BlockSpec(memory_space=pltpu.VMEM)],
        out_specs=pl.BlockSpec(memory_space=pltpu.VMEM),
        scratch_shapes=[
            pltpu.VMEM((rows, lanes), jnp.float32),
            pltpu.VMEM((rows, lanes), jnp.bfloat16),
            pltpu.VMEM((2, 3, size, lanes), jnp.bfloat16),
            pltpu.SemaphoreType.DMA((2, 3)),
            pltpu.SemaphoreType.DMA((2, 3)),
            pltpu.SemaphoreType.REGULAR((2,)),
            pltpu.SemaphoreType.REGULAR((2,)),
            pltpu.SemaphoreType.DMA((2, n - 1)),
            pltpu.SemaphoreType.DMA((2, n - 1)),
        ],
        compiler_params=pltpu.CompilerParams(collective_id=0, has_side_effects=True),
    )(x)


def sum_over_seq(parts):
    n = lax.axis_size("seq")
    flat = jnp.concatenate([part.reshape(-1) for part in parts])
    grain = 2 * n * 16 * 128
    padded = -(-flat.size // grain) * grain
    flat = jnp.pad(flat, (0, padded - flat.size)).reshape(padded // 128, 128)
    total = ring_sum(flat, n).astype(jnp.float32).reshape(-1)
    pieces = []
    start = 0
    for part in parts:
        pieces.append(total[start : start + part.size].reshape(part.shape))
        start += part.size
    return pieces


def adjoint_kernel(starts_ref, lengths_ref, pow_ref, coef_ref, masks_ref, g_ref, states_ref, drive_ref, dg_ref, sums_ref, lam):
    count = g_ref.shape[0]
    width = coef_ref.shape[1]
    pad = 8
    f_re = coef_ref[2:3, :]
    f_im = coef_ref[3:4, :]
    zero_rows = jnp.zeros((pad, 4 * width), jnp.float32)
    lam[0:pad, :] = zero_rows
    lam[pad + count : 2 * pad + count, :] = zero_rows

    def load(column):
        def get(t):
            return g_ref[pl.ds(t, 8), pl.ds(column, width)], g_ref[pl.ds(t, 8), pl.ds(column + width, width)]

        return get

    def store(column):
        def put(t, h_re, h_im):
            lam[pl.ds(pad + t, 8), pl.ds(column, width)] = h_re
            lam[pl.ds(pad + t, 8), pl.ds(column + width, width)] = h_im

        return put

    blocked_scan(count, width, pow_ref, starts_ref, lengths_ref, load(2 * width), load(0), store(0), store(2 * width))

    rows = 16

    def part(ref, start, column):
        return ref[pl.ds(start, rows), pl.ds(column, width)]

    def epilogue(k, sums):
        gp_re, gp_im, gf_re, gf_im = sums
        r0 = pl.multiple_of(k * rows, rows)
        live = masks_ref[pl.ds(r0, rows), 0:1]
        keep_prev = masks_ref[pl.ds(r0, rows), 1:2]
        keep_next = masks_ref[pl.ds(r0, rows), 2:3]
        lb_re = part(lam, pad + r0, 0)
        lb_im = part(lam, pad + r0, width)
        la_re = part(lam, pad + r0, 2 * width)
        la_im = part(lam, pad + r0, 3 * width)
        gu_re = la_re + lb_re
        gu_im = la_im + lb_im
        dg_ref[pl.ds(r0, rows), pl.ds(0, width)] = ((f_re * gu_re + f_im * gu_im) * live).astype(dg_ref.dtype)
        dg_ref[pl.ds(r0, rows), pl.ds(width, width)] = ((f_re * gu_im - f_im * gu_re) * live).astype(dg_ref.dtype)
        d_re = part(drive_ref, r0, 0) * live
        d_im = part(drive_ref, r0, width) * live
        gf_re = gf_re + d_re * gu_re + d_im * gu_im
        gf_im = gf_im + d_re * gu_im - d_im * gu_re
        a_re = part(states_ref, r0, 0) * keep_next
        a_im = part(states_ref, r0, width) * keep_next
        b_re = part(states_ref, r0, 2 * width) * keep_prev
        b_im = part(states_ref, r0, 3 * width) * keep_prev
        ahead_rows = lam[pl.ds(pad + r0, rows + 8), pl.ds(2 * width, 2 * width)][1 : rows + 1]
        behind_rows = lam[pl.ds(r0, rows + 8), pl.ds(0, 2 * width)][pad - 1 : pad - 1 + rows]
        na_re = ahead_rows[:, :width]
        na_im = ahead_rows[:, width:]
        pb_re = behind_rows[:, :width]
        pb_im = behind_rows[:, width:]
        gp_re = gp_re + a_re * na_re + a_im * na_im + b_re * pb_re + b_im * pb_im
        gp_im = gp_im + a_re * na_im - a_im * na_re + b_re * pb_im - b_im * pb_re
        return (gp_re, gp_im, gf_re, gf_im)

    block = jnp.zeros((rows, width), jnp.float32)
    sums = lax.fori_loop(0, count // rows, epilogue, (block, block, block, block))
    for k, value in enumerate(sums):
        sums_ref[k : k + 1, :] = jnp.sum(value, 0, keepdims=True)


def adjoint(starts, lengths, powers, coef, masks, states_grad, states, drive):
    count, quad = states_grad.shape
    width = quad // 4
    vmem = pl.BlockSpec(memory_space=pltpu.VMEM)
    smem = pl.BlockSpec(memory_space=pltpu.SMEM)
    return pl.pallas_call(
        adjoint_kernel,
        out_shape=(
            jax.ShapeDtypeStruct((count, 2 * width), jnp.bfloat16),
            jax.ShapeDtypeStruct((4, width), jnp.float32),
        ),
        in_specs=[smem, smem] + [vmem] * 6,
        out_specs=(vmem, vmem),
        scratch_shapes=[pltpu.VMEM((count + 16, 4 * width), jnp.float32)],
        cost_estimate=pl.CostEstimate(
            flops=60 * count * width, transcendentals=0, bytes_accessed=48 * count * width
        ),
    )(starts, lengths, powers, coef, masks, states_grad, states, drive)


def update(weight, gradient, velocity, average, rate, decay):
    adjusted = gradient + decay * weight
    velocity_new = momentum * velocity + adjusted
    change = -rate * (adjusted + momentum * velocity_new)
    weight_new = weight + change
    average_new = smoothing * average + (1.0 - smoothing) * weight_new
    return (weight_new, velocity_new, average_new, change)


def contract_rows(left, right):
    return lax.dot_general(
        left, right, (((0,), (0,)), ((), ())), preferred_element_type=jnp.float32
    )


def contract_cols(left, right):
    return lax.dot_general(
        left, right, (((1,), (1,)), ((), ())), preferred_element_type=jnp.float32
    )


def gather_feat(value, axis):
    return lax.all_gather(value, "feat", axis=axis, tiled=True)


def split_exact(value):
    high = lax.reduce_precision(value, exponent_bits=8, mantissa_bits=7)
    rest = value - high
    middle = lax.reduce_precision(rest, exponent_bits=8, mantissa_bits=7)
    little = rest - middle
    return jnp.concatenate([high, middle, little], 0).astype(jnp.bfloat16)


def join_exact(pieces):
    third = pieces.shape[0] // 3
    pieces = pieces.astype(jnp.float32)
    return pieces[:third] + (pieces[third : 2 * third] + pieces[2 * third :])


def body(
    activations_in,
    cotangent,
    seq_start,
    seq_length,
    input_matrix,
    output_matrix,
    gate_matrix,
    feature_vectors,
    state_vectors,
    velocity_input,
    velocity_output,
    velocity_gate,
    velocity_feature,
    velocity_state,
    average_input,
    average_output,
    average_gate,
    average_feature,
    average_state,
):
    count = activations_in.shape[0]
    shard = activations_in.shape[1]
    layers = input_matrix.shape[0]
    width = state_vectors.shape[2]
    me = lax.axis_index("feat")
    offset = me * shard

    def mine(value):
        return lax.dynamic_slice_in_dim(value, offset, shard, axis=value.ndim - 1)

    alive, carry_prev, carry_next = masks_of(seq_start, seq_length, count)
    zero = jnp.zeros((1,), jnp.float32)
    after_next = jnp.concatenate([zero, carry_next[:-1]])
    before_prev = jnp.concatenate([carry_prev[1:], zero])
    mask_columns = jnp.stack([alive, carry_prev, carry_next, jnp.zeros_like(alive)], 1)


    in_all = gather_feat(input_matrix.astype(jnp.bfloat16), 1)
    rows_out = output_matrix.shape[1]
    paired = [
        gather_feat(jnp.concatenate([output_matrix[k], gate_matrix[k]], 0).astype(jnp.bfloat16), 1)
        for k in range(layers)
    ]
    out_all = [pair[:rows_out] for pair in paired]
    gate_all = [pair[rows_out:] for pair in paired]
    feature_pieces = split_exact(feature_vectors.reshape(-1, activations_in.shape[1]))
    feature_rows = feature_pieces.shape[0]
    feature_pad = -(-feature_rows // 16) * 16
    feature_pieces = jnp.pad(feature_pieces, ((0, feature_pad - feature_rows), (0, 0)))
    first = gather_feat(jnp.concatenate([activations_in, feature_pieces], 0), 1)
    stream = first[:count].astype(jnp.float32)
    feature_all = join_exact(first[count : count + feature_rows]).reshape(feature_vectors.shape[:-1] + (-1,))

    saved = []
    for layer in range(layers):
        in_low = in_all[layer]
        out_low = out_all[layer]
        gate_low = gate_all[layer]
        feature_row = feature_all[layer]
        pole_re, pole_im, factor_re, factor_im = coefficients(state_vectors[layer])
        center = jnp.mean(stream, 1, keepdims=True)
        spread = stream - center
        scale = lax.rsqrt(jnp.mean(spread * spread, 1, keepdims=True) + epsilon)
        unit = spread * scale
        normed = unit * feature_row[0] + feature_row[1]
        normed_low = normed.astype(jnp.bfloat16)
        drive = jnp.dot(normed_low, in_low, preferred_element_type=jnp.float32)
        drive_re = drive[:, :width]
        drive_im = drive[:, width:]
        source = jnp.concatenate(
            [
                (drive_re * factor_re - drive_im * factor_im) * alive[:, None],
                (drive_re * factor_im + drive_im * factor_re) * alive[:, None],
            ],
            1,
        )
        states = recurrence(seq_start, seq_length, pole_powers(pole_re, pole_im), source)
        states_low = states.astype(jnp.bfloat16)
        mixed = (
            jnp.dot(states_low, out_low, preferred_element_type=jnp.float32)
            + feature_row[2] * normed
        )
        cdf = (lax.erf(mixed * (1.0 / math.sqrt(2.0))) + 1.0) / 2.0
        act = mixed * cdf
        act_low = act.astype(jnp.bfloat16)
        pre = jnp.dot(act_low, gate_low, preferred_element_type=jnp.float32) + feature_row[3]
        saved.append((scale, unit, normed_low, drive, states, states_low, mixed, act, act_low, pre, cdf))
        stream = stream + act * jax.nn.sigmoid(pre)

    grad = gather_feat(cotangent, 1).astype(jnp.float32) * alive[:, None]
    layer_grads = [None] * layers
    for layer in reversed(range(layers)):
        scale, unit, normed_low, drive, states, states_low, mixed, act, act_low, pre, cdf = saved[layer]
        in_low = in_all[layer]
        out_low = out_all[layer]
        gate_low = gate_all[layer]
        feature_row = feature_all[layer]
        state_row = state_vectors[layer]
        pole_re, pole_im, factor_re, factor_im = coefficients(state_row)
        gate = jax.nn.sigmoid(pre)
        pre_grad = (grad * act * gate * (1.0 - gate)).astype(jnp.bfloat16)
        gate_grad = contract_rows(act_low, mine(pre_grad))
        gate_bias_grad = jnp.sum(pre_grad.astype(jnp.float32), 0)
        act_grad = grad * gate + contract_cols(pre_grad, gate_low)
        density = jnp.exp(mixed * mixed * -0.5) * (1.0 / math.sqrt(2.0 * math.pi))
        mixed_grad = act_grad * (cdf + mixed * density)
        normed = unit * feature_row[0] + feature_row[1]
        skip_grad = jnp.sum(mixed_grad * normed, 0)
        mixed_low = mixed_grad.astype(jnp.bfloat16)
        out_grad = contract_rows(states_low, mine(mixed_low))
        states_grad = contract_cols(mixed_low, out_low)
        coef = jnp.stack([pole_re, pole_im, factor_re, factor_im])
        drive_low, sums = adjoint(
            seq_start,
            seq_length,
            pole_powers(pole_re, -pole_im),
            coef,
            mask_columns,
            states_grad,
            states,
            drive,
        )
        gp_re, gp_im, gf_re, gf_im = sums[0], sums[1], sums[2], sums[3]
        row_grad = jax.vjp(coefficients, state_row)[1]((gp_re, gp_im, gf_re, gf_im))[0]
        in_grad = contract_rows(mine(normed_low), drive_low)
        normed_grad = mixed_grad * feature_row[2] + jnp.dot(
            drive_low, in_low.T, preferred_element_type=jnp.float32
        )
        gain_grad = jnp.sum(normed_grad * unit, 0)
        bias_grad = jnp.sum(normed_grad, 0)
        unit_grad = normed_grad * feature_row[0]
        first_mean = jnp.mean(unit_grad, 1, keepdims=True)
        second_mean = jnp.mean(unit_grad * unit, 1, keepdims=True)
        grad = grad + scale * (unit_grad - first_mean - unit * second_mean)
        feature_grad = mine(jnp.stack([gain_grad, bias_grad, skip_grad, gate_bias_grad]))
        layer_grads[layer] = (in_grad, out_grad, gate_grad, feature_grad, row_grad)
    stacked_in = jnp.stack([entry[0] for entry in layer_grads])
    stacked_out = jnp.stack([entry[1] for entry in layer_grads])
    stacked_gate = jnp.stack([entry[2] for entry in layer_grads])
    stacked_feature = jnp.stack([entry[3] for entry in layer_grads])
    stacked_state = jnp.stack([entry[4] for entry in layer_grads])
    summed = sum_over_seq((stacked_in, stacked_out, stacked_gate, stacked_feature, stacked_state))
    factor = 1.0 / math.sqrt(count * lax.axis_size("seq"))
    grad_in = summed[0] * factor
    grad_out = summed[1] * factor
    grad_gate = summed[2] * factor
    grad_feature = summed[3] * factor
    grad_state = summed[4] * factor
    new_in = update(input_matrix, grad_in, velocity_input, average_input, slow_rate, 0.0)
    new_out = update(output_matrix, grad_out, velocity_output, average_output, slow_rate, 0.0)
    new_gate = update(gate_matrix, grad_gate, velocity_gate, average_gate, main_rate, weight_decay)
    new_feature = update(
        feature_vectors, grad_feature, velocity_feature, average_feature, main_rate, weight_decay
    )
    new_state = update(state_vectors, grad_state, velocity_state, average_state, slow_rate, 0.0)
    return (
        mine(stream),
        mine(grad),
        grad_in,
        grad_out,
        grad_gate,
        grad_feature,
        grad_state,
        new_in[0],
        new_out[0],
        new_gate[0],
        new_feature[0],
        new_state[3],
        new_in[1],
        new_out[1],
        new_gate[1],
        new_feature[1],
        new_state[1],
        new_in[2],
        new_out[2],
        new_gate[2],
        new_feature[2],
        new_state[2],
    )


def solution(mesh):
    feat = P(None, None, "feat")
    rows = P(None, "feat", None)
    tokens = P("seq", "feat")
    return jax.shard_map(
        body,
        mesh=mesh,
        in_specs=(
            tokens,
            tokens,
            P("seq"),
            P("seq"),
            rows,
            feat,
            feat,
            feat,
            P(),
            rows,
            feat,
            feat,
            feat,
            P(),
            rows,
            feat,
            feat,
            feat,
            P(),
        ),
        out_specs=(
            tokens,
            tokens,
            rows,
            feat,
            feat,
            feat,
            P(),
            rows,
            feat,
            feat,
            feat,
            P(),
            rows,
            feat,
            feat,
            feat,
            P(),
            rows,
            feat,
            feat,
            feat,
            P(),
        ),
        check_vma=False,
    )
```
